32 devices in a mesh: seq: 4 (over y, x), fsdp: 8 (over z, core).
Axes of the slice: x: 2, y: 2, z: 4, core: 2. Of those that a mesh axis runs over, the one named last changes fastest.
Arguments:
- tokens: bfloat16 [8, 1024, 1024], P('fsdp', 'seq'), may hold values from -6 to 6
- segments: int32 [8, 1024], P('fsdp', 'seq'), may hold values from 0 to 2, as said below
- qkv_weight: bfloat16 [1024, 3072], P(('seq', 'fsdp')), may hold values from -0.1875 to 0.1875
- out_weight: bfloat16 [1024, 1024], P(('seq', 'fsdp')), may hold values from -0.1875 to 0.1875
- up_weight: bfloat16 [1024, 4096], P(('seq', 'fsdp')), may hold values from -0.1875 to 0.1875
- up_bias: bfloat16 [4096], P(('seq', 'fsdp')), may hold values from -3 to 3
- down_weight: bfloat16 [4096, 1024], P(('seq', 'fsdp')), may hold values from -0.09375 to 0.09375
- first_gain: bfloat16 [1024], P(('seq', 'fsdp')), may hold values from 0.5 to 1.5
- first_shift: bfloat16 [1024], P(('seq', 'fsdp')), may hold values from -3 to 3
- second_gain: bfloat16 [1024], P(('seq', 'fsdp')), may hold values from 0.5 to 1.5
- second_shift: bfloat16 [1024], P(('seq', 'fsdp')), may hold values from -3 to 3
- third_gain: bfloat16 [1024], P(('seq', 'fsdp')), may hold values from 0.5 to 1.5
- third_shift: bfloat16 [1024], P(('seq', 'fsdp')), may hold values from -3 to 3
- fourth_gain: bfloat16 [1024], P(('seq', 'fsdp')), may hold values from 0.5 to 1.5
- fourth_shift: bfloat16 [1024], P(('seq', 'fsdp')), may hold values from -3 to 3
- out_cotangent: bfloat16 [8, 1024, 1024], P('fsdp', 'seq'), may hold values from -6 to 6
Outputs:
- layer_out: bfloat16 [8, 1024, 1024], P('fsdp', 'seq')
- tokens_grad: float32 [8, 1024, 1024], P('fsdp', 'seq')
- qkv_weight_grad: float32 [1024, 3072], P(('seq', 'fsdp'))
- out_weight_grad: float32 [1024, 1024], P(('seq', 'fsdp'))
- up_weight_grad: float32 [1024, 4096], P(('seq', 'fsdp'))
- up_bias_grad: float32 [4096], P(('seq', 'fsdp'))
- down_weight_grad: float32 [4096, 1024], P(('seq', 'fsdp'))
- first_gain_grad: float32 [1024], P(('seq', 'fsdp'))
- first_shift_grad: float32 [1024], P(('seq', 'fsdp'))
- second_gain_grad: float32 [1024], P(('seq', 'fsdp'))
- second_shift_grad: float32 [1024], P(('seq', 'fsdp'))
- third_gain_grad: float32 [1024], P(('seq', 'fsdp'))
- third_shift_grad: float32 [1024], P(('seq', 'fsdp'))
- fourth_gain_grad: float32 [1024], P(('seq', 'fsdp'))
- fourth_shift_grad: float32 [1024], P(('seq', 'fsdp'))
The draws below stay inside these ranges and needn't reach their ends.
Inputs may be any that keep to these rules, and one draw needn't show every extreme that they name: `segments`: within a sequence document numbers never fall; each sequence holds 3 documents of 200 to 512 tokens, one of exactly 512.
All inputs are finite; a program needn't handle non-finite values.
Results may differ from the reference program's by a relative error of at most 0.012.
Values may be sent and summed in bfloat16 or wider, within the bound.
A program may use at most 192 MiB of HBM per device.

```python
import jax
import jax.numpy as jnp
from jax import lax

D = 1024
HEADS = 16
HEAD_DIM = 64
FF = 4096
DOC_LEAST = 200
LENGTH = 1024
SEQS = 8
SEG_MOST = 512


def draw_segments(key, part):
    seq_keys = jax.random.split(key, SEQS)

    def one_sequence(seq_key):
        cut_key, spot_key = jax.random.split(seq_key)
        remain = LENGTH - SEG_MOST
        cut = jax.random.randint(cut_key, (), DOC_LEAST, remain - DOC_LEAST + 1, dtype=jnp.int32)
        spot = jax.random.randint(spot_key, (), 0, 3, dtype=jnp.int32)
        first = jnp.where(spot == 0, SEG_MOST, cut).astype(jnp.int32)
        second = jnp.where(spot == 1, SEG_MOST, jnp.where(spot == 0, cut, remain - cut)).astype(jnp.int32)
        places = jnp.arange(LENGTH, dtype=jnp.int32)
        return (places >= first).astype(jnp.int32) + (places >= first + second).astype(jnp.int32)
    return jax.vmap(one_sequence)(seq_keys)


def strengthened(values, key, source, target, blocks, factor):
    def block_of(axis_at):
        return (jnp.arange(values.shape[axis_at]) // (values.shape[axis_at] // blocks)).reshape((-1,) + (1,) * (values.ndim - 1 - axis_at))

    first = jax.random.permutation(key, blocks)[block_of(target)]
    other_side = (block_of(target) + blocks // 2) % blocks
    return jnp.where((block_of(source) == first) | (block_of(source) == other_side), factor * values, values)


def levels(rng, extent, cuts, smallest, high):
    def one(dim, parts):
        steps = jax.random.uniform(jax.random.fold_in(jax.random.fold_in(rng, 6), dim), (parts,), jnp.float32, smallest / len(cuts), high / len(cuts))
        return jnp.repeat(jnp.exp(steps), extent[dim] // parts).reshape((-1,) + (1,) * (len(extent) - dim - 1))

    level = one(*cuts[0])
    for cut in cuts[1:]:
        level = level * one(*cut)
    return level


def gaussian(rng, extent, deviation, bound, cuts=(), kind=jnp.bfloat16):
    factor_of = levels(rng, extent, cuts, -0.22, 0.18) if cuts else 1.0
    entries = jax.random.normal(rng, extent, jnp.float32) * deviation * factor_of
    return jnp.minimum(jnp.maximum(entries, -bound), bound).astype(kind)


def bell_draw_with(own_key, dims, width, limit, shards, heavy, kind=jnp.bfloat16):
    drawn = width * jax.random.normal(own_key, dims, jnp.float32)
    if shards:
        drawn = drawn * levels(own_key, dims, shards, -0.22, 0.18)
    return jnp.clip(strengthened(drawn, jax.random.fold_in(own_key, 3), *heavy), -limit, limit).astype(kind)


def setup_inputs(seed: int = 0) -> dict:
    splits = jax.random.split(jax.random.key(seed), 17)
    tokens = gaussian(splits[0], (SEQS, LENGTH, D), 1.0, 6.0, ((0, 8), (1, 4)))
    segments = draw_segments(jax.random.fold_in(splits[16], 71), 0)
    qkv_weight = gaussian(splits[2], (D, 3 * D), D ** -0.5, 0.1875, ((0, 32),))
    out_weight = gaussian(splits[3], (D, D), D ** -0.5, 0.1875, ((0, 32),))
    up_weight = gaussian(splits[4], (D, FF), D ** -0.5, 0.1875, ((0, 32),))
    up_bias = gaussian(splits[5], (FF,), 0.5, 3.0, ((0, 32),))
    down_weight = gaussian(splits[6], (FF, D), FF ** -0.5, 0.09375, ((0, 32),))
    first_gain = jnp.clip(1.0 + 0.1 * jax.random.normal(splits[7], (D,), jnp.float32), 0.5, 1.5).astype(jnp.bfloat16)
    first_shift = gaussian(splits[8], (D,), 0.5, 3.0, ((0, 32),))
    second_gain = jnp.clip(1.0 + 0.1 * jax.random.normal(splits[9], (D,), jnp.float32), 0.5, 1.5).astype(jnp.bfloat16)
    second_shift = gaussian(splits[10], (D,), 0.5, 3.0, ((0, 32),))
    third_gain = jnp.clip(1.0 + 0.1 * jax.random.normal(splits[11], (D,), jnp.float32), 0.5, 1.5).astype(jnp.bfloat16)
    third_shift = gaussian(splits[12], (D,), 0.5, 3.0, ((0, 32),))
    fourth_gain = jnp.clip(1.0 + 0.1 * jax.random.normal(splits[13], (D,), jnp.float32), 0.5, 1.5).astype(jnp.bfloat16)
    fourth_shift = gaussian(splits[14], (D,), 0.5, 3.0, ((0, 32),))
    out_cotangent = bell_draw_with(splits[15], (SEQS, LENGTH, D), 1.0, 6.0, ((0, 8), (1, 4)), (0, 2, 8, 2.0))
    return dict(tokens=tokens, segments=segments, qkv_weight=qkv_weight, out_weight=out_weight, up_weight=up_weight, up_bias=up_bias, down_weight=down_weight, first_gain=first_gain, first_shift=first_shift, second_gain=second_gain, second_shift=second_shift, third_gain=third_gain, third_shift=third_shift, fourth_gain=fourth_gain, fourth_shift=fourth_shift, out_cotangent=out_cotangent)


@jax.custom_vjp
def low(v):
    return lax.optimization_barrier(v.astype(jnp.bfloat16)).astype(jnp.float32)

@jax.custom_vjp
def low_back(v):
    return v

def low_keep(v):
    return (low(v), None)

def low_pass(kept, grad):
    return (grad,)

def back_keep(v):
    return (v, None)

def back_low(kept, grad):
    return (low(grad),)
low.defvjp(low_keep, low_pass)
low_back.defvjp(back_keep, back_low)

def matmul_high(left, right):
    return jnp.dot(left, right, precision=lax.Precision.HIGHEST, preferred_element_type=jnp.float32)

def layer_norm(value, gain, shift):
    center = value - lax.optimization_barrier(jnp.mean(value, -1, keepdims=True))
    spread = lax.optimization_barrier(jnp.mean(center * center, -1, keepdims=True))
    return center * lax.rsqrt(spread + 1e-05) * gain + shift

def forward_one(inputs, segment, params):
    qkv_w, out_w, up_w, up_b, down_w, gain_a, shift_a, gain_b, shift_b, gain_c, shift_c, gain_d, shift_d = params
    length = inputs.shape[0]
    normed = low(layer_norm(inputs, gain_a, shift_a))
    triple = low(low_back(matmul_high(normed, qkv_w)))
    heads = triple.reshape(length, 3, HEADS, HEAD_DIM).transpose(1, 2, 0, 3)
    places = jnp.arange(length)
    allowed = (segment[:, None] == segment[None, :]) & (places[None, :] <= places[:, None])

    def one_head(trio):
        query, key_rows, value_rows = trio
        scores = low_back(matmul_high(query, key_rows.T) * 0.125)
        scores = jnp.where(allowed, scores, -jnp.inf)
        expo = jnp.exp(scores - lax.optimization_barrier(jnp.max(scores, -1, keepdims=True)))
        probs = low(expo / lax.optimization_barrier(jnp.sum(expo, -1, keepdims=True)))
        return matmul_high(probs, value_rows)
    attended = lax.map(jax.checkpoint(one_head), (heads[0], heads[1], heads[2]))
    attended = low(low_back(attended.transpose(1, 0, 2).reshape(length, HEADS * HEAD_DIM)))
    branch = low_back(matmul_high(attended, out_w))
    middle = inputs + layer_norm(branch, gain_b, shift_b)
    inner = low(layer_norm(middle, gain_c, shift_c))
    pre = low_back(matmul_high(inner, up_w) + up_b)
    activ = low(jax.nn.gelu(pre, approximate=True))
    mixed = low_back(matmul_high(activ, down_w))
    return middle + layer_norm(mixed, gain_d, shift_d)

def reference(tokens, segments, qkv_weight, out_weight, up_weight, up_bias, down_weight, first_gain, first_shift, second_gain, second_shift, third_gain, third_shift, fourth_gain, fourth_shift, out_cotangent):
    params = tuple((p.astype(jnp.float32) for p in (qkv_weight, out_weight, up_weight, up_bias, down_weight, first_gain, first_shift, second_gain, second_shift, third_gain, third_shift, fourth_gain, fourth_shift)))

    def one_sequence(totals, item):
        inputs, segment, cotangent = item
        result, pull = jax.vjp(lambda vals, prms: forward_one(vals, segment, prms), inputs.astype(jnp.float32), params)
        grad_inputs, grad_params = pull(cotangent.astype(jnp.float32))
        totals = jax.tree.map(jnp.add, totals, grad_params)
        return (totals, (result.astype(jnp.bfloat16), grad_inputs))
    zeros = tuple((jnp.zeros(p.shape, jnp.float32) for p in params))
    totals, (results, grads) = lax.scan(one_sequence, zeros, (tokens, segments, out_cotangent))
    return (results, grads, totals[0], totals[1], totals[2], totals[3], totals[4], totals[5], totals[6], totals[7], totals[8], totals[9], totals[10], totals[11], totals[12])
```

```python
from functools import partial

import jax
import jax.numpy as jnp
from jax import lax
from jax.sharding import PartitionSpec as P

HEAD_DIM = 64
F32 = jnp.float32
BF16 = jnp.bfloat16


def layer_norm(value, gain, shift):
    center = value - jnp.mean(value, -1, keepdims=True)
    spread = jnp.mean(center * center, -1, keepdims=True)
    return center * lax.rsqrt(spread + 1e-05) * gain + shift


def norm_pull(value, gain, grad):
    center = value - jnp.mean(value, -1, keepdims=True)
    spread = jnp.mean(center * center, -1, keepdims=True)
    scale = lax.rsqrt(spread + 1e-05)
    unit = center * scale
    pulled = grad * gain
    first = jnp.mean(pulled, -1, keepdims=True)
    second = jnp.mean(pulled * unit, -1, keepdims=True)
    return scale * (pulled - first - unit * second), jnp.sum(grad * unit, 0), jnp.sum(grad, 0)


def dot(left, right, dims):
    return lax.dot_general(left, right, (dims, ((), ())), preferred_element_type=F32)


def attention(triple, segment_all, grad_of):
    length = triple.shape[0]
    group = triple.shape[1] // (3 * HEAD_DIM)
    heads = triple.reshape(length, 3, group, HEAD_DIM)
    query, keys, values = heads[:, 0], heads[:, 1], heads[:, 2]
    places = jnp.arange(length, dtype=jnp.int32)
    allowed = (segment_all[:, None] == segment_all[None, :]) & (
        places[None, :] <= places[:, None]
    )
    scores = jnp.einsum("qhd,khd->hqk", query, keys, preferred_element_type=F32) * 0.125
    scores = jnp.where(allowed[None], scores, -jnp.inf)
    row_max = jnp.max(scores, -1, keepdims=True)
    expo = jnp.exp(scores - row_max)
    totals = jnp.sum(expo, -1, keepdims=True)
    probs = expo / totals
    probs_low = probs.astype(BF16)
    attended = jnp.einsum("hqk,khd->qhd", probs_low, values, preferred_element_type=F32)
    attended = attended.astype(BF16).reshape(length, -1)

    def pull(grad):
        grad = grad.reshape(length, group, HEAD_DIM)
        grad_probs = jnp.einsum("qhd,khd->hqk", grad, values, preferred_element_type=F32)
        inner_sum = jnp.sum(probs * grad_probs, -1, keepdims=True)
        grad_scores = (probs * (grad_probs - inner_sum)).astype(BF16)
        grad_query = (
            jnp.einsum("hqk,khd->qhd", grad_scores, keys, preferred_element_type=F32) * 0.125
        )
        grad_keys = (
            jnp.einsum("hqk,qhd->khd", grad_scores, query, preferred_element_type=F32) * 0.125
        )
        grad_values = jnp.einsum("hqk,qhd->khd", probs_low, grad, preferred_element_type=F32)
        stacked = jnp.stack([grad_query, grad_keys, grad_values], 1)
        return stacked.astype(BF16).reshape(length, -1)

    return attended, pull


def on_device(
    tokens,
    segments,
    qkv_weight,
    out_weight,
    up_weight,
    up_bias,
    down_weight,
    first_gain,
    first_shift,
    second_gain,
    second_shift,
    third_gain,
    third_shift,
    fourth_gain,
    fourth_shift,
    out_cotangent,
):
    n_seq = lax.axis_size("seq")
    n_fsdp = lax.axis_size("fsdp")
    width = tokens.shape[2]

    def columns(weight, parts):
        rows = weight.shape[0]
        cut = weight.reshape(rows, parts, n_seq, -1).transpose(2, 0, 1, 3).reshape(n_seq, rows, -1)
        cut = lax.all_to_all(cut, "seq", split_axis=0, concat_axis=0, tiled=True)
        whole = lax.all_gather(cut, "fsdp", axis=1, tiled=True)
        return whole.reshape(n_seq * n_fsdp * rows, -1)

    def columns_back(grad, parts):
        rows = grad.shape[0] // (n_seq * n_fsdp)
        cut = grad.astype(BF16).reshape(n_seq, n_fsdp, rows, -1).transpose(1, 0, 2, 3)
        cut = lax.psum_scatter(cut, "fsdp", scatter_dimension=0, tiled=True)[0]
        cut = lax.all_to_all(cut, "seq", split_axis=0, concat_axis=0, tiled=True)
        cut = cut.reshape(n_seq, rows, parts, -1).transpose(1, 2, 0, 3)
        return cut.reshape(rows, -1).astype(F32)

    def rows_back(grad):
        return lax.psum_scatter(
            grad.astype(BF16), "fsdp", scatter_dimension=0, tiled=True
        ).astype(F32)

    def spread_rows(value):
        return lax.all_gather(value, "seq", axis=0, tiled=True)

    def sum_rows(value):
        return lax.psum_scatter(
            value.astype(BF16), "seq", scatter_dimension=0, tiled=True
        ).astype(F32)

    segment_all = lax.all_gather(segments[0], "seq", axis=0, tiled=True)
    small = jnp.stack(
        [
            first_gain,
            first_shift,
            second_gain,
            second_shift,
            third_gain,
            third_shift,
            fourth_gain,
            fourth_shift,
        ]
    )
    small = lax.all_gather(small, ("seq", "fsdp"), axis=1, tiled=True).astype(F32)
    gain_a, shift_a, gain_b, shift_b, gain_c, shift_c, gain_d, shift_d = small
    qkv_w = columns(qkv_weight, 3)
    out_w = lax.all_gather(out_weight, "fsdp", axis=0, tiled=True)
    up_w = columns(up_weight, 1)
    up_b = lax.all_gather(up_bias, "fsdp", axis=0, tiled=True).astype(F32)
    down_w = lax.all_gather(down_weight, "fsdp", axis=0, tiled=True)

    inputs = tokens[0].astype(F32)
    cotangent = out_cotangent[0].astype(F32)
    normed = spread_rows(layer_norm(inputs, gain_a, shift_a).astype(BF16))
    triple = dot(normed, qkv_w, ((1,), (0,))).astype(BF16)
    attended, attend_pull = attention(triple, segment_all, None)
    branch = sum_rows(dot(attended, out_w, ((1,), (0,))))
    middle = inputs + layer_norm(branch, gain_b, shift_b)
    inner = spread_rows(layer_norm(middle, gain_c, shift_c).astype(BF16))
    pre = dot(inner, up_w, ((1,), (0,))) + up_b
    activ = jax.nn.gelu(pre, approximate=True).astype(BF16)
    mixed = sum_rows(dot(activ, down_w, ((1,), (0,))))
    result = middle + layer_norm(mixed, gain_d, shift_d)

    grad_mixed, grad_gain_d, grad_shift_d = norm_pull(mixed, gain_d, cotangent)
    grad_mixed = spread_rows(grad_mixed.astype(BF16))
    grad_activ = dot(grad_mixed, down_w, ((1,), (1,)))
    _, gelu_pull = jax.vjp(partial(jax.nn.gelu, approximate=True), pre)
    grad_pre = gelu_pull(grad_activ)[0].astype(BF16)
    grad_upbias = jnp.sum(grad_pre.astype(F32), 0)
    grad_inner = sum_rows(dot(grad_pre, up_w, ((1,), (1,))))
    grad_down = dot(activ, grad_mixed, ((0,), (0,)))
    grad_up = dot(inner, grad_pre, ((0,), (0,)))
    grad_side, grad_gain_c, grad_shift_c = norm_pull(middle, gain_c, grad_inner)
    grad_middle = cotangent + grad_side
    grad_branch, grad_gain_b, grad_shift_b = norm_pull(branch, gain_b, grad_middle)
    grad_branch = spread_rows(grad_branch.astype(BF16))
    grad_out = dot(attended, grad_branch, ((0,), (0,)))
    grad_attended = dot(grad_branch, out_w, ((1,), (1,))).astype(BF16)
    grad_triple = attend_pull(grad_attended)
    grad_qkv = dot(normed, grad_triple, ((0,), (0,)))
    grad_normed = sum_rows(dot(grad_triple, qkv_w, ((1,), (1,))))
    grad_first, grad_gain_a, grad_shift_a = norm_pull(inputs, gain_a, grad_normed)
    grad_inputs = grad_middle + grad_first

    small_grads = jnp.stack(
        [
            grad_gain_a,
            grad_shift_a,
            grad_gain_b,
            grad_shift_b,
            grad_gain_c,
            grad_shift_c,
            grad_gain_d,
            grad_shift_d,
        ]
    )
    small_grads = lax.psum_scatter(
        small_grads, ("seq", "fsdp"), scatter_dimension=1, tiled=True
    )
    grad_upbias = lax.psum_scatter(grad_upbias, "fsdp", scatter_dimension=0, tiled=True)
    return (
        result.astype(BF16)[None],
        grad_inputs[None],
        columns_back(grad_qkv, 3),
        rows_back(grad_out),
        columns_back(grad_up, 1),
        grad_upbias,
        rows_back(grad_down),
        small_grads[0],
        small_grads[1],
        small_grads[2],
        small_grads[3],
        small_grads[4],
        small_grads[5],
        small_grads[6],
        small_grads[7],
    )


def solution(mesh):
    rows = P(("seq", "fsdp"), None)
    vector = P(("seq", "fsdp"))
    acts = P("fsdp", "seq", None)
    placed = (acts, P("fsdp", "seq"), rows, rows, rows, vector, rows) + (vector,) * 8 + (acts,)
    return jax.shard_map(
        on_device,
        mesh=mesh,
        in_specs=placed,
        out_specs=(acts, acts, rows, rows, rows, vector, rows) + (vector,) * 8,
        check_vma=False,
    )
```

```python
from functools import partial

import jax
import jax.numpy as jnp
from jax import lax
from jax.experimental import pallas as pl
from jax.experimental.pallas import tpu as pltpu
from jax.sharding import PartitionSpec as P

HEAD_DIM = 64
F32 = jnp.float32
BF16 = jnp.bfloat16
NN = ((1,), (0,))
NT = ((1,), (1,))
NEG = -1e30
STEP = 32


def dot(left, right, dims=NN):
    return lax.dot_general(left, right, (dims, ((), ())), preferred_element_type=F32)


def unit_of(value):
    center = value - jnp.mean(value, -1, keepdims=True)
    scale = lax.rsqrt(jnp.mean(center * center, -1, keepdims=True) + 1e-05)
    return center * scale, scale


def pull_of(grad, gain, unit, scale):
    pulled = grad * gain
    first = jnp.mean(pulled, -1, keepdims=True)
    second = jnp.mean(pulled * unit, -1, keepdims=True)
    return scale * (pulled - first - unit * second)


def col_sum(value):
    return jnp.sum(value, 0, keepdims=True)


def layer_kernel(
    inside,
    n_f,
    tokens, seg_in, small_in, cot_in, qkv_in, out_in, up_in, down_in,
    result, tgrad, gqkv, gout, gup, gdown, gsmall,
    tok, normed, inner, gmix, gbr,
    qkv_w, out_w, up_w, down_w,
    segs, small_f, small_s, params, bias_row,
    triple, probs, attended, mask, activ, dgelu,
    part, land_a, land_b,
    branch, middle, gmid, cot,
    gtri, gatt, dkt, dvt, att_t,
    gw_qkv, gw_out, gw_up, gw_down,
    lp_qkv, lp_out, lp_up, lp_down,
    lz_qkv, lz_out, lz_up, lz_down,
    fin_qkv, fin_up,
    sg_s, sg_land_s, sg_f, sg_land_f,
    ag_send, ag_recv, rs_send, rs_recv,
    w_send, w_recv, p_send, p_recv,
    col_send, col_recv, col_local, upc_send, upc_recv,
    seg_send, seg_recv, sf_send, sf_recv, ss_send, ss_recv,
    loc_sem,
    gp_send, gp_recv, gz_send, gz_recv,
    gc_send, gc_recv, gu_send, gu_recv,
    ts_send, ts_recv, tf_send, tf_recv,
):
    rows, width = tokens.shape
    half = rows // 2
    group = out_w.shape[1]
    heads = group // HEAD_DIM
    window = probs.shape[3]
    s = lax.axis_index("seq")
    f = lax.axis_index("fsdp")
    x, y = s % 2, s // 2
    z, c = f // 2, f % 2

    def block(rel):
        return 2 * ((y + rel // 2) % 2) + (x + rel % 2) % 2

    sx, sy, sd = block(1), block(2), block(3)

    def remote(src, dst, send, recv, to_s, to_f):
        return pltpu.make_async_remote_copy(
            src_ref=src, dst_ref=dst, send_sem=send, recv_sem=recv,
            device_id=(to_s, to_f), device_id_type=pl.DeviceIdType.MESH,
        )

    class Gather:
        def __init__(self, full, index):
            self.full, self.index = full, index

        def piece(self, b, h):
            return self.full.at[b, pl.ds(h * half, half)]

        def copy(self, i, b, h, to, src=None):
            dst = self.piece(b, h)
            return remote(
                dst if src is None else src, dst,
                ag_send.at[self.index, i], ag_recv.at[self.index, i], to, f,
            )

        def start(self, src=None):
            def cut(h):
                return None if src is None else src.at[pl.ds(h * half, half)]

            self.copy(0, s, 0, sx, cut(0)).start()
            self.copy(1, s, 1, sy, cut(1)).start()
            self.copy(2, s, 1, sx, cut(1)).start()
            self.copy(3, s, 0, sy, cut(0)).start()

        def relay(self):
            self.copy(0, sx, 0, sx).wait_recv()
            self.copy(4, sx, 0, sy).start()
            self.copy(1, sy, 1, sy).wait_recv()
            self.copy(5, sy, 1, sx).start()

        def wait_x(self):
            self.copy(2, sx, 1, sx).wait_recv()

        def wait_y(self):
            self.copy(3, sy, 0, sy).wait_recv()

        def wait_d(self):
            self.copy(4, sd, 0, sy).wait_recv()
            self.copy(5, sd, 1, sx).wait_recv()

        def step(self, k):
            @pl.when(k == 1)
            def _():
                self.relay()
                self.wait_x()

            @pl.when(k == 2)
            def _():
                self.wait_y()

            @pl.when(k == 3)
            def _():
                self.wait_d()

        def drain(self):
            for i, (b, h, to) in enumerate(
                ((s, 0, sx), (s, 1, sy), (s, 1, sx), (s, 0, sy), (sx, 0, sy), (sy, 1, sx))
            ):
                self.copy(i, b, h, to).wait_send()

    class Scatter:
        plan = ((3, 0, 1), (1, 0, 1), (3, 1, 2), (2, 1, 2), (2, 0, 2), (1, 1, 1))

        def __init__(self, land, index):
            self.land, self.index = land, index

        def copy(self, i):
            rel, h, way = self.plan[i]
            return remote(
                part.at[rel, pl.ds(h * half, half)], self.land.at[i],
                rs_send.at[self.index, i], rs_recv.at[self.index, i],
                sx if way == 1 else sy, f,
            )

        def step(self, rel):
            @pl.when(rel == 3)
            def _():
                self.copy(0).start()
                self.copy(2).start()

            @pl.when(rel == 1)
            def _():
                self.copy(1).start()

            @pl.when(rel == 2)
            def _():
                self.copy(3).start()

        def relay(self):
            for arrived, i in ((0, 4), (2, 5)):
                self.copy(arrived).wait_recv()
                rel, h, _ = self.plan[i]

                def add(j, _, arrived=arrived, rel=rel, h=h):
                    here = pl.ds(pl.multiple_of(h * half + j * STEP, STEP), STEP)
                    there = pl.ds(pl.multiple_of(j * STEP, STEP), STEP)
                    total = part[rel, here].astype(F32) + self.land[arrived, there].astype(F32)
                    part[rel, here] = total.astype(BF16)
                    return 0

                lax.fori_loop(0, half // STEP, add, 0)
                self.copy(i).start()

        def wait(self):
            for i in (1, 3, 4, 5):
                self.copy(i).wait_recv()

        def total(self, j):
            per = half // STEP
            h = j // per
            there = pl.ds(pl.multiple_of((j % per) * STEP, STEP), STEP)
            here = pl.ds(pl.multiple_of(j * STEP, STEP), STEP)
            return (
                part[0, here].astype(F32)
                + self.land[1 + 2 * h, there].astype(F32)
                + self.land[4 + h, there].astype(F32)
            )

        def drain(self):
            for i in range(6):
                self.copy(i).wait_send()

    def by_rows(ref, size):
        def view(who):
            return ref.at[pl.ds(pl.multiple_of(who * size, size), size)]

        return view

    def by_cut(ref, size):
        def view(who):
            return ref.at[:, pl.ds(pl.multiple_of(who * size, size), size)]

        return view

    def peer(d):
        return 2 * ((z + d) % (n_f // 2)) + c

    def source(d):
        return 2 * ((z + n_f // 2 - d) % (n_f // 2)) + c

    partner = 2 * z + 1 - c
    far = range(1, n_f // 2)

    class Weight:
        def __init__(self, index, view):
            self.index, self.view = index, view

        def direct(self, d, who):
            return remote(
                self.view(who), self.view(who),
                w_send.at[self.index, d], w_recv.at[self.index, d], s, peer(d),
            )

        def across(self, d, who):
            return remote(
                self.view(who), self.view(who),
                p_send.at[self.index, d], p_recv.at[self.index, d], s, partner,
            )

        def start(self):
            for d in far:
                self.direct(d, f).start()
            self.across(0, f).start()

        def forward(self):
            for d in far:
                self.direct(d, source(d)).wait_recv()
                self.across(d, source(d)).start()

        def finish(self):
            self.across(0, partner).wait_recv()
            for d in far:
                who = source(d) + 1 - 2 * c
                self.across(d, who).wait_recv()

        def drain(self):
            for d in far:
                self.direct(d, f).wait_send()
                self.across(d, source(d)).wait_send()
            self.across(0, f).wait_send()

    class Shed:
        def __init__(self, index, gw, land_p, land_z):
            self.index, self.gw, self.land_p, self.land_z = index, gw, land_p, land_z

        def pair(self, to_z):
            return remote(
                self.gw.at[2 * to_z + 1 - c], self.land_p.at[to_z],
                gp_send.at[self.index, to_z], gp_recv.at[self.index, to_z], s, partner,
            )

        def along(self, d):
            return remote(
                self.gw.at[peer(d)], self.land_z.at[d - 1],
                gz_send.at[self.index, d], gz_recv.at[self.index, d], s, peer(d),
            )

        def add_pair(self, to_z):
            self.pair(to_z).wait_recv()
            who = 2 * to_z + c
            height = self.gw.shape[1]

            def add(j, _):
                at = pl.ds(pl.multiple_of(j * STEP, STEP), STEP)
                total = self.gw[who, at].astype(F32) + self.land_p[to_z, at].astype(F32)
                self.gw[who, at] = total.astype(BF16)
                return 0

            lax.fori_loop(0, height // STEP, add, 0)

        def middle(self):
            for d in far:
                self.add_pair((z + d) % (n_f // 2))
                self.along(d).start()
            self.add_pair(z)

        def wait(self):
            for d in far:
                self.along(d).wait_recv()

        def total(self, at):
            value = self.gw[f, at].astype(F32)
            for d in far:
                value = value + self.land_z[d - 1, at].astype(F32)
            return value

        def drain(self):
            def one(to_z, _):
                self.pair(to_z).wait_send()
                return 0

            lax.fori_loop(0, n_f // 2, one, 0)
            for d in far:
                self.along(d).wait_send()

    barrier = pltpu.get_barrier_semaphore()
    for who in (sx, sy, sd):
        pl.semaphore_signal(barrier, inc=1, device_id=(who, f), device_id_type=pl.DeviceIdType.MESH)
    n_peers = 3
    if inside:
        for d in range(1, n_f):
            pl.semaphore_signal(
                barrier, inc=1, device_id=(s, (f + d) % n_f), device_id_type=pl.DeviceIdType.MESH
            )
        n_peers += n_f - 1
    pl.semaphore_wait(barrier, n_peers)

    others = (sx, sy, sd)
    ag_tok = Gather(tok, 0)
    if inside:
        high = qkv_in.shape[0]
        high_d = down_in.shape[0]
        w_qkv = Weight(0, by_cut(qkv_w, high))
        w_out = Weight(1, by_rows(out_w.at[0], high))
        w_up = Weight(2, by_cut(up_w, high))
        w_down = Weight(3, by_rows(down_w, high_d))

        def qkv_copy(k, p, to):
            start = pl.multiple_of(p * width + to * group, 128)
            src = qkv_in.at[:, pl.ds(start, group)]
            dst = qkv_w.at[s, pl.ds(pl.multiple_of(f * high, high), high), pl.ds(p * group, group)]
            if k < 0:
                return pltpu.make_async_copy(src, dst, col_local.at[p])
            return remote(src, dst, col_send.at[k, p], col_recv.at[k, p], to, f)

        ff = up_w.shape[2]

        def up_copy(k, to):
            src = up_in.at[:, pl.ds(pl.multiple_of(to * ff, 128), ff)]
            dst = up_w.at[s, pl.ds(pl.multiple_of(f * high, high), high)]
            if k < 0:
                return pltpu.make_async_copy(src, dst, col_local.at[3])
            return remote(src, dst, upc_send.at[k], upc_recv.at[k], to, f)

        out_own = pltpu.make_async_copy(out_in, w_out.view(f), loc_sem.at[0])
        down_own = pltpu.make_async_copy(down_in, w_down.view(f), loc_sem.at[1])
        out_own.start()
        down_own.start()
        for p in range(3):
            for k, to in enumerate(others):
                qkv_copy(k, p, to).start()
            qkv_copy(-1, p, s).start()
    else:
        loads = [
            pltpu.make_async_copy(qkv_in, qkv_w, col_local.at[0]),
            pltpu.make_async_copy(up_in, up_w, col_local.at[3]),
            pltpu.make_async_copy(out_in, out_w, loc_sem.at[0]),
            pltpu.make_async_copy(down_in, down_w, loc_sem.at[1]),
        ]
        for load in loads:
            load.start()
    ag_tok.start(tokens)
    tok_own = pltpu.make_async_copy(tokens, tok.at[s], loc_sem.at[2])
    tok_own.start()
    cot_own = pltpu.make_async_copy(cot_in, cot, loc_sem.at[3])
    cot_own.start()
    seg_own = pltpu.make_async_copy(seg_in, segs.at[s], loc_sem.at[4])
    seg_own.start()

    def seg_copy(k, to):
        return remote(seg_in, segs.at[s], seg_send.at[k], seg_recv.at[k], to, f)

    for k, to in enumerate(others):
        seg_copy(k, to).start()

    if inside:
        small_f[f] = small_in[...]

        def small_copy(d):
            return remote(
                small_in, small_f.at[f], sf_send.at[d], sf_recv.at[d], s, (f + d) % n_f
            )

        for d in range(1, n_f):
            small_copy(d).start()
        out_own.wait()
        w_out.start()
        for p in range(3):
            qkv_copy(-1, p, s).wait()
            for k, to in enumerate(others):
                qkv_copy(k, p, to).wait_recv()
        w_qkv.start()
        for k, to in enumerate(others):
            up_copy(k, to).start()
        up_copy(-1, s).start()
        for d in range(1, n_f):
            remote(
                small_in, small_f.at[(f + n_f - d) % n_f], sf_send.at[d], sf_recv.at[d],
                s, (f + d) % n_f,
            ).wait_recv()
        per = n_f * high // 128
        each = n_f // per
        for t in range(per):
            value = small_f[t * each, 0:8]
            for e in range(1, each):
                value = value + small_f[t * each + e, 0:8]
            small_s[s, t] = value
        for e in range(n_f):
            bias_row[0:1, pl.ds(e * 128, 128)] = small_f[e, 8:9]

        def small_wide(k, to):
            return remote(small_s.at[s], small_s.at[s], ss_send.at[k], ss_recv.at[k], to, f)

        for k, to in enumerate(others):
            small_wide(k, to).start()
        for k, who in enumerate(others):
            remote(
                small_s.at[who], small_s.at[who], ss_send.at[k], ss_recv.at[k], who, f
            ).wait_recv()
        for b in range(4):
            for t in range(per):
                params[:, pl.ds((b * per + t) * 128, 128)] = small_s[b, t]
    else:
        params[...] = small_in[0:8]
        bias_row[...] = small_in[8:9, 0 : bias_row.shape[1]]

    def param(i):
        return params[i : i + 1, :]

    tok_own.wait()
    ag_tok.relay()

    def first_norm(b):
        def run(j, _):
            at = pl.ds(pl.multiple_of(j * STEP, STEP), STEP)
            unit, _s = unit_of(tok[b, at].astype(F32))
            normed[b, at] = (unit * param(0) + param(1)).astype(BF16)
            return 0

        lax.fori_loop(0, rows // STEP, run, 0)

    def norm_step(k, _):
        @pl.when(k == 1)
        def _():
            ag_tok.wait_x()

        @pl.when(k == 2)
        def _():
            ag_tok.wait_y()

        @pl.when(k == 3)
        def _():
            ag_tok.wait_d()

        first_norm(block(k))
        return 0

    lax.fori_loop(0, 4, norm_step, 0)
    if inside:
        w_qkv.forward()
        up_copy(-1, s).wait()
        for k, to in enumerate(others):
            up_copy(k, to).wait_recv()
        w_up.start()
        w_out.forward()
        w_qkv.finish()
    else:
        for load in loads:
            load.wait()

    def make_triple(b, _):
        value = dot(normed[b], qkv_w[...].reshape(width, 3 * group))
        triple[b, :, 0:group] = (value[:, 0:group] * 0.125).astype(BF16)
        triple[b, :, group : 3 * group] = value[:, group : 3 * group].astype(BF16)
        return 0

    lax.fori_loop(0, 4, make_triple, 0)
    if inside:
        w_out.finish()
        down_own.wait()
        w_down.start()

    seg_own.wait()
    for k, who in enumerate(others):
        remote(seg_in, segs.at[who], seg_send.at[k], seg_recv.at[k], who, f).wait_recv()
    seg_all = segs[...]

    def below(level):
        count = jnp.sum((seg_all < level).astype(F32), axis=0)
        return jnp.sum(count, axis=1, keepdims=True)

    bound_1, bound_2 = below(1), below(2)
    lane = lax.broadcasted_iota(jnp.int32, (1, 128), 1)
    left = (lane < HEAD_DIM).astype(F32)
    sides = (left.astype(BF16), (1.0 - left).astype(BF16))
    pick = lax.broadcasted_iota(jnp.int32, (rows, 128), 1) < HEAD_DIM
    blocks = window // rows

    def set_mask(r, first):
        i = (r * rows + lax.broadcasted_iota(jnp.int32, (rows, 128), 0)).astype(F32)
        start = jnp.where(i >= bound_2, bound_2, jnp.where(i >= bound_1, bound_1, 0.0))
        for t in range(window // 128):
            j = first * rows + t * 128 + lax.broadcasted_iota(jnp.int32, (rows, 128), 1)
            j = j.astype(F32)
            mask[:, t * 128 : (t + 1) * 128] = jnp.where((j <= i) & (j >= start), 0.0, NEG)

    def cut(r, part_at, p, count):
        at = pl.ds(part_at * group + p * 128, 128)
        return triple[pl.ds(r, count), :, at].reshape(count * rows, 128)

    rs_1 = Scatter(land_a, 0)

    def attend(i, _):
        rel = (1 - i // 2) + 2 * (1 - i % 2)
        r = block(rel)
        first = r // 3
        set_mask(r, first)
        for p in range(group // 128):
            query, keys, vals = cut(r, 0, p, 1), cut(first, 1, p, blocks), cut(first, 2, p, blocks)
            outs = []
            for e in range(2):
                scores = dot(query * sides[e], keys, NT) + mask[...]
                expo = jnp.exp(scores - jnp.max(scores, -1, keepdims=True))
                low = (expo * (1.0 / jnp.sum(expo, -1, keepdims=True))).astype(BF16)
                probs[r, 2 * p + e] = low
                outs.append(dot(low, vals))
            attended[r, :, p * 128 : (p + 1) * 128] = jnp.where(pick, outs[0], outs[1]).astype(BF16)
        part[rel] = dot(attended[r], out_w[0]).astype(BF16)
        rs_1.step(rel)
        return 0

    lax.fori_loop(0, 4, attend, 0)
    rs_1.relay()
    if inside:
        w_up.forward()
    rs_1.wait()

    def mid_norm(j, _):
        at = pl.ds(pl.multiple_of(j * STEP, STEP), STEP)
        value = rs_1.total(j)
        branch[at] = value
        unit, _s = unit_of(value)
        mid = tok[s, at].astype(F32) + (unit * param(2) + param(3))
        middle[at] = mid
        unit, _s = unit_of(mid)
        inner[s, at] = (unit * param(4) + param(5)).astype(BF16)
        return 0

    lax.fori_loop(0, rows // STEP, mid_norm, 0)
    ag_inner = Gather(inner, 1)
    ag_inner.start()
    rs_1.drain()
    if inside:
        w_up.finish()

    ff = up_w.shape[2]
    tile = 256
    rs_2 = Scatter(land_b, 1)

    def forward_step(k, _):
        ag_inner.step(k)
        r = block(k)

        def column(n, _):
            at = pl.ds(pl.multiple_of(n * tile, tile), tile)
            pre = dot(inner[r], up_w[:, :, at].reshape(width, tile)) + bias_row[:, at]
            square = pre * pre
            bend = jnp.tanh(0.7978845608028654 * pre * (1.0 + 0.044715 * square))
            near = 0.5 * (1.0 + bend)
            activ[r, :, at] = (pre * near).astype(BF16)
            slope = near + 0.5 * pre * (1.0 - bend * bend) * (
                0.7978845608028654 * (1.0 + 0.134145 * square)
            )
            dgelu[r, :, at] = slope.astype(BF16)
            return 0

        lax.fori_loop(0, ff // tile, column, 0)

        if inside:
            @pl.when(k == 0)
            def _():
                w_down.forward()
                w_down.finish()

        def column_b(n, _):
            at = pl.ds(pl.multiple_of(n * tile, tile), tile)
            part[k, :, at] = dot(activ[r], down_w[:, at]).astype(BF16)
            return 0

        lax.fori_loop(0, width // tile, column_b, 0)
        rs_2.step(k)
        return 0

    lax.fori_loop(0, 4, forward_step, 0)
    rs_2.relay()
    cot_own.wait()
    rs_2.wait()

    zero_row = jnp.zeros((1, width), F32)

    def last_norm(j, carry):
        at = pl.ds(pl.multiple_of(j * STEP, STEP), STEP)
        unit, scale = unit_of(rs_2.total(j))
        result[at] = (middle[at] + (unit * param(6) + param(7))).astype(BF16)
        grad = cot[at].astype(F32)
        gmix[s, at] = pull_of(grad, param(6), unit, scale).astype(BF16)
        return carry[0] + col_sum(grad * unit), carry[1] + col_sum(grad)

    grad_gain_d, grad_shift_d = lax.fori_loop(
        0, rows // STEP, last_norm, (zero_row, zero_row)
    )
    sg_rows = [None] * 8
    sg_rows[6], sg_rows[7] = grad_gain_d, grad_shift_d
    ag_mix = Gather(gmix, 2)
    ag_mix.start()
    rs_2.drain()

    rs_3 = Scatter(land_a, 2)
    sg_bias = bias_row

    def clear(n, _):
        at = pl.ds(pl.multiple_of(n * tile, tile), tile)
        sg_bias[:, at] = jnp.zeros((1, tile), F32)
        return 0

    lax.fori_loop(0, ff // tile, clear, 0)

    def back_step(k, _):
        ag_mix.step(k)
        r = block(k)

        def column(n, _):
            at = pl.ds(pl.multiple_of(n * tile, tile), tile)
            grad = dot(gmix[r], down_w[at], NT)
            low = (dgelu[r, :, at].astype(F32) * grad).astype(BF16)
            dgelu[r, :, at] = low
            sg_bias[:, at] = sg_bias[:, at] + col_sum(low.astype(F32))
            return 0

        lax.fori_loop(0, ff // tile, column, 0)

        def column_b(n, _):
            at = pl.ds(pl.multiple_of(n * tile, tile), tile)
            part[k, :, at] = dot(dgelu[r], up_w[n], NT).astype(BF16)
            return 0

        lax.fori_loop(0, width // tile, column_b, 0)
        rs_3.step(k)
        return 0

    lax.fori_loop(0, 4, back_step, 0)

    turned = tok

    def turn(source_ref, target):
        def run(b, _):
            def tiles(n, _):
                at = pl.ds(pl.multiple_of(n * tile, tile), tile)
                there = pl.ds(pl.multiple_of(b * rows, rows), rows)
                target[n, :, there] = source_ref[b, :, at].T
                return 0

            lax.fori_loop(0, target.shape[0], tiles, 0)
            return 0

        lax.fori_loop(0, 4, run, 0)

    def order(j):
        late = j // (n_f // 2)
        return 2 * (j % (n_f // 2)) + (1 - c) + late * (2 * c - 1)

    def cut_rows(who):
        at = pl.ds(pl.multiple_of(who * high, high), high)
        return turned[:, at, :].reshape(4 * high, 4 * rows)

    def plain_rows(who):
        per_block = rows // high_d
        at = pl.ds(pl.multiple_of((who % per_block) * high_d, high_d), high_d)
        return turned[who // per_block, at, :]

    def weight_grads(left_of, right, gw, shed):
        def run(j, _):
            who = order(j)
            value = dot(left_of(who), right[...].reshape(4 * rows, right.shape[2]))
            gw[who] = value.astype(BF16)

            @pl.when(j < n_f // 2)
            def _():
                shed.pair(j).start()

            return 0

        lax.fori_loop(0, n_f, run, 0)

    rs_3.relay()
    if inside:
        shed_down = Shed(0, gw_down, lp_down, lz_down)
        shed_up = Shed(1, gw_up, lp_up, lz_up)
        shed_out = Shed(2, gw_out, lp_out, lz_out)
        shed_qkv = Shed(3, gw_qkv, lp_qkv, lz_qkv)
        ag_tok.drain()
    rs_3.wait()

    def mid_back(j, carry):
        at = pl.ds(pl.multiple_of(j * STEP, STEP), STEP)
        grad = rs_3.total(j)
        unit, scale = unit_of(middle[at])
        total = cot[at].astype(F32) + pull_of(grad, param(4), unit, scale)
        gmid[at] = total
        out = [carry[0] + col_sum(grad * unit), carry[1] + col_sum(grad)]
        unit, scale = unit_of(branch[at])
        gbr[s, at] = pull_of(total, param(2), unit, scale).astype(BF16)
        return out[0], out[1], carry[2] + col_sum(total * unit), carry[3] + col_sum(total)

    sg_rows[4], sg_rows[5], sg_rows[2], sg_rows[3] = lax.fori_loop(
        0, rows // STEP, mid_back, (zero_row,) * 4
    )
    ag_br = Gather(gbr, 3)
    ag_br.start()
    tok_again = pltpu.make_async_copy(tokens, cot, loc_sem.at[5])
    tok_again.start()
    rs_3.drain()
    if inside:
        turn(activ, turned)
        weight_grads(plain_rows, gmix, gw_down, shed_down)
    ag_br.relay()
    if inside:
        shed_down.middle()
        turn(inner, turned)
        weight_grads(cut_rows, dgelu, gw_up, shed_up)
        shed_up.middle()
    ag_br.wait_x()
    ag_br.wait_y()
    ag_br.wait_d()

    def zero_acc(j, _):
        at = pl.ds(pl.multiple_of(j * STEP, STEP), STEP)
        dkt[at] = jnp.zeros((STEP, 4 * rows), F32)
        dvt[at] = jnp.zeros((STEP, 4 * rows), F32)
        return 0

    lax.fori_loop(0, group // STEP, zero_acc, 0)

    def attend_back(r, _):
        first = r // 3
        gatt[...] = dot(gbr[r], out_w[0], NT).astype(BF16)
        span = pl.ds(pl.multiple_of(first * rows, rows), window)
        for p in range(group // 128):
            query, keys, vals = cut(r, 0, p, 1), cut(first, 1, p, blocks), cut(first, 2, p, blocks)
            grad = gatt[:, p * 128 : (p + 1) * 128]
            query_t = query.T
            grad_t = grad.T
            outs = []
            for e in range(2):
                low = probs[r, 2 * p + e]
                grad_probs = dot(grad * sides[e], vals, NT)
                full = low.astype(F32)
                inner_sum = jnp.sum(full * grad_probs, -1, keepdims=True)
                grad_scores = (full * (grad_probs - inner_sum)).astype(BF16)
                outs.append(dot(grad_scores, keys))
                here = slice((2 * p + e) * HEAD_DIM, (2 * p + e + 1) * HEAD_DIM)
                side = slice(e * HEAD_DIM, (e + 1) * HEAD_DIM)
                dkt[here, span] = dkt[here, span] + dot(query_t[side], grad_scores)
                dvt[here, span] = dvt[here, span] + dot(grad_t[side], low)
            gtri[r, :, p * 128 : (p + 1) * 128] = (
                jnp.where(pick, outs[0], outs[1]) * 0.125
            ).astype(BF16)
        return 0

    lax.fori_loop(0, 4, attend_back, 0)

    def turn_back(b, _):
        at = pl.ds(pl.multiple_of(b * rows, rows), rows)
        gtri[b, :, group : 2 * group] = dkt[:, at].astype(BF16).T
        gtri[b, :, 2 * group : 3 * group] = dvt[:, at].astype(BF16).T
        return 0

    lax.fori_loop(0, 4, turn_back, 0)

    rs_4 = Scatter(land_b, 3)

    def normed_step(i, _):
        rel = (1 - i // 2) + 2 * (1 - i % 2)
        r = block(rel)
        part[rel] = dot(gtri[r], qkv_w[...].reshape(width, 3 * group), NT).astype(BF16)
        rs_4.step(rel)
        return 0

    lax.fori_loop(0, 4, normed_step, 0)
    if inside:
        turn(attended, att_t)
        gw_out[...] = (
            dot(att_t[0], gbr[...].reshape(4 * rows, width)).astype(BF16).reshape(gw_out.shape)
        )

        def out_pairs(j, _):
            shed_out.pair(j).start()
            return 0

        lax.fori_loop(0, n_f // 2, out_pairs, 0)
        turn(normed, turned)
        weight_grads(cut_rows, gtri, gw_qkv, shed_qkv)
    rs_4.relay()
    if inside:
        shed_out.middle()
        shed_qkv.middle()
    rs_4.wait()

    def first_back(j, carry):
        at = pl.ds(pl.multiple_of(j * STEP, STEP), STEP)
        grad = rs_4.total(j)
        value = cot[at].astype(F32)
        unit, scale = unit_of(value)
        tgrad[at] = gmid[at] + pull_of(grad, param(0), unit, scale)
        return carry[0] + col_sum(grad * unit), carry[1] + col_sum(grad)

    tok_again.wait()
    sg_rows[0], sg_rows[1] = lax.fori_loop(0, rows // STEP, first_back, (zero_row, zero_row))

    if inside:
        per = n_f * high // 128
        for b in range(4):
            for t in range(per):
                at = slice((b * per + t) * 128, (b * per + t + 1) * 128)
                for i in range(8):
                    sg_s[b, t, i : i + 1, :] = sg_rows[i][:, at]

        def ts_copy(k, to):
            return remote(sg_s.at[to], sg_land_s.at[k], ts_send.at[k], ts_recv.at[k], to, f)

        for k, to in enumerate(others):
            ts_copy(k, to).start()

        shed_down.wait()
        for j in range(high_d // STEP):
            at = pl.ds(j * STEP, STEP)
            gdown[at] = shed_down.total(at)
        shed_up.wait()

        def up_total(b, _):
            at = pl.ds(pl.multiple_of(b * high, high), high)
            fin_up[b] = shed_up.total(at)
            return 0

        lax.fori_loop(0, 4, up_total, 0)

        def gu_copy(k, to):
            dst = gup.at[:, pl.ds(pl.multiple_of(s * ff, 128), ff)]
            return remote(fin_up.at[to], dst, gu_send.at[k], gu_recv.at[k], to, f)

        for k, to in enumerate(others):
            gu_copy(k, to).start()
        gup[:, pl.ds(pl.multiple_of(s * ff, 128), ff)] = fin_up[s]

        for k, to in enumerate(others):
            ts_copy(k, to).wait_recv()
        for who in range(n_f):
            t = who * high // 128
            sg_f[who, 0:8] = (
                sg_s[s, t] + sg_land_s[0, t] + sg_land_s[1, t] + sg_land_s[2, t]
            )
            sg_f[who, 8:9] = sg_bias[:, who * 128 : (who + 1) * 128]

        def tf_copy(d):
            to = (f + d) % n_f
            return remote(
                sg_f.at[to], sg_land_f.at[d - 1], tf_send.at[d], tf_recv.at[d], s, to
            )

        for d in range(1, n_f):
            tf_copy(d).start()

        shed_out.wait()
        gout[...] = shed_out.total(slice(None))
        shed_qkv.wait()

        def qkv_total(b, _):
            at = pl.ds(pl.multiple_of(b * high, high), high)
            fin_qkv[b] = shed_qkv.total(at)
            return 0

        lax.fori_loop(0, 4, qkv_total, 0)

        def gc_copy(k, p, to):
            dst = gqkv.at[:, pl.ds(pl.multiple_of(p * width + s * group, 128), group)]
            return remote(
                fin_qkv.at[to, :, pl.ds(p * group, group)], dst,
                gc_send.at[k, p], gc_recv.at[k, p], to, f,
            )

        for p in range(3):
            for k, to in enumerate(others):
                gc_copy(k, p, to).start()
            at = pl.ds(pl.multiple_of(p * width + s * group, 128), group)
            gqkv[:, at] = fin_qkv[s, :, p * group : (p + 1) * group]
        for d in range(1, n_f):
            tf_copy(d).wait_recv()
        value = sg_f[f]
        for d in range(1, n_f):
            value = value + sg_land_f[d - 1]
        gsmall[...] = value

        for k, who in enumerate(others):
            remote(
                fin_up.at[0], gup.at[:, pl.ds(pl.multiple_of(who * ff, 128), ff)],
                gu_send.at[k], gu_recv.at[k], who, f,
            ).wait_recv()
            for p in range(3):
                remote(
                    fin_qkv.at[0, :, pl.ds(p * group, group)],
                    gqkv.at[:, pl.ds(pl.multiple_of(p * width + who * group, 128), group)],
                    gc_send.at[k, p], gc_recv.at[k, p], who, f,
                ).wait_recv()
        for k, to in enumerate(others):
            gu_copy(k, to).wait_send()
            ts_copy(k, to).wait_send()
            for p in range(3):
                gc_copy(k, p, to).wait_send()
                qkv_copy(k, p, to).wait_send()
            up_copy(k, to).wait_send()
            small_wide(k, to).wait_send()
        for d in range(1, n_f):
            tf_copy(d).wait_send()
            small_copy(d).wait_send()
        for weight in (w_qkv, w_out, w_up, w_down):
            weight.drain()
        for shed in (shed_down, shed_up, shed_out, shed_qkv):
            shed.drain()
    else:
        for i in range(8):
            gsmall[i : i + 1, :] = sg_rows[i]
        gsmall[8:9, 0:ff] = sg_bias[...]
    for k, to in enumerate(others):
        seg_copy(k, to).wait_send()
    for gather in (ag_inner, ag_mix, ag_br) + (() if inside else (ag_tok,)):
        gather.drain()
    rs_4.drain()


def on_device(n_seq, n_f, *args):
    (tokens, segments, qkv_weight, out_weight, up_weight, up_bias, down_weight) = args[:7]
    vectors, cotangent = args[7:15], args[15]
    rows, width = tokens.shape[1:]
    high, high_d = qkv_weight.shape[0], down_weight.shape[0]
    length = n_seq * rows
    group = qkv_weight.shape[1] // 3 // n_seq
    heads = group // HEAD_DIM
    ff = up_weight.shape[1] // n_seq
    half = rows // 2
    window = rows * min(n_seq, 1 + -(-511 // rows))
    inside = n_f == 8 and high % 32 == 0
    f = lax.axis_index("fsdp")
    small = jnp.stack([v.astype(F32) for v in vectors])
    if inside:
        each = 128 // high
        lane = lax.broadcasted_iota(jnp.int32, (8, 128), 1) // high
        small = jnp.where(lane == f % each, jnp.tile(small, (1, each)), 0.0)
        small = jnp.concatenate([small, up_bias.astype(F32)[None], jnp.zeros((7, 128), F32)])
        weights = (qkv_weight, out_weight, up_weight, down_weight)
    else:
        small = lax.all_gather(small, ("seq", "fsdp"), axis=1, tiled=True)
        bias = lax.all_gather(up_bias.astype(F32), "fsdp", axis=0, tiled=True)
        bias = jnp.pad(bias[None], ((0, 7), (0, width - ff)))
        small = jnp.concatenate([small, bias])

        def columns(weight, parts):
            cut = weight.reshape(high, parts, n_seq, -1).transpose(2, 0, 1, 3)
            cut = cut.reshape(n_seq, high, -1)
            cut = lax.all_to_all(cut, "seq", split_axis=0, concat_axis=0, tiled=True)
            return lax.all_gather(cut, "fsdp", axis=1, tiled=True)

        weights = (
            columns(qkv_weight, 3),
            lax.all_gather(out_weight, "fsdp", axis=0, tiled=True)[None],
            columns(up_weight, 1),
            lax.all_gather(down_weight, "fsdp", axis=0, tiled=True),
        )
    vmem, anywhere, dma = pltpu.VMEM, pl.BlockSpec(memory_space=pl.ANY), pltpu.SemaphoreType.DMA
    whole = pl.BlockSpec(memory_space=pltpu.VMEM)
    full = (4, rows, width)
    saved = {
        "normed": (full, BF16), "inner": (full, BF16), "gmix": (full, BF16), "gbr": (full, BF16),
        "attended": ((4, rows, group), BF16), "activ": ((4, rows, ff), BF16),
        "dgelu": ((4, rows, ff), BF16), "gtri": ((4, rows, 3 * group), BF16),
    }
    pieces = {"qkv": (n_seq * high, 3 * group), "out": (high, width),
              "up": (n_seq * high, ff), "down": (high_d, width)}
    scratch = {
        "tok": vmem(full, BF16), "normed": None, "inner": None, "gmix": None, "gbr": None,
        "qkv_w": vmem((n_seq, rows, 3 * group), BF16), "out_w": vmem((1, group, width), BF16),
        "up_w": vmem((n_seq, rows, ff), BF16), "down_w": vmem((ff, width), BF16),
        "segs": vmem((4, 1, rows), jnp.int32),
        "small_f": vmem((n_f if inside else 1, 16, 128), F32), "small_s": vmem((4, width // 512, 8, 128), F32),
        "params": vmem((8, width), F32), "bias_row": vmem((1, ff), F32),
        "triple": vmem((4, rows, 3 * group), BF16), "probs": vmem((4, heads, rows, window), BF16),
        "attended": None, "mask": vmem((rows, window), F32), "activ": None, "dgelu": None,
        "part": vmem(full, BF16), "land_a": vmem((6, half, width), BF16),
        "land_b": vmem((6, half, width), BF16),
        "branch": vmem((rows, width), F32), "middle": vmem((rows, width), F32),
        "gmid": vmem((rows, width), F32), "cot": vmem((rows, width), BF16),
        "gtri": None, "gatt": vmem((rows, group), BF16), "dkt": vmem((group, length), F32),
        "dvt": vmem((group, length), F32), "att_t": vmem((1, group, length), BF16),
    }
    for name, (tall, wide) in pieces.items():
        scratch["gw_" + name] = vmem((n_f if inside else 1, tall if inside else 16, wide), BF16)
    for name, (tall, wide) in pieces.items():
        scratch["lp_" + name] = vmem((n_f // 2 if inside else 1, tall if inside else 16, wide), BF16)
    for name, (tall, wide) in pieces.items():
        scratch["lz_" + name] = vmem((n_f // 2 - 1 if inside else 1, tall if inside else 16, wide), BF16)
    scratch["fin_qkv"] = vmem((4, high, 3 * group), F32)
    scratch["fin_up"] = vmem((4, high, ff), F32)
    tiles = width // 512
    scratch["sg_s"] = vmem((4, tiles, 8, 128), F32)
    scratch["sg_land_s"] = vmem((3, tiles, 8, 128), F32)
    scratch["sg_f"] = vmem((n_f if inside else 1, 16, 128), F32)
    scratch["sg_land_f"] = vmem((n_f - 1 if inside else 1, 16, 128), F32)
    for name, shape in (
        ("ag_send", (4, 6)), ("ag_recv", (4, 6)), ("rs_send", (4, 6)), ("rs_recv", (4, 6)),
        ("w_send", (4, 4)), ("w_recv", (4, 4)), ("p_send", (4, 4)), ("p_recv", (4, 4)),
        ("col_send", (3, 3)), ("col_recv", (3, 3)), ("col_local", (4,)),
        ("upc_send", (3,)), ("upc_recv", (3,)), ("seg_send", (3,)), ("seg_recv", (3,)),
        ("sf_send", (8,)), ("sf_recv", (8,)), ("ss_send", (3,)), ("ss_recv", (3,)),
        ("loc_sem", (6,)),
        ("gp_send", (4, 4)), ("gp_recv", (4, 4)), ("gz_send", (4, 4)), ("gz_recv", (4, 4)),
        ("gc_send", (3, 3)), ("gc_recv", (3, 3)), ("gu_send", (3,)), ("gu_recv", (3,)),
        ("ts_send", (3,)), ("ts_recv", (3,)), ("tf_send", (8,)), ("tf_recv", (8,)),
    ):
        scratch[name] = dma(shape)
    outs = {
        "result": ((rows, width), BF16), "tgrad": ((rows, width), F32),
        "gqkv": ((high, n_seq * 3 * group), F32), "gout": ((high, width), F32),
        "gup": ((high, n_seq * ff), F32), "gdown": ((high_d, width), F32),
        "gsmall": ((16, 128 if inside else width), F32),
    }
    if inside:
        for name, shape in saved.items():
            scratch[name] = vmem(*shape)
        extra = []
    else:
        extra = list(saved)
    names = list(scratch)

    def kernel(*refs):
        given = refs[:8]
        made = refs[8 : 8 + len(outs)]
        more = dict(zip(extra, refs[8 + len(outs) :]))
        rest = refs[8 + len(outs) + len(extra) :]
        more.update(zip([n for n in names if scratch[n] is not None], rest))
        layer_kernel(inside, n_f, *given, *made, *[more[n] for n in names])

    shapes = [*outs.values(), *[saved[n] for n in extra]]
    made = pl.pallas_call(
        kernel,
        out_shape=[jax.ShapeDtypeStruct(*shape) for shape in shapes],
        in_specs=[anywhere, anywhere, whole, anywhere] + [anywhere] * 4,
        out_specs=[whole] * len(shapes),
        scratch_shapes=[scratch[n] for n in names if scratch[n] is not None],
        compiler_params=pltpu.CompilerParams(
            collective_id=0, has_side_effects=True, vmem_limit_bytes=67043328
        ),
    )(tokens[0], segments, small, cotangent[0], *weights)
    result, tgrad, gqkv, gout, gup, gdown, gsmall = made[:7]
    if inside:
        start = (f % (128 // high)) * high
        vectors = lax.dynamic_slice(gsmall[:8], (0, start), (8, high))
        gbias = gsmall[8]
    else:
        kept = {n: v.reshape(length, -1) for n, v in zip(extra, made[7:])}

        def turned_dot(left, right):
            return lax.dot_general(
                kept[left], kept[right], (((0,), (0,)), ((), ())), preferred_element_type=F32
            ).astype(BF16)

        def shed(value):
            return lax.psum_scatter(value, "fsdp", scatter_dimension=0, tiled=True)

        def columns_back(value, parts):
            cut = value.reshape(n_seq, n_f, high, -1).transpose(1, 0, 2, 3)
            cut = lax.all_to_all(shed(cut)[0], "seq", split_axis=0, concat_axis=0, tiled=True)
            cut = cut.reshape(n_seq, high, parts, -1).transpose(1, 2, 0, 3)
            return cut.reshape(high, -1).astype(F32)

        gqkv = columns_back(turned_dot("normed", "gtri"), 3)
        gout = shed(turned_dot("attended", "gbr")).astype(F32)
        gup = columns_back(turned_dot("inner", "dgelu"), 1)
        gdown = shed(turned_dot("activ", "gmix")).astype(F32)
        vectors = lax.psum_scatter(gsmall[:8], ("seq", "fsdp"), scatter_dimension=1, tiled=True)
        gbias = shed(gsmall[8, :ff])
    return (result[None], tgrad[None], gqkv, gout, gup, gbias, gdown, *vectors)


def solution(mesh):
    rows = P(("seq", "fsdp"), None)
    vector = P(("seq", "fsdp"))
    acts = P("fsdp", "seq", None)
    return jax.shard_map(
        partial(on_device, mesh.shape["seq"], mesh.shape["fsdp"]),
        mesh=mesh,
        in_specs=(acts, P("fsdp", "seq"), rows, rows, rows, vector, rows, *(vector,) * 8, acts),
        out_specs=(acts, acts, rows, rows, rows, vector, rows, *(vector,) * 8),
        check_vma=False,
    )
```

```python
from functools import partial

import jax
import jax.numpy as jnp
from jax import lax
from jax.experimental import pallas as pl
from jax.experimental.pallas import tpu as pltpu
from jax.sharding import PartitionSpec as P

HEAD_DIM = 64
F32 = jnp.float32
BF16 = jnp.bfloat16
NN = ((1,), (0,))
NT = ((1,), (1,))
NEG = -1e30


def dot(left, right, dims=NN):
    return lax.dot_general(left, right, (dims, ((), ())), preferred_element_type=F32)


def unit_of(value):
    center = value - jnp.mean(value, -1, keepdims=True)
    scale = lax.rsqrt(jnp.mean(center * center, -1, keepdims=True) + 1e-05)
    return center * scale, scale


def pull_of(grad, gain, unit, scale):
    pulled = grad * gain
    first = jnp.mean(pulled, -1, keepdims=True)
    second = jnp.mean(pulled * unit, -1, keepdims=True)
    return scale * (pulled - first - unit * second)


def col_sum(value):
    return jnp.sum(value, 0, keepdims=True)


def layer_kernel(
    inside,
    n_f,
    tokens, seg_in, small_in, cot_in, qkv_in, out_in, up_in, down_in,
    result, tgrad, gqkv, gout, gup, gdown, gsmall,
    tok, normed, inner, gmix, gbr,
    qkv_w, out_w, up_w, down_w,
    segs, small_f, small_s, params, bias_row,
    triple, probs, attended, starts, activ, dgelu,
    part, land_a, land_b,
    branch, middle, gmid, cot,
    gtri, gatt, dkt, dvt,
    gw_q0, gw_q1, gw_out, gw_up, gw_down,
    lp_q0, lp_q1, lp_out, lp_up, lp_down,
    lz_q0, lz_q1, lz_out, lz_up, lz_down,
    result_v, fin_qkv, fin_up, fin_down, fin_out, gup_v, gqkv_v, small_sum,
    sg_s, sg_land_s, sg_f, sg_land_f,
    ag_send, ag_recv, rs_send, rs_recv,
    w_send, w_recv, p_send, p_recv,
    col_send, col_recv, col_local, upc_send, upc_recv,
    seg_send, seg_recv, sf_send, sf_recv, ss_send, ss_recv,
    loc_sem, o_sem,
    gp_send, gp_recv, gz_send, gz_recv,
    gc_send, gc_recv, gu_send, gu_recv,
    ts_send, ts_recv, tf_send, tf_recv,
):
    gw_qkv, lp_qkv, lz_qkv = (gw_q0, gw_q1), (lp_q0, lp_q1), (lz_q0, lz_q1)
    rows, width = tokens.shape
    half = rows // 2
    group = out_w.shape[1]
    pairs = group // 128
    window = probs.shape[3]
    s = lax.axis_index("seq")
    f = lax.axis_index("fsdp")
    x, y = s % 2, s // 2
    z, c = f // 2, f % 2

    def block(rel):
        return 2 * ((y + rel // 2) % 2) + (x + rel % 2) % 2

    sx, sy, sd = block(1), block(2), block(3)

    def remote(src, dst, send, recv, to_s, to_f):
        return pltpu.make_async_remote_copy(
            src_ref=src, dst_ref=dst, send_sem=send, recv_sem=recv,
            device_id=(to_s, to_f), device_id_type=pl.DeviceIdType.MESH,
        )

    class Gather:
        def __init__(self, full, index):
            self.full, self.index = full, index

        def piece(self, b, h):
            return self.full.at[b, pl.ds(h * half, half)]

        def copy(self, i, b, h, to, src=None):
            dst = self.piece(b, h)
            return remote(
                dst if src is None else src, dst,
                ag_send.at[self.index, i], ag_recv.at[self.index, i], to, f,
            )

        def start(self, src=None):
            def cut(h):
                return None if src is None else src.at[pl.ds(h * half, half)]

            self.copy(0, s, 0, sx, cut(0)).start()
            self.copy(1, s, 1, sy, cut(1)).start()
            self.copy(2, s, 1, sx, cut(1)).start()
            self.copy(3, s, 0, sy, cut(0)).start()

        def relay(self):
            self.copy(0, sx, 0, sx).wait_recv()
            self.copy(4, sx, 0, sy).start()
            self.copy(1, sy, 1, sy).wait_recv()
            self.copy(5, sy, 1, sx).start()

        def wait_x(self):
            self.copy(2, sx, 1, sx).wait_recv()

        def wait_y(self):
            self.copy(3, sy, 0, sy).wait_recv()

        def wait_d(self):
            self.copy(4, sd, 0, sy).wait_recv()
            self.copy(5, sd, 1, sx).wait_recv()

        def step(self, k):
            @pl.when(k == 1)
            def _():
                self.relay()
                self.wait_x()

            @pl.when(k == 2)
            def _():
                self.wait_y()

            @pl.when(k == 3)
            def _():
                self.wait_d()

        def drain(self):
            for i, (b, h, to) in enumerate(
                ((s, 0, sx), (s, 1, sy), (s, 1, sx), (s, 0, sy), (sx, 0, sy), (sy, 1, sx))
            ):
                self.copy(i, b, h, to).wait_send()

    def half_rows(h):
        return pl.ds(pl.multiple_of(h * half, half), half)

    class Scatter:
        plan = ((3, 0, 1), (1, 0, 1), (3, 1, 2), (2, 1, 2), (2, 0, 2), (1, 1, 1))

        def __init__(self, land, index):
            self.land, self.index = land, index

        def copy(self, i):
            rel, h, way = self.plan[i]
            return remote(
                part.at[rel, pl.ds(h * half, half)], self.land.at[i],
                rs_send.at[self.index, i], rs_recv.at[self.index, i],
                sx if way == 1 else sy, f,
            )

        def step(self, rel):
            @pl.when(rel == 3)
            def _():
                self.copy(0).start()
                self.copy(2).start()

            @pl.when(rel == 1)
            def _():
                self.copy(1).start()

            @pl.when(rel == 2)
            def _():
                self.copy(3).start()

        def relay(self):
            for arrived, i in ((0, 4), (2, 5)):
                self.copy(arrived).wait_recv()
                rel, h, _ = self.plan[i]

                here = pl.ds(h * half, half)
                total = part[rel, here].astype(F32) + self.land[arrived].astype(F32)
                part[rel, here] = total.astype(BF16)
                self.copy(i).start()

        def wait(self):
            for i in (1, 3, 4, 5):
                self.copy(i).wait_recv()

        def total(self, h):
            return (
                part[0, half_rows(h)].astype(F32)
                + self.land[1 + 2 * h].astype(F32)
                + self.land[4 + h].astype(F32)
            )

        def drain(self):
            for i in range(6):
                self.copy(i).wait_send()

    def by_rows(ref, size):
        def view(who):
            return ref.at[pl.ds(pl.multiple_of(who * size, size), size)]

        return view

    def by_cut(ref, size):
        def view(who):
            return ref.at[:, pl.ds(pl.multiple_of(who * size, size), size)]

        return view

    partner = 2 * z + 1 - c
    side = z // 2
    near = 4 * side + 1 - z
    mid_o, end_o = 2 - side, 3 - 3 * side
    is_mid = (z + side) % 2
    seen_as = 2 - is_mid
    owners = (near, mid_o, end_o)

    class Weight:
        def __init__(self, index, view):
            self.index, self.view = index, view

        def piece(self, to_z, i, k, owner_z, own=None):
            dst = self.view(2 * owner_z + c)
            return remote(
                dst if own is None else own, dst,
                w_send.at[self.index, i], w_recv.at[self.index, k], s, 2 * to_z + c,
            )

        def across(self, k, owner, own=None):
            dst = self.view(owner)
            return remote(
                dst if own is None else own, dst,
                p_send.at[self.index, k], p_recv.at[self.index, k], s, partner,
            )

        def start_far(self, own=None):
            self.piece(mid_o, 1, seen_as, z, own).start()

            @pl.when(is_mid == 0)
            def _():
                self.piece(near, 0, 0, z, own).start()

            self.across(3, f, own).start()

        def start_near(self, own=None):
            @pl.when(is_mid == 1)
            def _():
                self.piece(near, 0, 0, z, own).start()

        def start(self, own=None):
            self.start_far(own)
            self.start_near(own)

        def relay(self):
            @pl.when(is_mid == 1)
            def _():
                for k in (1, 2):
                    self.piece(z, 0, k, owners[k]).wait_recv()
                    self.piece(near, 1 + k, k, owners[k]).start()
                for k in (1, 2):
                    self.across(k, 2 * owners[k] + c).start()

        def rest(self):
            self.piece(z, 0, 0, near).wait_recv()
            self.across(0, 2 * near + c).start()

            @pl.when(is_mid == 0)
            def _():
                for k in (1, 2):
                    self.piece(z, 0, k, owners[k]).wait_recv()
                    self.across(k, 2 * owners[k] + c).start()

        def finish(self):
            self.across(3, partner).wait_recv()
            for k in (0, 1, 2):
                self.across(k, 2 * owners[k] + 1 - c).wait_recv()

        def drain(self):
            self.piece(mid_o, 1, seen_as, z).wait_send()
            self.piece(near, 0, 0, z).wait_send()
            self.across(3, f).wait_send()

            @pl.when(is_mid == 1)
            def _():
                for k in (1, 2):
                    self.piece(near, 1 + k, k, owners[k]).wait_send()

            for k in (0, 1, 2):
                self.across(k, 2 * owners[k] + c).wait_send()

    class Shed:
        def __init__(self, index, gw, land_p, land_z):
            self.index, self.gw, self.land_p, self.land_z = index, gw, land_p, land_z

        def pair(self, to_z):
            return remote(
                self.gw.at[2 * to_z + 1 - c], self.land_p.at[to_z],
                gp_send.at[self.index, to_z], gp_recv.at[self.index, to_z], s, partner,
            )

        def along(self, i, to_z, of_z, slot):
            return remote(
                self.gw.at[2 * of_z + c], self.land_z.at[slot],
                gz_send.at[self.index, i], gz_recv.at[self.index, slot], s, 2 * to_z + c,
            )

        def add(self, who, land, slot):
            self.gw[who] = (self.gw[who].astype(F32) + land[slot].astype(F32)).astype(BF16)

        def add_pair(self, to_z):
            self.pair(to_z).wait_recv()
            self.add(2 * to_z + c, self.land_p, to_z)

        def first(self):
            for slot, of_z in ((1, mid_o), (2, end_o), (0, near)):
                self.add_pair(of_z)

                @pl.when(is_mid == 0)
                def _(slot=slot, of_z=of_z):
                    self.along(slot, near, of_z, slot).start()

            @pl.when(is_mid == 1)
            def _():
                self.along(0, near, near, 0).start()

            self.add_pair(z)

        def second(self):
            @pl.when(is_mid == 1)
            def _():
                for i, of_z in ((1, mid_o), (2, end_o)):
                    self.along(i, near, of_z, i).wait_recv()
                    self.add(2 * of_z + c, self.land_z, i)
                    self.along(i, of_z, of_z, 3).start()

        def wait(self):
            self.along(0, near, z, 0).wait_recv()
            self.along(1, near, z, 3).wait_recv()

        def total(self, at):
            value = self.gw[f, at].astype(F32)
            return value + self.land_z[0, at].astype(F32) + self.land_z[3, at].astype(F32)

        def drain(self):
            def one(to_z, _):
                self.pair(to_z).wait_send()
                return 0

            lax.fori_loop(0, n_f // 2, one, 0)
            for i in range(3):
                self.along(i, near, near, 0).wait_send()

    barrier = pltpu.get_barrier_semaphore()
    for who in (sx, sy, sd):
        pl.semaphore_signal(barrier, inc=1, device_id=(who, f), device_id_type=pl.DeviceIdType.MESH)
    n_peers = 3
    if inside:
        for d in range(1, n_f):
            pl.semaphore_signal(
                barrier, inc=1, device_id=(s, (f + d) % n_f), device_id_type=pl.DeviceIdType.MESH
            )
        n_peers += n_f - 1
    pl.semaphore_wait(barrier, n_peers)

    others = (sx, sy, sd)
    ag_tok = Gather(tok, 0)
    if inside:
        high = qkv_in.shape[0]
        high_d = down_in.shape[0]
        w_qkv = [
            Weight(0, by_cut(qkv_w.at[0:2], high)), Weight(4, by_cut(qkv_w.at[2:4], high))
        ]
        w_out = Weight(1, by_rows(out_w.at[0], high))
        w_up = Weight(2, by_cut(up_w, high))
        w_down = Weight(3, by_rows(down_w, high_d))

        def qkv_copy(k, p, to):
            start = pl.multiple_of((p % 3) * width + to * group + (p // 3) * 128, 128)
            src = qkv_in.at[:, pl.ds(start, 128)]
            dst = qkv_w.at[s, pl.ds(pl.multiple_of(f * high, high), high), pl.ds(p * 128, 128)]
            if k < 0:
                return pltpu.make_async_copy(src, dst, col_local.at[p])
            return remote(src, dst, col_send.at[k, p], col_recv.at[k, p], to, f)

        n_cut = 3 * pairs

        ff = up_w.shape[2]

        def up_copy(k, to):
            src = up_in.at[:, pl.ds(pl.multiple_of(to * ff, 128), ff)]
            dst = up_w.at[s, pl.ds(pl.multiple_of(f * high, high), high)]
            if k < 0:
                return pltpu.make_async_copy(src, dst, loc_sem.at[6])
            return remote(src, dst, upc_send.at[k], upc_recv.at[k], to, f)

        out_own = pltpu.make_async_copy(out_in, w_out.view(f), loc_sem.at[0])
        down_own = pltpu.make_async_copy(down_in, w_down.view(f), loc_sem.at[1])

        def small_copy(d):
            return remote(
                small_in, small_f.at[f], sf_send.at[d], sf_recv.at[d], s, (f + d) % n_f
            )

        for d in range(1, n_f):
            small_copy(d).start()
        for p in range(n_cut):
            for k, to in enumerate(others):
                qkv_copy(k, p, to).start()
        for k, to in enumerate(others):
            up_copy(k, to).start()
        for p in range(n_cut):
            qkv_copy(-1, p, s).start()
        up_copy(-1, s).start()
        out_own.start()
        down_own.start()
        small_f[f] = small_in[...]
    else:
        loads = [
            pltpu.make_async_copy(qkv_in, qkv_w, col_local.at[0]),
            pltpu.make_async_copy(up_in, up_w, loc_sem.at[6]),
            pltpu.make_async_copy(out_in, out_w, loc_sem.at[0]),
            pltpu.make_async_copy(down_in, down_w, loc_sem.at[1]),
        ]
        for load in loads:
            load.start()
    tok_own = pltpu.make_async_copy(tokens, tok.at[s], loc_sem.at[2])
    tok_own.start()
    cot_own = pltpu.make_async_copy(cot_in, cot, loc_sem.at[3])
    cot_own.start()
    seg_own = pltpu.make_async_copy(seg_in, segs.at[s], loc_sem.at[4])
    seg_own.start()

    def seg_copy(k, to):
        return remote(seg_in, segs.at[s], seg_send.at[k], seg_recv.at[k], to, f)

    for k, to in enumerate(others):
        seg_copy(k, to).start()

    if inside:
        for d in range(1, n_f):
            remote(
                small_in, small_f.at[(f + n_f - d) % n_f], sf_send.at[d], sf_recv.at[d],
                s, (f + d) % n_f,
            ).wait_recv()
        per = n_f * high // 128
        each = n_f // per
        for t in range(per):
            value = small_f[t * each, 0:8]
            for e in range(1, each):
                value = value + small_f[t * each + e, 0:8]
            small_s[s, t] = value
        for e in range(n_f):
            bias_row[0:1, pl.ds(e * 128, 128)] = small_f[e, 8:9]

        def small_wide(k, to):
            return remote(small_s.at[s], small_s.at[s], ss_send.at[k], ss_recv.at[k], to, f)

        for k, to in enumerate(others):
            small_wide(k, to).start()
        ag_tok.start(tokens)
        for p in range(n_cut):
            qkv_copy(-1, p, s).wait()
            for k, to in enumerate(others):
                qkv_copy(k, p, to).wait_recv()
        for weight in w_qkv:
            weight.start()
        w_out.start(out_in)
        up_copy(-1, s).wait()
        for k, to in enumerate(others):
            up_copy(k, to).wait_recv()
        w_up.start_far()
        for k, who in enumerate(others):
            remote(
                small_s.at[who], small_s.at[who], ss_send.at[k], ss_recv.at[k], who, f
            ).wait_recv()
        for b in range(4):
            for t in range(per):
                params[:, pl.ds((b * per + t) * 128, 128)] = small_s[b, t]
    else:
        ag_tok.start(tokens)
        params[...] = small_in[0:8]
        bias_row[...] = small_in[8:9, 0 : bias_row.shape[1]]

    zero_row = jnp.zeros((1, width), F32)

    def both(run, count):
        def step(h, carry):
            return tuple(a + b for a, b in zip(carry, run(h)))

        return lax.fori_loop(0, 2, step, (zero_row,) * count)

    def far_first(i):
        return (1 - i // 2) + 2 * (1 - i % 2)

    def param(i):
        return params[i : i + 1, :]

    tok_own.wait()
    if inside:
        w_qkv[0].relay()
    ag_tok.relay()

    def first_norm(b):
        unit, _s = unit_of(tok[b].astype(F32))
        normed[b] = (unit * param(0) + param(1)).astype(BF16)

    def norm_step(k, _):
        @pl.when(k == 1)
        def _():
            ag_tok.wait_x()

        @pl.when(k == 2)
        def _():
            ag_tok.wait_y()

        @pl.when(k == 3)
        def _():
            ag_tok.wait_d()

        first_norm(block(k))
        return 0

    lax.fori_loop(0, 1, norm_step, 0)
    if inside:
        w_qkv[1].relay()
        w_out.relay()
        w_up.start_near()
        w_down.start_far(down_in)
    lax.fori_loop(1, 4, norm_step, 0)
    if inside:
        for weight in w_qkv:
            weight.rest()
        for weight in w_qkv:
            weight.finish()
    else:
        for load in loads:
            load.wait()

    rest = normed[...].reshape(4 * rows, width)
    for p in range(pairs):
        value = dot(rest, qkv_w[:, :, p * 384 : (p + 1) * 384].reshape(width, 384))
        for q in range(3):
            piece = value[:, q * 128 : (q + 1) * 128]
            piece = piece if q else piece * 0.125
            at = slice((3 * p + q) * 128, (3 * p + q + 1) * 128)
            triple[:, :, at] = piece.astype(BF16).reshape(4, rows, 128)
    if inside:
        out_own.wait()
        w_out.rest()
        w_out.finish()

    seg_own.wait()
    for k, who in enumerate(others):
        remote(seg_in, segs.at[who], seg_send.at[k], seg_recv.at[k], who, f).wait_recv()
    seg_all = segs[...]

    def below(level):
        count = jnp.sum((seg_all < level).astype(F32), axis=0)
        return jnp.sum(count, axis=1, keepdims=True)

    bound_1, bound_2 = below(1), below(2)
    blocks = window // rows
    lane = lax.broadcasted_iota(jnp.int32, (1, 128), 1)
    left = (lane < HEAD_DIM).astype(F32)
    sides = (left.astype(BF16), (1.0 - left).astype(BF16))
    pick = lax.broadcasted_iota(jnp.int32, (rows, 128), 1) < HEAD_DIM

    def set_starts(r, _):
        i = (r * rows + lax.broadcasted_iota(jnp.int32, (rows, 128), 0)).astype(F32)
        starts[r] = jnp.where(i >= bound_2, bound_2, jnp.where(i >= bound_1, bound_1, 0.0))
        return 0

    lax.fori_loop(0, 4, set_starts, 0)

    def cut(r, part_at, p, count):
        at = pl.ds(pl.multiple_of((3 * p + part_at) * 128, 128), 128)
        return triple[pl.ds(r, count), :, at].reshape(count * rows, 128)

    def masked(scores, r, first, count):
        start = starts[r]
        tiles = []
        for t in range(count * rows // 128):
            j = lax.broadcasted_iota(jnp.int32, (rows, 128), 1) + t * 128
            keep = (first * rows + j).astype(F32) >= start
            if t * 128 >= (count - 1) * rows:
                i = lax.broadcasted_iota(jnp.int32, (rows, 128), 0)
                keep = keep & (j - (count - 1) * rows <= i)
            tiles.append(jnp.where(keep, scores[:, t * 128 : (t + 1) * 128], NEG))
        return jnp.concatenate(tiles, axis=1)

    rs_1 = Scatter(land_a, 0)

    def attend_pair(r, first, count, p):
        query, keys, vals = cut(r, 0, p, 1), cut(first, 1, p, count), cut(first, 2, p, count)
        outs = []
        for e in range(2):
            scores = masked(dot(query * sides[e], keys, NT), r, first, count)
            expo = jnp.exp(scores - jnp.max(scores, -1, keepdims=True))
            low = (expo * (1.0 / jnp.sum(expo, -1, keepdims=True))).astype(BF16)
            probs[r, 2 * p + e, :, 0 : count * rows] = low
            outs.append(dot(low, vals))
        attended[r, :, p * 128 : (p + 1) * 128] = jnp.where(pick, outs[0], outs[1]).astype(BF16)

    def attend(i, _):
        rel = far_first(i)
        r = block(rel)
        for count in range(1, blocks + 1):
            @pl.when(r + 1 >= count if count == blocks else r + 1 == count)
            def _(count=count):
                for p in range(pairs):
                    attend_pair(r, r + 1 - count, count, p)

        part[rel] = dot(attended[r], out_w[0]).astype(BF16)
        rs_1.step(rel)
        if inside:
            @pl.when(i == 1)
            def _():
                w_up.relay()
                w_down.start_near(down_in)

        return 0

    lax.fori_loop(0, 4, attend, 0)
    rs_1.relay()
    if inside:
        w_down.relay()
        w_up.rest()
    rs_1.wait()

    def mid_norm(h):
        at = half_rows(h)
        value = rs_1.total(h)
        branch[at] = value
        unit, _s = unit_of(value)
        mid = tok[s, at].astype(F32) + (unit * param(2) + param(3))
        middle[at] = mid
        unit, _s = unit_of(mid)
        inner[s, at] = (unit * param(4) + param(5)).astype(BF16)

    for h in range(2):
        mid_norm(h)
    ag_inner = Gather(inner, 1)
    ag_inner.start()
    rs_1.drain()
    if inside:
        w_up.finish()

    ff = up_w.shape[2]
    tile = 512
    rs_2 = Scatter(land_b, 1)

    def forward_step(k, _):
        ag_inner.step(k)
        r = block(k)

        def column(n, _):
            at = pl.ds(pl.multiple_of(n * tile, tile), tile)
            pre = dot(inner[r], up_w[:, :, at].reshape(width, tile)) + bias_row[:, at]
            square = pre * pre
            bend = jnp.tanh(0.7978845608028654 * pre * (1.0 + 0.044715 * square))
            near = 0.5 + 0.5 * bend
            activ[r, :, at] = (pre * near).astype(BF16)
            slope = near + pre * (0.5 - 0.5 * bend * bend) * (
                0.7978845608028654 + 0.10703222440890037 * square
            )
            dgelu[r, :, at] = slope.astype(BF16)
            return 0

        lax.fori_loop(0, ff // tile, column, 0)
        return 0

    lax.fori_loop(0, 4, forward_step, 0)
    if inside:
        down_own.wait()
        w_down.rest()
        w_down.finish()

    def down_step(i, _):
        rel = far_first(i)
        r = block(rel)

        part[rel] = dot(activ[r], down_w[...]).astype(BF16)
        rs_2.step(rel)
        return 0

    lax.fori_loop(0, 4, down_step, 0)
    rs_2.relay()
    cot_own.wait()
    rs_2.wait()

    def last_norm(h):
        at = half_rows(h)
        unit, scale = unit_of(rs_2.total(h))
        result_v[at] = (middle[at] + (unit * param(6) + param(7))).astype(BF16)
        grad = cot[at].astype(F32)
        gmix[s, at] = pull_of(grad, param(6), unit, scale).astype(BF16)
        return col_sum(grad * unit), col_sum(grad)

    grad_gain_d, grad_shift_d = both(last_norm, 2)
    sg_rows = [None] * 8
    sg_rows[6], sg_rows[7] = grad_gain_d, grad_shift_d
    ag_mix = Gather(gmix, 2)
    ag_mix.start()
    result_out = pltpu.make_async_copy(result_v, result, o_sem.at[2])
    result_out.start()
    rs_2.drain()

    rs_3 = Scatter(land_a, 2)
    sg_bias = bias_row

    def clear(n, _):
        at = pl.ds(pl.multiple_of(n * tile, tile), tile)
        sg_bias[:, at] = jnp.zeros((1, tile), F32)
        return 0

    lax.fori_loop(0, ff // tile, clear, 0)

    def back_step(k, _):
        ag_mix.step(k)
        r = block(k)

        def column(n, _):
            at = pl.ds(pl.multiple_of(n * tile, tile), tile)
            grad = dot(gmix[r], down_w[at], NT)
            low = (dgelu[r, :, at].astype(F32) * grad).astype(BF16)
            dgelu[r, :, at] = low
            sg_bias[:, at] = sg_bias[:, at] + col_sum(low.astype(F32))
            return 0

        lax.fori_loop(0, ff // tile, column, 0)
        return 0

    lax.fori_loop(0, 4, back_step, 0)

    def inner_step(i, _):
        rel = far_first(i)
        r = block(rel)

        part[rel] = dot(dgelu[r], up_w[...].reshape(width, ff), NT).astype(BF16)
        rs_3.step(rel)
        return 0

    lax.fori_loop(0, 4, inner_step, 0)

    TN = ((0,), (0,))

    def flat(ref, lanes=slice(None)):
        held = ref[:, :, lanes]
        return held.reshape(4 * rows, held.shape[2])

    def all_pairs(shed):
        for to_z in range(n_f // 2):
            shed.pair(to_z).start()

    def cut_grads(left, right, gw, shed, lanes=slice(None)):
        for b in range(4):
            value = dot(flat(left, slice(b * rows, (b + 1) * rows)), flat(right, lanes), TN)
            gw[:, b * high : (b + 1) * high, :] = value.astype(BF16).reshape(n_f, high, -1)
        all_pairs(shed)

    def row_grads(left, right, gw, shed):
        each = left.shape[2] // n_f
        most = max(each, 256)
        for b in range(left.shape[2] // most):
            value = dot(flat(left, slice(b * most, (b + 1) * most)), flat(right), TN)
            count = most // each
            gw[b * count : (b + 1) * count] = value.astype(BF16).reshape(count, each, -1)
        all_pairs(shed)

    if inside:
        shed_down = Shed(0, gw_down, lp_down, lz_down)
        shed_up = Shed(1, gw_up, lp_up, lz_up)
        shed_out = Shed(2, gw_out, lp_out, lz_out)
        shed_qkv = [
            Shed(3 + p, gw_qkv[p], lp_qkv[p], lz_qkv[p]) for p in range(pairs)
        ]
        ag_tok.drain()
    rs_3.relay()
    if inside:
        row_grads(activ, gmix, gw_down, shed_down)
        shed_down.first()
    rs_3.wait()

    def mid_back(h):
        at = half_rows(h)
        grad = rs_3.total(h)
        unit, scale = unit_of(middle[at])
        total = cot[at].astype(F32) + pull_of(grad, param(4), unit, scale)
        gmid[at] = total
        out = [col_sum(grad * unit), col_sum(grad)]
        unit, scale = unit_of(branch[at])
        gbr[s, at] = pull_of(total, param(2), unit, scale).astype(BF16)
        return out[0], out[1], col_sum(total * unit), col_sum(total)

    sg_rows[4], sg_rows[5], sg_rows[2], sg_rows[3] = both(mid_back, 4)
    ag_br = Gather(gbr, 3)
    ag_br.start()
    rs_3.drain()
    if inside:
        cut_grads(inner, dgelu, gw_up, shed_up)
    ag_br.relay()
    if inside:
        shed_up.first()
    if inside:
        shed_down.second()
    ag_br.wait_x()
    ag_br.wait_y()
    ag_br.wait_d()

    if inside:
        per = n_f * high // 128
        gdown_out = pltpu.make_async_copy(fin_down, gdown, o_sem.at[3])
        gout_out = pltpu.make_async_copy(fin_out, gout, o_sem.at[4])
        gup_out = pltpu.make_async_copy(gup_v, gup, o_sem.at[5])
        gqkv_out = pltpu.make_async_copy(gqkv_v, gqkv, o_sem.at[6])
        gsmall_out = pltpu.make_async_copy(small_sum, gsmall, o_sem.at[7])

        def ts_copy(k, to):
            return remote(sg_s.at[to], sg_land_s.at[k], ts_send.at[k], ts_recv.at[k], to, f)

        def tf_copy(d):
            to = (f + d) % n_f
            return remote(
                sg_f.at[to], sg_land_f.at[d - 1], tf_send.at[d], tf_recv.at[d], s, to
            )

        def small_first():
            for b in range(4):
                for t in range(per):
                    at = slice((b * per + t) * 128, (b * per + t + 1) * 128)
                    for i in range(8):
                        sg_s[b, t, i : i + 1, :] = sg_rows[i][:, at]
            for k, to in enumerate(others):
                ts_copy(k, to).start()

        def small_second():
            for k, to in enumerate(others):
                ts_copy(k, to).wait_recv()
            for who in range(n_f):
                t = who * high // 128
                sg_f[who, 0:8] = (
                    sg_s[s, t] + sg_land_s[0, t] + sg_land_s[1, t] + sg_land_s[2, t]
                )
                sg_f[who, 8:9] = sg_bias[:, who * 128 : (who + 1) * 128]
            for d in range(1, n_f):
                tf_copy(d).start()

        def small_third():
            for d in range(1, n_f):
                tf_copy(d).wait_recv()
            value = sg_f[f]
            for d in range(1, n_f):
                value = value + sg_land_f[d - 1]
            small_sum[...] = value
            gsmall_out.start()

        def gu_copy(k, to, who):
            dst = gup_v.at[:, pl.ds(pl.multiple_of(who * ff, 128), ff)]
            return remote(fin_up.at[to], dst, gu_send.at[k], gu_recv.at[k], to, f)

        def gc_at(p, who):
            start = pl.multiple_of((p % 3) * width + who * group + (p // 3) * 128, 128)
            return pl.ds(start, 128)

        def gc_copy(k, p, to, who):
            return remote(
                fin_qkv.at[to, :, pl.ds(p * 128, 128)], gqkv_v.at[:, gc_at(p, who)],
                gc_send.at[k, p], gc_recv.at[k, p], to, f,
            )

    def make_gatt(r, _):
        gatt[r] = dot(gbr[r], out_w[0], NT).astype(BF16)
        return 0

    lax.fori_loop(0, 4, make_gatt, 0)
    if inside:
        shed_up.second()

    def back_pair(p):
        lanes = slice(p * 128, (p + 1) * 128)
        for r in range(3, -1, -1):
            first = max(r + 1 - blocks, 0)
            count = r + 1 - first
            query, keys, vals = cut(r, 0, p, 1), cut(first, 1, p, count), cut(first, 2, p, count)
            grad = gatt[r, :, lanes]
            query_t, grad_t = query.T, grad.T
            outs, key_parts, value_parts = [], [], []
            for e in range(2):
                low = probs[r, 2 * p + e, :, 0 : count * rows]
                grad_probs = dot(grad * sides[e], vals, NT)
                full = low.astype(F32)
                inner_sum = jnp.sum(full * grad_probs, -1, keepdims=True)
                grad_scores = (full * (grad_probs - inner_sum)).astype(BF16)
                outs.append(dot(grad_scores, keys))
                side = slice(e * HEAD_DIM, (e + 1) * HEAD_DIM)
                here = slice(p * 128 + e * HEAD_DIM, p * 128 + (e + 1) * HEAD_DIM)
                key_part = dot(query_t[side], grad_scores)
                value_part = dot(grad_t[side], low)
                for n in range(count):
                    span = slice((first + n) * rows, (first + n + 1) * rows)
                    cols = slice(n * rows, (n + 1) * rows)
                    if r == 3 or (first + n) < 4 - blocks and r == first + n + blocks - 1:
                        dkt[here, span] = key_part[:, cols]
                        dvt[here, span] = value_part[:, cols]
                    else:
                        dkt[here, span] = dkt[here, span] + key_part[:, cols]
                        dvt[here, span] = dvt[here, span] + value_part[:, cols]
            at = slice(3 * p * 128, (3 * p + 1) * 128)
            gtri[r, :, at] = (jnp.where(pick, outs[0], outs[1]) * 0.125).astype(BF16)
        for b in range(4):
            span = slice(b * rows, (b + 1) * rows)
            at = slice((3 * p + 1) * 128, (3 * p + 2) * 128)
            gtri[b, :, at] = dkt[lanes, span].astype(BF16).T
            at = slice((3 * p + 2) * 128, (3 * p + 3) * 128)
            gtri[b, :, at] = dvt[lanes, span].astype(BF16).T

    for p in range(pairs):
        back_pair(p)
        if inside and p < pairs - 1:
            cut_grads(normed, gtri, gw_qkv[p], shed_qkv[p], slice(p * 384, (p + 1) * 384))

    rs_4 = Scatter(land_b, 3)

    def normed_step(i, carry):
        rel = far_first(i)
        r = block(rel)
        grad = dot(gtri[r], qkv_w[...].reshape(width, 3 * group), NT)
        part[rel] = grad.astype(BF16)
        rs_4.step(rel)
        unit, _s = unit_of(tok[r].astype(F32))
        return carry[0] + col_sum(grad * unit), carry[1] + col_sum(grad)

    sg_rows[0], sg_rows[1] = lax.fori_loop(0, 4, normed_step, (zero_row, zero_row))
    if inside:
        for p in range(pairs - 1):
            shed_qkv[p].first()
        p = pairs - 1
        cut_grads(normed, gtri, gw_qkv[p], shed_qkv[p], slice(p * 384, (p + 1) * 384))
        row_grads(attended, gbr, gw_out, shed_out)
        small_first()
        shed_qkv[p].first()
        shed_out.first()
    rs_4.relay()
    if inside:
        small_second()
        shed_qkv[0].second()
        shed_down.wait()
        fin_down[...] = shed_down.total(slice(None))
        gdown_out.start()
        shed_up.wait()
        for b in range(4):
            fin_up[b] = shed_up.total(slice(b * high, (b + 1) * high))
        for k, to in enumerate(others):
            gu_copy(k, to, s).start()
        gup_v[:, pl.ds(pl.multiple_of(s * ff, 128), ff)] = fin_up[s]
        for shed in shed_qkv[1:]:
            shed.second()
        shed_out.second()
        for q, shed in enumerate(shed_qkv):
            shed.wait()
            for b in range(4):
                fin_qkv[b, :, q * 384 : (q + 1) * 384] = shed.total(
                    slice(b * high, (b + 1) * high)
                )
            for p in range(3 * q, 3 * q + 3):
                for k, to in enumerate(others):
                    gc_copy(k, p, to, s).start()
                gqkv_v[:, gc_at(p, s)] = fin_qkv[s, :, p * 128 : (p + 1) * 128]
        shed_out.wait()
        fin_out[...] = shed_out.total(slice(None))
        gout_out.start()
        for k, who in enumerate(others):
            gu_copy(k, who, who).wait_recv()
        gup_out.start()
        small_third()
    rs_4.wait()

    def first_back(h, _):
        at = half_rows(h)
        unit, scale = unit_of(tok[s, at].astype(F32))
        gmid[at] = gmid[at] + pull_of(rs_4.total(h), param(0), unit, scale)
        pltpu.make_async_copy(gmid.at[at], tgrad.at[at], o_sem.at[h]).start()
        return 0

    lax.fori_loop(0, 2, first_back, 0)
    if inside:
        for k, who in enumerate(others):
            for p in range(n_cut):
                gc_copy(k, p, who, who).wait_recv()
        gqkv_out.start()

    for h in range(2):
        pltpu.make_async_copy(gmid.at[half_rows(h)], tgrad.at[half_rows(h)], o_sem.at[h]).wait()
    result_out.wait()
    if inside:
        gsmall_out.wait()
        gdown_out.wait()
        gout_out.wait()
        gup_out.wait()
        gqkv_out.wait()
        for k, to in enumerate(others):
            gu_copy(k, to, s).wait_send()
            ts_copy(k, to).wait_send()
            for p in range(n_cut):
                gc_copy(k, p, to, s).wait_send()
                qkv_copy(k, p, to).wait_send()
            up_copy(k, to).wait_send()
            small_wide(k, to).wait_send()
        for d in range(1, n_f):
            tf_copy(d).wait_send()
            small_copy(d).wait_send()
        for weight in (*w_qkv, w_out, w_up, w_down):
            weight.drain()
        for shed in (shed_down, shed_up, shed_out, *shed_qkv):
            shed.drain()
    else:
        for i in range(8):
            small_sum[i : i + 1, :] = sg_rows[i]
        small_sum[8:9, 0:ff] = sg_bias[...]
        gsmall_out = pltpu.make_async_copy(small_sum, gsmall, o_sem.at[7])
        gsmall_out.start()
        gsmall_out.wait()
    for k, to in enumerate(others):
        seg_copy(k, to).wait_send()
    for gather in (ag_inner, ag_mix, ag_br) + (() if inside else (ag_tok,)):
        gather.drain()
    rs_4.drain()


def finish_kernel(n_f, n_big, *refs):
    small, given = refs[0], refs[1 : 1 + n_big]
    made, minor = refs[1 + n_big : 1 + 2 * n_big], refs[1 + 2 * n_big : 10 + 2 * n_big]
    held, (in_sem, out_sem) = refs[10 + 2 * n_big : 10 + 3 * n_big], refs[10 + 3 * n_big :]
    cuts = []
    for i in range(n_big):
        tall = given[i].shape[0]
        for j in range(max(1, tall // 64)):
            at = pl.ds(j * min(tall, 64), min(tall, 64))
            cuts.append((i, at, len(cuts)))
    for i, at, n in cuts:
        pltpu.make_async_copy(given[i].at[at], held[i].at[at], in_sem.at[n]).start()
    each = minor[0].shape[1]
    place = lax.axis_index("fsdp") % (128 // each)
    for i in range(8):
        row = small[i : i + 1, :]
        value = row[:, 0:each]
        for q in range(1, 128 // each):
            value = jnp.where(place == q, row[:, q * each : (q + 1) * each], value)
        minor[i][...] = value
    minor[8][...] = small[8:9, :]
    for i, at, n in cuts:
        pltpu.make_async_copy(given[i].at[at], held[i].at[at], in_sem.at[n]).wait()
        pltpu.make_async_copy(held[i].at[at], made[i].at[at], out_sem.at[n]).start()
    for i, at, n in cuts:
        pltpu.make_async_copy(held[i].at[at], made[i].at[at], out_sem.at[n]).wait()


def finish(n_f, high, *made):
    big, small = made[:6], made[6]
    whole, anywhere = pl.BlockSpec(memory_space=pltpu.VMEM), pl.BlockSpec(memory_space=pl.ANY)
    count = sum(max(1, v.shape[0] // 64) for v in big)
    minor = [jax.ShapeDtypeStruct((1, high), F32)] * 8 + [jax.ShapeDtypeStruct((1, 128), F32)]
    out = pl.pallas_call(
        partial(finish_kernel, n_f, 6),
        out_shape=[jax.ShapeDtypeStruct(v.shape, v.dtype) for v in big] + minor,
        in_specs=[whole] + [anywhere] * 6,
        out_specs=[anywhere] * 6 + [whole] * 9,
        scratch_shapes=[pltpu.VMEM(v.shape, v.dtype) for v in big]
        + [pltpu.SemaphoreType.DMA((count,))] * 2,
    )(small, *big)
    result, tgrad, gqkv, gout, gup, gdown = out[:6]
    small = [v[0] for v in out[6:]]
    return (result[None], tgrad[None], gqkv, gout, gup, small[8], gdown, *small[:8])


def on_device(n_seq, n_f, *args):
    (tokens, segments, qkv_weight, out_weight, up_weight, up_bias, down_weight) = args[:7]
    vectors, cotangent = args[7:15], args[15]
    rows, width = tokens.shape[1:]
    high, high_d = qkv_weight.shape[0], down_weight.shape[0]
    length = n_seq * rows
    group = qkv_weight.shape[1] // 3 // n_seq
    heads = group // HEAD_DIM
    ff = up_weight.shape[1] // n_seq
    half = rows // 2
    window = rows * min(n_seq, 1 + -(-511 // rows))
    inside = n_f == 8 and high % 32 == 0
    f = lax.axis_index("fsdp")
    small = jnp.stack([v.astype(F32) for v in vectors])
    if inside:
        each = 128 // high
        lane = lax.broadcasted_iota(jnp.int32, (8, 128), 1) // high
        small = jnp.where(lane == f % each, jnp.tile(small, (1, each)), 0.0)
        small = jnp.concatenate([small, up_bias.astype(F32)[None], jnp.zeros((7, 128), F32)])
        weights = (qkv_weight, out_weight, up_weight, down_weight)
    else:
        small = lax.all_gather(small, ("seq", "fsdp"), axis=1, tiled=True)
        bias = lax.all_gather(up_bias.astype(F32), "fsdp", axis=0, tiled=True)
        bias = jnp.pad(bias[None], ((0, 7), (0, width - ff)))
        small = jnp.concatenate([small, bias])

        def columns(weight, parts):
            cut = weight.reshape(high, parts, n_seq, -1, 128).transpose(2, 0, 3, 1, 4)
            cut = cut.reshape(n_seq, high, -1)
            cut = lax.all_to_all(cut, "seq", split_axis=0, concat_axis=0, tiled=True)
            return lax.all_gather(cut, "fsdp", axis=1, tiled=True)

        weights = (
            columns(qkv_weight, 3),
            lax.all_gather(out_weight, "fsdp", axis=0, tiled=True)[None],
            columns(up_weight, 1),
            lax.all_gather(down_weight, "fsdp", axis=0, tiled=True),
        )
    vmem, anywhere, dma = pltpu.VMEM, pl.BlockSpec(memory_space=pl.ANY), pltpu.SemaphoreType.DMA
    whole = pl.BlockSpec(memory_space=pltpu.VMEM)
    full = (4, rows, width)
    saved = {
        "normed": (full, BF16), "inner": (full, BF16), "gmix": (full, BF16), "gbr": (full, BF16),
        "attended": ((4, rows, group), BF16), "activ": ((4, rows, ff), BF16),
        "dgelu": ((4, rows, ff), BF16), "gtri": ((4, rows, 3 * group), BF16),
    }
    n_cut = 3 * (group // 128)
    pieces = {"q0": (n_seq * high, 384), "q1": (n_seq * high, 384), "out": (high, width),
              "up": (n_seq * high, ff), "down": (high_d, width)}
    scratch = {
        "tok": vmem(full, BF16), "normed": None, "inner": None, "gmix": None, "gbr": None,
        "qkv_w": vmem((n_seq, rows, 3 * group), BF16), "out_w": vmem((1, group, width), BF16),
        "up_w": vmem((n_seq, rows, ff), BF16), "down_w": vmem((ff, width), BF16),
        "segs": vmem((4, 1, rows), jnp.int32),
        "small_f": vmem((n_f if inside else 1, 16, 128), F32), "small_s": vmem((4, width // 512, 8, 128), F32),
        "params": vmem((8, width), F32), "bias_row": vmem((1, ff), F32),
        "triple": vmem((4, rows, 3 * group), BF16), "probs": vmem((4, heads, rows, window), BF16),
        "attended": None, "starts": vmem((4, rows, 128), F32), "activ": None, "dgelu": None,
        "part": vmem(full, BF16), "land_a": vmem((6, half, width), BF16),
        "land_b": vmem((6, half, width), BF16),
        "branch": vmem((rows, width), F32), "middle": vmem((rows, width), F32),
        "gmid": vmem((rows, width), F32), "cot": vmem((rows, width), BF16),
        "gtri": None, "gatt": vmem((4, rows, group), BF16), "dkt": vmem((group, length), F32),
        "dvt": vmem((group, length), F32),
    }
    for name, (tall, wide) in pieces.items():
        scratch["gw_" + name] = vmem((n_f if inside else 1, tall if inside else 16, wide), BF16)
    for name, (tall, wide) in pieces.items():
        scratch["lp_" + name] = vmem((n_f // 2 if inside else 1, tall if inside else 16, wide), BF16)
    for name, (tall, wide) in pieces.items():
        scratch["lz_" + name] = vmem((n_f // 2 if inside else 1, tall if inside else 16, wide), BF16)
    scratch["result_v"] = vmem((rows, width), BF16)
    scratch["fin_qkv"] = vmem((4, high, 3 * group), F32)
    scratch["fin_up"] = vmem((4, high, ff), F32)
    scratch["fin_down"] = vmem((high_d, width), F32)
    scratch["fin_out"] = vmem((high, width), F32)
    scratch["gup_v"] = vmem((high, n_seq * ff), F32)
    scratch["gqkv_v"] = vmem((high, n_seq * 3 * group), F32)
    scratch["small_sum"] = vmem((16, 128 if inside else width), F32)
    tiles = width // 512
    scratch["sg_s"] = vmem((4, tiles, 8, 128), F32)
    scratch["sg_land_s"] = vmem((3, tiles, 8, 128), F32)
    scratch["sg_f"] = vmem((n_f if inside else 1, 16, 128), F32)
    scratch["sg_land_f"] = vmem((n_f - 1 if inside else 1, 16, 128), F32)
    for name, shape in (
        ("ag_send", (4, 6)), ("ag_recv", (4, 6)), ("rs_send", (4, 6)), ("rs_recv", (4, 6)),
        ("w_send", (5, 4)), ("w_recv", (5, 3)), ("p_send", (5, 4)), ("p_recv", (5, 4)),
        ("col_send", (3, n_cut)), ("col_recv", (3, n_cut)), ("col_local", (n_cut,)),
        ("upc_send", (3,)), ("upc_recv", (3,)), ("seg_send", (3,)), ("seg_recv", (3,)),
        ("sf_send", (8,)), ("sf_recv", (8,)), ("ss_send", (3,)), ("ss_recv", (3,)),
        ("loc_sem", (7,)), ("o_sem", (8,)),
        ("gp_send", (5, 4)), ("gp_recv", (5, 4)), ("gz_send", (5, 4)), ("gz_recv", (5, 4)),
        ("gc_send", (3, n_cut)), ("gc_recv", (3, n_cut)), ("gu_send", (3,)), ("gu_recv", (3,)),
        ("ts_send", (3,)), ("ts_recv", (3,)), ("tf_send", (8,)), ("tf_recv", (8,)),
    ):
        scratch[name] = dma(shape)
    outs = {
        "result": ((rows, width), BF16), "tgrad": ((rows, width), F32),
        "gqkv": ((high, n_seq * 3 * group), F32), "gout": ((high, width), F32),
        "gup": ((high, n_seq * ff), F32), "gdown": ((high_d, width), F32),
        "gsmall": ((16, 128 if inside else width), F32),
    }
    if inside:
        for name, shape in saved.items():
            scratch[name] = vmem(*shape)
        extra = []
    else:
        extra = list(saved)
    names = list(scratch)

    def kernel(*refs):
        given = refs[:8]
        made = refs[8 : 8 + len(outs)]
        more = dict(zip(extra, refs[8 + len(outs) :]))
        rest = refs[8 + len(outs) + len(extra) :]
        more.update(zip([n for n in names if scratch[n] is not None], rest))
        layer_kernel(inside, n_f, *given, *made, *[more[n] for n in names])

    shapes = [*outs.values(), *[saved[n] for n in extra]]
    made = pl.pallas_call(
        kernel,
        out_shape=[jax.ShapeDtypeStruct(*shape) for shape in shapes],
        in_specs=[anywhere, anywhere, whole, anywhere] + [anywhere] * 4,
        out_specs=[anywhere] * len(outs) + [whole] * len(extra),
        scratch_shapes=[scratch[n] for n in names if scratch[n] is not None],
        compiler_params=pltpu.CompilerParams(
            collective_id=0, has_side_effects=True, vmem_limit_bytes=67043328
        ),
    )(tokens[0], segments, small, cotangent[0], *weights)
    result, tgrad, gqkv, gout, gup, gdown, gsmall = made[:7]
    if inside:
        return finish(n_f, high, *made[:7])
    else:
        kept = {n: v.reshape(length, -1) for n, v in zip(extra, made[7:])}

        def turned_dot(left, right):
            return lax.dot_general(
                kept[left], kept[right], (((0,), (0,)), ((), ())), preferred_element_type=F32
            ).astype(BF16)

        def shed(value):
            return lax.psum_scatter(value, "fsdp", scatter_dimension=0, tiled=True)

        def columns_back(value, parts):
            cut = value.reshape(n_seq, n_f, high, -1).transpose(1, 0, 2, 3)
            cut = lax.all_to_all(shed(cut)[0], "seq", split_axis=0, concat_axis=0, tiled=True)
            cut = cut.reshape(n_seq, high, -1, parts, 128).transpose(1, 3, 0, 2, 4)
            return cut.reshape(high, -1).astype(F32)

        gqkv = columns_back(turned_dot("normed", "gtri"), 3)
        gout = shed(turned_dot("attended", "gbr")).astype(F32)
        gup = columns_back(turned_dot("inner", "dgelu"), 1)
        gdown = shed(turned_dot("activ", "gmix")).astype(F32)
        vectors = lax.psum_scatter(gsmall[:8], ("seq", "fsdp"), scatter_dimension=1, tiled=True)
        gbias = shed(gsmall[8, :ff])
    return (result[None], tgrad[None], gqkv, gout, gup, gbias, gdown, *vectors)


def solution(mesh):
    rows = P(("seq", "fsdp"), None)
    vector = P(("seq", "fsdp"))
    acts = P("fsdp", "seq", None)
    return jax.shard_map(
        partial(on_device, mesh.shape["seq"], mesh.shape["fsdp"]),
        mesh=mesh,
        in_specs=(acts, P("fsdp", "seq"), rows, rows, rows, vector, rows, *(vector,) * 8, acts),
        out_specs=(acts, acts, rows, rows, rows, vector, rows, *(vector,) * 8),
        check_vma=False,
    )
```

```python
from functools import partial

import jax
import jax.numpy as jnp
from jax import lax
from jax.experimental import pallas as pl
from jax.experimental.pallas import tpu as pltpu
from jax.sharding import PartitionSpec as P

HEAD_DIM = 64
F32 = jnp.float32
BF16 = jnp.bfloat16
NN = ((1,), (0,))
NT = ((1,), (1,))
NEG = -1e30


def dot(left, right, dims=NN):
    return lax.dot_general(left, right, (dims, ((), ())), preferred_element_type=F32)


def unit_of(value):
    center = value - jnp.mean(value, -1, keepdims=True)
    scale = lax.rsqrt(jnp.mean(center * center, -1, keepdims=True) + 1e-05)
    return center * scale, scale


def pull_of(grad, gain, unit, scale):
    pulled = grad * gain
    first = jnp.mean(pulled, -1, keepdims=True)
    second = jnp.mean(pulled * unit, -1, keepdims=True)
    return scale * (pulled - first - unit * second)


def col_sum(value):
    return jnp.sum(value, 0, keepdims=True)


def layer_kernel(
    inside,
    n_f,
    tokens, seg_in, small_in, cot_in, qkv_in, out_in, up_in, down_in,
    result, tgrad, gqkv, gout, gup, gdown, gsmall,
    tok, normed, inner, gmix, gbr,
    qkv_w, out_w, up_w, down_w,
    segs, small_f, small_s, params, bias_row,
    triple, probs, attended, starts, activ, dgelu,
    part, land_a, land_b,
    branch, middle, gmid, cot,
    gtri, gatt, dkt, dvt,
    gw_q0, gw_q1, gw_out, gw_up, gw_down,
    lp_q0, lp_q1, lp_out, lp_up, lp_down,
    lz_q0, lz_q1, lz_out, lz_up, lz_down,
    result_v, fin_qkv, fin_up, land_qkv, land_up, fin_down, fin_out, gup_v, gqkv_v, small_sum,
    sg_s, sg_land_s, sg_f, sg_land_f,
    ag_send, ag_recv, rs_send, rs_recv,
    w_send, w_recv, p_send, p_recv,
    col_send, col_recv, col_local, upc_send, upc_recv,
    seg_send, seg_recv, sf_send, sf_recv, ss_send, ss_recv,
    loc_sem, o_sem,
    gp_send, gp_recv, gz_send, gz_recv,
    gc_send, gc_recv, gu_send, gu_recv,
    ts_send, ts_recv, tf_send, tf_recv, turn,
):
    gw_qkv, lp_qkv, lz_qkv = (gw_q0, gw_q1), (lp_q0, lp_q1), (lz_q0, lz_q1)
    rows, width = tokens.shape
    half = rows // 2
    group = out_w.shape[1]
    pairs = group // 128
    window = probs.shape[3]
    s = lax.axis_index("seq")
    f = lax.axis_index("fsdp")
    x, y = s % 2, s // 2
    z, c = f // 2, f % 2

    def block(rel):
        return 2 * ((y + rel // 2) % 2) + (x + rel % 2) % 2

    sx, sy, sd = block(1), block(2), block(3)

    def remote(src, dst, send, recv, to_s, to_f):
        return pltpu.make_async_remote_copy(
            src_ref=src, dst_ref=dst, send_sem=send, recv_sem=recv,
            device_id=(to_s, to_f), device_id_type=pl.DeviceIdType.MESH,
        )

    def my_turn(cores=(0, 1)):
        if inside:
            @pl.when(c >= cores[0])
            def _():
                pl.semaphore_wait(turn, 1)

    def hand_over(cores=(0, 1)):
        if inside:
            @pl.when(c <= cores[1])
            def _():
                pl.semaphore_signal(
                    turn, inc=1, device_id=(s, 2 * z + 1 - c),
                    device_id_type=pl.DeviceIdType.MESH,
                )

    class Gather:
        def __init__(self, full, index):
            self.full, self.index = full, index

        def piece(self, b, h):
            return self.full.at[b, pl.ds(h * half, half)]

        def copy(self, i, b, h, to, src=None):
            dst = self.piece(b, h)
            return remote(
                dst if src is None else src, dst,
                ag_send.at[self.index, i], ag_recv.at[self.index, i], to, f,
            )

        def start(self, src=None):
            def cut(h):
                return None if src is None else src.at[pl.ds(h * half, half)]

            self.copy(0, s, 0, sx, cut(0)).start()
            self.copy(1, s, 1, sy, cut(1)).start()
            self.copy(2, s, 1, sx, cut(1)).start()
            self.copy(3, s, 0, sy, cut(0)).start()

        def relay(self):
            self.copy(0, sx, 0, sx).wait_recv()
            self.copy(4, sx, 0, sy).start()
            self.copy(1, sy, 1, sy).wait_recv()
            self.copy(5, sy, 1, sx).start()
            if self.index:
                hand_over()

        def wait_x(self):
            self.copy(2, sx, 1, sx).wait_recv()

        def wait_y(self):
            self.copy(3, sy, 0, sy).wait_recv()

        def wait_d(self):
            self.copy(4, sd, 0, sy).wait_recv()
            self.copy(5, sd, 1, sx).wait_recv()

        def step(self, k):
            @pl.when(k == 1)
            def _():
                self.relay()
                self.wait_x()

            @pl.when(k == 2)
            def _():
                self.wait_y()

            @pl.when(k == 3)
            def _():
                self.wait_d()

        def drain(self):
            for i, (b, h, to) in enumerate(
                ((s, 0, sx), (s, 1, sy), (s, 1, sx), (s, 0, sy), (sx, 0, sy), (sy, 1, sx))
            ):
                self.copy(i, b, h, to).wait_send()

    def half_rows(h):
        return pl.ds(pl.multiple_of(h * half, half), half)

    class Scatter:
        plan = ((3, 0, 1), (1, 0, 1), (3, 1, 2), (2, 1, 2), (2, 0, 2), (1, 1, 1))

        def __init__(self, land, index):
            self.land, self.index = land, index

        def copy(self, i):
            rel, h, way = self.plan[i]
            return remote(
                part.at[rel, pl.ds(h * half, half)], self.land.at[i],
                rs_send.at[self.index, i], rs_recv.at[self.index, i],
                sx if way == 1 else sy, f,
            )

        def step(self, rel):
            @pl.when(rel == 3)
            def _():
                self.copy(0).start()
                self.copy(2).start()

            @pl.when(rel == 1)
            def _():
                self.copy(1).start()

            @pl.when(rel == 2)
            def _():
                self.copy(3).start()

        def relay(self):
            for arrived, i in ((0, 4), (2, 5)):
                self.copy(arrived).wait_recv()
                rel, h, _ = self.plan[i]

                here = pl.ds(h * half, half)
                total = part[rel, here].astype(F32) + self.land[arrived].astype(F32)
                part[rel, here] = total.astype(BF16)
                self.copy(i).start()
            hand_over((0, 0) if self.index == 3 else (0, 1))

        def wait(self):
            for i in (1, 3, 4, 5):
                self.copy(i).wait_recv()

        def total(self, h):
            return (
                part[0, half_rows(h)].astype(F32)
                + self.land[1 + 2 * h].astype(F32)
                + self.land[4 + h].astype(F32)
            )

        def drain(self):
            for i in range(6):
                self.copy(i).wait_send()

    def by_rows(ref, size):
        def view(who):
            return ref.at[pl.ds(pl.multiple_of(who * size, size), size)]

        return view

    def by_cut(ref, size):
        def view(who):
            return ref.at[:, pl.ds(pl.multiple_of(who * size, size), size)]

        return view

    partner = 2 * z + 1 - c
    side = z // 2
    near = 4 * side + 1 - z
    mid_o, end_o = 2 - side, 3 - 3 * side
    is_mid = (z + side) % 2
    seen_as = 2 - is_mid
    owners = (near, mid_o, end_o)

    class Weight:
        def __init__(self, index, view):
            self.index, self.view = index, view

        def piece(self, to_z, i, k, owner_z, own=None):
            dst = self.view(2 * owner_z + c)
            return remote(
                dst if own is None else own, dst,
                w_send.at[self.index, i], w_recv.at[self.index, k], s, 2 * to_z + c,
            )

        def across(self, k, owner, own=None):
            dst = self.view(owner)
            return remote(
                dst if own is None else own, dst,
                p_send.at[self.index, k], p_recv.at[self.index, k], s, partner,
            )

        def start_far(self, own=None):
            self.piece(mid_o, 1, seen_as, z, own).start()

            @pl.when(is_mid == 0)
            def _():
                self.piece(near, 0, 0, z, own).start()

            self.across(3, f, own).start()

        def start_near(self, own=None):
            @pl.when(is_mid == 1)
            def _():
                self.piece(near, 0, 0, z, own).start()

        def start(self, own=None):
            self.start_far(own)
            self.start_near(own)

        def relay(self, all_of_it=True):
            @pl.when(is_mid == 1)
            def _():
                for k in (1, 2):
                    self.piece(z, 0, k, owners[k]).wait_recv()
                    self.piece(near, 1 + k, k, owners[k]).start()
                for k in (1, 2):
                    self.across(k, 2 * owners[k] + c).start()

            if all_of_it:
                self.relay_rest()

        def relay_rest(self):
            @pl.when(is_mid == 1)
            def _():
                self.piece(z, 0, 0, near).wait_recv()
                self.across(0, 2 * near + c).start()

        def rest(self):
            @pl.when(is_mid == 0)
            def _():
                for k in (0, 1, 2):
                    self.piece(z, 0, k, owners[k]).wait_recv()
                    self.across(k, 2 * owners[k] + c).start()

        def finish(self):
            self.across(3, partner).wait_recv()
            for k in (0, 1, 2):
                self.across(k, 2 * owners[k] + 1 - c).wait_recv()

        def drain(self):
            self.piece(mid_o, 1, seen_as, z).wait_send()
            self.piece(near, 0, 0, z).wait_send()
            self.across(3, f).wait_send()

            @pl.when(is_mid == 1)
            def _():
                for k in (1, 2):
                    self.piece(near, 1 + k, k, owners[k]).wait_send()

            for k in (0, 1, 2):
                self.across(k, 2 * owners[k] + c).wait_send()

    class Shed:
        def __init__(self, index, gw, land_p, land_z):
            self.index, self.gw, self.land_p, self.land_z = index, gw, land_p, land_z

        def pair(self, to_z):
            return remote(
                self.gw.at[2 * to_z + 1 - c], self.land_p.at[to_z],
                gp_send.at[self.index, to_z], gp_recv.at[self.index, to_z], s, partner,
            )

        def along(self, i, to_z, of_z, slot):
            return remote(
                self.gw.at[2 * of_z + c], self.land_z.at[slot],
                gz_send.at[self.index, i], gz_recv.at[self.index, slot], s, 2 * to_z + c,
            )

        def add(self, who, land, slot):
            self.gw[who] = (self.gw[who].astype(F32) + land[slot].astype(F32)).astype(BF16)

        def add_pair(self, to_z):
            self.pair(to_z).wait_recv()
            self.add(2 * to_z + c, self.land_p, to_z)

        def first(self):
            for slot, of_z in ((1, mid_o), (2, end_o), (0, near)):
                self.add_pair(of_z)

                @pl.when(is_mid == 0)
                def _(slot=slot, of_z=of_z):
                    self.along(slot, near, of_z, slot).start()

            @pl.when(is_mid == 1)
            def _():
                self.along(0, near, near, 0).start()

            self.add_pair(z)

        def second(self):
            @pl.when(is_mid == 1)
            def _():
                for i, of_z in ((1, mid_o), (2, end_o)):
                    self.along(i, near, of_z, i).wait_recv()
                    self.add(2 * of_z + c, self.land_z, i)
                    self.along(i, of_z, of_z, 3).start()

        def wait(self):
            self.along(0, near, z, 0).wait_recv()
            self.along(1, near, z, 3).wait_recv()

        def total(self, at):
            value = self.gw[f, at].astype(F32)
            return value + self.land_z[0, at].astype(F32) + self.land_z[3, at].astype(F32)

        def drain(self):
            def one(to_z, _):
                self.pair(to_z).wait_send()
                return 0

            lax.fori_loop(0, n_f // 2, one, 0)
            for i in range(3):
                self.along(i, near, near, 0).wait_send()

    class Direct(Shed):
        def first(self):
            for d in (2, 1, 3):
                to_z = (z + d) % (n_f // 2)
                self.add_pair(to_z)
                self.along(d - 1, to_z, to_z, d - 1).start()
            self.add_pair(z)

        def second(self):
            pass

        def wait(self):
            for d in (1, 2, 3):
                self.along(d - 1, near, z, d - 1).wait_recv()

        def total(self, at):
            value = self.gw[f, at].astype(F32)
            for d in (1, 2, 3):
                value = value + self.land_z[d - 1, at].astype(F32)
            return value

    barrier = pltpu.get_barrier_semaphore()
    for who in (sx, sy, sd):
        pl.semaphore_signal(barrier, inc=1, device_id=(who, f), device_id_type=pl.DeviceIdType.MESH)
    n_peers = 3
    if inside:
        for d in range(1, n_f):
            pl.semaphore_signal(
                barrier, inc=1, device_id=(s, (f + d) % n_f), device_id_type=pl.DeviceIdType.MESH
            )
        n_peers += n_f - 1
    pl.semaphore_wait(barrier, n_peers)

    others = (sx, sy, sd)
    ag_tok = Gather(tok, 0)
    if inside:
        high = qkv_in.shape[0]
        high_d = down_in.shape[0]
        w_qkv = [
            Weight(0, by_cut(qkv_w.at[0:2], high)), Weight(4, by_cut(qkv_w.at[2:4], high))
        ]
        w_out = Weight(1, by_rows(out_w.at[0], high))
        w_up = Weight(2, by_cut(up_w, high))
        w_down = Weight(3, by_rows(down_w, high_d))

        def qkv_copy(k, p, to):
            start = pl.multiple_of((p % 3) * width + to * group + (p // 3) * 128, 128)
            src = qkv_in.at[:, pl.ds(start, 128)]
            dst = qkv_w.at[s, pl.ds(pl.multiple_of(f * high, high), high), pl.ds(p * 128, 128)]
            if k < 0:
                return pltpu.make_async_copy(src, dst, col_local.at[p])
            return remote(src, dst, col_send.at[k, p], col_recv.at[k, p], to, f)

        n_cut = 3 * pairs

        ff = up_w.shape[2]

        def up_copy(k, to):
            src = up_in.at[:, pl.ds(pl.multiple_of(to * ff, 128), ff)]
            dst = up_w.at[s, pl.ds(pl.multiple_of(f * high, high), high)]
            if k < 0:
                return pltpu.make_async_copy(src, dst, loc_sem.at[6])
            return remote(src, dst, upc_send.at[k], upc_recv.at[k], to, f)

        out_own = pltpu.make_async_copy(out_in, w_out.view(f), loc_sem.at[0])
        down_own = pltpu.make_async_copy(down_in, w_down.view(f), loc_sem.at[1])

        def small_copy(d):
            return remote(
                small_in, small_f.at[f], sf_send.at[d], sf_recv.at[d], s, (f + d) % n_f
            )

        for d in range(1, n_f):
            small_copy(d).start()
        for p in range(n_cut):
            for k, to in enumerate(others):
                qkv_copy(k, p, to).start()
        for k, to in enumerate(others):
            up_copy(k, to).start()
        for p in range(n_cut):
            qkv_copy(-1, p, s).start()
        up_copy(-1, s).start()
        out_own.start()
        down_own.start()
        small_f[f] = small_in[...]
    else:
        loads = [
            pltpu.make_async_copy(qkv_in, qkv_w, col_local.at[0]),
            pltpu.make_async_copy(up_in, up_w, loc_sem.at[6]),
            pltpu.make_async_copy(out_in, out_w, loc_sem.at[0]),
            pltpu.make_async_copy(down_in, down_w, loc_sem.at[1]),
        ]
        for load in loads:
            load.start()
    tok_own = pltpu.make_async_copy(tokens, tok.at[s], loc_sem.at[2])
    tok_own.start()
    cot_own = pltpu.make_async_copy(cot_in, cot, loc_sem.at[3])
    cot_own.start()
    seg_own = pltpu.make_async_copy(seg_in, segs.at[s], loc_sem.at[4])
    seg_own.start()

    def seg_copy(k, to):
        return remote(seg_in, segs.at[s], seg_send.at[k], seg_recv.at[k], to, f)

    for k, to in enumerate(others):
        seg_copy(k, to).start()

    if inside:
        for d in range(1, n_f):
            remote(
                small_in, small_f.at[(f + n_f - d) % n_f], sf_send.at[d], sf_recv.at[d],
                s, (f + d) % n_f,
            ).wait_recv()
        per = n_f * high // 128
        each = n_f // per
        for t in range(per):
            value = small_f[t * each, 0:8]
            for e in range(1, each):
                value = value + small_f[t * each + e, 0:8]
            small_s[s, t] = value
        for e in range(n_f):
            bias_row[0:1, pl.ds(e * 128, 128)] = small_f[e, 8:9]

        def small_wide(k, to):
            return remote(small_s.at[s], small_s.at[s], ss_send.at[k], ss_recv.at[k], to, f)

        for k, to in enumerate(others):
            small_wide(k, to).start()
        ag_tok.start(tokens)
        for p in range(n_cut):
            qkv_copy(-1, p, s).wait()
            for k, to in enumerate(others):
                qkv_copy(k, p, to).wait_recv()
        for weight in w_qkv:
            weight.start()
        w_out.start(out_in)
        up_copy(-1, s).wait()
        for k, to in enumerate(others):
            up_copy(k, to).wait_recv()
        for k, who in enumerate(others):
            remote(
                small_s.at[who], small_s.at[who], ss_send.at[k], ss_recv.at[k], who, f
            ).wait_recv()
        for b in range(4):
            for t in range(per):
                params[:, pl.ds((b * per + t) * 128, 128)] = small_s[b, t]
    else:
        ag_tok.start(tokens)
        params[...] = small_in[0:8]
        bias_row[...] = small_in[8:9, 0 : bias_row.shape[1]]

    zero_row = jnp.zeros((1, width), F32)

    def both(run, count):
        def step(h, carry):
            return tuple(a + b for a, b in zip(carry, run(h)))

        return lax.fori_loop(0, 2, step, (zero_row,) * count)

    def far_first(i):
        return (1 - i // 2) + 2 * (1 - i % 2)

    def param(i):
        return params[i : i + 1, :]

    tok_own.wait()
    if inside:
        w_qkv[0].relay()
    ag_tok.relay()
    if inside:
        w_up.start_far()

    def first_norm(b):
        unit, _s = unit_of(tok[b].astype(F32))
        normed[b] = (unit * param(0) + param(1)).astype(BF16)

    def norm_step(k, _):
        @pl.when(k == 1)
        def _():
            ag_tok.wait_x()

        @pl.when(k == 2)
        def _():
            ag_tok.wait_y()

        @pl.when(k == 3)
        def _():
            ag_tok.wait_d()

        first_norm(block(k))
        return 0

    lax.fori_loop(0, 1, norm_step, 0)
    if inside:
        w_qkv[1].relay()
        w_out.relay(False)
        w_up.start_near()
        w_down.start_far(down_in)
    lax.fori_loop(1, 4, norm_step, 0)
    if inside:
        for weight in w_qkv:
            weight.rest()
        for weight in w_qkv:
            weight.finish()
    else:
        for load in loads:
            load.wait()

    rest = normed[...].reshape(4 * rows, width)
    for p in range(pairs):
        value = dot(rest, qkv_w[:, :, p * 384 : (p + 1) * 384].reshape(width, 384))
        for q in range(3):
            piece = value[:, q * 128 : (q + 1) * 128]
            piece = piece if q else piece * 0.125
            at = slice((3 * p + q) * 128, (3 * p + q + 1) * 128)
            triple[:, :, at] = piece.astype(BF16).reshape(4, rows, 128)
    if inside:
        out_own.wait()
        w_out.relay_rest()
        w_out.rest()
        w_out.finish()

    seg_own.wait()
    for k, who in enumerate(others):
        remote(seg_in, segs.at[who], seg_send.at[k], seg_recv.at[k], who, f).wait_recv()
    seg_all = segs[...]

    def below(level):
        count = jnp.sum((seg_all < level).astype(F32), axis=0)
        return jnp.sum(count, axis=1, keepdims=True)

    bound_1, bound_2 = below(1), below(2)
    blocks = window // rows
    lane = lax.broadcasted_iota(jnp.int32, (1, 128), 1)
    left = (lane < HEAD_DIM).astype(F32)
    sides = (left.astype(BF16), (1.0 - left).astype(BF16))
    pick = lax.broadcasted_iota(jnp.int32, (rows, 128), 1) < HEAD_DIM

    def set_starts(r, _):
        i = (r * rows + lax.broadcasted_iota(jnp.int32, (rows, 128), 0)).astype(F32)
        starts[r] = jnp.where(i >= bound_2, bound_2, jnp.where(i >= bound_1, bound_1, 0.0))
        return 0

    lax.fori_loop(0, 4, set_starts, 0)

    def cut(r, part_at, p, count):
        at = pl.ds(pl.multiple_of((3 * p + part_at) * 128, 128), 128)
        return triple[pl.ds(r, count), :, at].reshape(count * rows, 128)

    def masked(scores, r, first, count):
        start = starts[r]
        tiles = []
        for t in range(count * rows // 128):
            j = lax.broadcasted_iota(jnp.int32, (rows, 128), 1) + t * 128
            keep = (first * rows + j).astype(F32) >= start
            if t * 128 >= (count - 1) * rows:
                i = lax.broadcasted_iota(jnp.int32, (rows, 128), 0)
                keep = keep & (j - (count - 1) * rows <= i)
            tiles.append(jnp.where(keep, scores[:, t * 128 : (t + 1) * 128], NEG))
        return jnp.concatenate(tiles, axis=1)

    rs_1 = Scatter(land_a, 0)

    def attend_pair(r, first, count, p):
        query, keys, vals = cut(r, 0, p, 1), cut(first, 1, p, count), cut(first, 2, p, count)
        outs = []
        for e in range(2):
            scores = masked(dot(query * sides[e], keys, NT), r, first, count)
            expo = jnp.exp(scores - jnp.max(scores, -1, keepdims=True))
            low = (expo * (1.0 / jnp.sum(expo, -1, keepdims=True))).astype(BF16)
            probs[r, 2 * p + e, :, 0 : count * rows] = low
            outs.append(dot(low, vals))
        attended[r, :, p * 128 : (p + 1) * 128] = jnp.where(pick, outs[0], outs[1]).astype(BF16)

    def attend(i, _):
        rel = far_first(i)
        r = block(rel)
        for count in range(1, blocks + 1):
            @pl.when(r + 1 >= count if count == blocks else r + 1 == count)
            def _(count=count):
                for p in range(pairs):
                    attend_pair(r, r + 1 - count, count, p)

        part[rel] = dot(attended[r], out_w[0]).astype(BF16)

        @pl.when(c == 0)
        def _():
            rs_1.step(rel)

        if inside:
            @pl.when(i == 1)
            def _():
                w_up.relay()
                w_down.start_near(down_in)

        return 0

    lax.fori_loop(0, 4, attend, 0)

    my_turn((1, 1))

    @pl.when(c == 1)
    def _():
        for i in (0, 2, 1, 3):
            rs_1.copy(i).start()

    rs_1.relay()
    if inside:
        w_down.relay()

        @pl.when(c == 1)
        def _():
            w_up.rest()

    rs_1.wait()

    def mid_norm(h):
        at = half_rows(h)
        value = rs_1.total(h)
        branch[at] = value
        unit, _s = unit_of(value)
        mid = tok[s, at].astype(F32) + (unit * param(2) + param(3))
        middle[at] = mid
        unit, _s = unit_of(mid)
        inner[s, at] = (unit * param(4) + param(5)).astype(BF16)

    for h in range(2):
        mid_norm(h)
    ag_inner = Gather(inner, 1)
    my_turn()
    ag_inner.start()
    rs_1.drain()
    if inside:
        @pl.when(c == 0)
        def _():
            w_up.rest()

        w_up.finish()

    ff = up_w.shape[2]
    tile = 512
    rs_2 = Scatter(land_b, 1)

    def forward_step(k, _):
        if inside:
            @pl.when((k == 1) & (c == 1))
            def _():
                ag_inner.relay()
                w_down.rest()
                ag_inner.wait_x()

            @pl.when((k == 1) & (c == 0))
            def _():
                ag_inner.relay()
                ag_inner.wait_x()

            @pl.when((k == 2) & (c == 0))
            def _():
                w_down.rest()

            @pl.when(k > 1)
            def _():
                ag_inner.step(k)
        else:
            ag_inner.step(k)
        r = block(k)

        def column(n, _):
            at = pl.ds(pl.multiple_of(n * tile, tile), tile)
            pre = dot(inner[r], up_w[:, :, at].reshape(width, tile)) + bias_row[:, at]
            square = pre * pre
            bend = jnp.tanh(0.7978845608028654 * pre * (1.0 + 0.044715 * square))
            near = 0.5 + 0.5 * bend
            activ[r, :, at] = (pre * near).astype(BF16)
            slope = near + pre * (0.5 - 0.5 * bend * bend) * (
                0.7978845608028654 + 0.10703222440890037 * square
            )
            dgelu[r, :, at] = slope.astype(BF16)
            return 0

        lax.fori_loop(0, ff // tile, column, 0)
        return 0

    lax.fori_loop(0, 4, forward_step, 0)
    if inside:
        down_own.wait()
        w_down.finish()

    def down_step(i, _):
        rel = far_first(i)
        r = block(rel)

        part[rel] = dot(activ[r], down_w[...]).astype(BF16)
        rs_2.step(rel)
        return 0

    my_turn()
    lax.fori_loop(0, 4, down_step, 0)
    rs_2.relay()
    cot_own.wait()
    rs_2.wait()

    def last_norm(h):
        at = half_rows(h)
        unit, scale = unit_of(rs_2.total(h))
        result_v[at] = (middle[at] + (unit * param(6) + param(7))).astype(BF16)
        grad = cot[at].astype(F32)
        gmix[s, at] = pull_of(grad, param(6), unit, scale).astype(BF16)
        return col_sum(grad * unit), col_sum(grad)

    grad_gain_d, grad_shift_d = both(last_norm, 2)
    sg_rows = [None] * 8
    sg_rows[6], sg_rows[7] = grad_gain_d, grad_shift_d
    ag_mix = Gather(gmix, 2)
    my_turn()
    ag_mix.start()
    result_out = pltpu.make_async_copy(result_v, result, o_sem.at[2])
    result_out.start()
    rs_2.drain()

    rs_3 = Scatter(land_a, 2)
    sg_bias = bias_row

    def clear(n, _):
        at = pl.ds(pl.multiple_of(n * tile, tile), tile)
        sg_bias[:, at] = jnp.zeros((1, tile), F32)
        return 0

    lax.fori_loop(0, ff // tile, clear, 0)

    def back_step(k, _):
        ag_mix.step(k)
        r = block(k)

        def column(n, _):
            at = pl.ds(pl.multiple_of(n * tile, tile), tile)
            grad = dot(gmix[r], down_w[at], NT)
            low = (dgelu[r, :, at].astype(F32) * grad).astype(BF16)
            dgelu[r, :, at] = low
            sg_bias[:, at] = sg_bias[:, at] + col_sum(low.astype(F32))
            return 0

        lax.fori_loop(0, ff // tile, column, 0)
        return 0

    lax.fori_loop(0, 4, back_step, 0)

    TN = ((0,), (0,))

    def flat(ref, lanes=slice(None)):
        held = ref[:, :, lanes]
        return held.reshape(4 * rows, held.shape[2])

    def all_pairs(shed):
        for to_z in range(n_f // 2):
            shed.pair(to_z).start()

    def cut_grads(left, right, gw, shed, lanes=slice(None)):
        for b in range(4):
            value = dot(flat(left, slice(b * rows, (b + 1) * rows)), flat(right, lanes), TN)
            gw[:, b * high : (b + 1) * high, :] = value.astype(BF16).reshape(n_f, high, -1)
        all_pairs(shed)

    def row_grads(left, right, gw, shed):
        each = left.shape[2] // n_f
        most = max(each, 256)
        for b in range(left.shape[2] // most):
            value = dot(flat(left, slice(b * most, (b + 1) * most)), flat(right), TN)
            count = most // each
            gw[b * count : (b + 1) * count] = value.astype(BF16).reshape(count, each, -1)
        all_pairs(shed)

    if inside:
        shed_down = Shed(0, gw_down, lp_down, lz_down)
        shed_up = Shed(1, gw_up, lp_up, lz_up)
        shed_out = Shed(2, gw_out, lp_out, lz_out)
        shed_qkv = [
            (Shed if p < pairs - 1 else Direct)(3 + p, gw_qkv[p], lp_qkv[p], lz_qkv[p])
            for p in range(pairs)
        ]
        ag_tok.drain()
        row_grads(activ, gmix, gw_down, shed_down)

        @pl.when(c == 1)
        def _():
            shed_down.first()

    def inner_step(i, _):
        rel = far_first(i)
        r = block(rel)

        part[rel] = dot(dgelu[r], up_w[...].reshape(width, ff), NT).astype(BF16)
        rs_3.step(rel)
        return 0

    my_turn()
    lax.fori_loop(0, 4, inner_step, 0)

    if inside:
        cut_grads(inner, dgelu, gw_up, shed_up)
    rs_3.relay()
    if inside:
        @pl.when(c == 1)
        def _():
            shed_up.first()

        @pl.when(c == 0)
        def _():
            shed_down.first()

    rs_3.wait()

    def mid_back(h):
        at = half_rows(h)
        grad = rs_3.total(h)
        unit, scale = unit_of(middle[at])
        total = cot[at].astype(F32) + pull_of(grad, param(4), unit, scale)
        gmid[at] = total
        out = [col_sum(grad * unit), col_sum(grad)]
        unit, scale = unit_of(branch[at])
        gbr[s, at] = pull_of(total, param(2), unit, scale).astype(BF16)
        return out[0], out[1], col_sum(total * unit), col_sum(total)

    sg_rows[4], sg_rows[5], sg_rows[2], sg_rows[3] = both(mid_back, 4)
    ag_br = Gather(gbr, 3)
    my_turn()
    ag_br.start()
    rs_3.drain()
    def arrive(k, _):
        if inside:
            @pl.when(k == 1)
            def _():
                ag_br.relay()

            @pl.when((k == 1) & (c == 0))
            def _():
                shed_up.first()

            @pl.when(k == 1)
            def _():
                ag_br.wait_x()

            @pl.when(k > 1)
            def _():
                ag_br.step(k)

            @pl.when(k == 2)
            def _():
                shed_down.second()
        else:
            ag_br.step(k)

        r = block(k)
        gatt[r] = dot(gbr[r], out_w[0], NT).astype(BF16)
        if inside:
            value = dot(attended[r], gbr[r], TN)

            @pl.when(k == 0)
            def _():
                branch[...] = value

            @pl.when(k > 0)
            def _():
                branch[...] = branch[...] + value

        return 0

    lax.fori_loop(0, 4, arrive, 0)
    if inside:
        gw_out[...] = branch[...].astype(BF16).reshape(gw_out.shape)
        all_pairs(shed_out)

    if inside:
        per = n_f * high // 128
        gdown_out = pltpu.make_async_copy(fin_down, gdown, o_sem.at[3])
        gout_out = pltpu.make_async_copy(fin_out, gout, o_sem.at[4])
        gup_out = pltpu.make_async_copy(gup_v, gup, o_sem.at[5])
        gqkv_out = pltpu.make_async_copy(gqkv_v, gqkv, o_sem.at[6])
        gsmall_out = pltpu.make_async_copy(small_sum, gsmall, o_sem.at[7])

        def ts_copy(k, to):
            return remote(sg_s.at[to], sg_land_s.at[k], ts_send.at[k], ts_recv.at[k], to, f)

        def tf_copy(d):
            to = (f + d) % n_f
            return remote(
                sg_f.at[to], sg_land_f.at[d - 1], tf_send.at[d], tf_recv.at[d], s, to
            )

        def small_first():
            for b in range(4):
                for t in range(per):
                    at = slice((b * per + t) * 128, (b * per + t + 1) * 128)
                    for i in range(8):
                        sg_s[b, t, i : i + 1, :] = sg_rows[i][:, at]
            for k, to in enumerate(others):
                ts_copy(k, to).start()

        def small_second():
            for k, to in enumerate(others):
                ts_copy(k, to).wait_recv()
            for who in range(n_f):
                t = who * high // 128
                sg_f[who, 0:8] = (
                    sg_s[s, t] + sg_land_s[0, t] + sg_land_s[1, t] + sg_land_s[2, t]
                )
                sg_f[who, 8:9] = sg_bias[:, who * 128 : (who + 1) * 128]
            for d in range(1, n_f):
                tf_copy(d).start()

        def small_third():
            for d in range(1, n_f):
                tf_copy(d).wait_recv()
            value = sg_f[f]
            for d in range(1, n_f):
                value = value + sg_land_f[d - 1]
            small_sum[...] = value
            gsmall_out.start()

        def gu_copy(k, to, who):
            return remote(fin_up.at[to], land_up.at[who], gu_send.at[k], gu_recv.at[k], to, f)

        def gc_at(p, who):
            start = pl.multiple_of((p % 3) * width + who * group + (p // 3) * 128, 128)
            return pl.ds(start, 128)

        def gc_copy(k, p, to, who):
            return remote(
                fin_qkv.at[p, to], land_qkv.at[p, who],
                gc_send.at[k, p], gc_recv.at[k, p], to, f,
            )

    def back_pair(p):
        lanes = slice(p * 128, (p + 1) * 128)
        for r in range(3, -1, -1):
            first = max(r + 1 - blocks, 0)
            count = r + 1 - first
            query, keys, vals = cut(r, 0, p, 1), cut(first, 1, p, count), cut(first, 2, p, count)
            grad = gatt[r, :, lanes]
            query_t, grad_t = query.T, grad.T
            outs, key_parts, value_parts = [], [], []
            for e in range(2):
                low = probs[r, 2 * p + e, :, 0 : count * rows]
                grad_probs = dot(grad * sides[e], vals, NT)
                full = low.astype(F32)
                inner_sum = jnp.sum(full * grad_probs, -1, keepdims=True)
                grad_scores = (full * (grad_probs - inner_sum)).astype(BF16)
                outs.append(dot(grad_scores, keys))
                side = slice(e * HEAD_DIM, (e + 1) * HEAD_DIM)
                here = slice(p * 128 + e * HEAD_DIM, p * 128 + (e + 1) * HEAD_DIM)
                key_part = dot(query_t[side], grad_scores)
                value_part = dot(grad_t[side], low)
                for n in range(count):
                    span = slice((first + n) * rows, (first + n + 1) * rows)
                    cols = slice(n * rows, (n + 1) * rows)
                    if r == 3 or (first + n) < 4 - blocks and r == first + n + blocks - 1:
                        dkt[here, span] = key_part[:, cols]
                        dvt[here, span] = value_part[:, cols]
                    else:
                        dkt[here, span] = dkt[here, span] + key_part[:, cols]
                        dvt[here, span] = dvt[here, span] + value_part[:, cols]
            at = slice(3 * p * 128, (3 * p + 1) * 128)
            gtri[r, :, at] = (jnp.where(pick, outs[0], outs[1]) * 0.125).astype(BF16)
        for b in range(4):
            span = slice(b * rows, (b + 1) * rows)
            at = slice((3 * p + 1) * 128, (3 * p + 2) * 128)
            gtri[b, :, at] = dkt[lanes, span].astype(BF16).T
            at = slice((3 * p + 2) * 128, (3 * p + 3) * 128)
            gtri[b, :, at] = dvt[lanes, span].astype(BF16).T

    for p in range(pairs):
        back_pair(p)
        if inside:
            cut_grads(normed, gtri, gw_qkv[p], shed_qkv[p], slice(p * 384, (p + 1) * 384))
            if p == 0:
                shed_up.second()

    rs_4 = Scatter(land_b, 3)

    def normed_step(i, carry):
        rel = far_first(i)
        r = block(rel)
        grad = dot(gtri[r], qkv_w[...].reshape(width, 3 * group), NT)
        part[rel] = grad.astype(BF16)
        rs_4.step(rel)
        unit, _s = unit_of(tok[r].astype(F32))
        return carry[0] + col_sum(grad * unit), carry[1] + col_sum(grad)

    if inside:
        @pl.when(c == 1)
        def _():
            for shed in (*shed_qkv, shed_out):
                shed.first()

    my_turn()
    sg_rows[0], sg_rows[1] = lax.fori_loop(0, 4, normed_step, (zero_row, zero_row))
    if inside:
        @pl.when(c == 0)
        def _():
            shed_qkv[0].first()

    rs_4.relay()
    if inside:
        @pl.when(c == 0)
        def _():
            for shed in (*shed_qkv[1:], shed_out):
                shed.first()

        small_first()
        shed_qkv[0].second()
        shed_up.wait()
        for b in range(4):
            fin_up[b] = shed_up.total(slice(b * high, (b + 1) * high)).astype(BF16)
        for k, to in enumerate(others):
            gu_copy(k, to, s).start()
        at = pl.ds(pl.multiple_of(s * high, high), high)
        gup_v[:, pl.ds(pl.multiple_of(s * ff, 128), ff)] = shed_up.total(at)
        small_second()
        shed_down.wait()
        fin_down[...] = shed_down.total(slice(None))
        gdown_out.start()
        for q, shed in enumerate(shed_qkv):
            shed.wait()
            for b in range(4):
                fin_qkv[q, b] = shed.total(slice(b * high, (b + 1) * high)).astype(BF16)
            for k, to in enumerate(others):
                gc_copy(k, q, to, s).start()
            own = shed.total(at)
            for p in range(3):
                gqkv_v[:, gc_at(3 * q + p, s)] = own[:, p * 128 : (p + 1) * 128]
        for k, who in enumerate(others):
            gu_copy(k, who, who).wait_recv()
            gup_v[:, pl.ds(pl.multiple_of(who * ff, 128), ff)] = land_up[who].astype(F32)
        gup_out.start()
        small_third()
        shed_out.second()
    rs_4.wait()

    def first_back(h, _):
        at = half_rows(h)
        unit, scale = unit_of(tok[s, at].astype(F32))
        gmid[at] = gmid[at] + pull_of(rs_4.total(h), param(0), unit, scale)
        pltpu.make_async_copy(gmid.at[at], tgrad.at[at], o_sem.at[h]).start()
        return 0

    lax.fori_loop(0, 2, first_back, 0)
    if inside:
        shed_out.wait()
        fin_out[...] = shed_out.total(slice(None))
        gout_out.start()
        for k, who in enumerate(others):
            for q in range(pairs):
                gc_copy(k, q, who, who).wait_recv()
                for p in range(3):
                    piece = land_qkv[q, who, :, p * 128 : (p + 1) * 128]
                    gqkv_v[:, gc_at(3 * q + p, who)] = piece.astype(F32)
        gqkv_out.start()

    for h in range(2):
        pltpu.make_async_copy(gmid.at[half_rows(h)], tgrad.at[half_rows(h)], o_sem.at[h]).wait()
    result_out.wait()
    if inside:
        gsmall_out.wait()
        gdown_out.wait()
        gout_out.wait()
        gup_out.wait()
        gqkv_out.wait()
        for k, to in enumerate(others):
            gu_copy(k, to, s).wait_send()
            ts_copy(k, to).wait_send()
            for q in range(pairs):
                gc_copy(k, q, to, s).wait_send()
            for p in range(n_cut):
                qkv_copy(k, p, to).wait_send()
            up_copy(k, to).wait_send()
            small_wide(k, to).wait_send()
        for d in range(1, n_f):
            tf_copy(d).wait_send()
            small_copy(d).wait_send()
        for weight in (*w_qkv, w_out, w_up, w_down):
            weight.drain()
        for shed in (shed_down, shed_up, shed_out, *shed_qkv):
            shed.drain()
    else:
        for i in range(8):
            small_sum[i : i + 1, :] = sg_rows[i]
        small_sum[8:9, 0:ff] = sg_bias[...]
        gsmall_out = pltpu.make_async_copy(small_sum, gsmall, o_sem.at[7])
        gsmall_out.start()
        gsmall_out.wait()
    for k, to in enumerate(others):
        seg_copy(k, to).wait_send()
    for gather in (ag_inner, ag_mix, ag_br) + (() if inside else (ag_tok,)):
        gather.drain()
    rs_4.drain()


def finish_kernel(n_f, n_big, *refs):
    small, given = refs[0], refs[1 : 1 + n_big]
    made, minor = refs[1 + n_big : 1 + 2 * n_big], refs[1 + 2 * n_big : 10 + 2 * n_big]
    held, (in_sem, out_sem) = refs[10 + 2 * n_big : 10 + 3 * n_big], refs[10 + 3 * n_big :]
    cuts = []
    for i in range(n_big):
        tall = given[i].shape[0]
        for j in range(max(1, tall // 64)):
            at = pl.ds(j * min(tall, 64), min(tall, 64))
            cuts.append((i, at, len(cuts)))
    for i, at, n in cuts:
        pltpu.make_async_copy(given[i].at[at], held[i].at[at], in_sem.at[n]).start()
    each = minor[0].shape[1]
    place = lax.axis_index("fsdp") % (128 // each)
    for i in range(8):
        row = small[i : i + 1, :]
        value = row[:, 0:each]
        for q in range(1, 128 // each):
            value = jnp.where(place == q, row[:, q * each : (q + 1) * each], value)
        minor[i][...] = value
    minor[8][...] = small[8:9, :]
    for i, at, n in cuts:
        pltpu.make_async_copy(given[i].at[at], held[i].at[at], in_sem.at[n]).wait()
        pltpu.make_async_copy(held[i].at[at], made[i].at[at], out_sem.at[n]).start()
    for i, at, n in cuts:
        pltpu.make_async_copy(held[i].at[at], made[i].at[at], out_sem.at[n]).wait()


def finish(n_f, high, *made):
    big, small = made[:6], made[6]
    whole, anywhere = pl.BlockSpec(memory_space=pltpu.VMEM), pl.BlockSpec(memory_space=pl.ANY)
    count = sum(max(1, v.shape[0] // 64) for v in big)
    minor = [jax.ShapeDtypeStruct((1, high), F32)] * 8 + [jax.ShapeDtypeStruct((1, 128), F32)]
    out = pl.pallas_call(
        partial(finish_kernel, n_f, 6),
        out_shape=[jax.ShapeDtypeStruct(v.shape, v.dtype) for v in big] + minor,
        in_specs=[whole] + [anywhere] * 6,
        out_specs=[anywhere] * 6 + [whole] * 9,
        scratch_shapes=[pltpu.VMEM(v.shape, v.dtype) for v in big]
        + [pltpu.SemaphoreType.DMA((count,))] * 2,
    )(small, *big)
    result, tgrad, gqkv, gout, gup, gdown = out[:6]
    small = [v[0] for v in out[6:]]
    return (result[None], tgrad[None], gqkv, gout, gup, small[8], gdown, *small[:8])


def on_device(n_seq, n_f, *args):
    (tokens, segments, qkv_weight, out_weight, up_weight, up_bias, down_weight) = args[:7]
    vectors, cotangent = args[7:15], args[15]
    rows, width = tokens.shape[1:]
    high, high_d = qkv_weight.shape[0], down_weight.shape[0]
    length = n_seq * rows
    group = qkv_weight.shape[1] // 3 // n_seq
    heads = group // HEAD_DIM
    ff = up_weight.shape[1] // n_seq
    half = rows // 2
    window = rows * min(n_seq, 1 + -(-511 // rows))
    inside = n_f == 8 and high % 32 == 0
    f = lax.axis_index("fsdp")
    small = jnp.stack([v.astype(F32) for v in vectors])
    if inside:
        each = 128 // high
        lane = lax.broadcasted_iota(jnp.int32, (8, 128), 1) // high
        small = jnp.where(lane == f % each, jnp.tile(small, (1, each)), 0.0)
        small = jnp.concatenate([small, up_bias.astype(F32)[None], jnp.zeros((7, 128), F32)])
        weights = (qkv_weight, out_weight, up_weight, down_weight)
    else:
        small = lax.all_gather(small, ("seq", "fsdp"), axis=1, tiled=True)
        bias = lax.all_gather(up_bias.astype(F32), "fsdp", axis=0, tiled=True)
        bias = jnp.pad(bias[None], ((0, 7), (0, width - ff)))
        small = jnp.concatenate([small, bias])

        def columns(weight, parts):
            cut = weight.reshape(high, parts, n_seq, -1, 128).transpose(2, 0, 3, 1, 4)
            cut = cut.reshape(n_seq, high, -1)
            cut = lax.all_to_all(cut, "seq", split_axis=0, concat_axis=0, tiled=True)
            return lax.all_gather(cut, "fsdp", axis=1, tiled=True)

        weights = (
            columns(qkv_weight, 3),
            lax.all_gather(out_weight, "fsdp", axis=0, tiled=True)[None],
            columns(up_weight, 1),
            lax.all_gather(down_weight, "fsdp", axis=0, tiled=True),
        )
    vmem, anywhere, dma = pltpu.VMEM, pl.BlockSpec(memory_space=pl.ANY), pltpu.SemaphoreType.DMA
    whole = pl.BlockSpec(memory_space=pltpu.VMEM)
    full = (4, rows, width)
    saved = {
        "normed": (full, BF16), "inner": (full, BF16), "gmix": (full, BF16), "gbr": (full, BF16),
        "attended": ((4, rows, group), BF16), "activ": ((4, rows, ff), BF16),
        "dgelu": ((4, rows, ff), BF16), "gtri": ((4, rows, 3 * group), BF16),
    }
    n_cut = 3 * (group // 128)
    pieces = {"q0": (n_seq * high, 384), "q1": (n_seq * high, 384), "out": (high, width),
              "up": (n_seq * high, ff), "down": (high_d, width)}
    scratch = {
        "tok": vmem(full, BF16), "normed": None, "inner": None, "gmix": None, "gbr": None,
        "qkv_w": vmem((n_seq, rows, 3 * group), BF16), "out_w": vmem((1, group, width), BF16),
        "up_w": vmem((n_seq, rows, ff), BF16), "down_w": vmem((ff, width), BF16),
        "segs": vmem((4, 1, rows), jnp.int32),
        "small_f": vmem((n_f if inside else 1, 16, 128), F32), "small_s": vmem((4, width // 512, 8, 128), F32),
        "params": vmem((8, width), F32), "bias_row": vmem((1, ff), F32),
        "triple": vmem((4, rows, 3 * group), BF16), "probs": vmem((4, heads, rows, window), BF16),
        "attended": None, "starts": vmem((4, rows, 128), F32), "activ": None, "dgelu": None,
        "part": vmem(full, BF16), "land_a": vmem((6, half, width), BF16),
        "land_b": vmem((6, half, width), BF16),
        "branch": vmem((rows, width), F32), "middle": vmem((rows, width), F32),
        "gmid": vmem((rows, width), F32), "cot": vmem((rows, width), BF16),
        "gtri": None, "gatt": vmem((4, rows, group), BF16), "dkt": vmem((group, length), F32),
        "dvt": vmem((group, length), F32),
    }
    for name, (tall, wide) in pieces.items():
        scratch["gw_" + name] = vmem((n_f if inside else 1, tall if inside else 16, wide), BF16)
    for name, (tall, wide) in pieces.items():
        scratch["lp_" + name] = vmem((n_f // 2 if inside else 1, tall if inside else 16, wide), BF16)
    for name, (tall, wide) in pieces.items():
        scratch["lz_" + name] = vmem((n_f // 2 if inside else 1, tall if inside else 16, wide), BF16)
    scratch["result_v"] = vmem((rows, width), BF16)
    scratch["fin_qkv"] = vmem((group // 128, 4, high, 384), BF16)
    scratch["fin_up"] = vmem((4, high, ff), BF16)
    scratch["land_qkv"] = vmem((group // 128, 4, high, 384), BF16)
    scratch["land_up"] = vmem((4, high, ff), BF16)
    scratch["fin_down"] = vmem((high_d, width), F32)
    scratch["fin_out"] = vmem((high, width), F32)
    scratch["gup_v"] = vmem((high, n_seq * ff), F32)
    scratch["gqkv_v"] = vmem((high, n_seq * 3 * group), F32)
    scratch["small_sum"] = vmem((16, 128 if inside else width), F32)
    tiles = width // 512
    scratch["sg_s"] = vmem((4, tiles, 8, 128), F32)
    scratch["sg_land_s"] = vmem((3, tiles, 8, 128), F32)
    scratch["sg_f"] = vmem((n_f if inside else 1, 16, 128), F32)
    scratch["sg_land_f"] = vmem((n_f - 1 if inside else 1, 16, 128), F32)
    for name, shape in (
        ("ag_send", (4, 6)), ("ag_recv", (4, 6)), ("rs_send", (4, 6)), ("rs_recv", (4, 6)),
        ("w_send", (5, 4)), ("w_recv", (5, 3)), ("p_send", (5, 4)), ("p_recv", (5, 4)),
        ("col_send", (3, n_cut)), ("col_recv", (3, n_cut)), ("col_local", (n_cut,)),
        ("upc_send", (3,)), ("upc_recv", (3,)), ("seg_send", (3,)), ("seg_recv", (3,)),
        ("sf_send", (8,)), ("sf_recv", (8,)), ("ss_send", (3,)), ("ss_recv", (3,)),
        ("loc_sem", (7,)), ("o_sem", (8,)),
        ("gp_send", (5, 4)), ("gp_recv", (5, 4)), ("gz_send", (5, 4)), ("gz_recv", (5, 4)),
        ("gc_send", (3, 2)), ("gc_recv", (3, 2)), ("gu_send", (3,)), ("gu_recv", (3,)),
        ("ts_send", (3,)), ("ts_recv", (3,)), ("tf_send", (8,)), ("tf_recv", (8,)),
    ):
        scratch[name] = dma(shape)
    scratch["turn"] = pltpu.SemaphoreType.REGULAR
    outs = {
        "result": ((rows, width), BF16), "tgrad": ((rows, width), F32),
        "gqkv": ((high, n_seq * 3 * group), F32), "gout": ((high, width), F32),
        "gup": ((high, n_seq * ff), F32), "gdown": ((high_d, width), F32),
        "gsmall": ((16, 128 if inside else width), F32),
    }
    if inside:
        for name, shape in saved.items():
            scratch[name] = vmem(*shape)
        extra = []
    else:
        extra = list(saved)
    names = list(scratch)

    def kernel(*refs):
        given = refs[:8]
        made = refs[8 : 8 + len(outs)]
        more = dict(zip(extra, refs[8 + len(outs) :]))
        rest = refs[8 + len(outs) + len(extra) :]
        more.update(zip([n for n in names if scratch[n] is not None], rest))
        layer_kernel(inside, n_f, *given, *made, *[more[n] for n in names])

    shapes = [*outs.values(), *[saved[n] for n in extra]]
    made = pl.pallas_call(
        kernel,
        out_shape=[jax.ShapeDtypeStruct(*shape) for shape in shapes],
        in_specs=[anywhere, anywhere, whole, anywhere] + [anywhere] * 4,
        out_specs=[anywhere] * len(outs) + [whole] * len(extra),
        scratch_shapes=[scratch[n] for n in names if scratch[n] is not None],
        compiler_params=pltpu.CompilerParams(
            collective_id=0, has_side_effects=True, vmem_limit_bytes=67043328
        ),
    )(tokens[0], segments, small, cotangent[0], *weights)
    result, tgrad, gqkv, gout, gup, gdown, gsmall = made[:7]
    if inside:
        return finish(n_f, high, *made[:7])
    else:
        kept = {n: v.reshape(length, -1) for n, v in zip(extra, made[7:])}

        def turned_dot(left, right):
            return lax.dot_general(
                kept[left], kept[right], (((0,), (0,)), ((), ())), preferred_element_type=F32
            ).astype(BF16)

        def shed(value):
            return lax.psum_scatter(value, "fsdp", scatter_dimension=0, tiled=True)

        def columns_back(value, parts):
            cut = value.reshape(n_seq, n_f, high, -1).transpose(1, 0, 2, 3)
            cut = lax.all_to_all(shed(cut)[0], "seq", split_axis=0, concat_axis=0, tiled=True)
            cut = cut.reshape(n_seq, high, -1, parts, 128).transpose(1, 3, 0, 2, 4)
            return cut.reshape(high, -1).astype(F32)

        gqkv = columns_back(turned_dot("normed", "gtri"), 3)
        gout = shed(turned_dot("attended", "gbr")).astype(F32)
        gup = columns_back(turned_dot("inner", "dgelu"), 1)
        gdown = shed(turned_dot("activ", "gmix")).astype(F32)
        vectors = lax.psum_scatter(gsmall[:8], ("seq", "fsdp"), scatter_dimension=1, tiled=True)
        gbias = shed(gsmall[8, :ff])
    return (result[None], tgrad[None], gqkv, gout, gup, gbias, gdown, *vectors)


def solution(mesh):
    rows = P(("seq", "fsdp"), None)
    vector = P(("seq", "fsdp"))
    acts = P("fsdp", "seq", None)
    return jax.shard_map(
        partial(on_device, mesh.shape["seq"], mesh.shape["fsdp"]),
        mesh=mesh,
        in_specs=(acts, P("fsdp", "seq"), rows, rows, rows, vector, rows, *(vector,) * 8, acts),
        out_specs=(acts, acts, rows, rows, rows, vector, rows, *(vector,) * 8),
        check_vma=False,
    )
```

```python
from functools import partial

import jax
import jax.numpy as jnp
from jax import lax
from jax.experimental import pallas as pl
from jax.experimental.pallas import tpu as pltpu
from jax.sharding import PartitionSpec as P

HEAD_DIM = 64
F32 = jnp.float32
BF16 = jnp.bfloat16
NN = ((1,), (0,))
NT = ((1,), (1,))
NEG = -1e30


def dot(left, right, dims=NN):
    return lax.dot_general(left, right, (dims, ((), ())), preferred_element_type=F32)


def unit_of(value):
    center = value - jnp.mean(value, -1, keepdims=True)
    scale = lax.rsqrt(jnp.mean(center * center, -1, keepdims=True) + 1e-05)
    return center * scale, scale


def pull_of(grad, gain, unit, scale):
    pulled = grad * gain
    first = jnp.mean(pulled, -1, keepdims=True)
    second = jnp.mean(pulled * unit, -1, keepdims=True)
    return scale * (pulled - first - unit * second)


def col_sum(value):
    return jnp.sum(value, 0, keepdims=True)


def layer_kernel(
    inside,
    n_f,
    tokens, seg_in, small_in, cot_in, qkv_in, out_in, up_in, down_in,
    result, tgrad, gqkv, gout, gup, gdown, gsmall,
    tok, normed, inner, gmix, gbr,
    qkv_w, out_w, up_w, down_w,
    segs, small_f, small_s, params, bias_row,
    triple, probs, attended, starts, activ, dgelu,
    part, land_a, land_b,
    branch, middle, gmid, cot,
    gtri, gatt, dkt, dvt,
    gw_q0, gw_q1, gw_out, gw_up, gw_down,
    lp_q0, lp_q1, lp_out, lp_up, lp_down,
    lz_q0, lz_q1, lz_out, lz_up, lz_down,
    result_v, fin_qkv, fin_up, land_qkv, land_up, fin_down, fin_out, gup_v, gqkv_v, small_sum,
    sg_s, sg_land_s, sg_f, sg_land_f,
    ag_send, ag_recv, rs_send, rs_recv,
    w_send, w_recv, p_send, p_recv,
    col_send, col_recv, col_local, upc_send, upc_recv,
    seg_send, seg_recv, sf_send, sf_recv, ss_send, ss_recv,
    loc_sem, o_sem,
    gp_send, gp_recv, gz_send, gz_recv,
    gc_send, gc_recv, gu_send, gu_recv,
    ts_send, ts_recv, tf_send, tf_recv, turn,
):
    gw_qkv, lp_qkv, lz_qkv = (gw_q0, gw_q1), (lp_q0, lp_q1), (lz_q0, lz_q1)
    rows, width = tokens.shape
    half = rows // 2
    group = out_w.shape[1]
    pairs = group // 128
    window = probs.shape[3]
    s = lax.axis_index("seq")
    f = lax.axis_index("fsdp")
    x, y = s % 2, s // 2
    z, c = f // 2, f % 2

    def block(rel):
        return 2 * ((y + rel // 2) % 2) + (x + rel % 2) % 2

    sx, sy, sd = block(1), block(2), block(3)

    def remote(src, dst, send, recv, to_s, to_f):
        return pltpu.make_async_remote_copy(
            src_ref=src, dst_ref=dst, send_sem=send, recv_sem=recv,
            device_id=(to_s, to_f), device_id_type=pl.DeviceIdType.MESH,
        )

    def my_turn(cores=(0, 1)):
        if inside:
            @pl.when(c >= cores[0])
            def _():
                pl.semaphore_wait(turn, 1)

    def hand_over(cores=(0, 1)):
        if inside:
            @pl.when(c <= cores[1])
            def _():
                pl.semaphore_signal(
                    turn, inc=1, device_id=(s, 2 * z + 1 - c),
                    device_id_type=pl.DeviceIdType.MESH,
                )

    class Gather:
        def __init__(self, full, index):
            self.full, self.index = full, index

        def piece(self, b, h):
            return self.full.at[b, pl.ds(h * half, half)]

        def copy(self, i, b, h, to, src=None):
            dst = self.piece(b, h)
            return remote(
                dst if src is None else src, dst,
                ag_send.at[self.index, i], ag_recv.at[self.index, i], to, f,
            )

        def start(self, src=None):
            def cut(h):
                return None if src is None else src.at[pl.ds(h * half, half)]

            self.copy(0, s, 0, sx, cut(0)).start()
            self.copy(1, s, 1, sy, cut(1)).start()
            self.copy(2, s, 1, sx, cut(1)).start()
            self.copy(3, s, 0, sy, cut(0)).start()

        def relay(self):
            self.copy(0, sx, 0, sx).wait_recv()
            self.copy(4, sx, 0, sy).start()
            self.copy(1, sy, 1, sy).wait_recv()
            self.copy(5, sy, 1, sx).start()
            if self.index:
                hand_over()

        def wait_x(self):
            self.copy(2, sx, 1, sx).wait_recv()

        def wait_y(self):
            self.copy(3, sy, 0, sy).wait_recv()

        def wait_d(self):
            self.copy(4, sd, 0, sy).wait_recv()
            self.copy(5, sd, 1, sx).wait_recv()

        def step(self, k):
            @pl.when(k == 1)
            def _():
                self.relay()
                self.wait_x()

            @pl.when(k == 2)
            def _():
                self.wait_y()

            @pl.when(k == 3)
            def _():
                self.wait_d()

        def drain(self):
            for i, (b, h, to) in enumerate(
                ((s, 0, sx), (s, 1, sy), (s, 1, sx), (s, 0, sy), (sx, 0, sy), (sy, 1, sx))
            ):
                self.copy(i, b, h, to).wait_send()

    def half_rows(h):
        return pl.ds(pl.multiple_of(h * half, half), half)

    class Scatter:
        plan = ((3, 0, 1), (1, 0, 1), (3, 1, 2), (2, 1, 2), (2, 0, 2), (1, 1, 1))

        def __init__(self, land, index):
            self.land, self.index = land, index

        def copy(self, i):
            rel, h, way = self.plan[i]
            return remote(
                part.at[rel, pl.ds(h * half, half)], self.land.at[i],
                rs_send.at[self.index, i], rs_recv.at[self.index, i],
                sx if way == 1 else sy, f,
            )

        def step(self, rel):
            @pl.when(rel == 3)
            def _():
                self.copy(0).start()
                self.copy(2).start()

            @pl.when(rel == 1)
            def _():
                self.copy(1).start()

            @pl.when(rel == 2)
            def _():
                self.copy(3).start()

        def relay(self):
            for arrived, i in ((0, 4), (2, 5)):
                self.copy(arrived).wait_recv()
                rel, h, _ = self.plan[i]

                here = pl.ds(h * half, half)
                total = part[rel, here].astype(F32) + self.land[arrived].astype(F32)
                part[rel, here] = total.astype(BF16)
                self.copy(i).start()
            hand_over((0, 0) if self.index == 3 else (0, 1))

        def wait(self):
            for i in (1, 3, 4, 5):
                self.copy(i).wait_recv()

        def total(self, h):
            return (
                part[0, half_rows(h)].astype(F32)
                + self.land[1 + 2 * h].astype(F32)
                + self.land[4 + h].astype(F32)
            )

        def drain(self):
            for i in range(6):
                self.copy(i).wait_send()

    def by_rows(ref, size):
        def view(who):
            return ref.at[pl.ds(pl.multiple_of(who * size, size), size)]

        return view

    def by_cut(ref, size):
        def view(who):
            return ref.at[:, pl.ds(pl.multiple_of(who * size, size), size)]

        return view

    partner = 2 * z + 1 - c
    side = z // 2
    near = 4 * side + 1 - z
    mid_o, end_o = 2 - side, 3 - 3 * side
    is_mid = (z + side) % 2
    seen_as = 2 - is_mid
    owners = (near, mid_o, end_o)

    class Weight:
        def __init__(self, index, view):
            self.index, self.view = index, view

        def piece(self, to_z, i, k, owner_z, own=None):
            dst = self.view(2 * owner_z + c)
            return remote(
                dst if own is None else own, dst,
                w_send.at[self.index, i], w_recv.at[self.index, k], s, 2 * to_z + c,
            )

        def across(self, k, owner, own=None):
            dst = self.view(owner)
            return remote(
                dst if own is None else own, dst,
                p_send.at[self.index, k], p_recv.at[self.index, k], s, partner,
            )

        def start_far(self, own=None, across=True):
            self.piece(mid_o, 1, seen_as, z, own).start()
            if across:
                @pl.when(is_mid == 0)
                def _():
                    self.piece(near, 0, 0, z, own).start()

                self.across(3, f, own).start()

        def start_near(self, own=None, everyone=False):
            @pl.when((is_mid == 1) | everyone)
            def _():
                self.piece(near, 0, 0, z, own).start()

        def start(self, own=None):
            self.start_far(own)
            self.start_near(own)

        def relay(self, all_of_it=True):
            @pl.when(is_mid == 1)
            def _():
                for k in (1, 2):
                    self.piece(z, 0, k, owners[k]).wait_recv()
                    self.piece(near, 1 + k, k, owners[k]).start()
                for k in (1, 2):
                    self.across(k, 2 * owners[k] + c).start()

            if all_of_it:
                self.relay_rest()

        def relay_rest(self):
            @pl.when(is_mid == 1)
            def _():
                self.piece(z, 0, 0, near).wait_recv()
                self.across(0, 2 * near + c).start()

        def rest(self):
            @pl.when(is_mid == 0)
            def _():
                for k in (0, 1, 2):
                    self.piece(z, 0, k, owners[k]).wait_recv()
                    self.across(k, 2 * owners[k] + c).start()

        def finish(self):
            self.across(3, partner).wait_recv()
            for k in (0, 1, 2):
                self.across(k, 2 * owners[k] + 1 - c).wait_recv()

        def drain(self):
            self.piece(mid_o, 1, seen_as, z).wait_send()
            self.piece(near, 0, 0, z).wait_send()
            self.across(3, f).wait_send()

            @pl.when(is_mid == 1)
            def _():
                for k in (1, 2):
                    self.piece(near, 1 + k, k, owners[k]).wait_send()

            for k in (0, 1, 2):
                self.across(k, 2 * owners[k] + c).wait_send()

    class Shed:
        def __init__(self, index, gw, land_p, land_z):
            self.index, self.gw, self.land_p, self.land_z = index, gw, land_p, land_z

        def pair(self, to_z):
            return remote(
                self.gw.at[2 * to_z + 1 - c], self.land_p.at[to_z],
                gp_send.at[self.index, to_z], gp_recv.at[self.index, to_z], s, partner,
            )

        def along(self, i, to_z, of_z, slot):
            return remote(
                self.gw.at[2 * of_z + c], self.land_z.at[slot],
                gz_send.at[self.index, i], gz_recv.at[self.index, slot], s, 2 * to_z + c,
            )

        def add(self, who, land, slot):
            self.gw[who] = (self.gw[who].astype(F32) + land[slot].astype(F32)).astype(BF16)

        def add_pair(self, to_z):
            self.pair(to_z).wait_recv()
            self.add(2 * to_z + c, self.land_p, to_z)

        def far(self):
            for slot, of_z in ((1, mid_o), (2, end_o)):
                self.add_pair(of_z)

                @pl.when(is_mid == 0)
                def _(slot=slot, of_z=of_z):
                    self.along(slot, near, of_z, slot).start()

        def close(self):
            self.add_pair(near)
            self.along(0, near, near, 0).start()
            self.add_pair(z)

        def second(self):
            @pl.when(is_mid == 1)
            def _():
                for i, of_z in ((1, mid_o), (2, end_o)):
                    self.along(i, near, of_z, i).wait_recv()
                    self.add(2 * of_z + c, self.land_z, i)
                    self.along(i, of_z, of_z, 3).start()

        def wait(self):
            self.along(0, near, z, 0).wait_recv()
            self.along(1, near, z, 3).wait_recv()

        def total(self, at):
            value = self.gw[f, at].astype(F32)
            return value + self.land_z[0, at].astype(F32) + self.land_z[3, at].astype(F32)

        def drain(self):
            def one(to_z, _):
                self.pair(to_z).wait_send()
                return 0

            lax.fori_loop(0, n_f // 2, one, 0)
            for i in range(3):
                self.along(i, near, near, 0).wait_send()

    barrier = pltpu.get_barrier_semaphore()
    for who in (sx, sy, sd):
        pl.semaphore_signal(barrier, inc=1, device_id=(who, f), device_id_type=pl.DeviceIdType.MESH)
    n_peers = 3
    if inside:
        for d in range(1, n_f):
            pl.semaphore_signal(
                barrier, inc=1, device_id=(s, (f + d) % n_f), device_id_type=pl.DeviceIdType.MESH
            )
        n_peers += n_f - 1
    pl.semaphore_wait(barrier, n_peers)

    others = (sx, sy, sd)
    ag_tok = Gather(tok, 0)
    if inside:
        high = qkv_in.shape[0]
        high_d = down_in.shape[0]
        w_qkv = [
            Weight(0, by_cut(qkv_w.at[0:2], high)), Weight(4, by_cut(qkv_w.at[2:4], high))
        ]
        w_out = Weight(1, by_rows(out_w.at[0], high))
        w_up = Weight(2, by_cut(up_w, high))
        w_down = Weight(3, by_rows(down_w, high_d))

        def qkv_copy(k, p, to):
            start = pl.multiple_of((p % 3) * width + to * group + (p // 3) * 128, 128)
            src = qkv_in.at[:, pl.ds(start, 128)]
            dst = qkv_w.at[s, pl.ds(pl.multiple_of(f * high, high), high), pl.ds(p * 128, 128)]
            if k < 0:
                return pltpu.make_async_copy(src, dst, col_local.at[p])
            return remote(src, dst, col_send.at[k, p], col_recv.at[k, p], to, f)

        n_cut = 3 * pairs

        ff = up_w.shape[2]

        def up_copy(k, to):
            src = up_in.at[:, pl.ds(pl.multiple_of(to * ff, 128), ff)]
            dst = up_w.at[s, pl.ds(pl.multiple_of(f * high, high), high)]
            if k < 0:
                return pltpu.make_async_copy(src, dst, loc_sem.at[6])
            return remote(src, dst, upc_send.at[k], upc_recv.at[k], to, f)

        out_own = pltpu.make_async_copy(out_in, w_out.view(f), loc_sem.at[0])
        down_own = pltpu.make_async_copy(down_in, w_down.view(f), loc_sem.at[1])

        def small_copy(d):
            return remote(
                small_in, small_f.at[f], sf_send.at[d], sf_recv.at[d], s, (f + d) % n_f
            )

        for d in range(1, n_f):
            small_copy(d).start()
        for p in range(n_cut):
            for k, to in enumerate(others):
                qkv_copy(k, p, to).start()
        ag_tok.start(tokens)
        for p in range(n_cut):
            qkv_copy(-1, p, s).start()
        up_copy(-1, s).start()
        out_own.start()
        down_own.start()
        small_f[f] = small_in[...]
    else:
        loads = [
            pltpu.make_async_copy(qkv_in, qkv_w, col_local.at[0]),
            pltpu.make_async_copy(up_in, up_w, loc_sem.at[6]),
            pltpu.make_async_copy(out_in, out_w, loc_sem.at[0]),
            pltpu.make_async_copy(down_in, down_w, loc_sem.at[1]),
        ]
        for load in loads:
            load.start()
    tok_own = pltpu.make_async_copy(tokens, tok.at[s], loc_sem.at[2])
    tok_own.start()
    cot_own = pltpu.make_async_copy(cot_in, cot, loc_sem.at[3])
    cot_own.start()
    seg_own = pltpu.make_async_copy(seg_in, segs.at[s], loc_sem.at[4])
    seg_own.start()

    def seg_copy(k, to):
        return remote(seg_in, segs.at[s], seg_send.at[k], seg_recv.at[k], to, f)

    for k, to in enumerate(others):
        seg_copy(k, to).start()

    if inside:
        for d in range(1, n_f):
            remote(
                small_in, small_f.at[(f + n_f - d) % n_f], sf_send.at[d], sf_recv.at[d],
                s, (f + d) % n_f,
            ).wait_recv()
        per = n_f * high // 128
        each = n_f // per
        for t in range(per):
            value = small_f[t * each, 0:8]
            for e in range(1, each):
                value = value + small_f[t * each + e, 0:8]
            small_s[s, t] = value
        for e in range(n_f):
            bias_row[0:1, pl.ds(e * 128, 128)] = small_f[e, 8:9]

        def small_wide(k, to):
            return remote(small_s.at[s], small_s.at[s], ss_send.at[k], ss_recv.at[k], to, f)

        for k, to in enumerate(others):
            small_wide(k, to).start()
        for p in range(n_cut):
            qkv_copy(-1, p, s).wait()
            for k, to in enumerate(others):
                qkv_copy(k, p, to).wait_recv()
        for weight in w_qkv:
            weight.start_far(across=False)
        for weight in w_qkv:
            weight.start_near(everyone=True)
            weight.across(3, f).start()
        w_out.start(out_in)
        w_down.start_far(down_in)
    else:
        ag_tok.start(tokens)
        params[...] = small_in[0:8]
        bias_row[...] = small_in[8:9, 0 : bias_row.shape[1]]

    zero_row = jnp.zeros((1, width), F32)

    def both(run, count):
        def step(h, carry):
            return tuple(a + b for a, b in zip(carry, run(h)))

        return lax.fori_loop(0, 2, step, (zero_row,) * count)

    def far_first(i):
        return (1 - i // 2) + 2 * (1 - i % 2)

    def param(i):
        return params[i : i + 1, :]

    tok_own.wait()
    if inside:
        w_qkv[0].relay()
    ag_tok.relay()
    if inside:
        for k, to in enumerate(others):
            up_copy(k, to).start()
        w_qkv[1].relay()
        w_out.relay(False)
        w_down.start_near(down_in)
        for k, who in enumerate(others):
            remote(
                small_s.at[who], small_s.at[who], ss_send.at[k], ss_recv.at[k], who, f
            ).wait_recv()
        for b in range(4):
            for t in range(per):
                params[:, pl.ds((b * per + t) * 128, 128)] = small_s[b, t]

    def first_norm(b):
        unit, _s = unit_of(tok[b].astype(F32))
        normed[b] = (unit * param(0) + param(1)).astype(BF16)

    def norm_step(k, _):
        @pl.when(k == 1)
        def _():
            ag_tok.wait_x()

        @pl.when(k == 2)
        def _():
            ag_tok.wait_y()

        @pl.when(k == 3)
        def _():
            ag_tok.wait_d()

        first_norm(block(k))
        return 0

    lax.fori_loop(0, 3, norm_step, 0)
    if inside:
        for weight in w_qkv:
            weight.rest()
    lax.fori_loop(3, 4, norm_step, 0)
    if inside:
        for weight in w_qkv:
            weight.finish()

    rest = normed[...].reshape(4 * rows, width)
    for p in range(pairs):
        value = dot(rest, qkv_w[:, :, p * 384 : (p + 1) * 384].reshape(width, 384))
        for q in range(3):
            piece = value[:, q * 128 : (q + 1) * 128]
            piece = piece if q else piece * 0.125
            at = slice((3 * p + q) * 128, (3 * p + q + 1) * 128)
            triple[:, :, at] = piece.astype(BF16).reshape(4, rows, 128)

    if inside:
        up_copy(-1, s).wait()
        for k, to in enumerate(others):
            up_copy(k, to).wait_recv()
        w_up.start_far()
        w_up.start_near()

    seg_own.wait()
    for k, who in enumerate(others):
        remote(seg_in, segs.at[who], seg_send.at[k], seg_recv.at[k], who, f).wait_recv()
    seg_all = segs[...]

    def below(level):
        count = jnp.sum((seg_all < level).astype(F32), axis=0)
        return jnp.sum(count, axis=1, keepdims=True)

    bound_1, bound_2 = below(1), below(2)
    blocks = window // rows
    lane = lax.broadcasted_iota(jnp.int32, (1, 128), 1)
    left = (lane < HEAD_DIM).astype(F32)
    sides = (left.astype(BF16), (1.0 - left).astype(BF16))
    pick = lax.broadcasted_iota(jnp.int32, (rows, 128), 1) < HEAD_DIM

    def set_starts(r, _):
        i = (r * rows + lax.broadcasted_iota(jnp.int32, (rows, 128), 0)).astype(F32)
        starts[r] = jnp.where(i >= bound_2, bound_2, jnp.where(i >= bound_1, bound_1, 0.0))
        return 0

    lax.fori_loop(0, 4, set_starts, 0)

    def cut(r, part_at, p, count):
        at = pl.ds(pl.multiple_of((3 * p + part_at) * 128, 128), 128)
        return triple[pl.ds(r, count), :, at].reshape(count * rows, 128)

    def masked(scores, r, first, count):
        start = starts[r]
        tiles = []
        for t in range(count * rows // 128):
            j = lax.broadcasted_iota(jnp.int32, (rows, 128), 1) + t * 128
            keep = (first * rows + j).astype(F32) >= start
            if t * 128 >= (count - 1) * rows:
                i = lax.broadcasted_iota(jnp.int32, (rows, 128), 0)
                keep = keep & (j - (count - 1) * rows <= i)
            tiles.append(jnp.where(keep, scores[:, t * 128 : (t + 1) * 128], NEG))
        return jnp.concatenate(tiles, axis=1)

    rs_1 = Scatter(land_a, 0)

    def attend_pair(r, first, count, p):
        query, keys, vals = cut(r, 0, p, 1), cut(first, 1, p, count), cut(first, 2, p, count)
        outs = []
        for e in range(2):
            scores = masked(dot(query * sides[e], keys, NT), r, first, count)
            expo = jnp.exp(scores - jnp.max(scores, -1, keepdims=True))
            low = (expo * (1.0 / jnp.sum(expo, -1, keepdims=True))).astype(BF16)
            probs[r, 2 * p + e, :, 0 : count * rows] = low
            outs.append(dot(low, vals))
        attended[r, :, p * 128 : (p + 1) * 128] = jnp.where(pick, outs[0], outs[1]).astype(BF16)

    def attend(i, _):
        rel = far_first(i)
        r = block(rel)
        for count in range(1, blocks + 1):
            @pl.when(r + 1 >= count if count == blocks else r + 1 == count)
            def _(count=count):
                for p in range(pairs):
                    attend_pair(r, r + 1 - count, count, p)

        if inside:
            @pl.when(i == 0)
            def _():
                out_own.wait()
                w_out.relay_rest()
                w_out.rest()
                w_out.finish()

        part[rel] = dot(attended[r], out_w[0]).astype(BF16)

        @pl.when(c == 0)
        def _():
            rs_1.step(rel)

        if inside:
            @pl.when(i == 1)
            def _():
                w_down.relay()

        return 0

    lax.fori_loop(0, 4, attend, 0)

    my_turn((1, 1))

    @pl.when(c == 1)
    def _():
        for i in (0, 2, 1, 3):
            rs_1.copy(i).start()

    rs_1.relay()
    if inside:
        w_up.relay()

        @pl.when(c == 1)
        def _():
            w_down.rest()

    rs_1.wait()

    def mid_norm(h):
        at = half_rows(h)
        value = rs_1.total(h)
        branch[at] = value
        unit, _s = unit_of(value)
        mid = tok[s, at].astype(F32) + (unit * param(2) + param(3))
        middle[at] = mid
        unit, _s = unit_of(mid)
        inner[s, at] = (unit * param(4) + param(5)).astype(BF16)

    for h in range(2):
        mid_norm(h)
    ag_inner = Gather(inner, 1)
    my_turn()
    ag_inner.start()
    rs_1.drain()
    if inside:
        @pl.when(c == 1)
        def _():
            w_up.rest()

    ag_inner.relay()
    if inside:
        @pl.when(c == 0)
        def _():
            w_down.rest()
            w_up.rest()

        w_up.finish()

    ff = up_w.shape[2]
    tile = 512
    rs_2 = Scatter(land_b, 1)

    def forward_step(k, _):
        @pl.when(k == 1)
        def _():
            ag_inner.wait_x()

        @pl.when(k > 1)
        def _():
            ag_inner.step(k)

        r = block(k)

        def column(n, _):
            at = pl.ds(pl.multiple_of(n * tile, tile), tile)
            pre = dot(inner[r], up_w[:, :, at].reshape(width, tile)) + bias_row[:, at]
            square = pre * pre
            bend = jnp.tanh(0.7978845608028654 * pre * (1.0 + 0.044715 * square))
            near = 0.5 + 0.5 * bend
            activ[r, :, at] = (pre * near).astype(BF16)
            slope = near + pre * (0.5 - 0.5 * bend * bend) * (
                0.7978845608028654 + 0.10703222440890037 * square
            )
            dgelu[r, :, at] = slope.astype(BF16)
            return 0

        lax.fori_loop(0, ff // tile, column, 0)
        return 0

    lax.fori_loop(0, 4, forward_step, 0)
    if inside:
        down_own.wait()
        w_down.finish()

    def down_step(i, _):
        rel = far_first(i)
        r = block(rel)

        part[rel] = dot(activ[r], down_w[...]).astype(BF16)
        rs_2.step(rel)
        return 0

    my_turn()
    lax.fori_loop(0, 4, down_step, 0)
    rs_2.relay()
    cot_own.wait()
    rs_2.wait()

    def last_norm(h):
        at = half_rows(h)
        unit, scale = unit_of(rs_2.total(h))
        result_v[at] = (middle[at] + (unit * param(6) + param(7))).astype(BF16)
        grad = cot[at].astype(F32)
        gmix[s, at] = pull_of(grad, param(6), unit, scale).astype(BF16)
        return col_sum(grad * unit), col_sum(grad)

    grad_gain_d, grad_shift_d = both(last_norm, 2)
    sg_rows = [None] * 8
    sg_rows[6], sg_rows[7] = grad_gain_d, grad_shift_d
    ag_mix = Gather(gmix, 2)
    my_turn()
    ag_mix.start()
    result_out = pltpu.make_async_copy(result_v, result, o_sem.at[2])
    result_out.start()
    rs_2.drain()

    rs_3 = Scatter(land_a, 2)
    sg_bias = bias_row

    def clear(n, _):
        at = pl.ds(pl.multiple_of(n * tile, tile), tile)
        sg_bias[:, at] = jnp.zeros((1, tile), F32)
        return 0

    lax.fori_loop(0, ff // tile, clear, 0)

    TN = ((0,), (0,))

    def flat(ref, lanes=slice(None)):
        held = ref[:, :, lanes]
        return held.reshape(4 * rows, held.shape[2])

    def all_pairs(shed):
        for to_z in range(n_f // 2):
            shed.pair(to_z).start()

    def cut_grads(left, right, gw, shed, lanes=slice(None)):
        for b in range(4):
            value = dot(flat(left, slice(b * rows, (b + 1) * rows)), flat(right, lanes), TN)
            gw[:, b * high : (b + 1) * high, :] = value.astype(BF16).reshape(n_f, high, -1)
        all_pairs(shed)

    def down_grads(rels):
        each = ff // n_f
        count = 256 // each
        for b in range(n_f // count):
            at = slice(b * count, (b + 1) * count)
            cols = slice(b * 256, (b + 1) * 256)
            value = dot(activ[block(rels[0]), :, cols], gmix[block(rels[0])], TN)
            for rel in rels[1:]:
                value = value + dot(activ[block(rel), :, cols], gmix[block(rel)], TN)
            if len(rels) == 1:
                value = value + gw_down[at].astype(F32).reshape(256, width)
            gw_down[at] = value.astype(BF16).reshape(count, each, width)

    if inside:
        shed_down = Shed(0, gw_down, lp_down, lz_down)
        shed_up = Shed(1, gw_up, lp_up, lz_up)
        shed_out = Shed(2, gw_out, lp_out, lz_out)
        shed_qkv = [
            Shed(3 + p, gw_qkv[p], lp_qkv[p], lz_qkv[p])
            for p in range(pairs)
        ]
        ag_tok.drain()

    def back_step(k, _):
        if inside:
            @pl.when(k == 3)
            def _():
                down_grads((0, 1, 2))

        ag_mix.step(k)
        r = block(k)

        def column(n, _):
            at = pl.ds(pl.multiple_of(n * tile, tile), tile)
            grad = dot(gmix[r], down_w[at], NT)
            low = (dgelu[r, :, at].astype(F32) * grad).astype(BF16)
            dgelu[r, :, at] = low
            sg_bias[:, at] = sg_bias[:, at] + col_sum(low.astype(F32))
            return 0

        lax.fori_loop(0, ff // tile, column, 0)
        return 0

    lax.fori_loop(0, 4, back_step, 0)

    if inside:
        down_grads((3,))
        all_pairs(shed_down)

        @pl.when(c == 1)
        def _():
            shed_down.far()

    def inner_step(i, _):
        rel = far_first(i)
        r = block(rel)

        part[rel] = dot(dgelu[r], up_w[...].reshape(width, ff), NT).astype(BF16)
        rs_3.step(rel)
        return 0

    my_turn()
    lax.fori_loop(0, 4, inner_step, 0)

    if inside:
        cut_grads(inner, dgelu, gw_up, shed_up)
    rs_3.relay()
    if inside:
        @pl.when(c == 1)
        def _():
            shed_up.far()
            shed_down.close()
            shed_up.close()

        @pl.when(c == 0)
        def _():
            shed_down.far()

    rs_3.wait()

    def mid_back(h):
        at = half_rows(h)
        grad = rs_3.total(h)
        unit, scale = unit_of(middle[at])
        total = cot[at].astype(F32) + pull_of(grad, param(4), unit, scale)
        gmid[at] = total
        out = [col_sum(grad * unit), col_sum(grad)]
        unit, scale = unit_of(branch[at])
        gbr[s, at] = pull_of(total, param(2), unit, scale).astype(BF16)
        return out[0], out[1], col_sum(total * unit), col_sum(total)

    sg_rows[4], sg_rows[5], sg_rows[2], sg_rows[3] = both(mid_back, 4)
    ag_br = Gather(gbr, 3)
    my_turn()
    ag_br.start()
    rs_3.drain()
    def arrive(k, _):
        if inside:
            @pl.when(k == 1)
            def _():
                ag_br.relay()

            @pl.when((k == 1) & (c == 0))
            def _():
                shed_up.far()
                shed_down.close()
                shed_up.close()

            @pl.when(k == 1)
            def _():
                ag_br.wait_x()

            @pl.when(k > 1)
            def _():
                ag_br.step(k)

            @pl.when(k == 2)
            def _():
                shed_down.second()
        else:
            ag_br.step(k)

        r = block(k)
        gatt[r] = dot(gbr[r], out_w[0], NT).astype(BF16)
        if inside:
            value = dot(attended[r], gbr[r], TN)

            @pl.when(k == 0)
            def _():
                branch[...] = value

            @pl.when(k > 0)
            def _():
                branch[...] = branch[...] + value

        return 0

    lax.fori_loop(0, 4, arrive, 0)
    if inside:
        gw_out[...] = branch[...].astype(BF16).reshape(gw_out.shape)
        all_pairs(shed_out)

    if inside:
        per = n_f * high // 128
        gdown_out = pltpu.make_async_copy(fin_down, gdown, o_sem.at[3])
        gout_out = pltpu.make_async_copy(fin_out, gout, o_sem.at[4])
        gup_out = pltpu.make_async_copy(gup_v, gup, o_sem.at[5])
        gqkv_out = pltpu.make_async_copy(gqkv_v, gqkv, o_sem.at[6])
        gsmall_out = pltpu.make_async_copy(small_sum, gsmall, o_sem.at[7])

        def ts_copy(k, to):
            return remote(sg_s.at[to], sg_land_s.at[k], ts_send.at[k], ts_recv.at[k], to, f)

        def tf_copy(d):
            to = (f + d) % n_f
            return remote(
                sg_f.at[to], sg_land_f.at[d - 1], tf_send.at[d], tf_recv.at[d], s, to
            )

        def small_first():
            for b in range(4):
                for t in range(per):
                    at = slice((b * per + t) * 128, (b * per + t + 1) * 128)
                    for i in range(8):
                        sg_s[b, t, i : i + 1, :] = sg_rows[i][:, at]
            for k, to in enumerate(others):
                ts_copy(k, to).start()

        def small_second():
            for k, to in enumerate(others):
                ts_copy(k, to).wait_recv()
            for who in range(n_f):
                t = who * high // 128
                sg_f[who, 0:8] = (
                    sg_s[s, t] + sg_land_s[0, t] + sg_land_s[1, t] + sg_land_s[2, t]
                )
                sg_f[who, 8:9] = sg_bias[:, who * 128 : (who + 1) * 128]
            for d in range(1, n_f):
                tf_copy(d).start()

        def small_third():
            for d in range(1, n_f):
                tf_copy(d).wait_recv()
            value = sg_f[f]
            for d in range(1, n_f):
                value = value + sg_land_f[d - 1]
            small_sum[...] = value
            gsmall_out.start()

        def gu_copy(k, to, who):
            return remote(fin_up.at[to], land_up.at[who], gu_send.at[k], gu_recv.at[k], to, f)

        def gc_at(p, who):
            start = pl.multiple_of((p % 3) * width + who * group + (p // 3) * 128, 128)
            return pl.ds(start, 128)

        def gc_copy(k, p, to, who):
            return remote(
                fin_qkv.at[p, to], land_qkv.at[p, who],
                gc_send.at[k, p], gc_recv.at[k, p], to, f,
            )

    def back_pair(p):
        lanes = slice(p * 128, (p + 1) * 128)
        for r in range(3, -1, -1):
            first = max(r + 1 - blocks, 0)
            count = r + 1 - first
            query, keys, vals = cut(r, 0, p, 1), cut(first, 1, p, count), cut(first, 2, p, count)
            grad = gatt[r, :, lanes]
            query_t, grad_t = query.T, grad.T
            outs, key_parts, value_parts = [], [], []
            for e in range(2):
                low = probs[r, 2 * p + e, :, 0 : count * rows]
                grad_probs = dot(grad * sides[e], vals, NT)
                full = low.astype(F32)
                inner_sum = jnp.sum(full * grad_probs, -1, keepdims=True)
                grad_scores = (full * (grad_probs - inner_sum)).astype(BF16)
                outs.append(dot(grad_scores, keys))
                side = slice(e * HEAD_DIM, (e + 1) * HEAD_DIM)
                here = slice(p * 128 + e * HEAD_DIM, p * 128 + (e + 1) * HEAD_DIM)
                key_part = dot(query_t[side], grad_scores)
                value_part = dot(grad_t[side], low)
                for n in range(count):
                    span = slice((first + n) * rows, (first + n + 1) * rows)
                    cols = slice(n * rows, (n + 1) * rows)
                    if r == 3 or (first + n) < 4 - blocks and r == first + n + blocks - 1:
                        dkt[here, span] = key_part[:, cols]
                        dvt[here, span] = value_part[:, cols]
                    else:
                        dkt[here, span] = dkt[here, span] + key_part[:, cols]
                        dvt[here, span] = dvt[here, span] + value_part[:, cols]
            at = slice(3 * p * 128, (3 * p + 1) * 128)
            gtri[r, :, at] = (jnp.where(pick, outs[0], outs[1]) * 0.125).astype(BF16)
        for b in range(4):
            span = slice(b * rows, (b + 1) * rows)
            at = slice((3 * p + 1) * 128, (3 * p + 2) * 128)
            gtri[b, :, at] = dkt[lanes, span].astype(BF16).T
            at = slice((3 * p + 2) * 128, (3 * p + 3) * 128)
            gtri[b, :, at] = dvt[lanes, span].astype(BF16).T

    def qkv_grads(p):
        cut_grads(normed, gtri, gw_qkv[p], shed_qkv[p], slice(p * 384, (p + 1) * 384))

    for p in range(pairs):
        back_pair(p)
        if inside and p == 0:
            qkv_grads(p)
            shed_up.second()

            @pl.when(c == 1)
            def _():
                shed_out.far()
                shed_qkv[0].far()

    if inside:
        @pl.when(c == 1)
        def _():
            qkv_grads(1)
            shed_qkv[1].far()
            for shed in (shed_out, *shed_qkv):
                shed.close()

        @pl.when(c == 0)
        def _():
            shed_out.far()
            shed_qkv[0].far()

    rs_4 = Scatter(land_b, 3)

    def normed_step(i, carry):
        rel = far_first(i)
        r = block(rel)
        grad = dot(gtri[r], qkv_w[...].reshape(width, 3 * group), NT)
        part[rel] = grad.astype(BF16)
        rs_4.step(rel)
        unit, _s = unit_of(tok[r].astype(F32))
        return carry[0] + col_sum(grad * unit), carry[1] + col_sum(grad)

    my_turn()
    sg_rows[0], sg_rows[1] = lax.fori_loop(0, 4, normed_step, (zero_row, zero_row))
    if inside:
        small_first()

        @pl.when(c == 0)
        def _():
            qkv_grads(1)

    rs_4.relay()
    if inside:
        @pl.when(c == 0)
        def _():
            shed_qkv[1].far()
            for shed in (shed_out, *shed_qkv):
                shed.close()

        for shed in (shed_out, *shed_qkv):
            shed.second()
        small_second()
        at = pl.ds(pl.multiple_of(s * high, high), high)
        shed_up.wait()
        for b in range(4):
            fin_up[b] = shed_up.total(slice(b * high, (b + 1) * high)).astype(BF16)
        gup_v[:, pl.ds(pl.multiple_of(s * ff, 128), ff)] = shed_up.total(at)

        def give_up():
            for k, to in enumerate(others):
                gu_copy(k, to, s).start()

        @pl.when(c == 1)
        def _():
            give_up()

        shed_down.wait()
        fin_down[...] = shed_down.total(slice(None))
        gdown_out.start()
    rs_4.wait()

    def first_back(h, _):
        at = half_rows(h)
        unit, scale = unit_of(tok[s, at].astype(F32))
        gmid[at] = gmid[at] + pull_of(rs_4.total(h), param(0), unit, scale)
        pltpu.make_async_copy(gmid.at[at], tgrad.at[at], o_sem.at[h]).start()
        return 0

    lax.fori_loop(0, 2, first_back, 0)
    if inside:
        for q, shed in enumerate(shed_qkv):
            shed.wait()
            for b in range(4):
                fin_qkv[q, b] = shed.total(slice(b * high, (b + 1) * high)).astype(BF16)
            for k, to in enumerate(others):
                gc_copy(k, q, to, s).start()
            own = shed.total(at)
            for p in range(3):
                gqkv_v[:, gc_at(3 * q + p, s)] = own[:, p * 128 : (p + 1) * 128]

        @pl.when(c == 0)
        def _():
            give_up()

        for k, who in enumerate(others):
            gu_copy(k, who, who).wait_recv()
            gup_v[:, pl.ds(pl.multiple_of(who * ff, 128), ff)] = land_up[who].astype(F32)
        gup_out.start()
        shed_out.wait()
        fin_out[...] = shed_out.total(slice(None))
        gout_out.start()
        small_third()
        for k, who in enumerate(others):
            for q in range(pairs):
                gc_copy(k, q, who, who).wait_recv()
                for p in range(3):
                    piece = land_qkv[q, who, :, p * 128 : (p + 1) * 128]
                    gqkv_v[:, gc_at(3 * q + p, who)] = piece.astype(F32)
        gqkv_out.start()

    for h in range(2):
        pltpu.make_async_copy(gmid.at[half_rows(h)], tgrad.at[half_rows(h)], o_sem.at[h]).wait()
    result_out.wait()
    if inside:
        gsmall_out.wait()
        gdown_out.wait()
        gout_out.wait()
        gup_out.wait()
        gqkv_out.wait()
        for k, to in enumerate(others):
            gu_copy(k, to, s).wait_send()
            ts_copy(k, to).wait_send()
            for q in range(pairs):
                gc_copy(k, q, to, s).wait_send()
            for p in range(n_cut):
                qkv_copy(k, p, to).wait_send()
            up_copy(k, to).wait_send()
            small_wide(k, to).wait_send()
        for d in range(1, n_f):
            tf_copy(d).wait_send()
            small_copy(d).wait_send()
        for weight in (*w_qkv, w_out, w_up, w_down):
            weight.drain()
        for shed in (shed_down, shed_up, shed_out, *shed_qkv):
            shed.drain()
    else:
        for i in range(8):
            small_sum[i : i + 1, :] = sg_rows[i]
        small_sum[8:9, 0:ff] = sg_bias[...]
        gsmall_out = pltpu.make_async_copy(small_sum, gsmall, o_sem.at[7])
        gsmall_out.start()
        gsmall_out.wait()
    for k, to in enumerate(others):
        seg_copy(k, to).wait_send()
    for gather in (ag_inner, ag_mix, ag_br) + (() if inside else (ag_tok,)):
        gather.drain()
    rs_4.drain()


def finish_kernel(n_f, n_big, *refs):
    small, given = refs[0], refs[1 : 1 + n_big]
    made, minor = refs[1 + n_big : 1 + 2 * n_big], refs[1 + 2 * n_big : 10 + 2 * n_big]
    held, (in_sem, out_sem) = refs[10 + 2 * n_big : 10 + 3 * n_big], refs[10 + 3 * n_big :]
    cuts = []
    for i in range(n_big):
        tall = given[i].shape[0]
        for j in range(max(1, tall // 64)):
            at = pl.ds(j * min(tall, 64), min(tall, 64))
            cuts.append((i, at, len(cuts)))
    for i, at, n in cuts:
        pltpu.make_async_copy(given[i].at[at], held[i].at[at], in_sem.at[n]).start()
    each = minor[0].shape[1]
    place = lax.axis_index("fsdp") % (128 // each)
    for i in range(8):
        row = small[i : i + 1, :]
        value = row[:, 0:each]
        for q in range(1, 128 // each):
            value = jnp.where(place == q, row[:, q * each : (q + 1) * each], value)
        minor[i][...] = value
    minor[8][...] = small[8:9, :]
    for i, at, n in cuts:
        pltpu.make_async_copy(given[i].at[at], held[i].at[at], in_sem.at[n]).wait()
        pltpu.make_async_copy(held[i].at[at], made[i].at[at], out_sem.at[n]).start()
    for i, at, n in cuts:
        pltpu.make_async_copy(held[i].at[at], made[i].at[at], out_sem.at[n]).wait()


def finish(n_f, high, *made):
    big, small = made[:6], made[6]
    whole, anywhere = pl.BlockSpec(memory_space=pltpu.VMEM), pl.BlockSpec(memory_space=pl.ANY)
    count = sum(max(1, v.shape[0] // 64) for v in big)
    minor = [jax.ShapeDtypeStruct((1, high), F32)] * 8 + [jax.ShapeDtypeStruct((1, 128), F32)]
    out = pl.pallas_call(
        partial(finish_kernel, n_f, 6),
        out_shape=[jax.ShapeDtypeStruct(v.shape, v.dtype) for v in big] + minor,
        in_specs=[whole] + [anywhere] * 6,
        out_specs=[anywhere] * 6 + [whole] * 9,
        scratch_shapes=[pltpu.VMEM(v.shape, v.dtype) for v in big]
        + [pltpu.SemaphoreType.DMA((count,))] * 2,
    )(small, *big)
    result, tgrad, gqkv, gout, gup, gdown = out[:6]
    small = [v[0] for v in out[6:]]
    return (result[None], tgrad[None], gqkv, gout, gup, small[8], gdown, *small[:8])


def on_device(n_seq, n_f, *args):
    (tokens, segments, qkv_weight, out_weight, up_weight, up_bias, down_weight) = args[:7]
    vectors, cotangent = args[7:15], args[15]
    rows, width = tokens.shape[1:]
    high, high_d = qkv_weight.shape[0], down_weight.shape[0]
    length = n_seq * rows
    group = qkv_weight.shape[1] // 3 // n_seq
    heads = group // HEAD_DIM
    ff = up_weight.shape[1] // n_seq
    half = rows // 2
    window = rows * min(n_seq, 1 + -(-511 // rows))
    inside = n_f == 8 and high % 32 == 0
    f = lax.axis_index("fsdp")
    small = jnp.stack([v.astype(F32) for v in vectors])
    if inside:
        each = 128 // high
        lane = lax.broadcasted_iota(jnp.int32, (8, 128), 1) // high
        small = jnp.where(lane == f % each, jnp.tile(small, (1, each)), 0.0)
        small = jnp.concatenate([small, up_bias.astype(F32)[None], jnp.zeros((7, 128), F32)])
        weights = (qkv_weight, out_weight, up_weight, down_weight)
    else:
        small = lax.all_gather(small, ("seq", "fsdp"), axis=1, tiled=True)
        bias = lax.all_gather(up_bias.astype(F32), "fsdp", axis=0, tiled=True)
        bias = jnp.pad(bias[None], ((0, 7), (0, width - ff)))
        small = jnp.concatenate([small, bias])

        def columns(weight, parts):
            cut = weight.reshape(high, parts, n_seq, -1, 128).transpose(2, 0, 3, 1, 4)
            cut = cut.reshape(n_seq, high, -1)
            cut = lax.all_to_all(cut, "seq", split_axis=0, concat_axis=0, tiled=True)
            return lax.all_gather(cut, "fsdp", axis=1, tiled=True)

        weights = (
            columns(qkv_weight, 3),
            lax.all_gather(out_weight, "fsdp", axis=0, tiled=True)[None],
            columns(up_weight, 1),
            lax.all_gather(down_weight, "fsdp", axis=0, tiled=True),
        )
    vmem, anywhere, dma = pltpu.VMEM, pl.BlockSpec(memory_space=pl.ANY), pltpu.SemaphoreType.DMA
    whole = pl.BlockSpec(memory_space=pltpu.VMEM)
    full = (4, rows, width)
    saved = {
        "normed": (full, BF16), "inner": (full, BF16), "gmix": (full, BF16), "gbr": (full, BF16),
        "attended": ((4, rows, group), BF16), "activ": ((4, rows, ff), BF16),
        "dgelu": ((4, rows, ff), BF16), "gtri": ((4, rows, 3 * group), BF16),
    }
    n_cut = 3 * (group // 128)
    pieces = {"q0": (n_seq * high, 384), "q1": (n_seq * high, 384), "out": (high, width),
              "up": (n_seq * high, ff), "down": (high_d, width)}
    scratch = {
        "tok": vmem(full, BF16), "normed": None, "inner": None, "gmix": None, "gbr": None,
        "qkv_w": vmem((n_seq, rows, 3 * group), BF16), "out_w": vmem((1, group, width), BF16),
        "up_w": vmem((n_seq, rows, ff), BF16), "down_w": vmem((ff, width), BF16),
        "segs": vmem((4, 1, rows), jnp.int32),
        "small_f": vmem((n_f if inside else 1, 16, 128), F32), "small_s": vmem((4, width // 512, 8, 128), F32),
        "params": vmem((8, width), F32), "bias_row": vmem((1, ff), F32),
        "triple": vmem((4, rows, 3 * group), BF16), "probs": vmem((4, heads, rows, window), BF16),
        "attended": None, "starts": vmem((4, rows, 128), F32), "activ": None, "dgelu": None,
        "part": vmem(full, BF16), "land_a": vmem((6, half, width), BF16),
        "land_b": vmem((6, half, width), BF16),
        "branch": vmem((rows, width), F32), "middle": vmem((rows, width), F32),
        "gmid": vmem((rows, width), F32), "cot": vmem((rows, width), BF16),
        "gtri": None, "gatt": vmem((4, rows, group), BF16), "dkt": vmem((group, length), F32),
        "dvt": vmem((group, length), F32),
    }
    for name, (tall, wide) in pieces.items():
        scratch["gw_" + name] = vmem((n_f if inside else 1, tall if inside else 16, wide), BF16)
    for name, (tall, wide) in pieces.items():
        scratch["lp_" + name] = vmem((n_f // 2 if inside else 1, tall if inside else 16, wide), BF16)
    for name, (tall, wide) in pieces.items():
        scratch["lz_" + name] = vmem((n_f // 2 if inside else 1, tall if inside else 16, wide), BF16)
    scratch["result_v"] = vmem((rows, width), BF16)
    scratch["fin_qkv"] = vmem((group // 128, 4, high, 384), BF16)
    scratch["fin_up"] = vmem((4, high, ff), BF16)
    scratch["land_qkv"] = vmem((group // 128, 4, high, 384), BF16)
    scratch["land_up"] = vmem((4, high, ff), BF16)
    scratch["fin_down"] = vmem((high_d, width), F32)
    scratch["fin_out"] = vmem((high, width), F32)
    scratch["gup_v"] = vmem((high, n_seq * ff), F32)
    scratch["gqkv_v"] = vmem((high, n_seq * 3 * group), F32)
    scratch["small_sum"] = vmem((16, 128 if inside else width), F32)
    tiles = width // 512
    scratch["sg_s"] = vmem((4, tiles, 8, 128), F32)
    scratch["sg_land_s"] = vmem((3, tiles, 8, 128), F32)
    scratch["sg_f"] = vmem((n_f if inside else 1, 16, 128), F32)
    scratch["sg_land_f"] = vmem((n_f - 1 if inside else 1, 16, 128), F32)
    for name, shape in (
        ("ag_send", (4, 6)), ("ag_recv", (4, 6)), ("rs_send", (4, 6)), ("rs_recv", (4, 6)),
        ("w_send", (5, 4)), ("w_recv", (5, 3)), ("p_send", (5, 4)), ("p_recv", (5, 4)),
        ("col_send", (3, n_cut)), ("col_recv", (3, n_cut)), ("col_local", (n_cut,)),
        ("upc_send", (3,)), ("upc_recv", (3,)), ("seg_send", (3,)), ("seg_recv", (3,)),
        ("sf_send", (8,)), ("sf_recv", (8,)), ("ss_send", (3,)), ("ss_recv", (3,)),
        ("loc_sem", (7,)), ("o_sem", (8,)),
        ("gp_send", (5, 4)), ("gp_recv", (5, 4)), ("gz_send", (5, 4)), ("gz_recv", (5, 4)),
        ("gc_send", (3, 2)), ("gc_recv", (3, 2)), ("gu_send", (3,)), ("gu_recv", (3,)),
        ("ts_send", (3,)), ("ts_recv", (3,)), ("tf_send", (8,)), ("tf_recv", (8,)),
    ):
        scratch[name] = dma(shape)
    scratch["turn"] = pltpu.SemaphoreType.REGULAR
    outs = {
        "result": ((rows, width), BF16), "tgrad": ((rows, width), F32),
        "gqkv": ((high, n_seq * 3 * group), F32), "gout": ((high, width), F32),
        "gup": ((high, n_seq * ff), F32), "gdown": ((high_d, width), F32),
        "gsmall": ((16, 128 if inside else width), F32),
    }
    if inside:
        for name, shape in saved.items():
            scratch[name] = vmem(*shape)
        extra = []
    else:
        extra = list(saved)
    names = list(scratch)

    def kernel(*refs):
        given = refs[:8]
        made = refs[8 : 8 + len(outs)]
        more = dict(zip(extra, refs[8 + len(outs) :]))
        rest = refs[8 + len(outs) + len(extra) :]
        more.update(zip([n for n in names if scratch[n] is not None], rest))
        layer_kernel(inside, n_f, *given, *made, *[more[n] for n in names])

    shapes = [*outs.values(), *[saved[n] for n in extra]]
    made = pl.pallas_call(
        kernel,
        out_shape=[jax.ShapeDtypeStruct(*shape) for shape in shapes],
        in_specs=[anywhere, anywhere, whole, anywhere] + [anywhere] * 4,
        out_specs=[anywhere] * len(outs) + [whole] * len(extra),
        scratch_shapes=[scratch[n] for n in names if scratch[n] is not None],
        compiler_params=pltpu.CompilerParams(
            collective_id=0, has_side_effects=True, vmem_limit_bytes=67043328
        ),
    )(tokens[0], segments, small, cotangent[0], *weights)
    result, tgrad, gqkv, gout, gup, gdown, gsmall = made[:7]
    if inside:
        return finish(n_f, high, *made[:7])
    else:
        kept = {n: v.reshape(length, -1) for n, v in zip(extra, made[7:])}

        def turned_dot(left, right):
            return lax.dot_general(
                kept[left], kept[right], (((0,), (0,)), ((), ())), preferred_element_type=F32
            ).astype(BF16)

        def shed(value):
            return lax.psum_scatter(value, "fsdp", scatter_dimension=0, tiled=True)

        def columns_back(value, parts):
            cut = value.reshape(n_seq, n_f, high, -1).transpose(1, 0, 2, 3)
            cut = lax.all_to_all(shed(cut)[0], "seq", split_axis=0, concat_axis=0, tiled=True)
            cut = cut.reshape(n_seq, high, -1, parts, 128).transpose(1, 3, 0, 2, 4)
            return cut.reshape(high, -1).astype(F32)

        gqkv = columns_back(turned_dot("normed", "gtri"), 3)
        gout = shed(turned_dot("attended", "gbr")).astype(F32)
        gup = columns_back(turned_dot("inner", "dgelu"), 1)
        gdown = shed(turned_dot("activ", "gmix")).astype(F32)
        vectors = lax.psum_scatter(gsmall[:8], ("seq", "fsdp"), scatter_dimension=1, tiled=True)
        gbias = shed(gsmall[8, :ff])
    return (result[None], tgrad[None], gqkv, gout, gup, gbias, gdown, *vectors)


def solution(mesh):
    rows = P(("seq", "fsdp"), None)
    vector = P(("seq", "fsdp"))
    acts = P("fsdp", "seq", None)
    return jax.shard_map(
        partial(on_device, mesh.shape["seq"], mesh.shape["fsdp"]),
        mesh=mesh,
        in_specs=(acts, P("fsdp", "seq"), rows, rows, rows, vector, rows, *(vector,) * 8, acts),
        out_specs=(acts, acts, rows, rows, rows, vector, rows, *(vector,) * 8),
        check_vma=False,
    )
```

```python
from functools import partial

import jax
import jax.numpy as jnp
from jax import lax
from jax.experimental import pallas as pl
from jax.experimental.pallas import tpu as pltpu
from jax.sharding import PartitionSpec as P

HEAD_DIM = 64
F32 = jnp.float32
BF16 = jnp.bfloat16
NN = ((1,), (0,))
NT = ((1,), (1,))
NEG = -1e30


def dot(left, right, dims=NN):
    return lax.dot_general(left, right, (dims, ((), ())), preferred_element_type=F32)


def unit_of(value):
    center = value - jnp.mean(value, -1, keepdims=True)
    scale = lax.rsqrt(jnp.mean(center * center, -1, keepdims=True) + 1e-05)
    return center * scale, scale


def pull_of(grad, gain, unit, scale):
    pulled = grad * gain
    first = jnp.mean(pulled, -1, keepdims=True)
    second = jnp.mean(pulled * unit, -1, keepdims=True)
    return scale * (pulled - first - unit * second)


def col_sum(value):
    return jnp.sum(value, 0, keepdims=True)


def layer_kernel(
    inside,
    n_f,
    tokens, seg_in, small_given, cot_in, qkv_in, out_in, up_in, down_in,
    result, tgrad, gqkv, gout, gup, gdown, gsmall,
    tok, normed, inner, gmix, gbr,
    qkv_w, out_w, up_w, down_w,
    segs, small_f, small_s, params, bias_row,
    triple, probs, attended, starts, activ, dgelu,
    part, land_a, land_b,
    branch, middle, gmid, cot,
    gtri, gatt, dkt, dvt,
    gw_q0, gw_q1, gw_out, gw_up, gw_down,
    lp_q0, lp_q1, lp_out, lp_up, lp_down,
    lz_q0, lz_q1, lz_out, lz_up, lz_down,
    result_v, fin_qkv, fin_up, land_qkv, land_up, fin_down, fin_out, gup_v, gqkv_v, small_sum,
    sg_s, sg_land_s, sg_f, sg_land_f,
    ag_send, ag_recv, rs_send, rs_recv,
    w_send, w_recv, p_send, p_recv,
    col_send, col_recv, col_local, upc_send, upc_recv,
    seg_send, seg_recv, sf_send, sf_recv, ss_send, ss_recv,
    loc_sem, o_sem,
    gp_send, gp_recv, gz_send, gz_recv,
    gc_send, gc_recv, gu_send, gu_recv,
    ts_send, ts_recv, tf_send, tf_recv, turn,
    small_raw, bias_raw, small_rows, small_tile, raw_sem,
):
    gw_qkv, lp_qkv, lz_qkv = (gw_q0, gw_q1), (lp_q0, lp_q1), (lz_q0, lz_q1)
    rows, width = tokens.shape
    half = rows // 2
    group = out_w.shape[1]
    pairs = group // 128
    window = probs.shape[3]
    s = lax.axis_index("seq")
    f = lax.axis_index("fsdp")
    x, y = s % 2, s // 2
    z, c = f // 2, f % 2

    def block(rel):
        return 2 * ((y + rel // 2) % 2) + (x + rel % 2) % 2

    sx, sy, sd = block(1), block(2), block(3)

    def remote(src, dst, send, recv, to_s, to_f):
        return pltpu.make_async_remote_copy(
            src_ref=src, dst_ref=dst, send_sem=send, recv_sem=recv,
            device_id=(to_s, to_f), device_id_type=pl.DeviceIdType.MESH,
        )

    def my_turn(cores=(0, 1)):
        if inside:
            @pl.when(c >= cores[0])
            def _():
                pl.semaphore_wait(turn, 1)

    def hand_over(cores=(0, 1)):
        if inside:
            @pl.when(c <= cores[1])
            def _():
                pl.semaphore_signal(
                    turn, inc=1, device_id=(s, 2 * z + 1 - c),
                    device_id_type=pl.DeviceIdType.MESH,
                )

    class Gather:
        def __init__(self, full, index):
            self.full, self.index = full, index

        def piece(self, b, h):
            return self.full.at[b, pl.ds(h * half, half)]

        def copy(self, i, b, h, to, src=None):
            dst = self.piece(b, h)
            return remote(
                dst if src is None else src, dst,
                ag_send.at[self.index, i], ag_recv.at[self.index, i], to, f,
            )

        def start(self, src=None):
            def cut(h):
                return None if src is None else src.at[pl.ds(h * half, half)]

            self.copy(0, s, 0, sx, cut(0)).start()
            self.copy(1, s, 1, sy, cut(1)).start()
            self.copy(2, s, 1, sx, cut(1)).start()
            self.copy(3, s, 0, sy, cut(0)).start()

        def relay(self):
            self.copy(0, sx, 0, sx).wait_recv()
            self.copy(4, sx, 0, sy).start()
            self.copy(1, sy, 1, sy).wait_recv()
            self.copy(5, sy, 1, sx).start()
            if self.index:
                hand_over()

        def wait_x(self):
            self.copy(2, sx, 1, sx).wait_recv()

        def wait_y(self):
            self.copy(3, sy, 0, sy).wait_recv()

        def wait_d(self):
            self.copy(4, sd, 0, sy).wait_recv()
            self.copy(5, sd, 1, sx).wait_recv()

        def step(self, k):
            @pl.when(k == 1)
            def _():
                self.relay()
                self.wait_x()

            @pl.when(k == 2)
            def _():
                self.wait_y()

            @pl.when(k == 3)
            def _():
                self.wait_d()

        def drain(self):
            for i, (b, h, to) in enumerate(
                ((s, 0, sx), (s, 1, sy), (s, 1, sx), (s, 0, sy), (sx, 0, sy), (sy, 1, sx))
            ):
                self.copy(i, b, h, to).wait_send()

    def half_rows(h):
        return pl.ds(pl.multiple_of(h * half, half), half)

    class Scatter:
        plan = ((3, 0, 1), (1, 0, 1), (3, 1, 2), (2, 1, 2), (2, 0, 2), (1, 1, 1))

        def __init__(self, land, index):
            self.land, self.index = land, index

        def copy(self, i):
            rel, h, way = self.plan[i]
            return remote(
                part.at[rel, pl.ds(h * half, half)], self.land.at[i],
                rs_send.at[self.index, i], rs_recv.at[self.index, i],
                sx if way == 1 else sy, f,
            )

        def step(self, rel):
            @pl.when(rel == 3)
            def _():
                self.copy(0).start()
                self.copy(2).start()

            @pl.when(rel == 1)
            def _():
                self.copy(1).start()

            @pl.when(rel == 2)
            def _():
                self.copy(3).start()

        def relay(self):
            for arrived, i in ((0, 4), (2, 5)):
                self.copy(arrived).wait_recv()
                rel, h, _ = self.plan[i]

                here = pl.ds(h * half, half)
                total = part[rel, here].astype(F32) + self.land[arrived].astype(F32)
                part[rel, here] = total.astype(BF16)
                self.copy(i).start()
            hand_over((0, 0) if self.index == 3 else (0, 1))

        def wait(self):
            for i in (1, 3, 4, 5):
                self.copy(i).wait_recv()

        def total(self, h):
            return (
                part[0, half_rows(h)].astype(F32)
                + self.land[1 + 2 * h].astype(F32)
                + self.land[4 + h].astype(F32)
            )

        def drain(self):
            for i in range(6):
                self.copy(i).wait_send()

    def by_rows(ref, size):
        def view(who):
            return ref.at[pl.ds(pl.multiple_of(who * size, size), size)]

        return view

    def by_cut(ref, size):
        def view(who):
            return ref.at[:, pl.ds(pl.multiple_of(who * size, size), size)]

        return view

    partner = 2 * z + 1 - c
    side = z // 2
    near = 4 * side + 1 - z
    mid_o, end_o = 2 - side, 3 - 3 * side
    is_mid = (z + side) % 2
    seen_as = 2 - is_mid
    owners = (near, mid_o, end_o)

    class Weight:
        def __init__(self, index, view):
            self.index, self.view = index, view

        def piece(self, to_z, i, k, owner_z, own=None):
            dst = self.view(2 * owner_z + c)
            return remote(
                dst if own is None else own, dst,
                w_send.at[self.index, i], w_recv.at[self.index, k], s, 2 * to_z + c,
            )

        def across(self, k, owner, own=None):
            dst = self.view(owner)
            return remote(
                dst if own is None else own, dst,
                p_send.at[self.index, k], p_recv.at[self.index, k], s, partner,
            )

        def start_far(self, own=None, across=True):
            self.piece(mid_o, 1, seen_as, z, own).start()
            if across:
                @pl.when(is_mid == 0)
                def _():
                    self.piece(near, 0, 0, z, own).start()

                self.across(3, f, own).start()

        def start_near(self, own=None, everyone=False):
            @pl.when((is_mid == 1) | everyone)
            def _():
                self.piece(near, 0, 0, z, own).start()

        def start(self, own=None):
            self.start_far(own)
            self.start_near(own)

        def relay(self, all_of_it=True):
            @pl.when(is_mid == 1)
            def _():
                for k in (1, 2):
                    self.piece(z, 0, k, owners[k]).wait_recv()
                    self.piece(near, 1 + k, k, owners[k]).start()
                for k in (1, 2):
                    self.across(k, 2 * owners[k] + c).start()

            if all_of_it:
                self.relay_rest()

        def relay_rest(self):
            @pl.when(is_mid == 1)
            def _():
                self.piece(z, 0, 0, near).wait_recv()
                self.across(0, 2 * near + c).start()

        def rest(self):
            @pl.when(is_mid == 0)
            def _():
                for k in (0, 1, 2):
                    self.piece(z, 0, k, owners[k]).wait_recv()
                    self.across(k, 2 * owners[k] + c).start()

        def finish(self):
            self.across(3, partner).wait_recv()
            for k in (0, 1, 2):
                self.across(k, 2 * owners[k] + 1 - c).wait_recv()

        def drain(self):
            self.piece(mid_o, 1, seen_as, z).wait_send()
            self.piece(near, 0, 0, z).wait_send()
            self.across(3, f).wait_send()

            @pl.when(is_mid == 1)
            def _():
                for k in (1, 2):
                    self.piece(near, 1 + k, k, owners[k]).wait_send()

            for k in (0, 1, 2):
                self.across(k, 2 * owners[k] + c).wait_send()

    class Shed:
        def __init__(self, index, gw, land_p, land_z):
            self.index, self.gw, self.land_p, self.land_z = index, gw, land_p, land_z

        def pair(self, to_z):
            return remote(
                self.gw.at[2 * to_z + 1 - c], self.land_p.at[to_z],
                gp_send.at[self.index, to_z], gp_recv.at[self.index, to_z], s, partner,
            )

        def along(self, i, to_z, of_z, slot):
            return remote(
                self.gw.at[2 * of_z + c], self.land_z.at[slot],
                gz_send.at[self.index, i], gz_recv.at[self.index, slot], s, 2 * to_z + c,
            )

        def add(self, who, land, slot):
            self.gw[who] = (self.gw[who].astype(F32) + land[slot].astype(F32)).astype(BF16)

        def add_pair(self, to_z):
            self.pair(to_z).wait_recv()
            self.add(2 * to_z + c, self.land_p, to_z)

        def far(self):
            for slot, of_z in ((1, mid_o), (2, end_o)):
                self.add_pair(of_z)

                @pl.when(is_mid == 0)
                def _(slot=slot, of_z=of_z):
                    self.along(slot, near, of_z, slot).start()

        def close(self):
            self.add_pair(near)
            self.along(0, near, near, 0).start()
            self.add_pair(z)

        def second(self):
            @pl.when(is_mid == 1)
            def _():
                for i, of_z in ((1, mid_o), (2, end_o)):
                    self.along(i, near, of_z, i).wait_recv()
                    self.add(2 * of_z + c, self.land_z, i)
                    self.along(i, of_z, of_z, 3).start()

        def wait(self):
            self.along(0, near, z, 0).wait_recv()
            self.along(1, near, z, 3).wait_recv()

        def total(self, at):
            value = self.gw[f, at].astype(F32)
            return value + self.land_z[0, at].astype(F32) + self.land_z[3, at].astype(F32)

        def drain(self):
            def one(to_z, _):
                self.pair(to_z).wait_send()
                return 0

            lax.fori_loop(0, n_f // 2, one, 0)
            for i in range(3):
                self.along(i, near, near, 0).wait_send()

    if inside:
        fetch = [
            pltpu.make_async_copy(ref, small_raw.at[i], raw_sem.at[i])
            for i, ref in enumerate(small_given[:8])
        ]
        fetch.append(pltpu.make_async_copy(small_given[8], bias_raw, raw_sem.at[8]))
        for one in fetch:
            one.start()

    barrier = pltpu.get_barrier_semaphore()
    for who in (sx, sy, sd):
        pl.semaphore_signal(barrier, inc=1, device_id=(who, f), device_id_type=pl.DeviceIdType.MESH)
    n_peers = 3
    if inside:
        for d in range(1, n_f):
            pl.semaphore_signal(
                barrier, inc=1, device_id=(s, (f + d) % n_f), device_id_type=pl.DeviceIdType.MESH
            )
        n_peers += n_f - 1
    if inside:
        for one in fetch:
            one.wait()
        for i in range(8):
            small_rows[i : i + 1, :] = small_raw[i].astype(F32)
        tall = small_rows.shape[1]
        lanes = lax.broadcasted_iota(jnp.int32, (tall, 128), 1)
        places = lax.broadcasted_iota(jnp.int32, (tall, 128), 0) + (f % (128 // tall)) * tall
        chosen = jnp.where(lanes == places, 1.0, 0.0).astype(BF16)
        small_in = small_tile
        small_in[0:8] = dot(small_rows[...].astype(BF16), chosen)
        small_in[8:9] = bias_raw[...].astype(F32)
    else:
        small_in = small_given[0]
    pl.semaphore_wait(barrier, n_peers)

    others = (sx, sy, sd)
    ag_tok = Gather(tok, 0)
    if inside:
        high = qkv_in.shape[0]
        high_d = down_in.shape[0]
        w_qkv = [
            Weight(0, by_cut(qkv_w.at[0:2], high)), Weight(4, by_cut(qkv_w.at[2:4], high))
        ]
        w_out = Weight(1, by_rows(out_w.at[0], high))
        w_up = Weight(2, by_cut(up_w, high))
        w_down = Weight(3, by_rows(down_w, high_d))

        def qkv_copy(k, p, to):
            start = pl.multiple_of((p % 3) * width + to * group + (p // 3) * 128, 128)
            src = qkv_in.at[:, pl.ds(start, 128)]
            dst = qkv_w.at[s, pl.ds(pl.multiple_of(f * high, high), high), pl.ds(p * 128, 128)]
            if k < 0:
                return pltpu.make_async_copy(src, dst, col_local.at[p])
            return remote(src, dst, col_send.at[k, p], col_recv.at[k, p], to, f)

        n_cut = 3 * pairs

        ff = up_w.shape[2]

        def up_copy(k, to):
            src = up_in.at[:, pl.ds(pl.multiple_of(to * ff, 128), ff)]
            dst = up_w.at[s, pl.ds(pl.multiple_of(f * high, high), high)]
            if k < 0:
                return pltpu.make_async_copy(src, dst, loc_sem.at[6])
            return remote(src, dst, upc_send.at[k], upc_recv.at[k], to, f)

        out_own = pltpu.make_async_copy(out_in, w_out.view(f), loc_sem.at[0])
        down_own = pltpu.make_async_copy(down_in, w_down.view(f), loc_sem.at[1])

        def small_copy(d):
            return remote(
                small_in, small_f.at[f], sf_send.at[d], sf_recv.at[d], s, (f + d) % n_f
            )

        for d in range(1, n_f):
            small_copy(d).start()
        for p in range(n_cut):
            for k, to in enumerate(others):
                qkv_copy(k, p, to).start()
        ag_tok.start(tokens)
        for p in range(n_cut):
            qkv_copy(-1, p, s).start()
        up_copy(-1, s).start()
        out_own.start()
        down_own.start()
        small_f[f] = small_in[...]
    else:
        loads = [
            pltpu.make_async_copy(qkv_in, qkv_w, col_local.at[0]),
            pltpu.make_async_copy(up_in, up_w, loc_sem.at[6]),
            pltpu.make_async_copy(out_in, out_w, loc_sem.at[0]),
            pltpu.make_async_copy(down_in, down_w, loc_sem.at[1]),
        ]
        for load in loads:
            load.start()
    tok_own = pltpu.make_async_copy(tokens, tok.at[s], loc_sem.at[2])
    tok_own.start()
    cot_own = pltpu.make_async_copy(cot_in, cot, loc_sem.at[3])
    cot_own.start()
    seg_own = pltpu.make_async_copy(seg_in, segs.at[s], loc_sem.at[4])
    seg_own.start()

    def seg_copy(k, to):
        return remote(seg_in, segs.at[s], seg_send.at[k], seg_recv.at[k], to, f)

    for k, to in enumerate(others):
        seg_copy(k, to).start()

    if inside:
        for d in range(1, n_f):
            remote(
                small_in, small_f.at[(f + n_f - d) % n_f], sf_send.at[d], sf_recv.at[d],
                s, (f + d) % n_f,
            ).wait_recv()
        per = n_f * high // 128
        each = n_f // per
        for t in range(per):
            value = small_f[t * each, 0:8]
            for e in range(1, each):
                value = value + small_f[t * each + e, 0:8]
            small_s[s, t] = value
        for e in range(n_f):
            bias_row[0:1, pl.ds(e * 128, 128)] = small_f[e, 8:9]

        def small_wide(k, to):
            return remote(small_s.at[s], small_s.at[s], ss_send.at[k], ss_recv.at[k], to, f)

        for k, to in enumerate(others):
            small_wide(k, to).start()
        for p in range(n_cut):
            qkv_copy(-1, p, s).wait()
            for k, to in enumerate(others):
                qkv_copy(k, p, to).wait_recv()
        for weight in w_qkv:
            weight.start_far(across=False)
        for weight in w_qkv:
            weight.start_near(everyone=True)
            weight.across(3, f).start()
        w_out.start(out_in)
        w_down.start_far(down_in)
    else:
        ag_tok.start(tokens)
        params[...] = small_in[0:8]
        bias_row[...] = small_in[8:9, 0 : bias_row.shape[1]]

    zero_row = jnp.zeros((1, width), F32)

    def both(run, count):
        def step(h, carry):
            return tuple(a + b for a, b in zip(carry, run(h)))

        return lax.fori_loop(0, 2, step, (zero_row,) * count)

    def far_first(i):
        return (1 - i // 2) + 2 * (1 - i % 2)

    def param(i):
        return params[i : i + 1, :]

    tok_own.wait()
    if inside:
        w_qkv[0].relay()
    ag_tok.relay()
    if inside:
        for k, to in enumerate(others):
            up_copy(k, to).start()
        w_qkv[1].relay()
        w_out.relay(False)
        w_down.start_near(down_in)
        for k, who in enumerate(others):
            remote(
                small_s.at[who], small_s.at[who], ss_send.at[k], ss_recv.at[k], who, f
            ).wait_recv()
        for b in range(4):
            for t in range(per):
                params[:, pl.ds((b * per + t) * 128, 128)] = small_s[b, t]

    def first_norm(b):
        unit, _s = unit_of(tok[b].astype(F32))
        normed[b] = (unit * param(0) + param(1)).astype(BF16)

    def norm_step(k, _):
        @pl.when(k == 1)
        def _():
            ag_tok.wait_x()

        @pl.when(k == 2)
        def _():
            ag_tok.wait_y()

        @pl.when(k == 3)
        def _():
            ag_tok.wait_d()

        first_norm(block(k))
        return 0

    lax.fori_loop(0, 3, norm_step, 0)
    if inside:
        for weight in w_qkv:
            weight.rest()
    lax.fori_loop(3, 4, norm_step, 0)
    if inside:
        for weight in w_qkv:
            weight.finish()

    rest = normed[...].reshape(4 * rows, width)
    for p in range(pairs):
        value = dot(rest, qkv_w[:, :, p * 384 : (p + 1) * 384].reshape(width, 384))
        for q in range(3):
            piece = value[:, q * 128 : (q + 1) * 128]
            piece = piece if q else piece * 0.125
            at = slice((3 * p + q) * 128, (3 * p + q + 1) * 128)
            triple[:, :, at] = piece.astype(BF16).reshape(4, rows, 128)

    if inside:
        up_copy(-1, s).wait()
        for k, to in enumerate(others):
            up_copy(k, to).wait_recv()
        w_up.start_far()
        w_up.start_near()

    seg_own.wait()
    for k, who in enumerate(others):
        remote(seg_in, segs.at[who], seg_send.at[k], seg_recv.at[k], who, f).wait_recv()
    seg_all = segs[...]

    def below(level):
        count = jnp.sum((seg_all < level).astype(F32), axis=0)
        return jnp.sum(count, axis=1, keepdims=True)

    bound_1, bound_2 = below(1), below(2)
    blocks = window // rows
    lane = lax.broadcasted_iota(jnp.int32, (1, 128), 1)
    left = (lane < HEAD_DIM).astype(F32)
    sides = (left.astype(BF16), (1.0 - left).astype(BF16))
    pick = lax.broadcasted_iota(jnp.int32, (rows, 128), 1) < HEAD_DIM

    def set_starts(r, _):
        i = (r * rows + lax.broadcasted_iota(jnp.int32, (rows, 128), 0)).astype(F32)
        starts[r] = jnp.where(i >= bound_2, bound_2, jnp.where(i >= bound_1, bound_1, 0.0))
        return 0

    lax.fori_loop(0, 4, set_starts, 0)

    def cut(r, part_at, p, count):
        at = pl.ds(pl.multiple_of((3 * p + part_at) * 128, 128), 128)
        return triple[pl.ds(r, count), :, at].reshape(count * rows, 128)

    def masked(scores, r, first, count):
        start = starts[r]
        tiles = []
        for t in range(count * rows // 128):
            j = lax.broadcasted_iota(jnp.int32, (rows, 128), 1) + t * 128
            keep = (first * rows + j).astype(F32) >= start
            if t * 128 >= (count - 1) * rows:
                i = lax.broadcasted_iota(jnp.int32, (rows, 128), 0)
                keep = keep & (j - (count - 1) * rows <= i)
            tiles.append(jnp.where(keep, scores[:, t * 128 : (t + 1) * 128], NEG))
        return jnp.concatenate(tiles, axis=1)

    rs_1 = Scatter(land_a, 0)

    def attend_pair(r, first, count, p):
        query, keys, vals = cut(r, 0, p, 1), cut(first, 1, p, count), cut(first, 2, p, count)
        outs = []
        for e in range(2):
            scores = masked(dot(query * sides[e], keys, NT), r, first, count)
            expo = jnp.exp(scores - jnp.max(scores, -1, keepdims=True))
            low = (expo * (1.0 / jnp.sum(expo, -1, keepdims=True))).astype(BF16)
            probs[r, 2 * p + e, :, 0 : count * rows] = low
            outs.append(dot(low, vals))
        attended[r, :, p * 128 : (p + 1) * 128] = jnp.where(pick, outs[0], outs[1]).astype(BF16)

    def attend(i, _):
        rel = far_first(i)
        r = block(rel)
        for count in range(1, blocks + 1):
            @pl.when(r + 1 >= count if count == blocks else r + 1 == count)
            def _(count=count):
                for p in range(pairs):
                    attend_pair(r, r + 1 - count, count, p)

        if inside:
            @pl.when(i == 0)
            def _():
                out_own.wait()
                w_out.finish()

        part[rel] = dot(attended[r], out_w[0]).astype(BF16)

        @pl.when(c == 0)
        def _():
            rs_1.step(rel)

        @pl.when((c == 1) & (i == 2))
        def _():
            rs_1.step(3)

        if inside:
            @pl.when(i == 1)
            def _():
                w_down.relay()

        return 0

    if inside:
        w_out.relay_rest()
        w_out.rest()
    lax.fori_loop(0, 4, attend, 0)

    my_turn((1, 1))

    @pl.when(c == 1)
    def _():
        for i in (1, 3):
            rs_1.copy(i).start()

    rs_1.relay()
    if inside:
        w_up.relay()

        @pl.when(c == 1)
        def _():
            w_down.rest()

    rs_1.wait()

    def mid_norm(h):
        at = half_rows(h)
        value = rs_1.total(h)
        branch[at] = value
        unit, _s = unit_of(value)
        mid = tok[s, at].astype(F32) + (unit * param(2) + param(3))
        middle[at] = mid
        unit, _s = unit_of(mid)
        inner[s, at] = (unit * param(4) + param(5)).astype(BF16)

    for h in range(2):
        mid_norm(h)
    ag_inner = Gather(inner, 1)
    my_turn()
    ag_inner.start()
    rs_1.drain()
    if inside:
        @pl.when(c == 1)
        def _():
            w_up.rest()

    ag_inner.relay()
    if inside:
        @pl.when(c == 0)
        def _():
            w_down.rest()
            w_up.rest()

        w_up.finish()

    ff = up_w.shape[2]
    tile = ff
    rs_2 = Scatter(land_b, 1)

    def forward_step(k, _):
        @pl.when(k == 1)
        def _():
            ag_inner.wait_x()

        @pl.when(k > 1)
        def _():
            ag_inner.step(k)

        r = block(k)

        def column(n, _):
            at = pl.ds(pl.multiple_of(n * tile, tile), tile)
            pre = dot(inner[r], up_w[:, :, at].reshape(width, tile)) + bias_row[:, at]
            square = pre * pre
            bend = jnp.tanh(0.7978845608028654 * pre * (1.0 + 0.044715 * square))
            near = 0.5 + 0.5 * bend
            activ[r, :, at] = (pre * near).astype(BF16)
            slope = near + pre * (0.5 - 0.5 * bend * bend) * (
                0.7978845608028654 + 0.10703222440890037 * square
            )
            dgelu[r, :, at] = slope.astype(BF16)
            return 0

        lax.fori_loop(0, ff // tile, column, 0)
        return 0

    lax.fori_loop(0, 4, forward_step, 0)
    if inside:
        down_own.wait()
        w_down.finish()

    def down_step(i, _):
        rel = far_first(i)
        r = block(rel)

        part[rel] = dot(activ[r], down_w[...]).astype(BF16)
        rs_2.step(rel)
        return 0

    my_turn()
    lax.fori_loop(0, 4, down_step, 0)
    rs_2.relay()
    cot_own.wait()
    rs_2.wait()

    def last_norm(h):
        at = half_rows(h)
        unit, scale = unit_of(rs_2.total(h))
        result_v[at] = (middle[at] + (unit * param(6) + param(7))).astype(BF16)
        grad = cot[at].astype(F32)
        gmix[s, at] = pull_of(grad, param(6), unit, scale).astype(BF16)
        return col_sum(grad * unit), col_sum(grad)

    grad_gain_d, grad_shift_d = both(last_norm, 2)
    sg_rows = [None] * 8
    sg_rows[6], sg_rows[7] = grad_gain_d, grad_shift_d
    ag_mix = Gather(gmix, 2)
    my_turn()
    ag_mix.start()
    result_out = pltpu.make_async_copy(result_v, result, o_sem.at[2])
    result_out.start()
    rs_2.drain()

    rs_3 = Scatter(land_a, 2)
    sg_bias = bias_row

    def clear(n, _):
        at = pl.ds(pl.multiple_of(n * tile, tile), tile)
        sg_bias[:, at] = jnp.zeros((1, tile), F32)
        return 0

    lax.fori_loop(0, ff // tile, clear, 0)

    TN = ((0,), (0,))

    def flat(ref, lanes=slice(None)):
        held = ref[:, :, lanes]
        return held.reshape(4 * rows, held.shape[2])

    def all_pairs(shed):
        for to_z in range(n_f // 2):
            shed.pair(to_z).start()

    def cut_grads(left, right, gw, shed, lanes=slice(None)):
        for b in range(4):
            value = dot(flat(left, slice(b * rows, (b + 1) * rows)), flat(right, lanes), TN)
            gw[:, b * high : (b + 1) * high, :] = value.astype(BF16).reshape(n_f, high, -1)
        all_pairs(shed)

    def down_grads(rels):
        each = ff // n_f
        count = 256 // each
        for b in range(n_f // count):
            at = slice(b * count, (b + 1) * count)
            cols = slice(b * 256, (b + 1) * 256)
            value = dot(activ[block(rels[0]), :, cols], gmix[block(rels[0])], TN)
            for rel in rels[1:]:
                value = value + dot(activ[block(rel), :, cols], gmix[block(rel)], TN)
            if len(rels) == 1:
                value = value + gw_down[at].astype(F32).reshape(256, width)
            gw_down[at] = value.astype(BF16).reshape(count, each, width)

    if inside:
        shed_down = Shed(0, gw_down, lp_down, lz_down)
        shed_up = Shed(1, gw_up, lp_up, lz_up)
        shed_out = Shed(2, gw_out, lp_out, lz_out)
        shed_qkv = [
            Shed(3 + p, gw_qkv[p], lp_qkv[p], lz_qkv[p])
            for p in range(pairs)
        ]
        ag_tok.drain()

    def back_step(k, _):
        if inside:
            @pl.when(k == 3)
            def _():
                down_grads((0, 1, 2))

        ag_mix.step(k)
        r = block(k)

        def column(n, _):
            at = pl.ds(pl.multiple_of(n * tile, tile), tile)
            grad = dot(gmix[r], down_w[at], NT)
            low = (dgelu[r, :, at].astype(F32) * grad).astype(BF16)
            dgelu[r, :, at] = low
            sg_bias[:, at] = sg_bias[:, at] + col_sum(low.astype(F32))
            return 0

        lax.fori_loop(0, ff // tile, column, 0)
        return 0

    lax.fori_loop(0, 4, back_step, 0)

    if inside:
        down_grads((3,))
        all_pairs(shed_down)

        @pl.when(c == 1)
        def _():
            shed_down.far()

    def inner_step(i, _):
        rel = far_first(i)
        r = block(rel)

        part[rel] = dot(dgelu[r], up_w[...].reshape(width, ff), NT).astype(BF16)
        rs_3.step(rel)
        return 0

    my_turn()
    lax.fori_loop(0, 4, inner_step, 0)

    if inside:
        cut_grads(inner, dgelu, gw_up, shed_up)
    rs_3.relay()
    if inside:
        @pl.when(c == 1)
        def _():
            shed_up.far()
            shed_down.close()
            shed_up.close()

        @pl.when(c == 0)
        def _():
            shed_down.far()

    rs_3.wait()

    def mid_back(h):
        at = half_rows(h)
        grad = rs_3.total(h)
        unit, scale = unit_of(middle[at])
        total = cot[at].astype(F32) + pull_of(grad, param(4), unit, scale)
        gmid[at] = total
        out = [col_sum(grad * unit), col_sum(grad)]
        unit, scale = unit_of(branch[at])
        gbr[s, at] = pull_of(total, param(2), unit, scale).astype(BF16)
        return out[0], out[1], col_sum(total * unit), col_sum(total)

    sg_rows[4], sg_rows[5], sg_rows[2], sg_rows[3] = both(mid_back, 4)
    ag_br = Gather(gbr, 3)
    my_turn()
    ag_br.start()
    rs_3.drain()
    def arrive(k, _):
        if inside:
            @pl.when(k == 1)
            def _():
                ag_br.relay()

            @pl.when((k == 1) & (c == 0))
            def _():
                shed_up.far()
                shed_down.close()
                shed_up.close()

            @pl.when(k == 1)
            def _():
                ag_br.wait_x()

            @pl.when(k > 1)
            def _():
                ag_br.step(k)

            @pl.when(k == 2)
            def _():
                shed_down.second()
        else:
            ag_br.step(k)

        r = block(k)
        gatt[r] = dot(gbr[r], out_w[0], NT).astype(BF16)
        if inside:
            value = dot(attended[r], gbr[r], TN)

            @pl.when(k == 0)
            def _():
                branch[...] = value

            @pl.when(k > 0)
            def _():
                branch[...] = branch[...] + value

        return 0

    lax.fori_loop(0, 4, arrive, 0)
    if inside:
        gw_out[...] = branch[...].astype(BF16).reshape(gw_out.shape)
        all_pairs(shed_out)

        @pl.when(c == 1)
        def _():
            shed_out.far()
            shed_out.close()

    if inside:
        per = n_f * high // 128
        gdown_out = pltpu.make_async_copy(fin_down, gdown, o_sem.at[3])
        gout_out = pltpu.make_async_copy(fin_out, gout, o_sem.at[4])
        gup_out = pltpu.make_async_copy(gup_v, gup, o_sem.at[5])
        gqkv_out = pltpu.make_async_copy(gqkv_v, gqkv, o_sem.at[6])
        gsmall_out = pltpu.make_async_copy(small_sum, gsmall, o_sem.at[7])

        def ts_copy(k, to):
            return remote(sg_s.at[to], sg_land_s.at[k], ts_send.at[k], ts_recv.at[k], to, f)

        def tf_copy(d):
            to = (f + d) % n_f
            return remote(
                sg_f.at[to], sg_land_f.at[d - 1], tf_send.at[d], tf_recv.at[d], s, to
            )

        def small_first():
            for b in range(4):
                for t in range(per):
                    at = slice((b * per + t) * 128, (b * per + t + 1) * 128)
                    for i in range(8):
                        sg_s[b, t, i : i + 1, :] = sg_rows[i][:, at]
            for k, to in enumerate(others):
                ts_copy(k, to).start()

        def small_second():
            for k, to in enumerate(others):
                ts_copy(k, to).wait_recv()
            for who in range(n_f):
                t = who * high // 128
                sg_f[who, 0:8] = (
                    sg_s[s, t] + sg_land_s[0, t] + sg_land_s[1, t] + sg_land_s[2, t]
                )
                sg_f[who, 8:9] = sg_bias[:, who * 128 : (who + 1) * 128]
            for d in range(1, n_f):
                tf_copy(d).start()

        def small_third():
            for d in range(1, n_f):
                tf_copy(d).wait_recv()
            value = sg_f[f]
            for d in range(1, n_f):
                value = value + sg_land_f[d - 1]
            small_sum[...] = value
            gsmall_out.start()

        def gu_copy(k, to, who):
            return remote(fin_up.at[to], land_up.at[who], gu_send.at[k], gu_recv.at[k], to, f)

        def gc_at(p, who):
            start = pl.multiple_of((p % 3) * width + who * group + (p // 3) * 128, 128)
            return pl.ds(start, 128)

        def gc_copy(k, p, to, who):
            return remote(
                fin_qkv.at[p, to], land_qkv.at[p, who],
                gc_send.at[k, p], gc_recv.at[k, p], to, f,
            )

    def back_pair(p):
        lanes = slice(p * 128, (p + 1) * 128)
        for r in range(3, -1, -1):
            first = max(r + 1 - blocks, 0)
            count = r + 1 - first
            query, keys, vals = cut(r, 0, p, 1), cut(first, 1, p, count), cut(first, 2, p, count)
            grad = gatt[r, :, lanes]
            query_t, grad_t = query.T, grad.T
            outs, key_parts, value_parts = [], [], []
            for e in range(2):
                low = probs[r, 2 * p + e, :, 0 : count * rows]
                grad_probs = dot(grad * sides[e], vals, NT)
                full = low.astype(F32)
                inner_sum = jnp.sum(full * grad_probs, -1, keepdims=True)
                grad_scores = (full * (grad_probs - inner_sum)).astype(BF16)
                outs.append(dot(grad_scores, keys))
                side = slice(e * HEAD_DIM, (e + 1) * HEAD_DIM)
                here = slice(p * 128 + e * HEAD_DIM, p * 128 + (e + 1) * HEAD_DIM)
                key_part = dot(query_t[side], grad_scores)
                value_part = dot(grad_t[side], low)
                for n in range(count):
                    span = slice((first + n) * rows, (first + n + 1) * rows)
                    cols = slice(n * rows, (n + 1) * rows)
                    if r == 3 or (first + n) < 4 - blocks and r == first + n + blocks - 1:
                        dkt[here, span] = key_part[:, cols]
                        dvt[here, span] = value_part[:, cols]
                    else:
                        dkt[here, span] = dkt[here, span] + key_part[:, cols]
                        dvt[here, span] = dvt[here, span] + value_part[:, cols]
            at = slice(3 * p * 128, (3 * p + 1) * 128)
            gtri[r, :, at] = (jnp.where(pick, outs[0], outs[1]) * 0.125).astype(BF16)
        for b in range(4):
            span = slice(b * rows, (b + 1) * rows)
            at = slice((3 * p + 1) * 128, (3 * p + 2) * 128)
            gtri[b, :, at] = dkt[lanes, span].astype(BF16).T
            at = slice((3 * p + 2) * 128, (3 * p + 3) * 128)
            gtri[b, :, at] = dvt[lanes, span].astype(BF16).T

    def qkv_grads(p):
        cut_grads(normed, gtri, gw_qkv[p], shed_qkv[p], slice(p * 384, (p + 1) * 384))

    for p in range(pairs):
        back_pair(p)
        if inside and p == 0:
            qkv_grads(p)
            shed_up.second()

            @pl.when(c == 1)
            def _():
                shed_qkv[0].far()

    if inside:
        @pl.when(c == 1)
        def _():
            qkv_grads(1)
            shed_qkv[1].far()
            for shed in shed_qkv:
                shed.close()

        @pl.when(c == 0)
        def _():
            shed_out.far()
            shed_qkv[0].far()

    rs_4 = Scatter(land_b, 3)

    def normed_step(i, carry):
        rel = far_first(i)
        r = block(rel)
        grad = dot(gtri[r], qkv_w[...].reshape(width, 3 * group), NT)
        part[rel] = grad.astype(BF16)
        rs_4.step(rel)
        unit, _s = unit_of(tok[r].astype(F32))
        return carry[0] + col_sum(grad * unit), carry[1] + col_sum(grad)

    my_turn()
    sg_rows[0], sg_rows[1] = lax.fori_loop(0, 4, normed_step, (zero_row, zero_row))
    if inside:
        small_first()

        @pl.when(c == 0)
        def _():
            qkv_grads(1)

    rs_4.relay()
    if inside:
        @pl.when(c == 0)
        def _():
            shed_qkv[1].far()
            for shed in (shed_out, *shed_qkv):
                shed.close()

        for shed in (shed_out, *shed_qkv):
            shed.second()
        small_second()
        at = pl.ds(pl.multiple_of(s * high, high), high)
        shed_up.wait()
        for b in range(4):
            fin_up[b] = shed_up.total(slice(b * high, (b + 1) * high)).astype(BF16)
        gup_v[:, pl.ds(pl.multiple_of(s * ff, 128), ff)] = shed_up.total(at)

        def give_up():
            for k, to in enumerate(others):
                gu_copy(k, to, s).start()

        @pl.when(c == 1)
        def _():
            give_up()

        shed_down.wait()
        fin_down[...] = shed_down.total(slice(None))
        gdown_out.start()
    rs_4.wait()

    def first_back(h, _):
        at = half_rows(h)
        unit, scale = unit_of(tok[s, at].astype(F32))
        gmid[at] = gmid[at] + pull_of(rs_4.total(h), param(0), unit, scale)
        pltpu.make_async_copy(gmid.at[at], tgrad.at[at], o_sem.at[h]).start()
        return 0

    lax.fori_loop(0, 2, first_back, 0)
    if inside:
        for q, shed in enumerate(shed_qkv):
            shed.wait()
            for b in range(4):
                fin_qkv[q, b] = shed.total(slice(b * high, (b + 1) * high)).astype(BF16)
            for k, to in enumerate(others):
                gc_copy(k, q, to, s).start()
            own = shed.total(at)
            for p in range(3):
                gqkv_v[:, gc_at(3 * q + p, s)] = own[:, p * 128 : (p + 1) * 128]

        @pl.when(c == 0)
        def _():
            give_up()

        for k, who in enumerate(others):
            gu_copy(k, who, who).wait_recv()
            gup_v[:, pl.ds(pl.multiple_of(who * ff, 128), ff)] = land_up[who].astype(F32)
        gup_out.start()
        shed_out.wait()
        fin_out[...] = shed_out.total(slice(None))
        gout_out.start()
        small_third()
        for k, who in enumerate(others):
            for q in range(pairs):
                gc_copy(k, q, who, who).wait_recv()
                for p in range(3):
                    piece = land_qkv[q, who, :, p * 128 : (p + 1) * 128]
                    gqkv_v[:, gc_at(3 * q + p, who)] = piece.astype(F32)
        gqkv_out.start()

    for h in range(2):
        pltpu.make_async_copy(gmid.at[half_rows(h)], tgrad.at[half_rows(h)], o_sem.at[h]).wait()
    result_out.wait()
    if inside:
        gsmall_out.wait()
        gdown_out.wait()
        gout_out.wait()
        gup_out.wait()
        gqkv_out.wait()
        for k, to in enumerate(others):
            gu_copy(k, to, s).wait_send()
            ts_copy(k, to).wait_send()
            for q in range(pairs):
                gc_copy(k, q, to, s).wait_send()
            for p in range(n_cut):
                qkv_copy(k, p, to).wait_send()
            up_copy(k, to).wait_send()
            small_wide(k, to).wait_send()
        for d in range(1, n_f):
            tf_copy(d).wait_send()
            small_copy(d).wait_send()
        for weight in (*w_qkv, w_out, w_up, w_down):
            weight.drain()
        for shed in (shed_down, shed_up, shed_out, *shed_qkv):
            shed.drain()
    else:
        for i in range(8):
            small_sum[i : i + 1, :] = sg_rows[i]
        small_sum[8:9, 0:ff] = sg_bias[...]
        gsmall_out = pltpu.make_async_copy(small_sum, gsmall, o_sem.at[7])
        gsmall_out.start()
        gsmall_out.wait()
    for k, to in enumerate(others):
        seg_copy(k, to).wait_send()
    for gather in (ag_inner, ag_mix, ag_br) + (() if inside else (ag_tok,)):
        gather.drain()
    rs_4.drain()


def finish_kernel(n_f, n_big, *refs):
    small, given = refs[0], refs[1 : 1 + n_big]
    made, minor = refs[1 + n_big : 1 + 2 * n_big], refs[1 + 2 * n_big : 10 + 2 * n_big]
    held, (in_sem, out_sem) = refs[10 + 2 * n_big : 10 + 3 * n_big], refs[10 + 3 * n_big :]
    cuts = []
    for i in range(n_big):
        tall = given[i].shape[0]
        for j in range(max(1, tall // 64)):
            at = pl.ds(j * min(tall, 64), min(tall, 64))
            cuts.append((i, at, len(cuts)))
    for i, at, n in cuts:
        pltpu.make_async_copy(given[i].at[at], held[i].at[at], in_sem.at[n]).start()
    each = minor[0].shape[1]
    place = lax.axis_index("fsdp") % (128 // each)
    for i in range(8):
        row = small[i : i + 1, :]
        value = row[:, 0:each]
        for q in range(1, 128 // each):
            value = jnp.where(place == q, row[:, q * each : (q + 1) * each], value)
        minor[i][...] = value
    minor[8][...] = small[8:9, :]
    for i, at, n in cuts:
        pltpu.make_async_copy(given[i].at[at], held[i].at[at], in_sem.at[n]).wait()
        pltpu.make_async_copy(held[i].at[at], made[i].at[at], out_sem.at[n]).start()
    for i, at, n in cuts:
        pltpu.make_async_copy(held[i].at[at], made[i].at[at], out_sem.at[n]).wait()


def finish(n_f, high, *made):
    big, small = made[:6], made[6]
    whole, anywhere = pl.BlockSpec(memory_space=pltpu.VMEM), pl.BlockSpec(memory_space=pl.ANY)
    count = sum(max(1, v.shape[0] // 64) for v in big)
    minor = [jax.ShapeDtypeStruct((1, high), F32)] * 8 + [jax.ShapeDtypeStruct((1, 128), F32)]
    out = pl.pallas_call(
        partial(finish_kernel, n_f, 6),
        out_shape=[jax.ShapeDtypeStruct(v.shape, v.dtype) for v in big] + minor,
        in_specs=[whole] + [anywhere] * 6,
        out_specs=[anywhere] * 6 + [whole] * 9,
        scratch_shapes=[pltpu.VMEM(v.shape, v.dtype) for v in big]
        + [pltpu.SemaphoreType.DMA((count,))] * 2,
    )(small, *big)
    result, tgrad, gqkv, gout, gup, gdown = out[:6]
    small = [v[0] for v in out[6:]]
    return (result[None], tgrad[None], gqkv, gout, gup, small[8], gdown, *small[:8])


def on_device(n_seq, n_f, *args):
    (tokens, segments, qkv_weight, out_weight, up_weight, up_bias, down_weight) = args[:7]
    vectors, cotangent = args[7:15], args[15]
    rows, width = tokens.shape[1:]
    high, high_d = qkv_weight.shape[0], down_weight.shape[0]
    length = n_seq * rows
    group = qkv_weight.shape[1] // 3 // n_seq
    heads = group // HEAD_DIM
    ff = up_weight.shape[1] // n_seq
    half = rows // 2
    window = rows * min(n_seq, 1 + -(-511 // rows))
    inside = n_f == 8 and high % 32 == 0
    f = lax.axis_index("fsdp")
    if inside:
        small = [v[None] for v in (*vectors, up_bias)]
        weights = (qkv_weight, out_weight, up_weight, down_weight)
    else:
        small = jnp.stack([v.astype(F32) for v in vectors])
        small = lax.all_gather(small, ("seq", "fsdp"), axis=1, tiled=True)
        bias = lax.all_gather(up_bias.astype(F32), "fsdp", axis=0, tiled=True)
        bias = jnp.pad(bias[None], ((0, 7), (0, width - ff)))
        small = [jnp.concatenate([small, bias])]

        def columns(weight, parts):
            cut = weight.reshape(high, parts, n_seq, -1, 128).transpose(2, 0, 3, 1, 4)
            cut = cut.reshape(n_seq, high, -1)
            cut = lax.all_to_all(cut, "seq", split_axis=0, concat_axis=0, tiled=True)
            return lax.all_gather(cut, "fsdp", axis=1, tiled=True)

        weights = (
            columns(qkv_weight, 3),
            lax.all_gather(out_weight, "fsdp", axis=0, tiled=True)[None],
            columns(up_weight, 1),
            lax.all_gather(down_weight, "fsdp", axis=0, tiled=True),
        )
    vmem, anywhere, dma = pltpu.VMEM, pl.BlockSpec(memory_space=pl.ANY), pltpu.SemaphoreType.DMA
    whole = pl.BlockSpec(memory_space=pltpu.VMEM)
    full = (4, rows, width)
    saved = {
        "normed": (full, BF16), "inner": (full, BF16), "gmix": (full, BF16), "gbr": (full, BF16),
        "attended": ((4, rows, group), BF16), "activ": ((4, rows, ff), BF16),
        "dgelu": ((4, rows, ff), BF16), "gtri": ((4, rows, 3 * group), BF16),
    }
    n_cut = 3 * (group // 128)
    pieces = {"q0": (n_seq * high, 384), "q1": (n_seq * high, 384), "out": (high, width),
              "up": (n_seq * high, ff), "down": (high_d, width)}
    scratch = {
        "tok": vmem(full, BF16), "normed": None, "inner": None, "gmix": None, "gbr": None,
        "qkv_w": vmem((n_seq, rows, 3 * group), BF16), "out_w": vmem((1, group, width), BF16),
        "up_w": vmem((n_seq, rows, ff), BF16), "down_w": vmem((ff, width), BF16),
        "segs": vmem((4, 1, rows), jnp.int32),
        "small_f": vmem((n_f if inside else 1, 16, 128), F32), "small_s": vmem((4, width // 512, 8, 128), F32),
        "params": vmem((8, width), F32), "bias_row": vmem((1, ff), F32),
        "triple": vmem((4, rows, 3 * group), BF16), "probs": vmem((4, heads, rows, window), BF16),
        "attended": None, "starts": vmem((4, rows, 128), F32), "activ": None, "dgelu": None,
        "part": vmem(full, BF16), "land_a": vmem((6, half, width), BF16),
        "land_b": vmem((6, half, width), BF16),
        "branch": vmem((rows, width), F32), "middle": vmem((rows, width), F32),
        "gmid": vmem((rows, width), F32), "cot": vmem((rows, width), BF16),
        "gtri": None, "gatt": vmem((4, rows, group), BF16), "dkt": vmem((group, length), F32),
        "dvt": vmem((group, length), F32),
    }
    for name, (tall, wide) in pieces.items():
        scratch["gw_" + name] = vmem((n_f if inside else 1, tall if inside else 16, wide), BF16)
    for name, (tall, wide) in pieces.items():
        scratch["lp_" + name] = vmem((n_f // 2 if inside else 1, tall if inside else 16, wide), BF16)
    for name, (tall, wide) in pieces.items():
        scratch["lz_" + name] = vmem((n_f // 2 if inside else 1, tall if inside else 16, wide), BF16)
    scratch["result_v"] = vmem((rows, width), BF16)
    scratch["fin_qkv"] = vmem((group // 128, 4, high, 384), BF16)
    scratch["fin_up"] = vmem((4, high, ff), BF16)
    scratch["land_qkv"] = vmem((group // 128, 4, high, 384), BF16)
    scratch["land_up"] = vmem((4, high, ff), BF16)
    scratch["fin_down"] = vmem((high_d, width), F32)
    scratch["fin_out"] = vmem((high, width), F32)
    scratch["gup_v"] = vmem((high, n_seq * ff), F32)
    scratch["gqkv_v"] = vmem((high, n_seq * 3 * group), F32)
    scratch["small_sum"] = vmem((16, 128 if inside else width), F32)
    tiles = width // 512
    scratch["sg_s"] = vmem((4, tiles, 8, 128), F32)
    scratch["sg_land_s"] = vmem((3, tiles, 8, 128), F32)
    scratch["sg_f"] = vmem((n_f if inside else 1, 16, 128), F32)
    scratch["sg_land_f"] = vmem((n_f - 1 if inside else 1, 16, 128), F32)
    for name, shape in (
        ("ag_send", (4, 6)), ("ag_recv", (4, 6)), ("rs_send", (4, 6)), ("rs_recv", (4, 6)),
        ("w_send", (5, 4)), ("w_recv", (5, 3)), ("p_send", (5, 4)), ("p_recv", (5, 4)),
        ("col_send", (3, n_cut)), ("col_recv", (3, n_cut)), ("col_local", (n_cut,)),
        ("upc_send", (3,)), ("upc_recv", (3,)), ("seg_send", (3,)), ("seg_recv", (3,)),
        ("sf_send", (8,)), ("sf_recv", (8,)), ("ss_send", (3,)), ("ss_recv", (3,)),
        ("loc_sem", (7,)), ("o_sem", (8,)),
        ("gp_send", (5, 4)), ("gp_recv", (5, 4)), ("gz_send", (5, 4)), ("gz_recv", (5, 4)),
        ("gc_send", (3, 2)), ("gc_recv", (3, 2)), ("gu_send", (3,)), ("gu_recv", (3,)),
        ("ts_send", (3,)), ("ts_recv", (3,)), ("tf_send", (8,)), ("tf_recv", (8,)),
    ):
        scratch[name] = dma(shape)
    scratch["turn"] = pltpu.SemaphoreType.REGULAR
    scratch["small_raw"] = vmem((8, 1, high), BF16)
    scratch["bias_raw"] = vmem((1, up_bias.shape[0]), BF16)
    scratch["small_rows"] = vmem((8, high), F32)
    scratch["small_tile"] = vmem((16, 128), F32)
    scratch["raw_sem"] = dma((9,))
    outs = {
        "result": ((rows, width), BF16), "tgrad": ((rows, width), F32),
        "gqkv": ((high, n_seq * 3 * group), F32), "gout": ((high, width), F32),
        "gup": ((high, n_seq * ff), F32), "gdown": ((high_d, width), F32),
        "gsmall": ((16, 128 if inside else width), F32),
    }
    if inside:
        for name, shape in saved.items():
            scratch[name] = vmem(*shape)
        extra = []
    else:
        extra = list(saved)
    names = list(scratch)

    def kernel(*refs):
        n_in = 7 + len(small)
        given = (*refs[:2], refs[2 : 2 + len(small)], *refs[2 + len(small) : n_in])
        made = refs[n_in : n_in + len(outs)]
        more = dict(zip(extra, refs[n_in + len(outs) :]))
        rest = refs[n_in + len(outs) + len(extra) :]
        more.update(zip([n for n in names if scratch[n] is not None], rest))
        layer_kernel(inside, n_f, *given, *made, *[more[n] for n in names])

    shapes = [*outs.values(), *[saved[n] for n in extra]]
    made = pl.pallas_call(
        kernel,
        out_shape=[jax.ShapeDtypeStruct(*shape) for shape in shapes],
        in_specs=[anywhere] * 2 + [anywhere if inside else whole] * len(small) + [anywhere] * 5,
        out_specs=[anywhere] * len(outs) + [whole] * len(extra),
        scratch_shapes=[scratch[n] for n in names if scratch[n] is not None],
        compiler_params=pltpu.CompilerParams(
            collective_id=0, has_side_effects=True, vmem_limit_bytes=67043328
        ),
    )(tokens[0], segments, *small, cotangent[0], *weights)
    result, tgrad, gqkv, gout, gup, gdown, gsmall = made[:7]
    if inside:
        return finish(n_f, high, *made[:7])
    else:
        kept = {n: v.reshape(length, -1) for n, v in zip(extra, made[7:])}

        def turned_dot(left, right):
            return lax.dot_general(
                kept[left], kept[right], (((0,), (0,)), ((), ())), preferred_element_type=F32
            ).astype(BF16)

        def shed(value):
            return lax.psum_scatter(value, "fsdp", scatter_dimension=0, tiled=True)

        def columns_back(value, parts):
            cut = value.reshape(n_seq, n_f, high, -1).transpose(1, 0, 2, 3)
            cut = lax.all_to_all(shed(cut)[0], "seq", split_axis=0, concat_axis=0, tiled=True)
            cut = cut.reshape(n_seq, high, -1, parts, 128).transpose(1, 3, 0, 2, 4)
            return cut.reshape(high, -1).astype(F32)

        gqkv = columns_back(turned_dot("normed", "gtri"), 3)
        gout = shed(turned_dot("attended", "gbr")).astype(F32)
        gup = columns_back(turned_dot("inner", "dgelu"), 1)
        gdown = shed(turned_dot("activ", "gmix")).astype(F32)
        vectors = lax.psum_scatter(gsmall[:8], ("seq", "fsdp"), scatter_dimension=1, tiled=True)
        gbias = shed(gsmall[8, :ff])
    return (result[None], tgrad[None], gqkv, gout, gup, gbias, gdown, *vectors)


def solution(mesh):
    rows = P(("seq", "fsdp"), None)
    vector = P(("seq", "fsdp"))
    acts = P("fsdp", "seq", None)
    return jax.shard_map(
        partial(on_device, mesh.shape["seq"], mesh.shape["fsdp"]),
        mesh=mesh,
        in_specs=(acts, P("fsdp", "seq"), rows, rows, rows, vector, rows, *(vector,) * 8, acts),
        out_specs=(acts, acts, rows, rows, rows, vector, rows, *(vector,) * 8),
        check_vma=False,
    )
```

```python
from functools import partial

import jax
import jax.numpy as jnp
from jax import lax
from jax.experimental import pallas as pl
from jax.experimental.pallas import tpu as pltpu
from jax.sharding import PartitionSpec as P

HEAD_DIM = 64
F32 = jnp.float32
BF16 = jnp.bfloat16
NN = ((1,), (0,))
NT = ((1,), (1,))
NEG = -1e30


def dot(left, right, dims=NN):
    return lax.dot_general(left, right, (dims, ((), ())), preferred_element_type=F32)


def unit_of(value):
    center = value - jnp.mean(value, -1, keepdims=True)
    scale = lax.rsqrt(jnp.mean(center * center, -1, keepdims=True) + 1e-05)
    return center * scale, scale


def pull_of(grad, gain, unit, scale):
    pulled = grad * gain
    first = jnp.mean(pulled, -1, keepdims=True)
    second = jnp.mean(pulled * unit, -1, keepdims=True)
    return scale * (pulled - first - unit * second)


def col_sum(value):
    return jnp.sum(value, 0, keepdims=True)


def layer_kernel(
    inside,
    n_f,
    tokens, seg_in, small_given, cot_in, qkv_in, out_in, up_in, down_in,
    result, tgrad, gqkv, gout, gup, gdown, gsmall,
    tok, normed, inner, gmix, gbr,
    qkv_w, out_w, up_w, down_w,
    segs, small_f, small_s, params, bias_row,
    triple, probs, attended, starts, activ, dgelu,
    part, land_a, land_b,
    branch, middle, gmid, cot,
    gtri, gatt, dkt, dvt,
    gw_q0, gw_q1, gw_out, gw_up, gw_down,
    lp_q0, lp_q1, lp_out, lp_up, lp_down,
    lz_q0, lz_q1, lz_out, lz_up, lz_down,
    fin_qkv, land_qkv, small_sum,
    sg_s, sg_land_s, sg_f, sg_land_f,
    ag_send, ag_recv, rs_send, rs_recv,
    w_send, w_recv, p_send, p_recv,
    col_send, col_recv, col_local, upc_send, upc_recv,
    seg_send, seg_recv, sf_send, sf_recv, ss_send, ss_recv,
    loc_sem, o_sem,
    gp_send, gp_recv, gz_send, gz_recv,
    gc_send, gc_recv, gu_send, gu_recv,
    ts_send, ts_recv, tf_send, tf_recv, turn,
    small_raw, bias_raw, small_rows, small_tile, raw_sem,
):
    gw_qkv, lp_qkv, lz_qkv = (gw_q0, gw_q1), (lp_q0, lp_q1), (lz_q0, lz_q1)
    rows, width = tokens.shape
    half = rows // 2
    group = out_w.shape[1]
    pairs = group // 128
    window = probs.shape[3]
    s = lax.axis_index("seq")
    f = lax.axis_index("fsdp")
    x, y = s % 2, s // 2
    z, c = f // 2, f % 2

    def block(rel):
        return 2 * ((y + rel // 2) % 2) + (x + rel % 2) % 2

    sx, sy, sd = block(1), block(2), block(3)

    def remote(src, dst, send, recv, to_s, to_f):
        return pltpu.make_async_remote_copy(
            src_ref=src, dst_ref=dst, send_sem=send, recv_sem=recv,
            device_id=(to_s, to_f), device_id_type=pl.DeviceIdType.MESH,
        )

    def my_turn(cores=(0, 1)):
        if inside:
            @pl.when(c >= cores[0])
            def _():
                pl.semaphore_wait(turn, 1)

    def hand_over(cores=(0, 1)):
        if inside:
            @pl.when(c <= cores[1])
            def _():
                pl.semaphore_signal(
                    turn, inc=1, device_id=(s, 2 * z + 1 - c),
                    device_id_type=pl.DeviceIdType.MESH,
                )

    class Gather:
        def __init__(self, full, index):
            self.full, self.index = full, index

        def piece(self, b, h):
            return self.full.at[b, pl.ds(h * half, half)]

        def copy(self, i, b, h, to, src=None):
            dst = self.piece(b, h)
            return remote(
                dst if src is None else src, dst,
                ag_send.at[self.index, i], ag_recv.at[self.index, i], to, f,
            )

        def start(self, src=None):
            def cut(h):
                return None if src is None else src.at[pl.ds(h * half, half)]

            self.copy(0, s, 0, sx, cut(0)).start()
            self.copy(1, s, 1, sy, cut(1)).start()
            self.copy(2, s, 1, sx, cut(1)).start()
            self.copy(3, s, 0, sy, cut(0)).start()

        def relay(self):
            self.copy(0, sx, 0, sx).wait_recv()
            self.copy(4, sx, 0, sy).start()
            self.copy(1, sy, 1, sy).wait_recv()
            self.copy(5, sy, 1, sx).start()
            if self.index:
                hand_over()

        def wait_x(self):
            self.copy(2, sx, 1, sx).wait_recv()

        def wait_y(self):
            self.copy(3, sy, 0, sy).wait_recv()

        def wait_d(self):
            self.copy(4, sd, 0, sy).wait_recv()
            self.copy(5, sd, 1, sx).wait_recv()

        def step(self, k):
            @pl.when(k == 1)
            def _():
                self.relay()
                self.wait_x()

            @pl.when(k == 2)
            def _():
                self.wait_y()

            @pl.when(k == 3)
            def _():
                self.wait_d()

        def drain(self):
            for i, (b, h, to) in enumerate(
                ((s, 0, sx), (s, 1, sy), (s, 1, sx), (s, 0, sy), (sx, 0, sy), (sy, 1, sx))
            ):
                self.copy(i, b, h, to).wait_send()

    def half_rows(h):
        return pl.ds(pl.multiple_of(h * half, half), half)

    class Scatter:
        plan = ((3, 0, 1), (1, 0, 1), (3, 1, 2), (2, 1, 2), (2, 0, 2), (1, 1, 1))

        def __init__(self, land, index):
            self.land, self.index = land, index

        def copy(self, i):
            rel, h, way = self.plan[i]
            return remote(
                part.at[rel, pl.ds(h * half, half)], self.land.at[i],
                rs_send.at[self.index, i], rs_recv.at[self.index, i],
                sx if way == 1 else sy, f,
            )

        def step(self, rel):
            @pl.when(rel == 3)
            def _():
                self.copy(0).start()
                self.copy(2).start()

            @pl.when(rel == 1)
            def _():
                self.copy(1).start()

            @pl.when(rel == 2)
            def _():
                self.copy(3).start()

        def relay(self):
            for arrived, i in ((0, 4), (2, 5)):
                self.copy(arrived).wait_recv()
                rel, h, _ = self.plan[i]

                here = pl.ds(h * half, half)
                total = part[rel, here].astype(F32) + self.land[arrived].astype(F32)
                part[rel, here] = total.astype(BF16)
                self.copy(i).start()
            hand_over((0, 0) if self.index == 3 else (0, 1))

        def wait(self):
            for i in (1, 3, 4, 5):
                self.copy(i).wait_recv()

        def total(self, h):
            return (
                part[0, half_rows(h)].astype(F32)
                + self.land[1 + 2 * h].astype(F32)
                + self.land[4 + h].astype(F32)
            )

        def drain(self):
            for i in range(6):
                self.copy(i).wait_send()

    def by_rows(ref, size):
        def view(who):
            return ref.at[pl.ds(pl.multiple_of(who * size, size), size)]

        return view

    def by_cut(ref, size):
        def view(who):
            return ref.at[:, pl.ds(pl.multiple_of(who * size, size), size)]

        return view

    partner = 2 * z + 1 - c
    side = z // 2
    near = 4 * side + 1 - z
    mid_o, end_o = 2 - side, 3 - 3 * side
    is_mid = (z + side) % 2
    seen_as = 2 - is_mid
    owners = (near, mid_o, end_o)

    class Weight:
        def __init__(self, index, view):
            self.index, self.view = index, view

        def piece(self, to_z, i, k, owner_z, own=None):
            dst = self.view(2 * owner_z + c)
            return remote(
                dst if own is None else own, dst,
                w_send.at[self.index, i], w_recv.at[self.index, k], s, 2 * to_z + c,
            )

        def across(self, k, owner, own=None):
            dst = self.view(owner)
            return remote(
                dst if own is None else own, dst,
                p_send.at[self.index, k], p_recv.at[self.index, k], s, partner,
            )

        def start_far(self, own=None, across=True):
            self.piece(mid_o, 1, seen_as, z, own).start()
            if across:
                @pl.when(is_mid == 0)
                def _():
                    self.piece(near, 0, 0, z, own).start()

                self.across(3, f, own).start()

        def start_near(self, own=None, everyone=False):
            @pl.when((is_mid == 1) | everyone)
            def _():
                self.piece(near, 0, 0, z, own).start()

        def start(self, own=None):
            self.start_far(own)
            self.start_near(own)

        def relay(self, all_of_it=True):
            @pl.when(is_mid == 1)
            def _():
                for k in (1, 2):
                    self.piece(z, 0, k, owners[k]).wait_recv()
                    self.piece(near, 1 + k, k, owners[k]).start()
                for k in (1, 2):
                    self.across(k, 2 * owners[k] + c).start()

            if all_of_it:
                self.relay_rest()

        def relay_rest(self):
            @pl.when(is_mid == 1)
            def _():
                self.piece(z, 0, 0, near).wait_recv()
                self.across(0, 2 * near + c).start()

        def rest(self):
            @pl.when(is_mid == 0)
            def _():
                for k in (0, 1, 2):
                    self.piece(z, 0, k, owners[k]).wait_recv()
                    self.across(k, 2 * owners[k] + c).start()

        def finish(self):
            self.across(3, partner).wait_recv()
            for k in (0, 1, 2):
                self.across(k, 2 * owners[k] + 1 - c).wait_recv()

        def drain(self):
            self.piece(mid_o, 1, seen_as, z).wait_send()
            self.piece(near, 0, 0, z).wait_send()
            self.across(3, f).wait_send()

            @pl.when(is_mid == 1)
            def _():
                for k in (1, 2):
                    self.piece(near, 1 + k, k, owners[k]).wait_send()

            for k in (0, 1, 2):
                self.across(k, 2 * owners[k] + c).wait_send()

    class Shed:
        def __init__(self, index, gw, land_p, land_z):
            self.index, self.gw, self.land_p, self.land_z = index, gw, land_p, land_z

        def pair(self, to_z):
            return remote(
                self.gw.at[2 * to_z + 1 - c], self.land_p.at[to_z],
                gp_send.at[self.index, to_z], gp_recv.at[self.index, to_z], s, partner,
            )

        def along(self, i, to_z, of_z, slot):
            return remote(
                self.gw.at[2 * of_z + c], self.land_z.at[slot],
                gz_send.at[self.index, i], gz_recv.at[self.index, slot], s, 2 * to_z + c,
            )

        def add(self, who, land, slot):
            self.gw[who] = (self.gw[who].astype(F32) + land[slot].astype(F32)).astype(BF16)

        def add_pair(self, to_z):
            self.pair(to_z).wait_recv()
            self.add(2 * to_z + c, self.land_p, to_z)

        def far(self):
            for slot, of_z in ((1, mid_o), (2, end_o)):
                self.add_pair(of_z)

                @pl.when(is_mid == 0)
                def _(slot=slot, of_z=of_z):
                    self.along(slot, near, of_z, slot).start()

        def close(self):
            self.add_pair(near)
            self.along(0, near, near, 0).start()
            self.add_pair(z)

        def second(self):
            @pl.when(is_mid == 1)
            def _():
                for i, of_z in ((1, mid_o), (2, end_o)):
                    self.along(i, near, of_z, i).wait_recv()
                    self.add(2 * of_z + c, self.land_z, i)
                    self.along(i, of_z, of_z, 3).start()

        def wait(self):
            self.along(0, near, z, 0).wait_recv()
            self.along(1, near, z, 3).wait_recv()

        def total(self, at):
            value = self.gw[f, at].astype(F32)
            return value + self.land_z[0, at].astype(F32) + self.land_z[3, at].astype(F32)

        def drain(self):
            def one(to_z, _):
                self.pair(to_z).wait_send()
                return 0

            lax.fori_loop(0, n_f // 2, one, 0)
            for i in range(3):
                self.along(i, near, near, 0).wait_send()

    if inside:
        fetch = [
            pltpu.make_async_copy(ref, small_raw.at[i], raw_sem.at[i])
            for i, ref in enumerate(small_given[:8])
        ]
        fetch.append(pltpu.make_async_copy(small_given[8], bias_raw, raw_sem.at[8]))
        for one in fetch:
            one.start()

    barrier = pltpu.get_barrier_semaphore()
    for who in (sx, sy, sd):
        pl.semaphore_signal(barrier, inc=1, device_id=(who, f), device_id_type=pl.DeviceIdType.MESH)
    n_peers = 3
    if inside:
        for d in range(1, n_f):
            pl.semaphore_signal(
                barrier, inc=1, device_id=(s, (f + d) % n_f), device_id_type=pl.DeviceIdType.MESH
            )
        n_peers += n_f - 1
    if inside:
        for one in fetch:
            one.wait()
        for i in range(8):
            small_rows[i : i + 1, :] = small_raw[i].astype(F32)
        tall = small_rows.shape[1]
        lanes = lax.broadcasted_iota(jnp.int32, (tall, 128), 1)
        places = lax.broadcasted_iota(jnp.int32, (tall, 128), 0) + (f % (128 // tall)) * tall
        chosen = jnp.where(lanes == places, 1.0, 0.0).astype(BF16)
        small_in = small_tile
        small_in[0:8] = dot(small_rows[...].astype(BF16), chosen)
        small_in[8:9] = bias_raw[...].astype(F32)
    else:
        small_in = small_given[0]
    pl.semaphore_wait(barrier, n_peers)

    others = (sx, sy, sd)
    ag_tok = Gather(tok, 0)
    if inside:
        high = qkv_in.shape[0]
        high_d = down_in.shape[0]
        w_qkv = [
            Weight(0, by_cut(qkv_w.at[0:2], high)), Weight(4, by_cut(qkv_w.at[2:4], high))
        ]
        w_out = Weight(1, by_rows(out_w.at[0], high))
        w_up = Weight(2, by_cut(up_w, high))
        w_down = Weight(3, by_rows(down_w, high_d))

        def qkv_copy(k, p, to):
            start = pl.multiple_of((p % 3) * width + to * group + (p // 3) * 128, 128)
            src = qkv_in.at[:, pl.ds(start, 128)]
            dst = qkv_w.at[s, pl.ds(pl.multiple_of(f * high, high), high), pl.ds(p * 128, 128)]
            if k < 0:
                return pltpu.make_async_copy(src, dst, col_local.at[p])
            return remote(src, dst, col_send.at[k, p], col_recv.at[k, p], to, f)

        n_cut = 3 * pairs

        ff = up_w.shape[2]

        def up_copy(k, to):
            src = up_in.at[:, pl.ds(pl.multiple_of(to * ff, 128), ff)]
            dst = up_w.at[s, pl.ds(pl.multiple_of(f * high, high), high)]
            if k < 0:
                return pltpu.make_async_copy(src, dst, loc_sem.at[6])
            return remote(src, dst, upc_send.at[k], upc_recv.at[k], to, f)

        out_own = pltpu.make_async_copy(out_in, w_out.view(f), loc_sem.at[0])
        down_own = pltpu.make_async_copy(down_in, w_down.view(f), loc_sem.at[1])

        def small_copy(d):
            return remote(
                small_in, small_f.at[f], sf_send.at[d], sf_recv.at[d], s, (f + d) % n_f
            )

        for d in range(1, n_f):
            small_copy(d).start()
        for p in range(n_cut):
            for k, to in enumerate(others):
                qkv_copy(k, p, to).start()
        ag_tok.start(tokens)
        for p in range(n_cut):
            qkv_copy(-1, p, s).start()
        up_copy(-1, s).start()
        out_own.start()
        down_own.start()
        small_f[f] = small_in[...]
    else:
        loads = [
            pltpu.make_async_copy(qkv_in, qkv_w, col_local.at[0]),
            pltpu.make_async_copy(up_in, up_w, loc_sem.at[6]),
            pltpu.make_async_copy(out_in, out_w, loc_sem.at[0]),
            pltpu.make_async_copy(down_in, down_w, loc_sem.at[1]),
        ]
        for load in loads:
            load.start()
    tok_own = pltpu.make_async_copy(tokens, tok.at[s], loc_sem.at[2])
    tok_own.start()
    cot_own = pltpu.make_async_copy(cot_in, cot, loc_sem.at[3])
    cot_own.start()
    seg_own = pltpu.make_async_copy(seg_in, segs.at[s], loc_sem.at[4])
    seg_own.start()

    def seg_copy(k, to):
        return remote(seg_in, segs.at[s], seg_send.at[k], seg_recv.at[k], to, f)

    for k, to in enumerate(others):
        seg_copy(k, to).start()

    if inside:
        for d in range(1, n_f):
            remote(
                small_in, small_f.at[(f + n_f - d) % n_f], sf_send.at[d], sf_recv.at[d],
                s, (f + d) % n_f,
            ).wait_recv()
        per = n_f * high // 128
        each = n_f // per
        for t in range(per):
            value = small_f[t * each, 0:8]
            for e in range(1, each):
                value = value + small_f[t * each + e, 0:8]
            small_s[s, t] = value
        for e in range(n_f):
            bias_row[0:1, pl.ds(e * 128, 128)] = small_f[e, 8:9]

        def small_wide(k, to):
            return remote(small_s.at[s], small_s.at[s], ss_send.at[k], ss_recv.at[k], to, f)

        for k, to in enumerate(others):
            small_wide(k, to).start()
        for p in range(n_cut):
            qkv_copy(-1, p, s).wait()
            for k, to in enumerate(others):
                qkv_copy(k, p, to).wait_recv()
        for weight in w_qkv:
            weight.start_far(across=False)
        for weight in w_qkv:
            weight.start_near(everyone=True)
            weight.across(3, f).start()
        w_out.start(out_in)
        w_down.start_far(down_in)
    else:
        ag_tok.start(tokens)
        params[...] = small_in[0:8]
        bias_row[...] = small_in[8:9, 0 : bias_row.shape[1]]

    zero_row = jnp.zeros((1, width), F32)

    def both(run, count):
        def step(h, carry):
            return tuple(a + b for a, b in zip(carry, run(h)))

        return lax.fori_loop(0, 2, step, (zero_row,) * count)

    def far_first(i):
        return (1 - i // 2) + 2 * (1 - i % 2)

    def param(i):
        return params[i : i + 1, :]

    tok_own.wait()
    if inside:
        w_qkv[0].relay()
    ag_tok.relay()
    if inside:
        for k, to in enumerate(others):
            up_copy(k, to).start()
        w_qkv[1].relay()
        w_out.relay(False)
        w_down.start_near(down_in)
        for k, who in enumerate(others):
            remote(
                small_s.at[who], small_s.at[who], ss_send.at[k], ss_recv.at[k], who, f
            ).wait_recv()
        for b in range(4):
            for t in range(per):
                params[:, pl.ds((b * per + t) * 128, 128)] = small_s[b, t]

    def first_norm(b):
        unit, _s = unit_of(tok[b].astype(F32))
        normed[b] = (unit * param(0) + param(1)).astype(BF16)

    def norm_step(k, _):
        @pl.when(k == 1)
        def _():
            ag_tok.wait_x()

        @pl.when(k == 2)
        def _():
            ag_tok.wait_y()

        @pl.when(k == 3)
        def _():
            ag_tok.wait_d()

        first_norm(block(k))
        return 0

    lax.fori_loop(0, 3, norm_step, 0)
    if inside:
        for weight in w_qkv:
            weight.rest()
    lax.fori_loop(3, 4, norm_step, 0)
    if inside:
        for weight in w_qkv:
            weight.finish()

    rest = normed[...].reshape(4 * rows, width)
    for p in range(pairs):
        value = dot(rest, qkv_w[:, :, p * 384 : (p + 1) * 384].reshape(width, 384))
        for q in range(3):
            piece = value[:, q * 128 : (q + 1) * 128]
            piece = piece if q else piece * 0.125
            at = slice((3 * p + q) * 128, (3 * p + q + 1) * 128)
            triple[:, :, at] = piece.astype(BF16).reshape(4, rows, 128)

    if inside:
        up_copy(-1, s).wait()
        for k, to in enumerate(others):
            up_copy(k, to).wait_recv()
        w_up.start_far()
        w_up.start_near()

    seg_own.wait()
    for k, who in enumerate(others):
        remote(seg_in, segs.at[who], seg_send.at[k], seg_recv.at[k], who, f).wait_recv()
    seg_all = segs[...]

    def below(level):
        count = jnp.sum((seg_all < level).astype(F32), axis=0)
        return jnp.sum(count, axis=1, keepdims=True)

    bound_1, bound_2 = below(1), below(2)
    blocks = window // rows
    lane = lax.broadcasted_iota(jnp.int32, (1, 128), 1)
    left = (lane < HEAD_DIM).astype(F32)
    sides = (left.astype(BF16), (1.0 - left).astype(BF16))
    pick = lax.broadcasted_iota(jnp.int32, (rows, 128), 1) < HEAD_DIM

    def set_starts(r, _):
        i = (r * rows + lax.broadcasted_iota(jnp.int32, (rows, 128), 0)).astype(F32)
        starts[r] = jnp.where(i >= bound_2, bound_2, jnp.where(i >= bound_1, bound_1, 0.0))
        return 0

    lax.fori_loop(0, 4, set_starts, 0)

    def cut(r, part_at, p, count):
        at = pl.ds(pl.multiple_of((3 * p + part_at) * 128, 128), 128)
        return triple[pl.ds(r, count), :, at].reshape(count * rows, 128)

    def masked(scores, r, first, count):
        start = starts[r]
        tiles = []
        for t in range(count * rows // 128):
            j = lax.broadcasted_iota(jnp.int32, (rows, 128), 1) + t * 128
            keep = (first * rows + j).astype(F32) >= start
            if t * 128 >= (count - 1) * rows:
                i = lax.broadcasted_iota(jnp.int32, (rows, 128), 0)
                keep = keep & (j - (count - 1) * rows <= i)
            tiles.append(jnp.where(keep, scores[:, t * 128 : (t + 1) * 128], NEG))
        return jnp.concatenate(tiles, axis=1)

    rs_1 = Scatter(land_a, 0)

    def attend_heads(r, first, count):
        scores, values = [], []
        for p in range(pairs):
            query, keys = cut(r, 0, p, 1), cut(first, 1, p, count)
            for e in range(2):
                scores.append(masked(dot(query * sides[e], keys, NT), r, first, count))
                values.append(cut(first, 2, p, count))
        tops = [jnp.max(score, -1, keepdims=True) for score in scores]
        expos = [jnp.exp(score - top) for score, top in zip(scores, tops)]
        sums = [jnp.sum(expo, -1, keepdims=True) for expo in expos]
        lows = [(expo * (1.0 / total)).astype(BF16) for expo, total in zip(expos, sums)]
        for n, low in enumerate(lows):
            probs[r, n, :, 0 : count * rows] = low
        outs = [dot(low, value) for low, value in zip(lows, values)]
        for p in range(pairs):
            both_sides = jnp.where(pick, outs[2 * p], outs[2 * p + 1])
            attended[r, :, p * 128 : (p + 1) * 128] = both_sides.astype(BF16)

    def attend(i, _):
        rel = far_first(i)
        r = block(rel)
        for count in range(1, blocks + 1):
            @pl.when(r + 1 >= count if count == blocks else r + 1 == count)
            def _(count=count):
                attend_heads(r, r + 1 - count, count)

        if inside:
            @pl.when(i == 0)
            def _():
                out_own.wait()
                w_out.finish()

        part[rel] = dot(attended[r], out_w[0]).astype(BF16)

        @pl.when(c == 0)
        def _():
            rs_1.step(rel)

        @pl.when((c == 1) & (i == 2))
        def _():
            rs_1.step(3)

        if inside:
            @pl.when(i == 1)
            def _():
                w_down.relay()

        return 0

    if inside:
        w_out.relay_rest()
        w_out.rest()
    lax.fori_loop(0, 4, attend, 0)

    my_turn((1, 1))

    @pl.when(c == 1)
    def _():
        for i in (1, 3):
            rs_1.copy(i).start()

    rs_1.relay()
    if inside:
        w_up.relay()

        @pl.when(c == 1)
        def _():
            w_down.rest()

    rs_1.wait()

    def mid_norm(h):
        at = half_rows(h)
        value = rs_1.total(h)
        branch[at] = value
        unit, _s = unit_of(value)
        mid = tok[s, at].astype(F32) + (unit * param(2) + param(3))
        middle[at] = mid
        unit, _s = unit_of(mid)
        inner[s, at] = (unit * param(4) + param(5)).astype(BF16)

    for h in range(2):
        mid_norm(h)
    ag_inner = Gather(inner, 1)
    my_turn()
    ag_inner.start()
    rs_1.drain()
    if inside:
        @pl.when(c == 1)
        def _():
            w_up.rest()

    ag_inner.relay()
    if inside:
        @pl.when(c == 0)
        def _():
            w_down.rest()
            w_up.rest()

        w_up.finish()

    ff = up_w.shape[2]
    tile = ff
    rs_2 = Scatter(land_b, 1)

    def forward_step(k, _):
        @pl.when(k == 1)
        def _():
            ag_inner.wait_x()

        @pl.when(k > 1)
        def _():
            ag_inner.step(k)

        r = block(k)

        def column(n, _):
            at = pl.ds(pl.multiple_of(n * tile, tile), tile)
            pre = dot(inner[r], up_w[:, :, at].reshape(width, tile)) + bias_row[:, at]
            square = pre * pre
            bend = jnp.tanh(0.7978845608028654 * pre * (1.0 + 0.044715 * square))
            near = 0.5 + 0.5 * bend
            activ[r, :, at] = (pre * near).astype(BF16)
            slope = near + pre * (0.5 - 0.5 * bend * bend) * (
                0.7978845608028654 + 0.10703222440890037 * square
            )
            dgelu[r, :, at] = slope.astype(BF16)
            return 0

        lax.fori_loop(0, ff // tile, column, 0)
        return 0

    lax.fori_loop(0, 4, forward_step, 0)
    if inside:
        down_own.wait()
        w_down.finish()

    def down_step(i, _):
        rel = far_first(i)
        r = block(rel)

        part[rel] = dot(activ[r], down_w[...]).astype(BF16)
        rs_2.step(rel)
        return 0

    my_turn()
    lax.fori_loop(0, 4, down_step, 0)
    rs_2.relay()
    cot_own.wait()
    rs_2.wait()

    def last_norm(h):
        at = half_rows(h)
        unit, scale = unit_of(rs_2.total(h))
        gbr[s, at] = (middle[at] + (unit * param(6) + param(7))).astype(BF16)
        grad = cot[at].astype(F32)
        gmix[s, at] = pull_of(grad, param(6), unit, scale).astype(BF16)
        return col_sum(grad * unit), col_sum(grad)

    grad_gain_d, grad_shift_d = both(last_norm, 2)
    sg_rows = [None] * 8
    sg_rows[6], sg_rows[7] = grad_gain_d, grad_shift_d
    ag_mix = Gather(gmix, 2)
    my_turn()
    ag_mix.start()
    result_out = pltpu.make_async_copy(gbr.at[s], result, o_sem.at[2])
    result_out.start()
    rs_2.drain()

    rs_3 = Scatter(land_a, 2)
    sg_bias = bias_row

    def clear(n, _):
        at = pl.ds(pl.multiple_of(n * tile, tile), tile)
        sg_bias[:, at] = jnp.zeros((1, tile), F32)
        return 0

    lax.fori_loop(0, ff // tile, clear, 0)

    TN = ((0,), (0,))

    def flat(ref, lanes=slice(None)):
        held = ref[:, :, lanes]
        return held.reshape(4 * rows, held.shape[2])

    def all_pairs(shed):
        for to_z in range(n_f // 2):
            shed.pair(to_z).start()

    def cut_grads(left, right, gw, shed, lanes=slice(None)):
        for b in range(4):
            value = dot(flat(left, slice(b * rows, (b + 1) * rows)), flat(right, lanes), TN)
            gw[:, b * high : (b + 1) * high, :] = value.astype(BF16).reshape(n_f, high, -1)
        all_pairs(shed)

    def down_grads(rels):
        each = ff // n_f
        count = 256 // each
        for b in range(n_f // count):
            at = slice(b * count, (b + 1) * count)
            cols = slice(b * 256, (b + 1) * 256)
            value = dot(activ[block(rels[0]), :, cols], gmix[block(rels[0])], TN)
            for rel in rels[1:]:
                value = value + dot(activ[block(rel), :, cols], gmix[block(rel)], TN)
            if len(rels) == 1:
                value = value + gw_down[at].astype(F32).reshape(256, width)
            gw_down[at] = value.astype(BF16).reshape(count, each, width)

    if inside:
        shed_down = Shed(0, gw_down, lp_down, lz_down)
        shed_up = Shed(1, gw_up, lp_up, lz_up)
        shed_out = Shed(2, gw_out, lp_out, lz_out)
        shed_qkv = [
            Shed(3 + p, gw_qkv[p], lp_qkv[p], lz_qkv[p])
            for p in range(pairs)
        ]
        ag_tok.drain()

    def back_step(k, _):
        if inside:
            @pl.when(k == 3)
            def _():
                down_grads((0, 1, 2))

        ag_mix.step(k)
        r = block(k)

        def column(n, _):
            at = pl.ds(pl.multiple_of(n * tile, tile), tile)
            grad = dot(gmix[r], down_w[at], NT)
            low = (dgelu[r, :, at].astype(F32) * grad).astype(BF16)
            dgelu[r, :, at] = low
            sg_bias[:, at] = sg_bias[:, at] + col_sum(low.astype(F32))
            return 0

        lax.fori_loop(0, ff // tile, column, 0)
        return 0

    lax.fori_loop(0, 4, back_step, 0)

    if inside:
        down_grads((3,))
        all_pairs(shed_down)

        @pl.when(c == 1)
        def _():
            shed_down.far()

    def inner_step(i, _):
        rel = far_first(i)
        r = block(rel)

        part[rel] = dot(dgelu[r], up_w[...].reshape(width, ff), NT).astype(BF16)
        rs_3.step(rel)
        return 0

    my_turn()
    lax.fori_loop(0, 4, inner_step, 0)

    if inside:
        cut_grads(inner, dgelu, gw_up, shed_up)
    rs_3.relay()
    if inside:
        @pl.when(c == 1)
        def _():
            shed_up.far()
            shed_down.close()
            shed_up.close()

        @pl.when(c == 0)
        def _():
            shed_down.far()

    rs_3.wait()

    result_out.wait()

    def mid_back(h):
        at = half_rows(h)
        grad = rs_3.total(h)
        unit, scale = unit_of(middle[at])
        total = cot[at].astype(F32) + pull_of(grad, param(4), unit, scale)
        gmid[at] = total
        out = [col_sum(grad * unit), col_sum(grad)]
        unit, scale = unit_of(branch[at])
        gbr[s, at] = pull_of(total, param(2), unit, scale).astype(BF16)
        return out[0], out[1], col_sum(total * unit), col_sum(total)

    sg_rows[4], sg_rows[5], sg_rows[2], sg_rows[3] = both(mid_back, 4)
    ag_br = Gather(gbr, 3)
    my_turn()
    ag_br.start()
    rs_3.drain()
    def arrive(k, _):
        if inside:
            @pl.when(k == 1)
            def _():
                ag_br.relay()

            @pl.when((k == 1) & (c == 0))
            def _():
                shed_up.far()
                shed_down.close()
                shed_up.close()

            @pl.when(k == 1)
            def _():
                ag_br.wait_x()

            @pl.when(k > 1)
            def _():
                ag_br.step(k)

            @pl.when(k == 2)
            def _():
                shed_down.second()
        else:
            ag_br.step(k)

        r = block(k)
        gatt[r] = dot(gbr[r], out_w[0], NT).astype(BF16)
        if inside:
            value = dot(attended[r], gbr[r], TN)

            @pl.when(k == 0)
            def _():
                branch[...] = value

            @pl.when(k > 0)
            def _():
                branch[...] = branch[...] + value

        return 0

    lax.fori_loop(0, 4, arrive, 0)
    if inside:
        gw_out[...] = branch[...].astype(BF16).reshape(gw_out.shape)
        all_pairs(shed_out)

        @pl.when(c == 1)
        def _():
            shed_out.far()
            shed_out.close()

    if inside:
        per = n_f * high // 128
        fin_down = branch.at[0:high_d]
        fin_out = branch.at[high_d : high_d + high]
        gdown_out = pltpu.make_async_copy(fin_down, gdown, o_sem.at[3])
        gout_out = pltpu.make_async_copy(fin_out, gout, o_sem.at[4])

        def rows_at(n):
            return pl.ds(pl.multiple_of(n * high, high), high)

        gup_out = [
            pltpu.make_async_copy(
                middle.at[rows_at(b)], gup.at[:, b * ff : (b + 1) * ff], o_sem.at[8 + b]
            )
            for b in range(4)
        ]
        gqkv_out = [
            pltpu.make_async_copy(
                middle.at[rows_at(4 + p)], gqkv.at[:, p * width : (p + 1) * width],
                o_sem.at[12 + p],
            )
            for p in range(3)
        ]
        gsmall_out = pltpu.make_async_copy(small_sum, gsmall, o_sem.at[7])

        def ts_copy(k, to):
            return remote(sg_s.at[to], sg_land_s.at[k], ts_send.at[k], ts_recv.at[k], to, f)

        def tf_copy(d):
            to = (f + d) % n_f
            return remote(
                sg_f.at[to], sg_land_f.at[d - 1], tf_send.at[d], tf_recv.at[d], s, to
            )

        def small_first():
            for b in range(4):
                for t in range(per):
                    at = slice((b * per + t) * 128, (b * per + t + 1) * 128)
                    for i in range(8):
                        sg_s[b, t, i : i + 1, :] = sg_rows[i][:, at]
            for k, to in enumerate(others):
                ts_copy(k, to).start()

        def small_second():
            for k, to in enumerate(others):
                ts_copy(k, to).wait_recv()
            for who in range(n_f):
                t = who * high // 128
                sg_f[who, 0:8] = (
                    sg_s[s, t] + sg_land_s[0, t] + sg_land_s[1, t] + sg_land_s[2, t]
                )
                sg_f[who, 8:9] = sg_bias[:, who * 128 : (who + 1) * 128]
            for d in range(1, n_f):
                tf_copy(d).start()

        def small_third():
            for d in range(1, n_f):
                tf_copy(d).wait_recv()
            value = sg_f[f]
            for d in range(1, n_f):
                value = value + sg_land_f[d - 1]
            small_sum[...] = value
            gsmall_out.start()

        def gu_copy(k, to, who):
            return remote(
                cot.at[rows_at(to)], cot.at[rows_at(4 + who)],
                gu_send.at[k], gu_recv.at[k], to, f,
            )

        def put_qkv(q, who, value):
            lanes = pl.ds(pl.multiple_of(who * group + q * 128, 128), 128)
            for p in range(3):
                piece = value[:, p * 128 : (p + 1) * 128]
                middle[rows_at(4 + p), lanes] = piece.astype(F32)

        def gc_copy(k, p, to, who):
            return remote(
                fin_qkv.at[p, to], land_qkv.at[p, who],
                gc_send.at[k, p], gc_recv.at[k, p], to, f,
            )

    def back_rows(p, r_group):
        lanes = slice(p * 128, (p + 1) * 128)
        items = []
        for r in r_group:
            first = max(r + 1 - blocks, 0)
            count = r + 1 - first
            query, grad = cut(r, 0, p, 1), gatt[r, :, lanes]
            keys, vals = cut(first, 1, p, count), cut(first, 2, p, count)
            for e in range(2):
                low = probs[r, 2 * p + e, :, 0 : count * rows]
                items.append((r, e, first, count, query, keys, grad, low, vals))
        pulled = [dot(grad * sides[e], vals, NT) for _, e, _, _, _, _, grad, _, vals in items]
        sums = [
            jnp.sum(item[7].astype(F32) * pull, -1, keepdims=True)
            for item, pull in zip(items, pulled)
        ]
        slopes = [
            (item[7].astype(F32) * (pull - total)).astype(BF16)
            for item, pull, total in zip(items, pulled, sums)
        ]
        for n in range(0, len(items), 2):
            r, _, first, count, query, keys, grad, _, _ = items[n]
            query_t, grad_t = query.T, grad.T
            outs = [dot(slopes[n + e], keys) for e in range(2)]
            for e in range(2):
                side = slice(e * HEAD_DIM, (e + 1) * HEAD_DIM)
                here = slice(p * 128 + e * HEAD_DIM, p * 128 + (e + 1) * HEAD_DIM)
                key_part = dot(query_t[side], slopes[n + e])
                value_part = dot(grad_t[side], items[n + e][7])
                for m in range(count):
                    span = slice((first + m) * rows, (first + m + 1) * rows)
                    cols = slice(m * rows, (m + 1) * rows)
                    if r == 3 or (first + m) < 4 - blocks and r == first + m + blocks - 1:
                        dkt[here, span] = key_part[:, cols]
                        dvt[here, span] = value_part[:, cols]
                    else:
                        dkt[here, span] = dkt[here, span] + key_part[:, cols]
                        dvt[here, span] = dvt[here, span] + value_part[:, cols]
            at = slice(3 * p * 128, (3 * p + 1) * 128)
            gtri[r, :, at] = (jnp.where(pick, outs[0], outs[1]) * 0.125).astype(BF16)

    def back_pair(p):
        lanes = slice(p * 128, (p + 1) * 128)
        for r_group in ((3, 2), (1, 0)):
            back_rows(p, r_group)
            if inside and p and r_group[0] == 3:
                @pl.when(c == 0)
                def _():
                    shed_out.far()
                    shed_out.close()

        for b in range(4):
            span = slice(b * rows, (b + 1) * rows)
            at = slice((3 * p + 1) * 128, (3 * p + 2) * 128)
            gtri[b, :, at] = dkt[lanes, span].astype(BF16).T
            at = slice((3 * p + 2) * 128, (3 * p + 3) * 128)
            gtri[b, :, at] = dvt[lanes, span].astype(BF16).T

    def qkv_grads(p):
        cut_grads(normed, gtri, gw_qkv[p], shed_qkv[p], slice(p * 384, (p + 1) * 384))

    for p in range(pairs):
        back_pair(p)
        if inside and p == 0:
            qkv_grads(p)
            shed_up.second()

            @pl.when(c == 1)
            def _():
                shed_qkv[0].far()

    if inside:
        @pl.when(c == 1)
        def _():
            qkv_grads(1)
            shed_qkv[1].far()
            for shed in shed_qkv:
                shed.close()

        @pl.when(c == 0)
        def _():
            shed_qkv[0].far()

    rs_4 = Scatter(land_b, 3)

    def normed_step(i, carry):
        rel = far_first(i)
        r = block(rel)
        grad = dot(gtri[r], qkv_w[...].reshape(width, 3 * group), NT)
        part[rel] = grad.astype(BF16)
        rs_4.step(rel)
        unit, _s = unit_of(tok[r].astype(F32))
        return carry[0] + col_sum(grad * unit), carry[1] + col_sum(grad)

    my_turn()
    sg_rows[0], sg_rows[1] = lax.fori_loop(0, 4, normed_step, (zero_row, zero_row))
    if inside:
        small_first()

        @pl.when(c == 0)
        def _():
            qkv_grads(1)

    rs_4.relay()
    if inside:
        @pl.when(c == 0)
        def _():
            shed_qkv[1].far()
            for shed in shed_qkv:
                shed.close()

        for shed in (shed_out, *shed_qkv):
            shed.second()
        small_second()
        at = pl.ds(pl.multiple_of(s * high, high), high)
        shed_up.wait()
        for b in range(4):
            cot[rows_at(b)] = shed_up.total(slice(b * high, (b + 1) * high)).astype(BF16)
        middle[rows_at(s)] = shed_up.total(at)

        def give_up():
            for k, to in enumerate(others):
                gu_copy(k, to, s).start()

        @pl.when(c == 1)
        def _():
            give_up()

        shed_down.wait()
        fin_down[...] = shed_down.total(slice(None))
        gdown_out.start()
    rs_4.wait()

    def first_back(h, _):
        at = half_rows(h)
        unit, scale = unit_of(tok[s, at].astype(F32))
        gmid[at] = gmid[at] + pull_of(rs_4.total(h), param(0), unit, scale)
        pltpu.make_async_copy(gmid.at[at], tgrad.at[at], o_sem.at[h]).start()
        return 0

    lax.fori_loop(0, 2, first_back, 0)
    if inside:
        for q, shed in enumerate(shed_qkv):
            shed.wait()
            for b in range(4):
                fin_qkv[q, b] = shed.total(slice(b * high, (b + 1) * high)).astype(BF16)
            for k, to in enumerate(others):
                gc_copy(k, q, to, s).start()
            own = shed.total(at)
            put_qkv(q, s, own)

        @pl.when(c == 0)
        def _():
            give_up()

        for k, who in enumerate(others):
            gu_copy(k, who, who).wait_recv()
            middle[rows_at(who)] = cot[rows_at(4 + who)].astype(F32)
        for one in gup_out:
            one.start()
        shed_out.wait()
        fin_out[...] = shed_out.total(slice(None))
        gout_out.start()
        small_third()
        for k, who in enumerate(others):
            for q in range(pairs):
                gc_copy(k, q, who, who).wait_recv()
                put_qkv(q, who, land_qkv[q, who])
        for one in gqkv_out:
            one.start()

    for h in range(2):
        pltpu.make_async_copy(gmid.at[half_rows(h)], tgrad.at[half_rows(h)], o_sem.at[h]).wait()
    if inside:
        gsmall_out.wait()
        gdown_out.wait()
        gout_out.wait()
        for one in (*gup_out, *gqkv_out):
            one.wait()
        for k, to in enumerate(others):
            gu_copy(k, to, s).wait_send()
            ts_copy(k, to).wait_send()
            for q in range(pairs):
                gc_copy(k, q, to, s).wait_send()
            for p in range(n_cut):
                qkv_copy(k, p, to).wait_send()
            up_copy(k, to).wait_send()
            small_wide(k, to).wait_send()
        for d in range(1, n_f):
            tf_copy(d).wait_send()
            small_copy(d).wait_send()
        for weight in (*w_qkv, w_out, w_up, w_down):
            weight.drain()
        for shed in (shed_down, shed_up, shed_out, *shed_qkv):
            shed.drain()
    else:
        for i in range(8):
            small_sum[i : i + 1, :] = sg_rows[i]
        small_sum[8:9, 0:ff] = sg_bias[...]
        gsmall_out = pltpu.make_async_copy(small_sum, gsmall, o_sem.at[7])
        gsmall_out.start()
        gsmall_out.wait()
    for k, to in enumerate(others):
        seg_copy(k, to).wait_send()
    for gather in (ag_inner, ag_mix, ag_br) + (() if inside else (ag_tok,)):
        gather.drain()
    rs_4.drain()


def finish_kernel(n_f, n_big, *refs):
    small, given = refs[0], refs[1 : 1 + n_big]
    made, minor = refs[1 + n_big : 1 + 2 * n_big], refs[1 + 2 * n_big : 10 + 2 * n_big]
    held, (in_sem, out_sem) = refs[10 + 2 * n_big : 10 + 3 * n_big], refs[10 + 3 * n_big :]
    cuts = []
    for i in range(n_big):
        tall = given[i].shape[0]
        for j in range(max(1, tall // 64)):
            at = pl.ds(j * min(tall, 64), min(tall, 64))
            cuts.append((i, at, len(cuts)))
    for i, at, n in cuts:
        pltpu.make_async_copy(given[i].at[at], held[i].at[at], in_sem.at[n]).start()
    each = minor[0].shape[1]
    place = lax.axis_index("fsdp") % (128 // each)
    for i in range(8):
        row = small[i : i + 1, :]
        value = row[:, 0:each]
        for q in range(1, 128 // each):
            value = jnp.where(place == q, row[:, q * each : (q + 1) * each], value)
        minor[i][...] = value
    minor[8][...] = small[8:9, :]
    for i, at, n in cuts:
        pltpu.make_async_copy(given[i].at[at], held[i].at[at], in_sem.at[n]).wait()
        pltpu.make_async_copy(held[i].at[at], made[i].at[at], out_sem.at[n]).start()
    for i, at, n in cuts:
        pltpu.make_async_copy(held[i].at[at], made[i].at[at], out_sem.at[n]).wait()


def finish(n_f, high, *made):
    big, small = made[:6], made[6]
    whole, anywhere = pl.BlockSpec(memory_space=pltpu.VMEM), pl.BlockSpec(memory_space=pl.ANY)
    count = sum(max(1, v.shape[0] // 64) for v in big)
    minor = [jax.ShapeDtypeStruct((1, high), F32)] * 8 + [jax.ShapeDtypeStruct((1, 128), F32)]
    out = pl.pallas_call(
        partial(finish_kernel, n_f, 6),
        out_shape=[jax.ShapeDtypeStruct(v.shape, v.dtype) for v in big] + minor,
        in_specs=[whole] + [anywhere] * 6,
        out_specs=[anywhere] * 6 + [whole] * 9,
        scratch_shapes=[pltpu.VMEM(v.shape, v.dtype) for v in big]
        + [pltpu.SemaphoreType.DMA((count,))] * 2,
    )(small, *big)
    result, tgrad, gqkv, gout, gup, gdown = out[:6]
    small = [v[0] for v in out[6:]]
    return (result[None], tgrad[None], gqkv, gout, gup, small[8], gdown, *small[:8])


def on_device(n_seq, n_f, *args):
    (tokens, segments, qkv_weight, out_weight, up_weight, up_bias, down_weight) = args[:7]
    vectors, cotangent = args[7:15], args[15]
    rows, width = tokens.shape[1:]
    high, high_d = qkv_weight.shape[0], down_weight.shape[0]
    length = n_seq * rows
    group = qkv_weight.shape[1] // 3 // n_seq
    heads = group // HEAD_DIM
    ff = up_weight.shape[1] // n_seq
    half = rows // 2
    window = rows * min(n_seq, 1 + -(-511 // rows))
    inside = n_f == 8 and high % 32 == 0 and ff == width and 8 * high <= rows
    f = lax.axis_index("fsdp")
    if inside:
        small = [v[None] for v in (*vectors, up_bias)]
        weights = (qkv_weight, out_weight, up_weight, down_weight)
    else:
        small = jnp.stack([v.astype(F32) for v in vectors])
        small = lax.all_gather(small, ("seq", "fsdp"), axis=1, tiled=True)
        bias = lax.all_gather(up_bias.astype(F32), "fsdp", axis=0, tiled=True)
        bias = jnp.pad(bias[None], ((0, 7), (0, width - ff)))
        small = [jnp.concatenate([small, bias])]

        def columns(weight, parts):
            cut = weight.reshape(high, parts, n_seq, -1, 128).transpose(2, 0, 3, 1, 4)
            cut = cut.reshape(n_seq, high, -1)
            cut = lax.all_to_all(cut, "seq", split_axis=0, concat_axis=0, tiled=True)
            return lax.all_gather(cut, "fsdp", axis=1, tiled=True)

        weights = (
            columns(qkv_weight, 3),
            lax.all_gather(out_weight, "fsdp", axis=0, tiled=True)[None],
            columns(up_weight, 1),
            lax.all_gather(down_weight, "fsdp", axis=0, tiled=True),
        )
    vmem, anywhere, dma = pltpu.VMEM, pl.BlockSpec(memory_space=pl.ANY), pltpu.SemaphoreType.DMA
    whole = pl.BlockSpec(memory_space=pltpu.VMEM)
    full = (4, rows, width)
    saved = {
        "normed": (full, BF16), "inner": (full, BF16), "gmix": (full, BF16), "gbr": (full, BF16),
        "attended": ((4, rows, group), BF16), "activ": ((4, rows, ff), BF16),
        "dgelu": ((4, rows, ff), BF16), "gtri": ((4, rows, 3 * group), BF16),
    }
    n_cut = 3 * (group // 128)
    pieces = {"q0": (n_seq * high, 384), "q1": (n_seq * high, 384), "out": (high, width),
              "up": (n_seq * high, ff), "down": (high_d, width)}
    scratch = {
        "tok": vmem(full, BF16), "normed": None, "inner": None, "gmix": None, "gbr": None,
        "qkv_w": vmem((n_seq, rows, 3 * group), BF16), "out_w": vmem((1, group, width), BF16),
        "up_w": vmem((n_seq, rows, ff), BF16), "down_w": vmem((ff, width), BF16),
        "segs": vmem((4, 1, rows), jnp.int32),
        "small_f": vmem((n_f if inside else 1, 16, 128), F32), "small_s": vmem((4, width // 512, 8, 128), F32),
        "params": vmem((8, width), F32), "bias_row": vmem((1, ff), F32),
        "triple": vmem((4, rows, 3 * group), BF16), "probs": vmem((4, heads, rows, window), BF16),
        "attended": None, "starts": vmem((4, rows, 128), F32), "activ": None, "dgelu": None,
        "part": vmem(full, BF16), "land_a": vmem((6, half, width), BF16),
        "land_b": vmem((6, half, width), BF16),
        "branch": vmem((rows, width), F32), "middle": vmem((rows, width), F32),
        "gmid": vmem((rows, width), F32), "cot": vmem((rows, width), BF16),
        "gtri": None, "gatt": vmem((4, rows, group), BF16), "dkt": vmem((group, length), F32),
        "dvt": vmem((group, length), F32),
    }
    for name, (tall, wide) in pieces.items():
        scratch["gw_" + name] = vmem((n_f if inside else 1, tall if inside else 16, wide), BF16)
    for name, (tall, wide) in pieces.items():
        scratch["lp_" + name] = vmem((n_f // 2 if inside else 1, tall if inside else 16, wide), BF16)
    for name, (tall, wide) in pieces.items():
        scratch["lz_" + name] = vmem((n_f // 2 if inside else 1, tall if inside else 16, wide), BF16)
    scratch["fin_qkv"] = vmem((group // 128, 4, high, 384), BF16)
    scratch["land_qkv"] = vmem((group // 128, 4, high, 384), BF16)
    scratch["small_sum"] = vmem((16, 128 if inside else width), F32)
    tiles = width // 512
    scratch["sg_s"] = vmem((4, tiles, 8, 128), F32)
    scratch["sg_land_s"] = vmem((3, tiles, 8, 128), F32)
    scratch["sg_f"] = vmem((n_f if inside else 1, 16, 128), F32)
    scratch["sg_land_f"] = vmem((n_f - 1 if inside else 1, 16, 128), F32)
    for name, shape in (
        ("ag_send", (4, 6)), ("ag_recv", (4, 6)), ("rs_send", (4, 6)), ("rs_recv", (4, 6)),
        ("w_send", (5, 4)), ("w_recv", (5, 3)), ("p_send", (5, 4)), ("p_recv", (5, 4)),
        ("col_send", (3, n_cut)), ("col_recv", (3, n_cut)), ("col_local", (n_cut,)),
        ("upc_send", (3,)), ("upc_recv", (3,)), ("seg_send", (3,)), ("seg_recv", (3,)),
        ("sf_send", (8,)), ("sf_recv", (8,)), ("ss_send", (3,)), ("ss_recv", (3,)),
        ("loc_sem", (7,)), ("o_sem", (16,)),
        ("gp_send", (5, 4)), ("gp_recv", (5, 4)), ("gz_send", (5, 4)), ("gz_recv", (5, 4)),
        ("gc_send", (3, 2)), ("gc_recv", (3, 2)), ("gu_send", (3,)), ("gu_recv", (3,)),
        ("ts_send", (3,)), ("ts_recv", (3,)), ("tf_send", (8,)), ("tf_recv", (8,)),
    ):
        scratch[name] = dma(shape)
    scratch["turn"] = pltpu.SemaphoreType.REGULAR
    scratch["small_raw"] = vmem((8, 1, high), BF16)
    scratch["bias_raw"] = vmem((1, up_bias.shape[0]), BF16)
    scratch["small_rows"] = vmem((8, high), F32)
    scratch["small_tile"] = vmem((16, 128), F32)
    scratch["raw_sem"] = dma((9,))
    outs = {
        "result": ((rows, width), BF16), "tgrad": ((rows, width), F32),
        "gqkv": ((high, n_seq * 3 * group), F32), "gout": ((high, width), F32),
        "gup": ((high, n_seq * ff), F32), "gdown": ((high_d, width), F32),
        "gsmall": ((16, 128 if inside else width), F32),
    }
    if inside:
        for name, shape in saved.items():
            scratch[name] = vmem(*shape)
        extra = []
    else:
        extra = list(saved)
    names = list(scratch)

    def kernel(*refs):
        n_in = 7 + len(small)
        given = (*refs[:2], refs[2 : 2 + len(small)], *refs[2 + len(small) : n_in])
        made = refs[n_in : n_in + len(outs)]
        more = dict(zip(extra, refs[n_in + len(outs) :]))
        rest = refs[n_in + len(outs) + len(extra) :]
        more.update(zip([n for n in names if scratch[n] is not None], rest))
        layer_kernel(inside, n_f, *given, *made, *[more[n] for n in names])

    shapes = [*outs.values(), *[saved[n] for n in extra]]
    made = pl.pallas_call(
        kernel,
        out_shape=[jax.ShapeDtypeStruct(*shape) for shape in shapes],
        in_specs=[anywhere] * 2 + [anywhere if inside else whole] * len(small) + [anywhere] * 5,
        out_specs=[anywhere] * len(outs) + [whole] * len(extra),
        scratch_shapes=[scratch[n] for n in names if scratch[n] is not None],
        compiler_params=pltpu.CompilerParams(
            collective_id=0, has_side_effects=True, vmem_limit_bytes=67043328
        ),
    )(tokens[0], segments, *small, cotangent[0], *weights)
    result, tgrad, gqkv, gout, gup, gdown, gsmall = made[:7]
    if inside:
        return finish(n_f, high, *made[:7])
    else:
        kept = {n: v.reshape(length, -1) for n, v in zip(extra, made[7:])}

        def turned_dot(left, right):
            return lax.dot_general(
                kept[left], kept[right], (((0,), (0,)), ((), ())), preferred_element_type=F32
            ).astype(BF16)

        def shed(value):
            return lax.psum_scatter(value, "fsdp", scatter_dimension=0, tiled=True)

        def columns_back(value, parts):
            cut = value.reshape(n_seq, n_f, high, -1).transpose(1, 0, 2, 3)
            cut = lax.all_to_all(shed(cut)[0], "seq", split_axis=0, concat_axis=0, tiled=True)
            cut = cut.reshape(n_seq, high, -1, parts, 128).transpose(1, 3, 0, 2, 4)
            return cut.reshape(high, -1).astype(F32)

        gqkv = columns_back(turned_dot("normed", "gtri"), 3)
        gout = shed(turned_dot("attended", "gbr")).astype(F32)
        gup = columns_back(turned_dot("inner", "dgelu"), 1)
        gdown = shed(turned_dot("activ", "gmix")).astype(F32)
        vectors = lax.psum_scatter(gsmall[:8], ("seq", "fsdp"), scatter_dimension=1, tiled=True)
        gbias = shed(gsmall[8, :ff])
    return (result[None], tgrad[None], gqkv, gout, gup, gbias, gdown, *vectors)


def solution(mesh):
    rows = P(("seq", "fsdp"), None)
    vector = P(("seq", "fsdp"))
    acts = P("fsdp", "seq", None)
    return jax.shard_map(
        partial(on_device, mesh.shape["seq"], mesh.shape["fsdp"]),
        mesh=mesh,
        in_specs=(acts, P("fsdp", "seq"), rows, rows, rows, vector, rows, *(vector,) * 8, acts),
        out_specs=(acts, acts, rows, rows, rows, vector, rows, *(vector,) * 8),
        check_vma=False,
    )
```

```python
from functools import partial

import jax
import jax.numpy as jnp
from jax import lax
from jax.experimental import pallas as pl
from jax.experimental.pallas import tpu as pltpu
from jax.sharding import PartitionSpec as P

HEAD_DIM = 64
F32 = jnp.float32
BF16 = jnp.bfloat16
NN = ((1,), (0,))
NT = ((1,), (1,))
NEG = -1e30


def dot(left, right, dims=NN):
    return lax.dot_general(left, right, (dims, ((), ())), preferred_element_type=F32)


def unit_of(value):
    center = value - jnp.mean(value, -1, keepdims=True)
    scale = lax.rsqrt(jnp.mean(center * center, -1, keepdims=True) + 1e-05)
    return center * scale, scale


def pull_of(grad, gain, unit, scale):
    pulled = grad * gain
    first = jnp.mean(pulled, -1, keepdims=True)
    second = jnp.mean(pulled * unit, -1, keepdims=True)
    return scale * (pulled - first - unit * second)


def col_sum(value):
    return jnp.sum(value, 0, keepdims=True)


def layer_kernel(
    inside,
    n_f,
    tokens, seg_in, small_given, cot_in, qkv_in, out_in, up_in, down_in,
    result, tgrad, gqkv, gout, gup, gdown, gsmall,
    tok, normed, inner, gmix, gbr,
    qkv_w, out_w, up_w, down_w,
    segs, small_f, small_s, params, bias_row,
    triple, probs, attended, starts, activ, dgelu,
    part, land_a, land_b,
    branch, middle, gmid, cot,
    gtri, gatt, dkt, dvt,
    gw_q0, gw_q1, gw_out, gw_up, gw_down,
    lp_q0, lp_q1, lp_out, lp_up, lp_down,
    lz_q0, lz_q1, lz_out, lz_up, lz_down,
    fin_qkv, land_qkv, small_sum,
    sg_s, sg_land_s, sg_f, sg_land_f,
    ag_send, ag_recv, rs_send, rs_recv,
    w_send, w_recv, p_send, p_recv,
    col_send, col_recv, col_local, upc_send, upc_recv,
    seg_send, seg_recv, sf_send, sf_recv, ss_send, ss_recv,
    loc_sem, o_sem,
    gp_send, gp_recv, gz_send, gz_recv,
    gc_send, gc_recv, gu_send, gu_recv,
    ts_send, ts_recv, tf_send, tf_recv, turn,
    small_raw, bias_raw, small_rows, small_tile, raw_sem,
):
    gw_qkv, lp_qkv, lz_qkv = (gw_q0, gw_q1), (lp_q0, lp_q1), (lz_q0, lz_q1)
    rows, width = tokens.shape
    half = rows // 2
    group = out_w.shape[1]
    pairs = group // 128
    window = probs.shape[3]
    s = lax.axis_index("seq")
    f = lax.axis_index("fsdp")
    x, y = s % 2, s // 2
    z, c = f // 2, f % 2

    def block(rel):
        return 2 * ((y + rel // 2) % 2) + (x + rel % 2) % 2

    sx, sy, sd = block(1), block(2), block(3)

    def remote(src, dst, send, recv, to_s, to_f):
        return pltpu.make_async_remote_copy(
            src_ref=src, dst_ref=dst, send_sem=send, recv_sem=recv,
            device_id=(to_s, to_f), device_id_type=pl.DeviceIdType.MESH,
        )

    def my_turn(cores=(0, 1)):
        if inside:
            @pl.when(c >= cores[0])
            def _():
                pl.semaphore_wait(turn, 1)

    def hand_over(cores=(0, 1)):
        if inside:
            @pl.when(c <= cores[1])
            def _():
                pl.semaphore_signal(
                    turn, inc=1, device_id=(s, 2 * z + 1 - c),
                    device_id_type=pl.DeviceIdType.MESH,
                )

    class Gather:
        def __init__(self, full, index):
            self.full, self.index = full, index

        def piece(self, b, h):
            return self.full.at[b, pl.ds(h * half, half)]

        def copy(self, i, b, h, to, src=None):
            dst = self.piece(b, h)
            return remote(
                dst if src is None else src, dst,
                ag_send.at[self.index, i], ag_recv.at[self.index, i], to, f,
            )

        def start(self, src=None):
            def cut(h):
                return None if src is None else src.at[pl.ds(h * half, half)]

            self.copy(0, s, 0, sx, cut(0)).start()
            self.copy(1, s, 1, sy, cut(1)).start()
            self.copy(2, s, 1, sx, cut(1)).start()
            self.copy(3, s, 0, sy, cut(0)).start()

        def relay(self):
            self.copy(0, sx, 0, sx).wait_recv()
            self.copy(4, sx, 0, sy).start()
            self.copy(1, sy, 1, sy).wait_recv()
            self.copy(5, sy, 1, sx).start()
            if self.index:
                hand_over()

        def wait_x(self):
            self.copy(2, sx, 1, sx).wait_recv()

        def wait_y(self):
            self.copy(3, sy, 0, sy).wait_recv()

        def wait_d(self):
            self.copy(4, sd, 0, sy).wait_recv()
            self.copy(5, sd, 1, sx).wait_recv()

        def step(self, k):
            @pl.when(k == 1)
            def _():
                self.relay()
                self.wait_x()

            @pl.when(k == 2)
            def _():
                self.wait_y()

            @pl.when(k == 3)
            def _():
                self.wait_d()

        def drain(self):
            for i, (b, h, to) in enumerate(
                ((s, 0, sx), (s, 1, sy), (s, 1, sx), (s, 0, sy), (sx, 0, sy), (sy, 1, sx))
            ):
                self.copy(i, b, h, to).wait_send()

    def half_rows(h):
        return pl.ds(pl.multiple_of(h * half, half), half)

    class Scatter:
        plan = ((3, 0, 1), (1, 0, 1), (3, 1, 2), (2, 1, 2), (2, 0, 2), (1, 1, 1))

        def __init__(self, land, index):
            self.land, self.index = land, index

        def copy(self, i):
            rel, h, way = self.plan[i]
            return remote(
                part.at[rel, pl.ds(h * half, half)], self.land.at[i],
                rs_send.at[self.index, i], rs_recv.at[self.index, i],
                sx if way == 1 else sy, f,
            )

        def step(self, rel):
            @pl.when(rel == 3)
            def _():
                self.copy(0).start()
                self.copy(2).start()

            @pl.when(rel == 1)
            def _():
                self.copy(1).start()

            @pl.when(rel == 2)
            def _():
                self.copy(3).start()

        def relay(self):
            for arrived, i in ((0, 4), (2, 5)):
                self.copy(arrived).wait_recv()
                rel, h, _ = self.plan[i]

                here = pl.ds(h * half, half)
                total = part[rel, here].astype(F32) + self.land[arrived].astype(F32)
                part[rel, here] = total.astype(BF16)
                self.copy(i).start()
            hand_over((0, 0) if self.index == 3 else (0, 1))

        def wait(self):
            for i in (1, 3, 4, 5):
                self.copy(i).wait_recv()

        def total(self, h):
            return (
                part[0, half_rows(h)].astype(F32)
                + self.land[1 + 2 * h].astype(F32)
                + self.land[4 + h].astype(F32)
            )

        def drain(self):
            for i in range(6):
                self.copy(i).wait_send()

    def by_rows(ref, size):
        def view(who):
            return ref.at[pl.ds(pl.multiple_of(who * size, size), size)]

        return view

    def by_cut(ref, size):
        def view(who):
            return ref.at[:, pl.ds(pl.multiple_of(who * size, size), size)]

        return view

    partner = 2 * z + 1 - c
    side = z // 2
    near = 4 * side + 1 - z
    mid_o, end_o = 2 - side, 3 - 3 * side
    is_mid = (z + side) % 2
    seen_as = 2 - is_mid
    owners = (near, mid_o, end_o)

    class Weight:
        def __init__(self, index, view):
            self.index, self.view = index, view

        def piece(self, to_z, i, k, owner_z, own=None):
            dst = self.view(2 * owner_z + c)
            return remote(
                dst if own is None else own, dst,
                w_send.at[self.index, i], w_recv.at[self.index, k], s, 2 * to_z + c,
            )

        def across(self, k, owner, own=None):
            dst = self.view(owner)
            return remote(
                dst if own is None else own, dst,
                p_send.at[self.index, k], p_recv.at[self.index, k], s, partner,
            )

        def start_far(self, own=None, across=True):
            self.piece(mid_o, 1, seen_as, z, own).start()
            if across:
                @pl.when(is_mid == 0)
                def _():
                    self.piece(near, 0, 0, z, own).start()

                self.across(3, f, own).start()

        def start_near(self, own=None, everyone=False):
            @pl.when((is_mid == 1) | everyone)
            def _():
                self.piece(near, 0, 0, z, own).start()

        def start(self, own=None):
            self.start_far(own)
            self.start_near(own)

        def relay(self, all_of_it=True):
            @pl.when(is_mid == 1)
            def _():
                for k in (1, 2):
                    self.piece(z, 0, k, owners[k]).wait_recv()
                    self.piece(near, 1 + k, k, owners[k]).start()
                for k in (1, 2):
                    self.across(k, 2 * owners[k] + c).start()

            if all_of_it:
                self.relay_rest()

        def relay_rest(self):
            @pl.when(is_mid == 1)
            def _():
                self.piece(z, 0, 0, near).wait_recv()
                self.across(0, 2 * near + c).start()

        def rest(self):
            @pl.when(is_mid == 0)
            def _():
                for k in (0, 1, 2):
                    self.piece(z, 0, k, owners[k]).wait_recv()
                    self.across(k, 2 * owners[k] + c).start()

        def finish(self):
            self.across(3, partner).wait_recv()
            for k in (0, 1, 2):
                self.across(k, 2 * owners[k] + 1 - c).wait_recv()

        def drain(self):
            self.piece(mid_o, 1, seen_as, z).wait_send()
            self.piece(near, 0, 0, z).wait_send()
            self.across(3, f).wait_send()

            @pl.when(is_mid == 1)
            def _():
                for k in (1, 2):
                    self.piece(near, 1 + k, k, owners[k]).wait_send()

            for k in (0, 1, 2):
                self.across(k, 2 * owners[k] + c).wait_send()

    class Shed:
        def __init__(self, index, gw, land_p, land_z):
            self.index, self.gw, self.land_p, self.land_z = index, gw, land_p, land_z

        def pair(self, to_z):
            return remote(
                self.gw.at[2 * to_z + 1 - c], self.land_p.at[to_z],
                gp_send.at[self.index, to_z], gp_recv.at[self.index, to_z], s, partner,
            )

        def along(self, i, to_z, of_z, slot):
            return remote(
                self.gw.at[2 * of_z + c], self.land_z.at[slot],
                gz_send.at[self.index, i], gz_recv.at[self.index, slot], s, 2 * to_z + c,
            )

        def add(self, who, land, slot):
            self.gw[who] = (self.gw[who].astype(F32) + land[slot].astype(F32)).astype(BF16)

        def add_pair(self, to_z):
            self.pair(to_z).wait_recv()
            self.add(2 * to_z + c, self.land_p, to_z)

        def far(self):
            for slot, of_z in ((1, mid_o), (2, end_o)):
                self.add_pair(of_z)

                @pl.when(is_mid == 0)
                def _(slot=slot, of_z=of_z):
                    self.along(slot, near, of_z, slot).start()

        def close(self):
            self.add_pair(near)
            self.along(0, near, near, 0).start()
            self.add_pair(z)

        def second(self):
            @pl.when(is_mid == 1)
            def _():
                for i, of_z in ((1, mid_o), (2, end_o)):
                    self.along(i, near, of_z, i).wait_recv()
                    self.add(2 * of_z + c, self.land_z, i)
                    self.along(i, of_z, of_z, 3).start()

        def wait(self):
            self.along(0, near, z, 0).wait_recv()
            self.along(1, near, z, 3).wait_recv()

        def total(self, at):
            value = self.gw[f, at].astype(F32)
            return value + self.land_z[0, at].astype(F32) + self.land_z[3, at].astype(F32)

        def drain(self):
            def one(to_z, _):
                self.pair(to_z).wait_send()
                return 0

            lax.fori_loop(0, n_f // 2, one, 0)
            for i in range(3):
                self.along(i, near, near, 0).wait_send()

    if inside:
        fetch = [
            pltpu.make_async_copy(ref, small_raw.at[i], raw_sem.at[i])
            for i, ref in enumerate(small_given[:8])
        ]
        fetch.append(pltpu.make_async_copy(small_given[8], bias_raw, raw_sem.at[8]))
        for one in fetch:
            one.start()

    barrier = pltpu.get_barrier_semaphore()
    for who in (sx, sy, sd):
        pl.semaphore_signal(barrier, inc=1, device_id=(who, f), device_id_type=pl.DeviceIdType.MESH)
    n_peers = 3
    if inside:
        for d in range(1, n_f):
            pl.semaphore_signal(
                barrier, inc=1, device_id=(s, (f + d) % n_f), device_id_type=pl.DeviceIdType.MESH
            )
        n_peers += n_f - 1
    if inside:
        for one in fetch:
            one.wait()
        for i in range(8):
            small_rows[i : i + 1, :] = small_raw[i].astype(F32)
        tall = small_rows.shape[1]
        lanes = lax.broadcasted_iota(jnp.int32, (tall, 128), 1)
        places = lax.broadcasted_iota(jnp.int32, (tall, 128), 0) + (f % (128 // tall)) * tall
        chosen = jnp.where(lanes == places, 1.0, 0.0).astype(BF16)
        small_in = small_tile
        small_in[0:8] = dot(small_rows[...].astype(BF16), chosen)
        small_in[8:9] = bias_raw[...].astype(F32)
    else:
        small_in = small_given[0]
    pl.semaphore_wait(barrier, n_peers)

    others = (sx, sy, sd)
    ag_tok = Gather(tok, 0)
    if inside:
        high = qkv_in.shape[0]
        high_d = down_in.shape[0]
        w_qkv = [
            Weight(0, by_cut(qkv_w.at[0:2], high)), Weight(4, by_cut(qkv_w.at[2:4], high))
        ]
        w_out = Weight(1, by_rows(out_w.at[0], high))
        w_up = Weight(2, by_cut(up_w, high))
        w_down = Weight(3, by_rows(down_w, high_d))

        def qkv_copy(k, p, to):
            start = pl.multiple_of((p % 3) * width + to * group + (p // 3) * 128, 128)
            src = qkv_in.at[:, pl.ds(start, 128)]
            dst = qkv_w.at[s, pl.ds(pl.multiple_of(f * high, high), high), pl.ds(p * 128, 128)]
            if k < 0:
                return pltpu.make_async_copy(src, dst, col_local.at[p])
            return remote(src, dst, col_send.at[k, p], col_recv.at[k, p], to, f)

        n_cut = 3 * pairs

        ff = up_w.shape[2]

        def up_copy(k, to):
            src = up_in.at[:, pl.ds(pl.multiple_of(to * ff, 128), ff)]
            dst = up_w.at[s, pl.ds(pl.multiple_of(f * high, high), high)]
            if k < 0:
                return pltpu.make_async_copy(src, dst, loc_sem.at[6])
            return remote(src, dst, upc_send.at[k], upc_recv.at[k], to, f)

        out_own = pltpu.make_async_copy(out_in, w_out.view(f), loc_sem.at[0])
        down_own = pltpu.make_async_copy(down_in, w_down.view(f), loc_sem.at[1])

        def small_copy(d):
            return remote(
                small_in, small_f.at[f], sf_send.at[d], sf_recv.at[d], s, (f + d) % n_f
            )

        for d in range(1, n_f):
            small_copy(d).start()
        for p in range(n_cut):
            for k, to in enumerate(others):
                qkv_copy(k, p, to).start()
        ag_tok.start(tokens)
        for p in range(n_cut):
            qkv_copy(-1, p, s).start()
        up_copy(-1, s).start()
        out_own.start()
        down_own.start()
        small_f[f] = small_in[...]
    else:
        loads = [
            pltpu.make_async_copy(qkv_in, qkv_w, col_local.at[0]),
            pltpu.make_async_copy(up_in, up_w, loc_sem.at[6]),
            pltpu.make_async_copy(out_in, out_w, loc_sem.at[0]),
            pltpu.make_async_copy(down_in, down_w, loc_sem.at[1]),
        ]
        for load in loads:
            load.start()
    tok_own = pltpu.make_async_copy(tokens, tok.at[s], loc_sem.at[2])
    tok_own.start()
    cot_own = pltpu.make_async_copy(cot_in, cot, loc_sem.at[3])
    cot_own.start()
    seg_own = pltpu.make_async_copy(seg_in, segs.at[s], loc_sem.at[4])
    seg_own.start()

    def seg_copy(k, to):
        return remote(seg_in, segs.at[s], seg_send.at[k], seg_recv.at[k], to, f)

    for k, to in enumerate(others):
        seg_copy(k, to).start()

    if inside:
        for d in range(1, n_f):
            remote(
                small_in, small_f.at[(f + n_f - d) % n_f], sf_send.at[d], sf_recv.at[d],
                s, (f + d) % n_f,
            ).wait_recv()
        per = n_f * high // 128
        each = n_f // per
        for t in range(per):
            value = small_f[t * each, 0:8]
            for e in range(1, each):
                value = value + small_f[t * each + e, 0:8]
            small_s[s, t] = value
        for e in range(n_f):
            bias_row[0:1, pl.ds(e * 128, 128)] = small_f[e, 8:9]

        def small_wide(k, to):
            return remote(small_s.at[s], small_s.at[s], ss_send.at[k], ss_recv.at[k], to, f)

        for k, to in enumerate(others):
            small_wide(k, to).start()
        for p in range(n_cut):
            qkv_copy(-1, p, s).wait()
            for k, to in enumerate(others):
                qkv_copy(k, p, to).wait_recv()
        for weight in w_qkv:
            weight.start_far(across=False)
        for weight in w_qkv:
            weight.start_near(everyone=True)
            weight.across(3, f).start()
        w_out.start(out_in)
        w_down.start_far(down_in)
    else:
        ag_tok.start(tokens)
        params[...] = small_in[0:8]
        bias_row[...] = small_in[8:9, 0 : bias_row.shape[1]]

    zero_row = jnp.zeros((1, width), F32)

    def both(run, count):
        def step(h, carry):
            return tuple(a + b for a, b in zip(carry, run(h)))

        return lax.fori_loop(0, 2, step, (zero_row,) * count)

    def far_first(i):
        return (1 - i // 2) + 2 * (1 - i % 2)

    def param(i):
        return params[i : i + 1, :]

    tok_own.wait()
    if inside:
        w_qkv[0].relay()
    ag_tok.relay()
    if inside:
        for k, to in enumerate(others):
            up_copy(k, to).start()
        w_qkv[1].relay()
        w_out.relay(False)
        w_down.start_near(down_in)
        for k, who in enumerate(others):
            remote(
                small_s.at[who], small_s.at[who], ss_send.at[k], ss_recv.at[k], who, f
            ).wait_recv()
        for b in range(4):
            for t in range(per):
                params[:, pl.ds((b * per + t) * 128, 128)] = small_s[b, t]

    def first_norm(b):
        unit, _s = unit_of(tok[b].astype(F32))
        normed[b] = (unit * param(0) + param(1)).astype(BF16)

    def norm_step(k, _):
        @pl.when(k == 1)
        def _():
            ag_tok.wait_x()

        @pl.when(k == 2)
        def _():
            ag_tok.wait_y()

        @pl.when(k == 3)
        def _():
            ag_tok.wait_d()

        first_norm(block(k))
        return 0

    lax.fori_loop(0, 3, norm_step, 0)
    if inside:
        for weight in w_qkv:
            weight.rest()
    lax.fori_loop(3, 4, norm_step, 0)
    if inside:
        for weight in w_qkv:
            weight.finish()

    rest = normed[...].reshape(4 * rows, width)
    for p in range(pairs):
        value = dot(rest, qkv_w[:, :, p * 384 : (p + 1) * 384].reshape(width, 384))
        for q in range(3):
            piece = value[:, q * 128 : (q + 1) * 128]
            piece = piece if q else piece * 0.125
            at = slice((3 * p + q) * 128, (3 * p + q + 1) * 128)
            triple[:, :, at] = piece.astype(BF16).reshape(4, rows, 128)

    if inside:
        up_copy(-1, s).wait()
        for k, to in enumerate(others):
            up_copy(k, to).wait_recv()
        w_up.start_far()
        w_up.start_near()

    seg_own.wait()
    for k, who in enumerate(others):
        remote(seg_in, segs.at[who], seg_send.at[k], seg_recv.at[k], who, f).wait_recv()
    seg_all = segs[...]

    def below(level):
        count = jnp.sum((seg_all < level).astype(F32), axis=0)
        return jnp.sum(count, axis=1, keepdims=True)

    bound_1, bound_2 = below(1), below(2)
    blocks = window // rows
    lane = lax.broadcasted_iota(jnp.int32, (1, 128), 1)
    left = (lane < HEAD_DIM).astype(F32)
    sides = (left.astype(BF16), (1.0 - left).astype(BF16))
    pick = lax.broadcasted_iota(jnp.int32, (rows, 128), 1) < HEAD_DIM

    def set_starts(r, _):
        i = (r * rows + lax.broadcasted_iota(jnp.int32, (rows, 128), 0)).astype(F32)
        starts[r] = jnp.where(i >= bound_2, bound_2, jnp.where(i >= bound_1, bound_1, 0.0))
        return 0

    lax.fori_loop(0, 4, set_starts, 0)

    def cut(r, part_at, p, count):
        at = pl.ds(pl.multiple_of((3 * p + part_at) * 128, 128), 128)
        return triple[pl.ds(r, count), :, at].reshape(count * rows, 128)

    def masked(scores, r, first, count):
        start = starts[r]
        tiles = []
        for t in range(count * rows // 128):
            j = lax.broadcasted_iota(jnp.int32, (rows, 128), 1) + t * 128
            keep = (first * rows + j).astype(F32) >= start
            if t * 128 >= (count - 1) * rows:
                i = lax.broadcasted_iota(jnp.int32, (rows, 128), 0)
                keep = keep & (j - (count - 1) * rows <= i)
            tiles.append(jnp.where(keep, scores[:, t * 128 : (t + 1) * 128], NEG))
        return jnp.concatenate(tiles, axis=1)

    rs_1 = Scatter(land_a, 0)

    def attend_heads(r, first, count):
        scores, values = [], []
        for p in range(pairs):
            query, keys = cut(r, 0, p, 1), cut(first, 1, p, count)
            for e in range(2):
                scores.append(masked(dot(query * sides[e], keys, NT), r, first, count))
                values.append(cut(first, 2, p, count))
        tops = [jnp.max(score, -1, keepdims=True) for score in scores]
        expos = [jnp.exp(score - top) for score, top in zip(scores, tops)]
        sums = [jnp.sum(expo, -1, keepdims=True) for expo in expos]
        lows = [(expo * (1.0 / total)).astype(BF16) for expo, total in zip(expos, sums)]
        for n, low in enumerate(lows):
            probs[r, n, :, 0 : count * rows] = low
        outs = [dot(low, value) for low, value in zip(lows, values)]
        for p in range(pairs):
            both_sides = jnp.where(pick, outs[2 * p], outs[2 * p + 1])
            attended[r, :, p * 128 : (p + 1) * 128] = both_sides.astype(BF16)

    def attend(i, _):
        rel = far_first(i)
        r = block(rel)
        for count in range(1, blocks + 1):
            @pl.when(r + 1 >= count if count == blocks else r + 1 == count)
            def _(count=count):
                attend_heads(r, r + 1 - count, count)

        if inside:
            @pl.when(i == 0)
            def _():
                out_own.wait()
                w_out.finish()

        part[rel] = dot(attended[r], out_w[0]).astype(BF16)

        @pl.when(c == 0)
        def _():
            rs_1.step(rel)

        @pl.when((c == 1) & (i == 2))
        def _():
            rs_1.step(3)

        if inside:
            @pl.when(i == 1)
            def _():
                w_down.relay()

        return 0

    if inside:
        w_out.relay_rest()
        w_out.rest()
    lax.fori_loop(0, 4, attend, 0)

    my_turn((1, 1))

    @pl.when(c == 1)
    def _():
        for i in (1, 3):
            rs_1.copy(i).start()

    rs_1.relay()
    if inside:
        w_up.relay()

        @pl.when(c == 1)
        def _():
            w_down.rest()

    rs_1.wait()

    def mid_norm(h):
        at = half_rows(h)
        value = rs_1.total(h)
        branch[at] = value
        unit, _s = unit_of(value)
        mid = tok[s, at].astype(F32) + (unit * param(2) + param(3))
        middle[at] = mid
        unit, _s = unit_of(mid)
        inner[s, at] = (unit * param(4) + param(5)).astype(BF16)

    for h in range(2):
        mid_norm(h)
    ag_inner = Gather(inner, 1)
    my_turn()
    ag_inner.start()
    rs_1.drain()
    if inside:
        @pl.when(c == 1)
        def _():
            w_up.rest()

    ag_inner.relay()
    if inside:
        @pl.when(c == 0)
        def _():
            w_down.rest()
            w_up.rest()

        w_up.finish()

    ff = up_w.shape[2]
    tile = ff
    rs_2 = Scatter(land_b, 1)

    def forward_step(k, _):
        @pl.when(k == 1)
        def _():
            ag_inner.wait_x()

        @pl.when(k > 1)
        def _():
            ag_inner.step(k)

        r = block(k)

        def column(n, _):
            at = pl.ds(pl.multiple_of(n * tile, tile), tile)
            pre = dot(inner[r], up_w[:, :, at].reshape(width, tile)) + bias_row[:, at]
            square = pre * pre
            bend = jnp.tanh(0.7978845608028654 * pre * (1.0 + 0.044715 * square))
            near = 0.5 + 0.5 * bend
            activ[r, :, at] = (pre * near).astype(BF16)
            slope = near + pre * (0.5 - 0.5 * bend * bend) * (
                0.7978845608028654 + 0.10703222440890037 * square
            )
            dgelu[r, :, at] = slope.astype(BF16)
            return 0

        lax.fori_loop(0, ff // tile, column, 0)
        return 0

    lax.fori_loop(0, 4, forward_step, 0)
    if inside:
        down_own.wait()
        w_down.finish()

    def down_step(i, _):
        rel = far_first(i)
        r = block(rel)

        part[rel] = dot(activ[r], down_w[...]).astype(BF16)
        rs_2.step(rel)
        return 0

    my_turn()
    lax.fori_loop(0, 4, down_step, 0)
    rs_2.relay()
    cot_own.wait()
    rs_2.wait()

    def last_norm(h):
        at = half_rows(h)
        unit, scale = unit_of(rs_2.total(h))
        gbr[s, at] = (middle[at] + (unit * param(6) + param(7))).astype(BF16)
        grad = cot[at].astype(F32)
        gmix[s, at] = pull_of(grad, param(6), unit, scale).astype(BF16)
        return col_sum(grad * unit), col_sum(grad)

    grad_gain_d, grad_shift_d = both(last_norm, 2)
    sg_rows = [None] * 8
    sg_rows[6], sg_rows[7] = grad_gain_d, grad_shift_d
    ag_mix = Gather(gmix, 2)
    my_turn()
    ag_mix.start()
    result_out = pltpu.make_async_copy(gbr.at[s], result, o_sem.at[2])
    result_out.start()
    rs_2.drain()

    rs_3 = Scatter(land_a, 2)
    sg_bias = bias_row

    def clear(n, _):
        at = pl.ds(pl.multiple_of(n * tile, tile), tile)
        sg_bias[:, at] = jnp.zeros((1, tile), F32)
        return 0

    lax.fori_loop(0, ff // tile, clear, 0)

    TN = ((0,), (0,))

    def flat(ref, lanes=slice(None)):
        held = ref[:, :, lanes]
        return held.reshape(4 * rows, held.shape[2])

    def all_pairs(shed):
        for to_z in range(n_f // 2):
            shed.pair(to_z).start()

    def cut_grads(left, right, gw, shed, lanes=slice(None)):
        for b in range(4):
            value = dot(flat(left, slice(b * rows, (b + 1) * rows)), flat(right, lanes), TN)
            gw[:, b * high : (b + 1) * high, :] = value.astype(BF16).reshape(n_f, high, -1)
        all_pairs(shed)

    def down_grads(rels):
        each = ff // n_f
        count = 256 // each
        for b in range(n_f // count):
            at = slice(b * count, (b + 1) * count)
            cols = slice(b * 256, (b + 1) * 256)
            value = dot(activ[block(rels[0]), :, cols], gmix[block(rels[0])], TN)
            for rel in rels[1:]:
                value = value + dot(activ[block(rel), :, cols], gmix[block(rel)], TN)
            if len(rels) == 1:
                value = value + gw_down[at].astype(F32).reshape(256, width)
            gw_down[at] = value.astype(BF16).reshape(count, each, width)

    if inside:
        shed_down = Shed(0, gw_down, lp_down, lz_down)
        shed_up = Shed(1, gw_up, lp_up, lz_up)
        shed_out = Shed(2, gw_out, lp_out, lz_out)
        shed_qkv = [
            Shed(3 + p, gw_qkv[p], lp_qkv[p], lz_qkv[p])
            for p in range(pairs)
        ]
        ag_tok.drain()

    def back_step(k, _):
        if inside:
            @pl.when(k == 3)
            def _():
                down_grads((0, 1, 2))

        ag_mix.step(k)
        r = block(k)

        def column(n, _):
            at = pl.ds(pl.multiple_of(n * tile, tile), tile)
            grad = dot(gmix[r], down_w[at], NT)
            low = (dgelu[r, :, at].astype(F32) * grad).astype(BF16)
            dgelu[r, :, at] = low
            sg_bias[:, at] = sg_bias[:, at] + col_sum(low.astype(F32))
            return 0

        lax.fori_loop(0, ff // tile, column, 0)
        return 0

    lax.fori_loop(0, 4, back_step, 0)

    if inside:
        down_grads((3,))
        all_pairs(shed_down)

        @pl.when(c == 1)
        def _():
            shed_down.far()

    def inner_step(i, _):
        rel = far_first(i)
        r = block(rel)

        part[rel] = dot(dgelu[r], up_w[...].reshape(width, ff), NT).astype(BF16)
        rs_3.step(rel)
        return 0

    my_turn()
    lax.fori_loop(0, 4, inner_step, 0)

    if inside:
        cut_grads(inner, dgelu, gw_up, shed_up)
    rs_3.relay()
    if inside:
        @pl.when(c == 1)
        def _():
            shed_up.far()
            shed_down.close()
            shed_up.close()

        @pl.when(c == 0)
        def _():
            shed_down.far()

    rs_3.wait()

    result_out.wait()

    def mid_back(h):
        at = half_rows(h)
        grad = rs_3.total(h)
        unit, scale = unit_of(middle[at])
        total = cot[at].astype(F32) + pull_of(grad, param(4), unit, scale)
        gmid[at] = total
        out = [col_sum(grad * unit), col_sum(grad)]
        unit, scale = unit_of(branch[at])
        gbr[s, at] = pull_of(total, param(2), unit, scale).astype(BF16)
        return out[0], out[1], col_sum(total * unit), col_sum(total)

    sg_rows[4], sg_rows[5], sg_rows[2], sg_rows[3] = both(mid_back, 4)
    ag_br = Gather(gbr, 3)
    my_turn()
    ag_br.start()
    rs_3.drain()
    def arrive(k, _):
        if inside:
            @pl.when(k == 1)
            def _():
                ag_br.relay()

            @pl.when((k == 1) & (c == 0))
            def _():
                shed_up.far()
                shed_down.close()
                shed_up.close()

            @pl.when(k == 1)
            def _():
                ag_br.wait_x()

            @pl.when(k > 1)
            def _():
                ag_br.step(k)

            @pl.when(k == 2)
            def _():
                shed_down.second()
        else:
            ag_br.step(k)

        r = block(k)
        gatt[r] = dot(gbr[r], out_w[0], NT).astype(BF16)
        if inside:
            value = dot(attended[r], gbr[r], TN)

            @pl.when(k == 0)
            def _():
                branch[...] = value

            @pl.when(k > 0)
            def _():
                branch[...] = branch[...] + value

        return 0

    lax.fori_loop(0, 4, arrive, 0)
    if inside:
        gw_out[...] = branch[...].astype(BF16).reshape(gw_out.shape)
        all_pairs(shed_out)

        @pl.when(c == 1)
        def _():
            shed_out.far()
            shed_out.close()

    if inside:
        per = n_f * high // 128
        fin_down = branch.at[0:high_d]
        fin_out = branch.at[high_d : high_d + high]
        gdown_out = pltpu.make_async_copy(fin_down, gdown, o_sem.at[3])
        gout_out = pltpu.make_async_copy(fin_out, gout, o_sem.at[4])

        def rows_at(n):
            return pl.ds(pl.multiple_of(n * high, high), high)

        gup_out = [
            pltpu.make_async_copy(
                middle.at[rows_at(b)], gup.at[:, b * ff : (b + 1) * ff], o_sem.at[8 + b]
            )
            for b in range(4)
        ]
        gqkv_out = [
            pltpu.make_async_copy(
                middle.at[rows_at(4 + p)], gqkv.at[:, p * width : (p + 1) * width],
                o_sem.at[12 + p],
            )
            for p in range(3)
        ]
        gsmall_out = pltpu.make_async_copy(small_sum, gsmall, o_sem.at[7])

        def ts_copy(k, to):
            return remote(sg_s.at[to], sg_land_s.at[k], ts_send.at[k], ts_recv.at[k], to, f)

        def tf_copy(d):
            to = (f + d) % n_f
            return remote(
                sg_f.at[to], sg_land_f.at[d - 1], tf_send.at[d], tf_recv.at[d], s, to
            )

        def small_first():
            for b in range(4):
                for t in range(per):
                    at = slice((b * per + t) * 128, (b * per + t + 1) * 128)
                    for i in range(8):
                        sg_s[b, t, i : i + 1, :] = sg_rows[i][:, at]
            for k, to in enumerate(others):
                ts_copy(k, to).start()

        def small_second():
            for k, to in enumerate(others):
                ts_copy(k, to).wait_recv()
            for who in range(n_f):
                t = who * high // 128
                sg_f[who, 0:8] = (
                    sg_s[s, t] + sg_land_s[0, t] + sg_land_s[1, t] + sg_land_s[2, t]
                )
                sg_f[who, 8:9] = sg_bias[:, who * 128 : (who + 1) * 128]
            for d in range(1, n_f):
                tf_copy(d).start()

        def small_third():
            for d in range(1, n_f):
                tf_copy(d).wait_recv()
            value = sg_f[f]
            for d in range(1, n_f):
                value = value + sg_land_f[d - 1]
            small_sum[...] = value
            gsmall_out.start()

        def gu_copy(k, to, who):
            return remote(
                cot.at[rows_at(to)], cot.at[rows_at(4 + who)],
                gu_send.at[k], gu_recv.at[k], to, f,
            )

        def put_qkv(q, who, value):
            lanes = pl.ds(pl.multiple_of(who * group + q * 128, 128), 128)
            for p in range(3):
                piece = value[:, p * 128 : (p + 1) * 128]
                middle[rows_at(4 + p), lanes] = piece.astype(F32)

        def gc_copy(k, p, to, who):
            return remote(
                fin_qkv.at[p, to], land_qkv.at[p, who],
                gc_send.at[k, p], gc_recv.at[k, p], to, f,
            )

    def back_rows(p, r_group):
        lanes = slice(p * 128, (p + 1) * 128)
        items = []
        for r in r_group:
            first = max(r + 1 - blocks, 0)
            count = r + 1 - first
            query, grad = cut(r, 0, p, 1), gatt[r, :, lanes]
            keys, vals = cut(first, 1, p, count), cut(first, 2, p, count)
            for e in range(2):
                low = probs[r, 2 * p + e, :, 0 : count * rows]
                items.append((r, e, first, count, query, keys, grad, low, vals))
        pulled = [dot(grad * sides[e], vals, NT) for _, e, _, _, _, _, grad, _, vals in items]
        sums = [
            jnp.sum(item[7].astype(F32) * pull, -1, keepdims=True)
            for item, pull in zip(items, pulled)
        ]
        slopes = [
            (item[7].astype(F32) * (pull - total)).astype(BF16)
            for item, pull, total in zip(items, pulled, sums)
        ]
        for n in range(0, len(items), 2):
            r, _, first, count, query, keys, grad, _, _ = items[n]
            query_t, grad_t = query.T, grad.T
            outs = [dot(slopes[n + e], keys) for e in range(2)]
            for e in range(2):
                side = slice(e * HEAD_DIM, (e + 1) * HEAD_DIM)
                here = slice(p * 128 + e * HEAD_DIM, p * 128 + (e + 1) * HEAD_DIM)
                key_part = dot(query_t[side], slopes[n + e])
                value_part = dot(grad_t[side], items[n + e][7])
                for m in range(count):
                    span = slice((first + m) * rows, (first + m + 1) * rows)
                    cols = slice(m * rows, (m + 1) * rows)
                    if r == 3 or (first + m) < 4 - blocks and r == first + m + blocks - 1:
                        dkt[here, span] = key_part[:, cols]
                        dvt[here, span] = value_part[:, cols]
                    else:
                        dkt[here, span] = dkt[here, span] + key_part[:, cols]
                        dvt[here, span] = dvt[here, span] + value_part[:, cols]
            at = slice(3 * p * 128, (3 * p + 1) * 128)
            gtri[r, :, at] = (jnp.where(pick, outs[0], outs[1]) * 0.125).astype(BF16)

    def back_pair(p):
        lanes = slice(p * 128, (p + 1) * 128)
        for r_group in ((3, 2), (1, 0)):
            back_rows(p, r_group)
            if inside and p and r_group[0] == 3:
                @pl.when(c == 0)
                def _():
                    shed_out.far()
                    shed_out.close()

        for b in range(4):
            span = slice(b * rows, (b + 1) * rows)
            at = slice((3 * p + 1) * 128, (3 * p + 2) * 128)
            gtri[b, :, at] = dkt[lanes, span].astype(BF16).T
            at = slice((3 * p + 2) * 128, (3 * p + 3) * 128)
            gtri[b, :, at] = dvt[lanes, span].astype(BF16).T

    def qkv_grads(p):
        cut_grads(normed, gtri, gw_qkv[p], shed_qkv[p], slice(p * 384, (p + 1) * 384))

    for p in range(pairs):
        back_pair(p)
        if inside and p == 0:
            qkv_grads(p)
            shed_up.second()

            @pl.when(c == 1)
            def _():
                shed_qkv[0].far()

    if inside:
        @pl.when(c == 1)
        def _():
            qkv_grads(1)
            shed_qkv[1].far()
            for shed in shed_qkv:
                shed.close()
            shed_out.second()

        @pl.when(c == 0)
        def _():
            shed_qkv[0].far()

    rs_4 = Scatter(land_b, 3)

    def normed_step(i, carry):
        rel = far_first(i)
        r = block(rel)
        grad = dot(gtri[r], qkv_w[...].reshape(width, 3 * group), NT)
        part[rel] = grad.astype(BF16)
        rs_4.step(rel)
        unit, _s = unit_of(tok[r].astype(F32))
        return carry[0] + col_sum(grad * unit), carry[1] + col_sum(grad)

    my_turn()
    sg_rows[0], sg_rows[1] = lax.fori_loop(0, 4, normed_step, (zero_row, zero_row))
    if inside:
        small_first()

        @pl.when(c == 0)
        def _():
            qkv_grads(1)

        @pl.when(c == 1)
        def _():
            shed_qkv[0].second()

    rs_4.relay()
    if inside:
        @pl.when(c == 0)
        def _():
            shed_qkv[1].far()
            for shed in shed_qkv:
                shed.close()

        @pl.when(c == 0)
        def _():
            shed_out.second()
            shed_qkv[0].second()

        shed_qkv[1].second()
        small_second()
        at = pl.ds(pl.multiple_of(s * high, high), high)
        shed_up.wait()
        for b in range(4):
            cot[rows_at(b)] = shed_up.total(slice(b * high, (b + 1) * high)).astype(BF16)
        middle[rows_at(s)] = shed_up.total(at)

        def give_up():
            for k, to in enumerate(others):
                gu_copy(k, to, s).start()

        @pl.when(c == 1)
        def _():
            give_up()

        shed_down.wait()
        fin_down[...] = shed_down.total(slice(None))
        gdown_out.start()

        def give_qkv(q):
            shed = shed_qkv[q]
            shed.wait()
            for b in range(4):
                fin_qkv[q, b] = shed.total(slice(b * high, (b + 1) * high)).astype(BF16)
            for k, to in enumerate(others):
                gc_copy(k, q, to, s).start()
            put_qkv(q, s, shed.total(at))

        @pl.when(c == 1)
        def _():
            give_qkv(0)
            give_qkv(1)

    rs_4.wait()

    def first_back(h, _):
        at = half_rows(h)
        unit, scale = unit_of(tok[s, at].astype(F32))
        gmid[at] = gmid[at] + pull_of(rs_4.total(h), param(0), unit, scale)
        pltpu.make_async_copy(gmid.at[at], tgrad.at[at], o_sem.at[h]).start()
        return 0

    lax.fori_loop(0, 2, first_back, 0)
    if inside:
        @pl.when(c == 0)
        def _():
            give_up()
            give_qkv(0)
            give_qkv(1)

        for k, who in enumerate(others):
            gu_copy(k, who, who).wait_recv()
            middle[rows_at(who)] = cot[rows_at(4 + who)].astype(F32)
        for one in gup_out:
            one.start()
        shed_out.wait()
        fin_out[...] = shed_out.total(slice(None))
        gout_out.start()
        small_third()
        for k, who in enumerate(others):
            for q in range(pairs):
                gc_copy(k, q, who, who).wait_recv()
                put_qkv(q, who, land_qkv[q, who])
        for one in gqkv_out:
            one.start()

    for h in range(2):
        pltpu.make_async_copy(gmid.at[half_rows(h)], tgrad.at[half_rows(h)], o_sem.at[h]).wait()
    if inside:
        gsmall_out.wait()
        gdown_out.wait()
        gout_out.wait()
        for one in (*gup_out, *gqkv_out):
            one.wait()
        for k, to in enumerate(others):
            gu_copy(k, to, s).wait_send()
            ts_copy(k, to).wait_send()
            for q in range(pairs):
                gc_copy(k, q, to, s).wait_send()
            for p in range(n_cut):
                qkv_copy(k, p, to).wait_send()
            up_copy(k, to).wait_send()
            small_wide(k, to).wait_send()
        for d in range(1, n_f):
            tf_copy(d).wait_send()
            small_copy(d).wait_send()
        for weight in (*w_qkv, w_out, w_up, w_down):
            weight.drain()
        for shed in (shed_down, shed_up, shed_out, *shed_qkv):
            shed.drain()
    else:
        for i in range(8):
            small_sum[i : i + 1, :] = sg_rows[i]
        small_sum[8:9, 0:ff] = sg_bias[...]
        gsmall_out = pltpu.make_async_copy(small_sum, gsmall, o_sem.at[7])
        gsmall_out.start()
        gsmall_out.wait()
    for k, to in enumerate(others):
        seg_copy(k, to).wait_send()
    for gather in (ag_inner, ag_mix, ag_br) + (() if inside else (ag_tok,)):
        gather.drain()
    rs_4.drain()


def finish_kernel(n_f, n_big, *refs):
    small, given = refs[0], refs[1 : 1 + n_big]
    made, minor = refs[1 + n_big : 1 + 2 * n_big], refs[1 + 2 * n_big : 10 + 2 * n_big]
    held, (in_sem, out_sem) = refs[10 + 2 * n_big : 10 + 3 * n_big], refs[10 + 3 * n_big :]
    cuts = []
    for i in range(n_big):
        tall = given[i].shape[0]
        for j in range(max(1, tall // 64)):
            at = pl.ds(j * min(tall, 64), min(tall, 64))
            cuts.append((i, at, len(cuts)))
    for i, at, n in cuts:
        pltpu.make_async_copy(given[i].at[at], held[i].at[at], in_sem.at[n]).start()
    each = minor[0].shape[1]
    place = lax.axis_index("fsdp") % (128 // each)
    for i in range(8):
        row = small[i : i + 1, :]
        value = row[:, 0:each]
        for q in range(1, 128 // each):
            value = jnp.where(place == q, row[:, q * each : (q + 1) * each], value)
        minor[i][...] = value
    minor[8][...] = small[8:9, :]
    for i, at, n in cuts:
        pltpu.make_async_copy(given[i].at[at], held[i].at[at], in_sem.at[n]).wait()
        pltpu.make_async_copy(held[i].at[at], made[i].at[at], out_sem.at[n]).start()
    for i, at, n in cuts:
        pltpu.make_async_copy(held[i].at[at], made[i].at[at], out_sem.at[n]).wait()


def finish(n_f, high, *made):
    big, small = made[:6], made[6]
    whole, anywhere = pl.BlockSpec(memory_space=pltpu.VMEM), pl.BlockSpec(memory_space=pl.ANY)
    count = sum(max(1, v.shape[0] // 64) for v in big)
    minor = [jax.ShapeDtypeStruct((1, high), F32)] * 8 + [jax.ShapeDtypeStruct((1, 128), F32)]
    out = pl.pallas_call(
        partial(finish_kernel, n_f, 6),
        out_shape=[jax.ShapeDtypeStruct(v.shape, v.dtype) for v in big] + minor,
        in_specs=[whole] + [anywhere] * 6,
        out_specs=[anywhere] * 6 + [whole] * 9,
        scratch_shapes=[pltpu.VMEM(v.shape, v.dtype) for v in big]
        + [pltpu.SemaphoreType.DMA((count,))] * 2,
    )(small, *big)
    result, tgrad, gqkv, gout, gup, gdown = out[:6]
    small = [v[0] for v in out[6:]]
    return (result[None], tgrad[None], gqkv, gout, gup, small[8], gdown, *small[:8])


def on_device(n_seq, n_f, *args):
    (tokens, segments, qkv_weight, out_weight, up_weight, up_bias, down_weight) = args[:7]
    vectors, cotangent = args[7:15], args[15]
    rows, width = tokens.shape[1:]
    high, high_d = qkv_weight.shape[0], down_weight.shape[0]
    length = n_seq * rows
    group = qkv_weight.shape[1] // 3 // n_seq
    heads = group // HEAD_DIM
    ff = up_weight.shape[1] // n_seq
    half = rows // 2
    window = rows * min(n_seq, 1 + -(-511 // rows))
    inside = n_f == 8 and high % 32 == 0 and ff == width and 8 * high <= rows
    f = lax.axis_index("fsdp")
    if inside:
        small = [v[None] for v in (*vectors, up_bias)]
        weights = (qkv_weight, out_weight, up_weight, down_weight)
    else:
        small = jnp.stack([v.astype(F32) for v in vectors])
        small = lax.all_gather(small, ("seq", "fsdp"), axis=1, tiled=True)
        bias = lax.all_gather(up_bias.astype(F32), "fsdp", axis=0, tiled=True)
        bias = jnp.pad(bias[None], ((0, 7), (0, width - ff)))
        small = [jnp.concatenate([small, bias])]

        def columns(weight, parts):
            cut = weight.reshape(high, parts, n_seq, -1, 128).transpose(2, 0, 3, 1, 4)
            cut = cut.reshape(n_seq, high, -1)
            cut = lax.all_to_all(cut, "seq", split_axis=0, concat_axis=0, tiled=True)
            return lax.all_gather(cut, "fsdp", axis=1, tiled=True)

        weights = (
            columns(qkv_weight, 3),
            lax.all_gather(out_weight, "fsdp", axis=0, tiled=True)[None],
            columns(up_weight, 1),
            lax.all_gather(down_weight, "fsdp", axis=0, tiled=True),
        )
    vmem, anywhere, dma = pltpu.VMEM, pl.BlockSpec(memory_space=pl.ANY), pltpu.SemaphoreType.DMA
    whole = pl.BlockSpec(memory_space=pltpu.VMEM)
    full = (4, rows, width)
    saved = {
        "normed": (full, BF16), "inner": (full, BF16), "gmix": (full, BF16), "gbr": (full, BF16),
        "attended": ((4, rows, group), BF16), "activ": ((4, rows, ff), BF16),
        "dgelu": ((4, rows, ff), BF16), "gtri": ((4, rows, 3 * group), BF16),
    }
    n_cut = 3 * (group // 128)
    pieces = {"q0": (n_seq * high, 384), "q1": (n_seq * high, 384), "out": (high, width),
              "up": (n_seq * high, ff), "down": (high_d, width)}
    scratch = {
        "tok": vmem(full, BF16), "normed": None, "inner": None, "gmix": None, "gbr": None,
        "qkv_w": vmem((n_seq, rows, 3 * group), BF16), "out_w": vmem((1, group, width), BF16),
        "up_w": vmem((n_seq, rows, ff), BF16), "down_w": vmem((ff, width), BF16),
        "segs": vmem((4, 1, rows), jnp.int32),
        "small_f": vmem((n_f if inside else 1, 16, 128), F32), "small_s": vmem((4, width // 512, 8, 128), F32),
        "params": vmem((8, width), F32), "bias_row": vmem((1, ff), F32),
        "triple": vmem((4, rows, 3 * group), BF16), "probs": vmem((4, heads, rows, window), BF16),
        "attended": None, "starts": vmem((4, rows, 128), F32), "activ": None, "dgelu": None,
        "part": vmem(full, BF16), "land_a": vmem((6, half, width), BF16),
        "land_b": vmem((6, half, width), BF16),
        "branch": vmem((rows, width), F32), "middle": vmem((rows, width), F32),
        "gmid": vmem((rows, width), F32), "cot": vmem((rows, width), BF16),
        "gtri": None, "gatt": vmem((4, rows, group), BF16), "dkt": vmem((group, length), F32),
        "dvt": vmem((group, length), F32),
    }
    for name, (tall, wide) in pieces.items():
        scratch["gw_" + name] = vmem((n_f if inside else 1, tall if inside else 16, wide), BF16)
    for name, (tall, wide) in pieces.items():
        scratch["lp_" + name] = vmem((n_f // 2 if inside else 1, tall if inside else 16, wide), BF16)
    for name, (tall, wide) in pieces.items():
        scratch["lz_" + name] = vmem((n_f // 2 if inside else 1, tall if inside else 16, wide), BF16)
    scratch["fin_qkv"] = vmem((group // 128, 4, high, 384), BF16)
    scratch["land_qkv"] = vmem((group // 128, 4, high, 384), BF16)
    scratch["small_sum"] = vmem((16, 128 if inside else width), F32)
    tiles = width // 512
    scratch["sg_s"] = vmem((4, tiles, 8, 128), F32)
    scratch["sg_land_s"] = vmem((3, tiles, 8, 128), F32)
    scratch["sg_f"] = vmem((n_f if inside else 1, 16, 128), F32)
    scratch["sg_land_f"] = vmem((n_f - 1 if inside else 1, 16, 128), F32)
    for name, shape in (
        ("ag_send", (4, 6)), ("ag_recv", (4, 6)), ("rs_send", (4, 6)), ("rs_recv", (4, 6)),
        ("w_send", (5, 4)), ("w_recv", (5, 3)), ("p_send", (5, 4)), ("p_recv", (5, 4)),
        ("col_send", (3, n_cut)), ("col_recv", (3, n_cut)), ("col_local", (n_cut,)),
        ("upc_send", (3,)), ("upc_recv", (3,)), ("seg_send", (3,)), ("seg_recv", (3,)),
        ("sf_send", (8,)), ("sf_recv", (8,)), ("ss_send", (3,)), ("ss_recv", (3,)),
        ("loc_sem", (7,)), ("o_sem", (16,)),
        ("gp_send", (5, 4)), ("gp_recv", (5, 4)), ("gz_send", (5, 4)), ("gz_recv", (5, 4)),
        ("gc_send", (3, 2)), ("gc_recv", (3, 2)), ("gu_send", (3,)), ("gu_recv", (3,)),
        ("ts_send", (3,)), ("ts_recv", (3,)), ("tf_send", (8,)), ("tf_recv", (8,)),
    ):
        scratch[name] = dma(shape)
    scratch["turn"] = pltpu.SemaphoreType.REGULAR
    scratch["small_raw"] = vmem((8, 1, high), BF16)
    scratch["bias_raw"] = vmem((1, up_bias.shape[0]), BF16)
    scratch["small_rows"] = vmem((8, high), F32)
    scratch["small_tile"] = vmem((16, 128), F32)
    scratch["raw_sem"] = dma((9,))
    outs = {
        "result": ((rows, width), BF16), "tgrad": ((rows, width), F32),
        "gqkv": ((high, n_seq * 3 * group), F32), "gout": ((high, width), F32),
        "gup": ((high, n_seq * ff), F32), "gdown": ((high_d, width), F32),
        "gsmall": ((16, 128 if inside else width), F32),
    }
    if inside:
        for name, shape in saved.items():
            scratch[name] = vmem(*shape)
        extra = []
    else:
        extra = list(saved)
    names = list(scratch)

    def kernel(*refs):
        n_in = 7 + len(small)
        given = (*refs[:2], refs[2 : 2 + len(small)], *refs[2 + len(small) : n_in])
        made = refs[n_in : n_in + len(outs)]
        more = dict(zip(extra, refs[n_in + len(outs) :]))
        rest = refs[n_in + len(outs) + len(extra) :]
        more.update(zip([n for n in names if scratch[n] is not None], rest))
        layer_kernel(inside, n_f, *given, *made, *[more[n] for n in names])

    shapes = [*outs.values(), *[saved[n] for n in extra]]
    made = pl.pallas_call(
        kernel,
        out_shape=[jax.ShapeDtypeStruct(*shape) for shape in shapes],
        in_specs=[anywhere] * 2 + [anywhere if inside else whole] * len(small) + [anywhere] * 5,
        out_specs=[anywhere] * len(outs) + [whole] * len(extra),
        scratch_shapes=[scratch[n] for n in names if scratch[n] is not None],
        compiler_params=pltpu.CompilerParams(
            collective_id=0, has_side_effects=True, vmem_limit_bytes=67043328
        ),
    )(tokens[0], segments, *small, cotangent[0], *weights)
    result, tgrad, gqkv, gout, gup, gdown, gsmall = made[:7]
    if inside:
        return finish(n_f, high, *made[:7])
    else:
        kept = {n: v.reshape(length, -1) for n, v in zip(extra, made[7:])}

        def turned_dot(left, right):
            return lax.dot_general(
                kept[left], kept[right], (((0,), (0,)), ((), ())), preferred_element_type=F32
            ).astype(BF16)

        def shed(value):
            return lax.psum_scatter(value, "fsdp", scatter_dimension=0, tiled=True)

        def columns_back(value, parts):
            cut = value.reshape(n_seq, n_f, high, -1).transpose(1, 0, 2, 3)
            cut = lax.all_to_all(shed(cut)[0], "seq", split_axis=0, concat_axis=0, tiled=True)
            cut = cut.reshape(n_seq, high, -1, parts, 128).transpose(1, 3, 0, 2, 4)
            return cut.reshape(high, -1).astype(F32)

        gqkv = columns_back(turned_dot("normed", "gtri"), 3)
        gout = shed(turned_dot("attended", "gbr")).astype(F32)
        gup = columns_back(turned_dot("inner", "dgelu"), 1)
        gdown = shed(turned_dot("activ", "gmix")).astype(F32)
        vectors = lax.psum_scatter(gsmall[:8], ("seq", "fsdp"), scatter_dimension=1, tiled=True)
        gbias = shed(gsmall[8, :ff])
    return (result[None], tgrad[None], gqkv, gout, gup, gbias, gdown, *vectors)


def solution(mesh):
    rows = P(("seq", "fsdp"), None)
    vector = P(("seq", "fsdp"))
    acts = P("fsdp", "seq", None)
    return jax.shard_map(
        partial(on_device, mesh.shape["seq"], mesh.shape["fsdp"]),
        mesh=mesh,
        in_specs=(acts, P("fsdp", "seq"), rows, rows, rows, vector, rows, *(vector,) * 8, acts),
        out_specs=(acts, acts, rows, rows, rows, vector, rows, *(vector,) * 8),
        check_vma=False,
    )
```

```python
from functools import partial

import jax
import jax.numpy as jnp
from jax import lax
from jax.experimental import pallas as pl
from jax.experimental.pallas import tpu as pltpu
from jax.sharding import PartitionSpec as P

HEAD_DIM = 64
F32 = jnp.float32
BF16 = jnp.bfloat16
NN = ((1,), (0,))
NT = ((1,), (1,))
NEG = -1e30


def dot(left, right, dims=NN):
    return lax.dot_general(left, right, (dims, ((), ())), preferred_element_type=F32)


def unit_of(value):
    center = value - jnp.mean(value, -1, keepdims=True)
    scale = lax.rsqrt(jnp.mean(center * center, -1, keepdims=True) + 1e-05)
    return center * scale, scale


def pull_of(grad, gain, unit, scale):
    pulled = grad * gain
    first = jnp.mean(pulled, -1, keepdims=True)
    second = jnp.mean(pulled * unit, -1, keepdims=True)
    return scale * (pulled - first - unit * second)


def col_sum(value):
    return jnp.sum(value, 0, keepdims=True)


def layer_kernel(
    inside,
    n_f,
    tokens, seg_in, small_given, cot_in, qkv_in, out_in, up_in, down_in,
    result, tgrad, gqkv, gout, gup, gdown, gsmall,
    tok, normed, inner, gmix, gbr,
    qkv_w, out_w, up_w, down_w,
    segs, small_f, small_s, params, bias_row,
    triple, probs, attended, starts, activ, dgelu,
    part, land_a, land_b,
    branch, middle, gmid, cot,
    gtri, gatt, dkt, dvt,
    gw_q0, gw_q1, gw_out, gw_up, gw_down,
    lp_q0, lp_q1, lp_out, lp_up, lp_down,
    lz_q0, lz_q1, lz_out, lz_up, lz_down,
    fin_qkv, land_qkv, small_sum,
    sg_s, sg_land_s, sg_f, sg_land_f,
    ag_send, ag_recv, rs_send, rs_recv,
    w_send, w_recv, p_send, p_recv,
    col_send, col_recv, col_local, upc_send, upc_recv,
    seg_send, seg_recv, sf_send, sf_recv, ss_send, ss_recv,
    loc_sem, o_sem,
    gp_send, gp_recv, gz_send, gz_recv,
    gc_send, gc_recv, gu_send, gu_recv,
    ts_send, ts_recv, tf_send, tf_recv, turn,
    small_raw, bias_raw, small_rows, small_tile, raw_sem,
):
    gw_qkv, lp_qkv, lz_qkv = (gw_q0, gw_q1), (lp_q0, lp_q1), (lz_q0, lz_q1)
    rows, width = tokens.shape
    half = rows // 2
    group = out_w.shape[1]
    pairs = group // 128
    window = probs.shape[3]
    s = lax.axis_index("seq")
    f = lax.axis_index("fsdp")
    x, y = s % 2, s // 2
    z, c = f // 2, f % 2

    def block(rel):
        return 2 * ((y + rel // 2) % 2) + (x + rel % 2) % 2

    sx, sy, sd = block(1), block(2), block(3)

    def remote(src, dst, send, recv, to_s, to_f):
        return pltpu.make_async_remote_copy(
            src_ref=src, dst_ref=dst, send_sem=send, recv_sem=recv,
            device_id=(to_s, to_f), device_id_type=pl.DeviceIdType.MESH,
        )

    def my_turn(cores=(0, 1)):
        if inside:
            @pl.when(c >= cores[0])
            def _():
                pl.semaphore_wait(turn, 1)

    def hand_over(cores=(0, 1)):
        if inside:
            @pl.when(c <= cores[1])
            def _():
                pl.semaphore_signal(
                    turn, inc=1, device_id=(s, 2 * z + 1 - c),
                    device_id_type=pl.DeviceIdType.MESH,
                )

    class Gather:
        def __init__(self, full, index):
            self.full, self.index = full, index

        def piece(self, b, h):
            return self.full.at[b, pl.ds(h * half, half)]

        def copy(self, i, b, h, to, src=None):
            dst = self.piece(b, h)
            return remote(
                dst if src is None else src, dst,
                ag_send.at[self.index, i], ag_recv.at[self.index, i], to, f,
            )

        def start(self, src=None):
            def cut(h):
                return None if src is None else src.at[pl.ds(h * half, half)]

            self.copy(0, s, 0, sx, cut(0)).start()
            self.copy(1, s, 1, sy, cut(1)).start()
            self.copy(2, s, 1, sx, cut(1)).start()
            self.copy(3, s, 0, sy, cut(0)).start()

        def relay(self):
            self.copy(0, sx, 0, sx).wait_recv()
            self.copy(4, sx, 0, sy).start()
            if self.index:
                hand_over()
            self.copy(1, sy, 1, sy).wait_recv()
            self.copy(5, sy, 1, sx).start()

        def wait_x(self):
            self.copy(2, sx, 1, sx).wait_recv()

        def wait_y(self):
            self.copy(3, sy, 0, sy).wait_recv()

        def wait_d(self):
            self.copy(4, sd, 0, sy).wait_recv()
            self.copy(5, sd, 1, sx).wait_recv()

        def step(self, k):
            @pl.when(k == 1)
            def _():
                self.relay()
                self.wait_x()

            @pl.when(k == 2)
            def _():
                self.wait_y()

            @pl.when(k == 3)
            def _():
                self.wait_d()

        def drain(self):
            for i, (b, h, to) in enumerate(
                ((s, 0, sx), (s, 1, sy), (s, 1, sx), (s, 0, sy), (sx, 0, sy), (sy, 1, sx))
            ):
                self.copy(i, b, h, to).wait_send()

    def half_rows(h):
        return pl.ds(pl.multiple_of(h * half, half), half)

    class Scatter:
        plan = ((3, 0, 1), (1, 0, 1), (3, 1, 2), (2, 1, 2), (2, 0, 2), (1, 1, 1))

        def __init__(self, land, index):
            self.land, self.index = land, index

        def copy(self, i):
            rel, h, way = self.plan[i]
            return remote(
                part.at[rel, pl.ds(h * half, half)], self.land.at[i],
                rs_send.at[self.index, i], rs_recv.at[self.index, i],
                sx if way == 1 else sy, f,
            )

        def step(self, rel):
            @pl.when(rel == 3)
            def _():
                self.copy(0).start()
                self.copy(2).start()

            @pl.when(rel == 1)
            def _():
                self.copy(1).start()

            @pl.when(rel == 2)
            def _():
                self.copy(3).start()

        def relay(self):
            for arrived, i in ((0, 4), (2, 5)):
                self.copy(arrived).wait_recv()
                rel, h, _ = self.plan[i]

                here = pl.ds(h * half, half)
                total = part[rel, here].astype(F32) + self.land[arrived].astype(F32)
                part[rel, here] = total.astype(BF16)
                self.copy(i).start()
            hand_over((0, 0) if self.index == 3 else (0, 1))

        def wait(self):
            for i in (1, 3, 4, 5):
                self.copy(i).wait_recv()

        def total(self, h):
            return (
                part[0, half_rows(h)].astype(F32)
                + self.land[1 + 2 * h].astype(F32)
                + self.land[4 + h].astype(F32)
            )

        def drain(self):
            for i in range(6):
                self.copy(i).wait_send()

    def by_rows(ref, size):
        def view(who):
            return ref.at[pl.ds(pl.multiple_of(who * size, size), size)]

        return view

    def by_cut(ref, size):
        def view(who):
            return ref.at[:, pl.ds(pl.multiple_of(who * size, size), size)]

        return view

    partner = 2 * z + 1 - c
    side = z // 2
    near = 4 * side + 1 - z
    mid_o, end_o = 2 - side, 3 - 3 * side
    is_mid = (z + side) % 2
    seen_as = 2 - is_mid
    owners = (near, mid_o, end_o)

    class Weight:
        def __init__(self, index, view):
            self.index, self.view = index, view

        def piece(self, to_z, i, k, owner_z, own=None):
            dst = self.view(2 * owner_z + c)
            return remote(
                dst if own is None else own, dst,
                w_send.at[self.index, i], w_recv.at[self.index, k], s, 2 * to_z + c,
            )

        def across(self, k, owner, own=None):
            dst = self.view(owner)
            return remote(
                dst if own is None else own, dst,
                p_send.at[self.index, k], p_recv.at[self.index, k], s, partner,
            )

        def start_far(self, own=None, across=True):
            self.piece(mid_o, 1, seen_as, z, own).start()
            if across:
                @pl.when(is_mid == 0)
                def _():
                    self.piece(near, 0, 0, z, own).start()

                self.across(3, f, own).start()

        def start_near(self, own=None, everyone=False):
            @pl.when((is_mid == 1) | everyone)
            def _():
                self.piece(near, 0, 0, z, own).start()

        def start(self, own=None):
            self.start_far(own)
            self.start_near(own)

        def relay(self, all_of_it=True):
            @pl.when(is_mid == 1)
            def _():
                for k in (1, 2):
                    self.piece(z, 0, k, owners[k]).wait_recv()
                    self.piece(near, 1 + k, k, owners[k]).start()
                for k in (1, 2):
                    self.across(k, 2 * owners[k] + c).start()

            if all_of_it:
                self.relay_rest()

        def relay_rest(self):
            @pl.when(is_mid == 1)
            def _():
                self.piece(z, 0, 0, near).wait_recv()
                self.across(0, 2 * near + c).start()

        def rest(self):
            @pl.when(is_mid == 0)
            def _():
                for k in (0, 1, 2):
                    self.piece(z, 0, k, owners[k]).wait_recv()
                    self.across(k, 2 * owners[k] + c).start()

        def finish(self):
            self.across(3, partner).wait_recv()
            for k in (0, 1, 2):
                self.across(k, 2 * owners[k] + 1 - c).wait_recv()

        def drain(self):
            self.piece(mid_o, 1, seen_as, z).wait_send()
            self.piece(near, 0, 0, z).wait_send()
            self.across(3, f).wait_send()

            @pl.when(is_mid == 1)
            def _():
                for k in (1, 2):
                    self.piece(near, 1 + k, k, owners[k]).wait_send()

            for k in (0, 1, 2):
                self.across(k, 2 * owners[k] + c).wait_send()

    class Shed:
        def __init__(self, index, gw, land_p, land_z):
            self.index, self.gw, self.land_p, self.land_z = index, gw, land_p, land_z

        def pair(self, to_z):
            return remote(
                self.gw.at[2 * to_z + 1 - c], self.land_p.at[to_z],
                gp_send.at[self.index, to_z], gp_recv.at[self.index, to_z], s, partner,
            )

        def along(self, i, to_z, of_z, slot):
            return remote(
                self.gw.at[2 * of_z + c], self.land_z.at[slot],
                gz_send.at[self.index, i], gz_recv.at[self.index, slot], s, 2 * to_z + c,
            )

        def add(self, who, land, slot):
            self.gw[who] = (self.gw[who].astype(F32) + land[slot].astype(F32)).astype(BF16)

        def add_pair(self, to_z):
            self.pair(to_z).wait_recv()
            self.add(2 * to_z + c, self.land_p, to_z)

        def far(self):
            for slot, of_z in ((1, mid_o), (2, end_o)):
                self.add_pair(of_z)

                @pl.when(is_mid == 0)
                def _(slot=slot, of_z=of_z):
                    self.along(slot, near, of_z, slot).start()

        def close(self):
            self.add_pair(near)
            self.along(0, near, near, 0).start()
            self.add_pair(z)

        def second(self):
            @pl.when(is_mid == 1)
            def _():
                for i, of_z in ((1, mid_o), (2, end_o)):
                    self.along(i, near, of_z, i).wait_recv()
                    self.add(2 * of_z + c, self.land_z, i)
                    self.along(i, of_z, of_z, 3).start()

        def wait(self):
            self.along(0, near, z, 0).wait_recv()
            self.along(1, near, z, 3).wait_recv()

        def total(self, at):
            value = self.gw[f, at].astype(F32)
            return value + self.land_z[0, at].astype(F32) + self.land_z[3, at].astype(F32)

        def drain(self):
            def one(to_z, _):
                self.pair(to_z).wait_send()
                return 0

            lax.fori_loop(0, n_f // 2, one, 0)
            for i in range(3):
                self.along(i, near, near, 0).wait_send()

    if inside:
        fetch = [
            pltpu.make_async_copy(ref, small_raw.at[i], raw_sem.at[i])
            for i, ref in enumerate(small_given[:8])
        ]
        fetch.append(pltpu.make_async_copy(small_given[8], bias_raw, raw_sem.at[8]))
        for one in fetch:
            one.start()

    barrier = pltpu.get_barrier_semaphore()
    for who in (sx, sy, sd):
        pl.semaphore_signal(barrier, inc=1, device_id=(who, f), device_id_type=pl.DeviceIdType.MESH)
    n_peers = 3
    if inside:
        for d in range(1, n_f):
            pl.semaphore_signal(
                barrier, inc=1, device_id=(s, (f + d) % n_f), device_id_type=pl.DeviceIdType.MESH
            )
        n_peers += n_f - 1
    if inside:
        for one in fetch:
            one.wait()
        for i in range(8):
            small_rows[i : i + 1, :] = small_raw[i].astype(F32)
        tall = small_rows.shape[1]
        lanes = lax.broadcasted_iota(jnp.int32, (tall, 128), 1)
        places = lax.broadcasted_iota(jnp.int32, (tall, 128), 0) + (f % (128 // tall)) * tall
        chosen = jnp.where(lanes == places, 1.0, 0.0).astype(BF16)
        small_in = small_tile
        small_in[0:8] = dot(small_rows[...].astype(BF16), chosen)
        small_in[8:9] = bias_raw[...].astype(F32)
    else:
        small_in = small_given[0]
    pl.semaphore_wait(barrier, n_peers)

    others = (sx, sy, sd)
    ag_tok = Gather(tok, 0)
    if inside:
        high = qkv_in.shape[0]
        high_d = down_in.shape[0]
        w_qkv = [
            Weight(0, by_cut(qkv_w.at[0:2], high)), Weight(4, by_cut(qkv_w.at[2:4], high))
        ]
        w_out = Weight(1, by_rows(out_w.at[0], high))
        w_up = Weight(2, by_cut(up_w, high))
        w_down = Weight(3, by_rows(down_w, high_d))

        def qkv_copy(k, p, to):
            start = pl.multiple_of((p % 3) * width + to * group + (p // 3) * 128, 128)
            src = qkv_in.at[:, pl.ds(start, 128)]
            dst = qkv_w.at[s, pl.ds(pl.multiple_of(f * high, high), high), pl.ds(p * 128, 128)]
            if k < 0:
                return pltpu.make_async_copy(src, dst, col_local.at[p])
            return remote(src, dst, col_send.at[k, p], col_recv.at[k, p], to, f)

        n_cut = 3 * pairs

        ff = up_w.shape[2]

        def up_copy(k, to):
            src = up_in.at[:, pl.ds(pl.multiple_of(to * ff, 128), ff)]
            dst = up_w.at[s, pl.ds(pl.multiple_of(f * high, high), high)]
            if k < 0:
                return pltpu.make_async_copy(src, dst, loc_sem.at[6])
            return remote(src, dst, upc_send.at[k], upc_recv.at[k], to, f)

        out_own = pltpu.make_async_copy(out_in, w_out.view(f), loc_sem.at[0])
        down_own = pltpu.make_async_copy(down_in, w_down.view(f), loc_sem.at[1])

        def small_copy(d):
            return remote(
                small_in, small_f.at[f], sf_send.at[d], sf_recv.at[d], s, (f + d) % n_f
            )

        for d in range(1, n_f):
            small_copy(d).start()
        for p in range(n_cut):
            for k, to in enumerate(others):
                qkv_copy(k, p, to).start()
        ag_tok.start(tokens)
        for p in range(n_cut):
            qkv_copy(-1, p, s).start()
        up_copy(-1, s).start()
        out_own.start()
        down_own.start()
        small_f[f] = small_in[...]
    else:
        loads = [
            pltpu.make_async_copy(qkv_in, qkv_w, col_local.at[0]),
            pltpu.make_async_copy(up_in, up_w, loc_sem.at[6]),
            pltpu.make_async_copy(out_in, out_w, loc_sem.at[0]),
            pltpu.make_async_copy(down_in, down_w, loc_sem.at[1]),
        ]
        for load in loads:
            load.start()
    tok_own = pltpu.make_async_copy(tokens, tok.at[s], loc_sem.at[2])
    tok_own.start()
    cot_own = pltpu.make_async_copy(cot_in, cot, loc_sem.at[3])
    cot_own.start()
    seg_own = pltpu.make_async_copy(seg_in, segs.at[s], loc_sem.at[4])
    seg_own.start()

    def seg_copy(k, to):
        return remote(seg_in, segs.at[s], seg_send.at[k], seg_recv.at[k], to, f)

    for k, to in enumerate(others):
        seg_copy(k, to).start()

    if inside:
        for d in range(1, n_f):
            remote(
                small_in, small_f.at[(f + n_f - d) % n_f], sf_send.at[d], sf_recv.at[d],
                s, (f + d) % n_f,
            ).wait_recv()
        per = n_f * high // 128
        each = n_f // per
        for t in range(per):
            value = small_f[t * each, 0:8]
            for e in range(1, each):
                value = value + small_f[t * each + e, 0:8]
            small_s[s, t] = value
        for e in range(n_f):
            bias_row[0:1, pl.ds(e * 128, 128)] = small_f[e, 8:9]

        def small_wide(k, to):
            return remote(small_s.at[s], small_s.at[s], ss_send.at[k], ss_recv.at[k], to, f)

        for k, to in enumerate(others):
            small_wide(k, to).start()
        for p in range(n_cut):
            qkv_copy(-1, p, s).wait()
            for k, to in enumerate(others):
                qkv_copy(k, p, to).wait_recv()
        for weight in w_qkv:
            weight.start_far(across=False)
        for weight in w_qkv:
            weight.start_near(everyone=True)
            weight.across(3, f).start()
        w_out.start(out_in)
        w_down.start_far(down_in)
    else:
        ag_tok.start(tokens)
        params[...] = small_in[0:8]
        bias_row[...] = small_in[8:9, 0 : bias_row.shape[1]]

    zero_row = jnp.zeros((1, width), F32)

    def both(run, count):
        def step(h, carry):
            return tuple(a + b for a, b in zip(carry, run(h)))

        return lax.fori_loop(0, 2, step, (zero_row,) * count)

    def far_first(i):
        return (1 - i // 2) + 2 * (1 - i % 2)

    def param(i):
        return params[i : i + 1, :]

    tok_own.wait()
    if inside:
        w_qkv[0].relay()
    ag_tok.relay()
    if inside:
        for k, to in enumerate(others):
            up_copy(k, to).start()
        w_qkv[1].relay()
        w_out.relay(False)
        w_down.start_near(down_in)
        for k, who in enumerate(others):
            remote(
                small_s.at[who], small_s.at[who], ss_send.at[k], ss_recv.at[k], who, f
            ).wait_recv()
        for b in range(4):
            for t in range(per):
                params[:, pl.ds((b * per + t) * 128, 128)] = small_s[b, t]

    def first_norm(b):
        unit, _s = unit_of(tok[b].astype(F32))
        normed[b] = (unit * param(0) + param(1)).astype(BF16)

    def norm_step(k, _):
        @pl.when(k == 1)
        def _():
            ag_tok.wait_x()

        @pl.when(k == 2)
        def _():
            ag_tok.wait_y()

        @pl.when(k == 3)
        def _():
            ag_tok.wait_d()

        first_norm(block(k))
        return 0

    lax.fori_loop(0, 3, norm_step, 0)
    if inside:
        for weight in w_qkv:
            weight.rest()
    lax.fori_loop(3, 4, norm_step, 0)
    if inside:
        for weight in w_qkv:
            weight.finish()

    rest = normed[...].reshape(4 * rows, width)
    for p in range(pairs):
        value = dot(rest, qkv_w[:, :, p * 384 : (p + 1) * 384].reshape(width, 384))
        for q in range(3):
            piece = value[:, q * 128 : (q + 1) * 128]
            piece = piece if q else piece * 0.125
            at = slice((3 * p + q) * 128, (3 * p + q + 1) * 128)
            triple[:, :, at] = piece.astype(BF16).reshape(4, rows, 128)

    if inside:
        up_copy(-1, s).wait()
        for k, to in enumerate(others):
            up_copy(k, to).wait_recv()
        w_up.start_far()
        w_up.start_near()

    seg_own.wait()
    for k, who in enumerate(others):
        remote(seg_in, segs.at[who], seg_send.at[k], seg_recv.at[k], who, f).wait_recv()
    seg_all = segs[...]

    def below(level):
        count = jnp.sum((seg_all < level).astype(F32), axis=0)
        return jnp.sum(count, axis=1, keepdims=True)

    bound_1, bound_2 = below(1), below(2)
    blocks = window // rows
    lane = lax.broadcasted_iota(jnp.int32, (1, 128), 1)
    left = (lane < HEAD_DIM).astype(F32)
    sides = (left.astype(BF16), (1.0 - left).astype(BF16))
    pick = lax.broadcasted_iota(jnp.int32, (rows, 128), 1) < HEAD_DIM

    def set_starts(r, _):
        i = (r * rows + lax.broadcasted_iota(jnp.int32, (rows, 128), 0)).astype(F32)
        starts[r] = jnp.where(i >= bound_2, bound_2, jnp.where(i >= bound_1, bound_1, 0.0))
        return 0

    lax.fori_loop(0, 4, set_starts, 0)

    def cut(r, part_at, p, count):
        at = pl.ds(pl.multiple_of((3 * p + part_at) * 128, 128), 128)
        return triple[pl.ds(r, count), :, at].reshape(count * rows, 128)

    def masked(scores, r, first, count):
        start = starts[r]
        tiles = []
        for t in range(count * rows // 128):
            j = lax.broadcasted_iota(jnp.int32, (rows, 128), 1) + t * 128
            keep = (first * rows + j).astype(F32) >= start
            if t * 128 >= (count - 1) * rows:
                i = lax.broadcasted_iota(jnp.int32, (rows, 128), 0)
                keep = keep & (j - (count - 1) * rows <= i)
            tiles.append(jnp.where(keep, scores[:, t * 128 : (t + 1) * 128], NEG))
        return jnp.concatenate(tiles, axis=1)

    rs_1 = Scatter(land_a, 0)

    def attend_heads(r, first, count):
        scores, values = [], []
        for p in range(pairs):
            query, keys = cut(r, 0, p, 1), cut(first, 1, p, count)
            for e in range(2):
                scores.append(masked(dot(query * sides[e], keys, NT), r, first, count))
                values.append(cut(first, 2, p, count))
        tops = [jnp.max(score, -1, keepdims=True) for score in scores]
        expos = [jnp.exp(score - top) for score, top in zip(scores, tops)]
        sums = [jnp.sum(expo, -1, keepdims=True) for expo in expos]
        lows = [(expo * (1.0 / total)).astype(BF16) for expo, total in zip(expos, sums)]
        for n, low in enumerate(lows):
            probs[r, n, :, 0 : count * rows] = low
        outs = [dot(low, value) for low, value in zip(lows, values)]
        for p in range(pairs):
            both_sides = jnp.where(pick, outs[2 * p], outs[2 * p + 1])
            attended[r, :, p * 128 : (p + 1) * 128] = both_sides.astype(BF16)

    def attend(i, _):
        rel = far_first(i)
        r = block(rel)
        for count in range(1, blocks + 1):
            @pl.when(r + 1 >= count if count == blocks else r + 1 == count)
            def _(count=count):
                attend_heads(r, r + 1 - count, count)

        if inside:
            @pl.when(i == 0)
            def _():
                out_own.wait()
                w_out.finish()

        part[rel] = dot(attended[r], out_w[0]).astype(BF16)

        @pl.when(c == 0)
        def _():
            rs_1.step(rel)

        @pl.when((c == 1) & (i == 2))
        def _():
            rs_1.step(3)

        if inside:
            @pl.when(i == 1)
            def _():
                w_down.relay()

        return 0

    if inside:
        w_out.relay_rest()
        w_out.rest()
    lax.fori_loop(0, 4, attend, 0)

    my_turn((1, 1))

    @pl.when(c == 1)
    def _():
        for i in (1, 3):
            rs_1.copy(i).start()

    rs_1.relay()
    if inside:
        w_up.relay()

        @pl.when(c == 1)
        def _():
            w_down.rest()

    rs_1.wait()

    def mid_norm(h):
        at = half_rows(h)
        value = rs_1.total(h)
        branch[at] = value
        unit, _s = unit_of(value)
        mid = tok[s, at].astype(F32) + (unit * param(2) + param(3))
        middle[at] = mid
        unit, _s = unit_of(mid)
        inner[s, at] = (unit * param(4) + param(5)).astype(BF16)

    for h in range(2):
        mid_norm(h)
    ag_inner = Gather(inner, 1)
    my_turn()
    ag_inner.start()
    rs_1.drain()
    if inside:
        @pl.when(c == 1)
        def _():
            w_up.rest()

    ag_inner.relay()
    if inside:
        @pl.when(c == 0)
        def _():
            w_down.rest()
            w_up.rest()

        w_up.finish()

    ff = up_w.shape[2]
    tile = ff
    rs_2 = Scatter(land_b, 1)

    def forward_step(k, _):
        @pl.when(k == 1)
        def _():
            ag_inner.wait_x()

        @pl.when(k > 1)
        def _():
            ag_inner.step(k)

        r = block(k)

        def column(n, _):
            at = pl.ds(pl.multiple_of(n * tile, tile), tile)
            pre = dot(inner[r], up_w[:, :, at].reshape(width, tile)) + bias_row[:, at]
            square = pre * pre
            bend = jnp.tanh(0.7978845608028654 * pre * (1.0 + 0.044715 * square))
            near = 0.5 + 0.5 * bend
            activ[r, :, at] = (pre * near).astype(BF16)
            slope = near + pre * (0.5 - 0.5 * bend * bend) * (
                0.7978845608028654 + 0.10703222440890037 * square
            )
            dgelu[r, :, at] = slope.astype(BF16)
            return 0

        lax.fori_loop(0, ff // tile, column, 0)
        return 0

    lax.fori_loop(0, 4, forward_step, 0)
    if inside:
        down_own.wait()
        w_down.finish()

    def down_step(i, _):
        rel = far_first(i)
        r = block(rel)

        part[rel] = dot(activ[r], down_w[...]).astype(BF16)
        rs_2.step(rel)
        return 0

    my_turn()
    lax.fori_loop(0, 4, down_step, 0)
    rs_2.relay()
    cot_own.wait()
    rs_2.wait()

    def last_norm(h):
        at = half_rows(h)
        unit, scale = unit_of(rs_2.total(h))
        gbr[s, at] = (middle[at] + (unit * param(6) + param(7))).astype(BF16)
        grad = cot[at].astype(F32)
        gmix[s, at] = pull_of(grad, param(6), unit, scale).astype(BF16)
        return col_sum(grad * unit), col_sum(grad)

    grad_gain_d, grad_shift_d = both(last_norm, 2)
    sg_rows = [None] * 8
    sg_rows[6], sg_rows[7] = grad_gain_d, grad_shift_d
    ag_mix = Gather(gmix, 2)
    my_turn()
    ag_mix.start()
    result_out = pltpu.make_async_copy(gbr.at[s], result, o_sem.at[2])
    result_out.start()
    rs_2.drain()

    rs_3 = Scatter(land_a, 2)
    sg_bias = bias_row

    def clear(n, _):
        at = pl.ds(pl.multiple_of(n * tile, tile), tile)
        sg_bias[:, at] = jnp.zeros((1, tile), F32)
        return 0

    lax.fori_loop(0, ff // tile, clear, 0)

    TN = ((0,), (0,))

    def flat(ref, lanes=slice(None)):
        held = ref[:, :, lanes]
        return held.reshape(4 * rows, held.shape[2])

    def all_pairs(shed):
        for to_z in range(n_f // 2):
            shed.pair(to_z).start()

    def cut_grads(left, right, gw, shed, lanes=slice(None)):
        for b in range(4):
            value = dot(flat(left, slice(b * rows, (b + 1) * rows)), flat(right, lanes), TN)
            gw[:, b * high : (b + 1) * high, :] = value.astype(BF16).reshape(n_f, high, -1)
        all_pairs(shed)

    def down_grads(rels):
        each = ff // n_f
        count = 256 // each
        for b in range(n_f // count):
            at = slice(b * count, (b + 1) * count)
            cols = slice(b * 256, (b + 1) * 256)
            value = dot(activ[block(rels[0]), :, cols], gmix[block(rels[0])], TN)
            for rel in rels[1:]:
                value = value + dot(activ[block(rel), :, cols], gmix[block(rel)], TN)
            if len(rels) == 1:
                value = value + gw_down[at].astype(F32).reshape(256, width)
            gw_down[at] = value.astype(BF16).reshape(count, each, width)

    if inside:
        shed_down = Shed(0, gw_down, lp_down, lz_down)
        shed_up = Shed(1, gw_up, lp_up, lz_up)
        shed_out = Shed(2, gw_out, lp_out, lz_out)
        shed_qkv = [
            Shed(3 + p, gw_qkv[p], lp_qkv[p], lz_qkv[p])
            for p in range(pairs)
        ]
        ag_tok.drain()

    def back_step(k, _):
        if inside:
            @pl.when(k == 3)
            def _():
                down_grads((0, 1, 2))

        ag_mix.step(k)
        r = block(k)

        def column(n, _):
            at = pl.ds(pl.multiple_of(n * tile, tile), tile)
            grad = dot(gmix[r], down_w[at], NT)
            low = (dgelu[r, :, at].astype(F32) * grad).astype(BF16)
            dgelu[r, :, at] = low
            sg_bias[:, at] = sg_bias[:, at] + col_sum(low.astype(F32))
            return 0

        lax.fori_loop(0, ff // tile, column, 0)
        return 0

    lax.fori_loop(0, 4, back_step, 0)

    if inside:
        down_grads((3,))
        all_pairs(shed_down)

        @pl.when(c == 1)
        def _():
            shed_down.far()

    def inner_step(i, _):
        rel = far_first(i)
        r = block(rel)

        part[rel] = dot(dgelu[r], up_w[...].reshape(width, ff), NT).astype(BF16)
        rs_3.step(rel)
        return 0

    my_turn()
    lax.fori_loop(0, 4, inner_step, 0)

    if inside:
        cut_grads(inner, dgelu, gw_up, shed_up)
    rs_3.relay()
    if inside:
        @pl.when(c == 1)
        def _():
            shed_up.far()
            shed_down.close()
            shed_up.close()

        @pl.when(c == 0)
        def _():
            shed_down.far()

    rs_3.wait()

    result_out.wait()

    def mid_back(h):
        at = half_rows(h)
        grad = rs_3.total(h)
        unit, scale = unit_of(middle[at])
        total = cot[at].astype(F32) + pull_of(grad, param(4), unit, scale)
        gmid[at] = total
        out = [col_sum(grad * unit), col_sum(grad)]
        unit, scale = unit_of(branch[at])
        gbr[s, at] = pull_of(total, param(2), unit, scale).astype(BF16)
        return out[0], out[1], col_sum(total * unit), col_sum(total)

    sg_rows[4], sg_rows[5], sg_rows[2], sg_rows[3] = both(mid_back, 4)
    ag_br = Gather(gbr, 3)
    my_turn()
    ag_br.start()
    rs_3.drain()
    def arrive(k, _):
        if inside:
            @pl.when(k == 1)
            def _():
                ag_br.relay()

            @pl.when((k == 1) & (c == 0))
            def _():
                shed_up.far()
                shed_down.close()
                shed_up.close()

            @pl.when(k == 1)
            def _():
                ag_br.wait_x()

            @pl.when(k > 1)
            def _():
                ag_br.step(k)

            @pl.when(k == 2)
            def _():
                shed_down.second()
        else:
            ag_br.step(k)

        r = block(k)
        gatt[r] = dot(gbr[r], out_w[0], NT).astype(BF16)
        if inside:
            value = dot(attended[r], gbr[r], TN)

            @pl.when(k == 0)
            def _():
                branch[...] = value

            @pl.when(k > 0)
            def _():
                branch[...] = branch[...] + value

        return 0

    lax.fori_loop(0, 4, arrive, 0)
    if inside:
        gw_out[...] = branch[...].astype(BF16).reshape(gw_out.shape)
        all_pairs(shed_out)

        @pl.when(c == 1)
        def _():
            shed_out.far()
            shed_out.close()

    if inside:
        per = n_f * high // 128
        fin_down = branch.at[0:high_d]
        fin_out = branch.at[high_d : high_d + high]
        gdown_out = pltpu.make_async_copy(fin_down, gdown, o_sem.at[3])
        gout_out = pltpu.make_async_copy(fin_out, gout, o_sem.at[4])

        def rows_at(n):
            return pl.ds(pl.multiple_of(n * high, high), high)

        gup_out = [
            pltpu.make_async_copy(
                middle.at[rows_at(b)], gup.at[:, b * ff : (b + 1) * ff], o_sem.at[8 + b]
            )
            for b in range(4)
        ]
        gqkv_out = [
            pltpu.make_async_copy(
                middle.at[rows_at(4 + p)], gqkv.at[:, p * width : (p + 1) * width],
                o_sem.at[12 + p],
            )
            for p in range(3)
        ]
        gsmall_out = pltpu.make_async_copy(small_sum, gsmall, o_sem.at[7])

        def ts_copy(k, to):
            return remote(sg_s.at[to], sg_land_s.at[k], ts_send.at[k], ts_recv.at[k], to, f)

        def tf_copy(d):
            to = (f + d) % n_f
            return remote(
                sg_f.at[to], sg_land_f.at[d - 1], tf_send.at[d], tf_recv.at[d], s, to
            )

        def small_first():
            for b in range(4):
                for t in range(per):
                    at = slice((b * per + t) * 128, (b * per + t + 1) * 128)
                    for i in range(8):
                        sg_s[b, t, i : i + 1, :] = sg_rows[i][:, at]
            for k, to in enumerate(others):
                ts_copy(k, to).start()

        def small_second():
            for k, to in enumerate(others):
                ts_copy(k, to).wait_recv()
            for who in range(n_f):
                t = who * high // 128
                sg_f[who, 0:8] = (
                    sg_s[s, t] + sg_land_s[0, t] + sg_land_s[1, t] + sg_land_s[2, t]
                )
                sg_f[who, 8:9] = sg_bias[:, who * 128 : (who + 1) * 128]
            for d in range(1, n_f):
                tf_copy(d).start()

        def small_third():
            for d in range(1, n_f):
                tf_copy(d).wait_recv()
            value = sg_f[f]
            for d in range(1, n_f):
                value = value + sg_land_f[d - 1]
            small_sum[...] = value
            gsmall_out.start()

        def gu_copy(k, to, who):
            return remote(
                cot.at[rows_at(to)], cot.at[rows_at(4 + who)],
                gu_send.at[k], gu_recv.at[k], to, f,
            )

        def put_qkv(q, who, value):
            lanes = pl.ds(pl.multiple_of(who * group + q * 128, 128), 128)
            for p in range(3):
                piece = value[:, p * 128 : (p + 1) * 128]
                middle[rows_at(4 + p), lanes] = piece.astype(F32)

        def gc_copy(k, p, to, who):
            return remote(
                fin_qkv.at[p, to], land_qkv.at[p, who],
                gc_send.at[k, p], gc_recv.at[k, p], to, f,
            )

    def back_rows(p, r_group):
        lanes = slice(p * 128, (p + 1) * 128)
        items = []
        for r in r_group:
            first = max(r + 1 - blocks, 0)
            count = r + 1 - first
            query, grad = cut(r, 0, p, 1), gatt[r, :, lanes]
            keys, vals = cut(first, 1, p, count), cut(first, 2, p, count)
            for e in range(2):
                low = probs[r, 2 * p + e, :, 0 : count * rows]
                items.append((r, e, first, count, query, keys, grad, low, vals))
        pulled = [dot(grad * sides[e], vals, NT) for _, e, _, _, _, _, grad, _, vals in items]
        sums = [
            jnp.sum(item[7].astype(F32) * pull, -1, keepdims=True)
            for item, pull in zip(items, pulled)
        ]
        slopes = [
            (item[7].astype(F32) * (pull - total)).astype(BF16)
            for item, pull, total in zip(items, pulled, sums)
        ]
        for n in range(0, len(items), 2):
            r, _, first, count, query, keys, grad, _, _ = items[n]
            query_t, grad_t = query.T, grad.T
            outs = [dot(slopes[n + e], keys) for e in range(2)]
            for e in range(2):
                side = slice(e * HEAD_DIM, (e + 1) * HEAD_DIM)
                here = slice(p * 128 + e * HEAD_DIM, p * 128 + (e + 1) * HEAD_DIM)
                key_part = dot(query_t[side], slopes[n + e])
                value_part = dot(grad_t[side], items[n + e][7])
                for m in range(count):
                    span = slice((first + m) * rows, (first + m + 1) * rows)
                    cols = slice(m * rows, (m + 1) * rows)
                    if r == 3 or (first + m) < 4 - blocks and r == first + m + blocks - 1:
                        dkt[here, span] = key_part[:, cols]
                        dvt[here, span] = value_part[:, cols]
                    else:
                        dkt[here, span] = dkt[here, span] + key_part[:, cols]
                        dvt[here, span] = dvt[here, span] + value_part[:, cols]
            at = slice(3 * p * 128, (3 * p + 1) * 128)
            gtri[r, :, at] = (jnp.where(pick, outs[0], outs[1]) * 0.125).astype(BF16)

    def back_pair(p):
        lanes = slice(p * 128, (p + 1) * 128)
        for r_group in ((3, 2), (1, 0)):
            back_rows(p, r_group)
            if inside and p and r_group[0] == 3:
                @pl.when(c == 0)
                def _():
                    shed_out.far()
                    shed_out.close()

        for b in range(4):
            span = slice(b * rows, (b + 1) * rows)
            at = slice((3 * p + 1) * 128, (3 * p + 2) * 128)
            gtri[b, :, at] = dkt[lanes, span].astype(BF16).T
            at = slice((3 * p + 2) * 128, (3 * p + 3) * 128)
            gtri[b, :, at] = dvt[lanes, span].astype(BF16).T

    def qkv_grads(p):
        cut_grads(normed, gtri, gw_qkv[p], shed_qkv[p], slice(p * 384, (p + 1) * 384))

    for p in range(pairs):
        back_pair(p)
        if inside and p == 0:
            qkv_grads(p)
            shed_up.second()

            @pl.when(c == 1)
            def _():
                shed_qkv[0].far()

    if inside:
        @pl.when(c == 1)
        def _():
            qkv_grads(1)
            shed_qkv[1].far()
            for shed in shed_qkv:
                shed.close()
            shed_out.second()

        @pl.when(c == 0)
        def _():
            shed_qkv[0].far()

    rs_4 = Scatter(land_b, 3)

    def normed_step(i, carry):
        rel = far_first(i)
        r = block(rel)
        grad = dot(gtri[r], qkv_w[...].reshape(width, 3 * group), NT)
        part[rel] = grad.astype(BF16)
        rs_4.step(rel)
        unit, _s = unit_of(tok[r].astype(F32))
        return carry[0] + col_sum(grad * unit), carry[1] + col_sum(grad)

    my_turn()
    sg_rows[0], sg_rows[1] = lax.fori_loop(0, 4, normed_step, (zero_row, zero_row))
    if inside:
        small_first()

        @pl.when(c == 0)
        def _():
            qkv_grads(1)

        @pl.when(c == 1)
        def _():
            shed_qkv[0].second()

    rs_4.relay()
    if inside:
        @pl.when(c == 0)
        def _():
            shed_qkv[1].far()
            for shed in shed_qkv:
                shed.close()

        @pl.when(c == 0)
        def _():
            shed_out.second()
            shed_qkv[0].second()

        shed_qkv[1].second()
        small_second()
        at = pl.ds(pl.multiple_of(s * high, high), high)
        shed_up.wait()
        for b in range(4):
            cot[rows_at(b)] = shed_up.total(slice(b * high, (b + 1) * high)).astype(BF16)
        middle[rows_at(s)] = shed_up.total(at)

        def give_up():
            for k, to in enumerate(others):
                gu_copy(k, to, s).start()

        @pl.when(c == 1)
        def _():
            give_up()

        shed_down.wait()
        fin_down[...] = shed_down.total(slice(None))
        gdown_out.start()

        def give_qkv(q):
            shed = shed_qkv[q]
            shed.wait()
            for b in range(4):
                fin_qkv[q, b] = shed.total(slice(b * high, (b + 1) * high)).astype(BF16)
            for k, to in enumerate(others):
                gc_copy(k, q, to, s).start()
            put_qkv(q, s, shed.total(at))

        @pl.when(c == 1)
        def _():
            give_qkv(0)
            give_qkv(1)

    rs_4.wait()

    def first_back(h, _):
        at = half_rows(h)
        unit, scale = unit_of(tok[s, at].astype(F32))
        gmid[at] = gmid[at] + pull_of(rs_4.total(h), param(0), unit, scale)
        pltpu.make_async_copy(gmid.at[at], tgrad.at[at], o_sem.at[h]).start()
        return 0

    lax.fori_loop(0, 2, first_back, 0)
    if inside:
        @pl.when(c == 0)
        def _():
            give_up()
            give_qkv(0)
            give_qkv(1)

        for k, who in enumerate(others):
            gu_copy(k, who, who).wait_recv()
            middle[rows_at(who)] = cot[rows_at(4 + who)].astype(F32)
        for one in gup_out:
            one.start()
        shed_out.wait()
        fin_out[...] = shed_out.total(slice(None))
        gout_out.start()
        small_third()
        for k, who in enumerate(others):
            for q in range(pairs):
                gc_copy(k, q, who, who).wait_recv()
                put_qkv(q, who, land_qkv[q, who])
        for one in gqkv_out:
            one.start()

    for h in range(2):
        pltpu.make_async_copy(gmid.at[half_rows(h)], tgrad.at[half_rows(h)], o_sem.at[h]).wait()
    if inside:
        gsmall_out.wait()
        gdown_out.wait()
        gout_out.wait()
        for one in (*gup_out, *gqkv_out):
            one.wait()
        for k, to in enumerate(others):
            gu_copy(k, to, s).wait_send()
            ts_copy(k, to).wait_send()
            for q in range(pairs):
                gc_copy(k, q, to, s).wait_send()
            for p in range(n_cut):
                qkv_copy(k, p, to).wait_send()
            up_copy(k, to).wait_send()
            small_wide(k, to).wait_send()
        for d in range(1, n_f):
            tf_copy(d).wait_send()
            small_copy(d).wait_send()
        for weight in (*w_qkv, w_out, w_up, w_down):
            weight.drain()
        for shed in (shed_down, shed_up, shed_out, *shed_qkv):
            shed.drain()
    else:
        for i in range(8):
            small_sum[i : i + 1, :] = sg_rows[i]
        small_sum[8:9, 0:ff] = sg_bias[...]
        gsmall_out = pltpu.make_async_copy(small_sum, gsmall, o_sem.at[7])
        gsmall_out.start()
        gsmall_out.wait()
    for k, to in enumerate(others):
        seg_copy(k, to).wait_send()
    for gather in (ag_inner, ag_mix, ag_br) + (() if inside else (ag_tok,)):
        gather.drain()
    rs_4.drain()


def finish_kernel(n_f, n_big, *refs):
    small, given = refs[0], refs[1 : 1 + n_big]
    made, minor = refs[1 + n_big : 1 + 2 * n_big], refs[1 + 2 * n_big : 10 + 2 * n_big]
    held, (in_sem, out_sem) = refs[10 + 2 * n_big : 10 + 3 * n_big], refs[10 + 3 * n_big :]
    cuts = []
    for i in range(n_big):
        tall = given[i].shape[0]
        for j in range(max(1, tall // 64)):
            at = pl.ds(j * min(tall, 64), min(tall, 64))
            cuts.append((i, at, len(cuts)))
    for i, at, n in cuts:
        pltpu.make_async_copy(given[i].at[at], held[i].at[at], in_sem.at[n]).start()
    each = minor[0].shape[1]
    place = lax.axis_index("fsdp") % (128 // each)
    for i in range(8):
        row = small[i : i + 1, :]
        value = row[:, 0:each]
        for q in range(1, 128 // each):
            value = jnp.where(place == q, row[:, q * each : (q + 1) * each], value)
        minor[i][...] = value
    minor[8][...] = small[8:9, :]
    for i, at, n in cuts:
        pltpu.make_async_copy(given[i].at[at], held[i].at[at], in_sem.at[n]).wait()
        pltpu.make_async_copy(held[i].at[at], made[i].at[at], out_sem.at[n]).start()
    for i, at, n in cuts:
        pltpu.make_async_copy(held[i].at[at], made[i].at[at], out_sem.at[n]).wait()


def finish(n_f, high, *made):
    big, small = made[:6], made[6]
    whole, anywhere = pl.BlockSpec(memory_space=pltpu.VMEM), pl.BlockSpec(memory_space=pl.ANY)
    count = sum(max(1, v.shape[0] // 64) for v in big)
    minor = [jax.ShapeDtypeStruct((1, high), F32)] * 8 + [jax.ShapeDtypeStruct((1, 128), F32)]
    out = pl.pallas_call(
        partial(finish_kernel, n_f, 6),
        out_shape=[jax.ShapeDtypeStruct(v.shape, v.dtype) for v in big] + minor,
        in_specs=[whole] + [anywhere] * 6,
        out_specs=[anywhere] * 6 + [whole] * 9,
        scratch_shapes=[pltpu.VMEM(v.shape, v.dtype) for v in big]
        + [pltpu.SemaphoreType.DMA((count,))] * 2,
    )(small, *big)
    result, tgrad, gqkv, gout, gup, gdown = out[:6]
    small = [v[0] for v in out[6:]]
    return (result[None], tgrad[None], gqkv, gout, gup, small[8], gdown, *small[:8])


def on_device(n_seq, n_f, *args):
    (tokens, segments, qkv_weight, out_weight, up_weight, up_bias, down_weight) = args[:7]
    vectors, cotangent = args[7:15], args[15]
    rows, width = tokens.shape[1:]
    high, high_d = qkv_weight.shape[0], down_weight.shape[0]
    length = n_seq * rows
    group = qkv_weight.shape[1] // 3 // n_seq
    heads = group // HEAD_DIM
    ff = up_weight.shape[1] // n_seq
    half = rows // 2
    window = rows * min(n_seq, 1 + -(-511 // rows))
    inside = n_f == 8 and high % 32 == 0 and ff == width and 8 * high <= rows
    f = lax.axis_index("fsdp")
    if inside:
        small = [v[None] for v in (*vectors, up_bias)]
        weights = (qkv_weight, out_weight, up_weight, down_weight)
    else:
        small = jnp.stack([v.astype(F32) for v in vectors])
        small = lax.all_gather(small, ("seq", "fsdp"), axis=1, tiled=True)
        bias = lax.all_gather(up_bias.astype(F32), "fsdp", axis=0, tiled=True)
        bias = jnp.pad(bias[None], ((0, 7), (0, width - ff)))
        small = [jnp.concatenate([small, bias])]

        def columns(weight, parts):
            cut = weight.reshape(high, parts, n_seq, -1, 128).transpose(2, 0, 3, 1, 4)
            cut = cut.reshape(n_seq, high, -1)
            cut = lax.all_to_all(cut, "seq", split_axis=0, concat_axis=0, tiled=True)
            return lax.all_gather(cut, "fsdp", axis=1, tiled=True)

        weights = (
            columns(qkv_weight, 3),
            lax.all_gather(out_weight, "fsdp", axis=0, tiled=True)[None],
            columns(up_weight, 1),
            lax.all_gather(down_weight, "fsdp", axis=0, tiled=True),
        )
    vmem, anywhere, dma = pltpu.VMEM, pl.BlockSpec(memory_space=pl.ANY), pltpu.SemaphoreType.DMA
    whole = pl.BlockSpec(memory_space=pltpu.VMEM)
    full = (4, rows, width)
    saved = {
        "normed": (full, BF16), "inner": (full, BF16), "gmix": (full, BF16), "gbr": (full, BF16),
        "attended": ((4, rows, group), BF16), "activ": ((4, rows, ff), BF16),
        "dgelu": ((4, rows, ff), BF16), "gtri": ((4, rows, 3 * group), BF16),
    }
    n_cut = 3 * (group // 128)
    pieces = {"q0": (n_seq * high, 384), "q1": (n_seq * high, 384), "out": (high, width),
              "up": (n_seq * high, ff), "down": (high_d, width)}
    scratch = {
        "tok": vmem(full, BF16), "normed": None, "inner": None, "gmix": None, "gbr": None,
        "qkv_w": vmem((n_seq, rows, 3 * group), BF16), "out_w": vmem((1, group, width), BF16),
        "up_w": vmem((n_seq, rows, ff), BF16), "down_w": vmem((ff, width), BF16),
        "segs": vmem((4, 1, rows), jnp.int32),
        "small_f": vmem((n_f if inside else 1, 16, 128), F32), "small_s": vmem((4, width // 512, 8, 128), F32),
        "params": vmem((8, width), F32), "bias_row": vmem((1, ff), F32),
        "triple": vmem((4, rows, 3 * group), BF16), "probs": vmem((4, heads, rows, window), BF16),
        "attended": None, "starts": vmem((4, rows, 128), F32), "activ": None, "dgelu": None,
        "part": vmem(full, BF16), "land_a": vmem((6, half, width), BF16),
        "land_b": vmem((6, half, width), BF16),
        "branch": vmem((rows, width), F32), "middle": vmem((rows, width), F32),
        "gmid": vmem((rows, width), F32), "cot": vmem((rows, width), BF16),
        "gtri": None, "gatt": vmem((4, rows, group), BF16), "dkt": vmem((group, length), F32),
        "dvt": vmem((group, length), F32),
    }
    for name, (tall, wide) in pieces.items():
        scratch["gw_" + name] = vmem((n_f if inside else 1, tall if inside else 16, wide), BF16)
    for name, (tall, wide) in pieces.items():
        scratch["lp_" + name] = vmem((n_f // 2 if inside else 1, tall if inside else 16, wide), BF16)
    for name, (tall, wide) in pieces.items():
        scratch["lz_" + name] = vmem((n_f // 2 if inside else 1, tall if inside else 16, wide), BF16)
    scratch["fin_qkv"] = vmem((group // 128, 4, high, 384), BF16)
    scratch["land_qkv"] = vmem((group // 128, 4, high, 384), BF16)
    scratch["small_sum"] = vmem((16, 128 if inside else width), F32)
    tiles = width // 512
    scratch["sg_s"] = vmem((4, tiles, 8, 128), F32)
    scratch["sg_land_s"] = vmem((3, tiles, 8, 128), F32)
    scratch["sg_f"] = vmem((n_f if inside else 1, 16, 128), F32)
    scratch["sg_land_f"] = vmem((n_f - 1 if inside else 1, 16, 128), F32)
    for name, shape in (
        ("ag_send", (4, 6)), ("ag_recv", (4, 6)), ("rs_send", (4, 6)), ("rs_recv", (4, 6)),
        ("w_send", (5, 4)), ("w_recv", (5, 3)), ("p_send", (5, 4)), ("p_recv", (5, 4)),
        ("col_send", (3, n_cut)), ("col_recv", (3, n_cut)), ("col_local", (n_cut,)),
        ("upc_send", (3,)), ("upc_recv", (3,)), ("seg_send", (3,)), ("seg_recv", (3,)),
        ("sf_send", (8,)), ("sf_recv", (8,)), ("ss_send", (3,)), ("ss_recv", (3,)),
        ("loc_sem", (7,)), ("o_sem", (16,)),
        ("gp_send", (5, 4)), ("gp_recv", (5, 4)), ("gz_send", (5, 4)), ("gz_recv", (5, 4)),
        ("gc_send", (3, 2)), ("gc_recv", (3, 2)), ("gu_send", (3,)), ("gu_recv", (3,)),
        ("ts_send", (3,)), ("ts_recv", (3,)), ("tf_send", (8,)), ("tf_recv", (8,)),
    ):
        scratch[name] = dma(shape)
    scratch["turn"] = pltpu.SemaphoreType.REGULAR
    scratch["small_raw"] = vmem((8, 1, high), BF16)
    scratch["bias_raw"] = vmem((1, up_bias.shape[0]), BF16)
    scratch["small_rows"] = vmem((8, high), F32)
    scratch["small_tile"] = vmem((16, 128), F32)
    scratch["raw_sem"] = dma((9,))
    outs = {
        "result": ((rows, width), BF16), "tgrad": ((rows, width), F32),
        "gqkv": ((high, n_seq * 3 * group), F32), "gout": ((high, width), F32),
        "gup": ((high, n_seq * ff), F32), "gdown": ((high_d, width), F32),
        "gsmall": ((16, 128 if inside else width), F32),
    }
    if inside:
        for name, shape in saved.items():
            scratch[name] = vmem(*shape)
        extra = []
    else:
        extra = list(saved)
    names = list(scratch)

    def kernel(*refs):
        n_in = 7 + len(small)
        given = (*refs[:2], refs[2 : 2 + len(small)], *refs[2 + len(small) : n_in])
        made = refs[n_in : n_in + len(outs)]
        more = dict(zip(extra, refs[n_in + len(outs) :]))
        rest = refs[n_in + len(outs) + len(extra) :]
        more.update(zip([n for n in names if scratch[n] is not None], rest))
        layer_kernel(inside, n_f, *given, *made, *[more[n] for n in names])

    shapes = [*outs.values(), *[saved[n] for n in extra]]
    made = pl.pallas_call(
        kernel,
        out_shape=[jax.ShapeDtypeStruct(*shape) for shape in shapes],
        in_specs=[anywhere] * 2 + [anywhere if inside else whole] * len(small) + [anywhere] * 5,
        out_specs=[anywhere] * len(outs) + [whole] * len(extra),
        scratch_shapes=[scratch[n] for n in names if scratch[n] is not None],
        compiler_params=pltpu.CompilerParams(
            collective_id=0, has_side_effects=True, vmem_limit_bytes=67043328
        ),
    )(tokens[0], segments, *small, cotangent[0], *weights)
    result, tgrad, gqkv, gout, gup, gdown, gsmall = made[:7]
    if inside:
        return finish(n_f, high, *made[:7])
    else:
        kept = {n: v.reshape(length, -1) for n, v in zip(extra, made[7:])}

        def turned_dot(left, right):
            return lax.dot_general(
                kept[left], kept[right], (((0,), (0,)), ((), ())), preferred_element_type=F32
            ).astype(BF16)

        def shed(value):
            return lax.psum_scatter(value, "fsdp", scatter_dimension=0, tiled=True)

        def columns_back(value, parts):
            cut = value.reshape(n_seq, n_f, high, -1).transpose(1, 0, 2, 3)
            cut = lax.all_to_all(shed(cut)[0], "seq", split_axis=0, concat_axis=0, tiled=True)
            cut = cut.reshape(n_seq, high, -1, parts, 128).transpose(1, 3, 0, 2, 4)
            return cut.reshape(high, -1).astype(F32)

        gqkv = columns_back(turned_dot("normed", "gtri"), 3)
        gout = shed(turned_dot("attended", "gbr")).astype(F32)
        gup = columns_back(turned_dot("inner", "dgelu"), 1)
        gdown = shed(turned_dot("activ", "gmix")).astype(F32)
        vectors = lax.psum_scatter(gsmall[:8], ("seq", "fsdp"), scatter_dimension=1, tiled=True)
        gbias = shed(gsmall[8, :ff])
    return (result[None], tgrad[None], gqkv, gout, gup, gbias, gdown, *vectors)


def solution(mesh):
    rows = P(("seq", "fsdp"), None)
    vector = P(("seq", "fsdp"))
    acts = P("fsdp", "seq", None)
    return jax.shard_map(
        partial(on_device, mesh.shape["seq"], mesh.shape["fsdp"]),
        mesh=mesh,
        in_specs=(acts, P("fsdp", "seq"), rows, rows, rows, vector, rows, *(vector,) * 8, acts),
        out_specs=(acts, acts, rows, rows, rows, vector, rows, *(vector,) * 8),
        check_vma=False,
    )
```
